32 devices in a mesh: ctx: 8 (over z, core), fsdp: 4 (over y, x).
Axes of the slice: x: 2, y: 2, z: 4, core: 2. Of those that a mesh axis runs over, the one named last changes fastest.
Arguments:
- hidden_in: bfloat16 [4, 2048, 2048], P('fsdp', 'ctx'), may hold values from -6 to 6
- weight_query: bfloat16 [2048, 2048], P('fsdp'), may hold values from -0.125 to 0.125
- key_weight_matrix: bfloat16 [2048, 1024], P('fsdp'), may hold values from -0.125 to 0.125
- weight_value: bfloat16 [2048, 1024], P('fsdp'), may hold values from -0.125 to 0.125
- weight_out: bfloat16 [2048, 2048], P(None, 'fsdp'), may hold values from -0.5 to 0.5
- weight_gate: bfloat16 [2048, 6144], P('fsdp'), may hold values from -0.125 to 0.125
- weight_up: bfloat16 [2048, 6144], P('fsdp'), may hold values from -0.125 to 0.125
- weight_down: bfloat16 [6144, 2048], P(None, 'fsdp'), may hold values from -0.078125 to 0.078125
- gain_attention: bfloat16 [2048], P('fsdp'), may hold values from 0.5 to 1.5
- gain_feed: bfloat16 [2048], P('fsdp'), may hold values from 0.5 to 1.5
- gain_query: bfloat16 [128], P('fsdp'), may hold values from 0.25 to 1.75
- gain_key: bfloat16 [128], P('fsdp'), may hold values from 0.25 to 1.75
- positions: int32 [4, 2048], P('fsdp', 'ctx'), may hold values from 0 to 4095
- token_block_index: int32 [4, 2048], P('fsdp', 'ctx'), may hold values from 0 to 15, never falling along the last dimension, each value on 1 to 256 neighbouring positions
- grad_out: bfloat16 [4, 2048, 2048], P('fsdp', 'ctx'), may hold values from -6 to 6
Outputs:
- hidden_out: bfloat16 [4, 2048, 2048], P('fsdp', 'ctx')
- grad_hidden: float32 [4, 2048, 2048], P('fsdp', 'ctx')
- grad_weight_query: float32 [2048, 2048], P('fsdp')
- grad_weight_key: float32 [2048, 1024], P('fsdp')
- grad_weight_value: float32 [2048, 1024], P('fsdp')
- grad_weight_out: float32 [2048, 2048], P(None, 'fsdp')
- grad_weight_gate: float32 [2048, 6144], P('fsdp')
- grad_weight_up: float32 [2048, 6144], P('fsdp')
- grad_weight_down: float32 [6144, 2048], P(None, 'fsdp')
- grad_gain_attention: float32 [2048], P('fsdp')
- grad_gain_feed: float32 [2048], P('fsdp')
- grad_gain_query: float32 [128], P('fsdp')
- grad_gain_key: float32 [128], P('fsdp')
The draws below stay inside these ranges and needn't reach their ends.
Inputs may be any that keep to these rules, and one draw needn't show every extreme that they name: `token_block_index`: within each sequence the block ids never fall; each block holds 1 to 256 consecutive tokens and one holds exactly 256.
All inputs are finite; a program needn't handle non-finite values.
Results may differ from the reference program's by a relative error of at most 0.025.
Values may be sent and summed in bfloat16 or wider, within the bound.
A program may use at most 640 MiB of HBM per device.

```python
import math
import jax
import jax.numpy as jnp
import numpy as np
from jax import lax

D = 2048
QUERY_HEADS = 16
KEY_VALUE_HEADS = 8
HEAD_SIZE = 128
FF = 6144
BLOCK = 256
QW = 2048
KW = 1024
SEQUENCE_TOKENS = 2048
SEQUENCE_COUNT = 4


def touch_ends(drawn, stream_key, smallest, high):
    spot = [jax.random.randint(jax.random.fold_in(stream_key, axis), (), 0, length) for axis, length in enumerate(drawn.shape)]
    widest = drawn.shape.index(max(drawn.shape))
    next_to = spot[:widest] + [(spot[widest] + 1) % drawn.shape[widest]] + spot[widest + 1:]
    return drawn.at[tuple(spot)].set(smallest).at[tuple(next_to)].set(high)


def block_levels(key, shape, split, low, high):
    def one(dim, shards_of):
        heights = jax.random.uniform(jax.random.fold_in(jax.random.fold_in(key, 6), dim), (shards_of,), jnp.float32, low / len(split), high / len(split))
        return jnp.repeat(jnp.exp(heights), shape[dim] // shards_of).reshape((-1,) + (1,) * (len(shape) - dim - 1))

    factor_of = one(*split[0])
    for cut in split[1:]:
        factor_of = factor_of * one(*cut)
    return factor_of


def split_up(amount, total, most, lean):
    weights = [(1 << 20) // math.isqrt(grade ** lean) + 1 for grade in range(2, amount + 1)]
    rest, given = total - most - (amount - 1), [1] * (amount - 1)
    while rest > 0:
        candidates = [i for i in range(amount - 1) if given[i] < most]
        whole, remaining = sum([weights[i] for i in candidates]), rest
        for i in candidates:
            addition = min(most - given[i], max(1, remaining * weights[i] // whole), rest)
            given[i] = given[i] + addition
            rest = rest - addition
    return np.array([most] + given)


def uneven(stream_key, amount, total, reach, slope):
    if amount == 2:
        one = jax.random.randint(stream_key, (), max(1, total - reach), min(reach, total - 1) + 1)
        return jnp.stack([one, total - one])
    sizes = jnp.asarray(split_up(amount, total, reach, slope), jnp.int32)
    pairs = (amount - 1) // 2
    source_of, taker = sizes[1:1 + 2 * pairs:2], sizes[2:2 + 2 * pairs:2]
    room = jnp.minimum(source_of - 1, reach - taker)
    passed = jax.random.randint(jax.random.fold_in(stream_key, 1), (pairs,), 0, 1 << 20) % (room + 1)
    sizes = sizes.at[1:1 + 2 * pairs:2].set(source_of - passed).at[2:2 + 2 * pairs:2].set(taker + passed)
    return sizes[jax.random.permutation(jax.random.fold_in(stream_key, 2), amount)]


def centred(own_key, shape, deviation, most, shards=(), held_as=jnp.bfloat16):
    drawn = deviation * jax.random.normal(own_key, shape, jnp.float32)
    if shards:
        drawn = drawn * block_levels(own_key, shape, shards, -0.22, 0.18)
    return jnp.clip(drawn, -most, most).astype(held_as)


def setup_inputs(seed: int = 0) -> dict:
    key_list = jax.random.split(jax.random.key(seed), 16)
    return {
        "hidden_in": centred(key_list[0], (SEQUENCE_COUNT, SEQUENCE_TOKENS, D), 1.0, 6.0, ((0, 4), (1, 8))),
        "weight_query": centred(key_list[1], (D, QW), D ** -0.5, 0.125, ((0, 4),)),
        "key_weight_matrix": centred(key_list[2], (D, KW), D ** -0.5, 0.125, ((0, 4),)),
        "weight_value": centred(key_list[3], (D, KW), D ** -0.5, 0.125, ((0, 4),)),
        "weight_out": centred(key_list[4], (QW, D), (QW // 16) ** -0.5, 0.5, ((1, 4),)),
        "weight_gate": centred(key_list[5], (D, FF), D ** -0.5, 0.125, ((0, 4),)),
        "weight_up": centred(key_list[6], (D, FF), D ** -0.5, 0.125, ((0, 4),)),
        "weight_down": centred(key_list[7], (FF, D), FF ** -0.5, 0.078125, ((1, 4),)),
        "gain_attention": jnp.clip(1.0 + 0.1 * jax.random.normal(key_list[8], (D,), jnp.float32), 0.5, 1.5).astype(jnp.bfloat16),
        "gain_feed": jnp.clip(1.0 + 0.1 * jax.random.normal(key_list[9], (D,), jnp.float32), 0.5, 1.5).astype(jnp.bfloat16),
        "gain_query": jnp.clip(1.0 + 0.15 * jax.random.normal(key_list[10], (HEAD_SIZE,), jnp.float32), 0.25, 1.75).astype(jnp.bfloat16),
        "gain_key": jnp.clip(1.0 + 0.15 * jax.random.normal(key_list[11], (HEAD_SIZE,), jnp.float32), 0.25, 1.75).astype(jnp.bfloat16),
        "positions": touch_ends(jax.random.randint(key_list[12], (SEQUENCE_COUNT, SEQUENCE_TOKENS), 0, 4096), jax.random.fold_in(key_list[12], 1), 0, 4095).astype(jnp.int32),
        "token_block_index": jax.vmap(lambda own: jnp.searchsorted(jnp.cumsum(uneven(own, 2 * SEQUENCE_TOKENS // BLOCK, SEQUENCE_TOKENS, BLOCK, 0)), jnp.arange(SEQUENCE_TOKENS), side="right"))(jax.random.split(key_list[13], SEQUENCE_COUNT)).reshape((SEQUENCE_COUNT, SEQUENCE_TOKENS)).astype(jnp.int32),
        "grad_out": centred(key_list[14], (SEQUENCE_COUNT, SEQUENCE_TOKENS, D), 1.0, 6.0, ((0, 4), (1, 8))),
    }


@jax.custom_vjp
def low(v):
    return lax.optimization_barrier(v.astype(jnp.bfloat16)).astype(jnp.float32)

@jax.custom_vjp
def lowered_backward(v):
    return v

def low_keep(v):
    return (low(v), None)

def low_pass(kept, grad):
    return (grad,)

def back_keep(v):
    return (v, None)

def back_low(kept, grad):
    return (low(grad),)
low.defvjp(low_keep, low_pass)
lowered_backward.defvjp(back_keep, back_low)
EPS = 1e-06
THETA = 1000000.0
NEGATIVE_LARGE = -1e+30

def matrix_multiply(left, right):
    return jnp.dot(left, right, precision=lax.Precision.HIGHEST, preferred_element_type=jnp.float32)

def rms_scale(value, gain):
    return value * lax.rsqrt(lax.optimization_barrier(jnp.mean(value * value, axis=-1, keepdims=True)) + EPS) * gain

def tables(positions):
    half = HEAD_SIZE // 2
    freq = THETA ** (-(jnp.arange(half).astype(jnp.float32) * 2.0 / HEAD_SIZE))
    angle = positions.astype(jnp.float32)[..., None] * freq
    return (jnp.cos(angle), jnp.sin(angle))

def rotary(value, cosine_table, sine_table):
    half = value.shape[-1] // 2
    first = value[..., :half]
    second = value[..., half:]
    return jnp.concatenate([first * cosine_table - second * sine_table, second * cosine_table + first * sine_table], axis=-1)

def attend_block(query_matrix, key_row_values, value_row_values, query_ids, key_ids):
    scores = jnp.einsum('qgrd,kgd->qgrk', query_matrix, key_row_values, precision=lax.Precision.HIGHEST)
    scores = lowered_backward(scores)
    allowed = (key_ids[None, :] <= query_ids[:, None])[:, None, None, :]
    scores = jnp.where(allowed, scores, NEGATIVE_LARGE)
    largest = lax.optimization_barrier(jnp.max(scores, axis=-1, keepdims=True))
    expon = jnp.where(allowed, jnp.exp(scores - largest), 0.0)
    weights = expon / lax.optimization_barrier(jnp.sum(expon, axis=-1, keepdims=True))
    return jnp.einsum('qgrk,kgd->qgrd', low(weights), value_row_values, precision=lax.Precision.HIGHEST)

def attend_one_sequence(items):
    query_matrix, key_row_values, value_row_values, seq_ids = items
    block = min(512, SEQUENCE_TOKENS)
    token_count = SEQUENCE_TOKENS // block
    query_blocks = query_matrix.reshape((token_count, block) + query_matrix.shape[1:])
    id_blocks = seq_ids.reshape(token_count, block)

    def one_block(pair):
        return attend_block(pair[0], key_row_values, value_row_values, pair[1], seq_ids)
    result = lax.map(jax.checkpoint(one_block), (query_blocks, id_blocks))
    return result.reshape(SEQUENCE_TOKENS, QUERY_HEADS * HEAD_SIZE)

def layer(hidden, weight_query, key_weight_matrix, weight_value, weight_out, weight_gate, weight_up, weight_down, gain_attention, gain_feed, gain_query, gain_key, positions, token_block_index):
    token_inputs = SEQUENCE_COUNT * SEQUENCE_TOKENS
    query_group = QUERY_HEADS // KEY_VALUE_HEADS
    normed = low(rms_scale(hidden, gain_attention))
    flatten_heads = normed.reshape(token_inputs, D)
    cosine_table, sine_table = tables(positions)
    cosine_table = cosine_table.reshape(token_inputs, 1, HEAD_SIZE // 2)
    sine_table = sine_table.reshape(token_inputs, 1, HEAD_SIZE // 2)
    query_proj = lowered_backward(matrix_multiply(flatten_heads, weight_query)).reshape(token_inputs, QUERY_HEADS, HEAD_SIZE)
    query_matrix = low(rotary(rms_scale(query_proj, gain_query), cosine_table, sine_table) * HEAD_SIZE ** (-0.5))
    key_projected = lowered_backward(matrix_multiply(flatten_heads, key_weight_matrix)).reshape(token_inputs, KEY_VALUE_HEADS, HEAD_SIZE)
    key_row_values = low(rotary(rms_scale(key_projected, gain_key), cosine_table, sine_table))
    value_row_values = low(lowered_backward(matrix_multiply(flatten_heads, weight_value)))
    mixed_heads = lax.map(attend_one_sequence, (query_matrix.reshape(SEQUENCE_COUNT, SEQUENCE_TOKENS, KEY_VALUE_HEADS, query_group, HEAD_SIZE), key_row_values.reshape(SEQUENCE_COUNT, SEQUENCE_TOKENS, KEY_VALUE_HEADS, HEAD_SIZE), value_row_values.reshape(SEQUENCE_COUNT, SEQUENCE_TOKENS, KEY_VALUE_HEADS, HEAD_SIZE), token_block_index))
    context = low(lowered_backward(mixed_heads.reshape(token_inputs, QUERY_HEADS * HEAD_SIZE)))
    attention_out = lowered_backward(matrix_multiply(context, weight_out))
    middle = hidden.reshape(token_inputs, D) + attention_out
    normed_two = low(rms_scale(middle, gain_feed))
    gate = lowered_backward(matrix_multiply(normed_two, weight_gate))
    upward = lowered_backward(matrix_multiply(normed_two, weight_up))
    activation = low(gate * jax.nn.sigmoid(gate) * upward)
    return (middle + matrix_multiply(activation, weight_down)).reshape(SEQUENCE_COUNT, SEQUENCE_TOKENS, D)

def reference(hidden_in, weight_query, key_weight_matrix, weight_value, weight_out, weight_gate, weight_up, weight_down, gain_attention, gain_feed, gain_query, gain_key, positions, token_block_index, grad_out):
    floats = tuple((item.astype(jnp.float32) for item in (hidden_in, weight_query, key_weight_matrix, weight_value, weight_out, weight_gate, weight_up, weight_down, gain_attention, gain_feed, gain_query, gain_key)))

    def forward(*params):
        return layer(*params, positions, token_block_index)
    result, pullback = jax.vjp(forward, *floats)
    grads = pullback(grad_out.astype(jnp.float32))
    return (result.astype(jnp.bfloat16), grads[0], grads[1], grads[2], grads[3], grads[4], grads[5], grads[6], grads[7], grads[8], grads[9], grads[10], grads[11])
```

```python
import jax
import jax.numpy as jnp
from jax import lax
from jax.sharding import PartitionSpec as P

D = 2048
QUERY_HEADS = 16
KEY_VALUE_HEADS = 8
HEAD_SIZE = 128
FF = 6144
EPS = 1e-06
THETA = 1000000.0
F32 = jnp.float32
BF16 = jnp.bfloat16


def dot(left, right):
    return jnp.dot(left, right, preferred_element_type=F32)


def tdot(left, right):
    return lax.dot_general(left, right, (((0,), (0,)), ((), ())), preferred_element_type=F32)


def rdot(left, right):
    return lax.dot_general(left, right, (((1,), (1,)), ((), ())), preferred_element_type=F32)


def tables(positions):
    half = HEAD_SIZE // 2
    freq = THETA ** (-(jnp.arange(half).astype(F32) * 2.0 / HEAD_SIZE))
    angle = positions.astype(F32)[..., None] * freq
    return jnp.cos(angle), jnp.sin(angle)


def rotary(value, cosine, sine):
    half = value.shape[-1] // 2
    first, second = value[..., :half], value[..., half:]
    return jnp.concatenate(
        [first * cosine - second * sine, second * cosine + first * sine], axis=-1
    )


def reverse_rotation(grad, cosine, sine):
    return rotary(grad, cosine, -sine)


def rms_forward(value, gain):
    inverse = lax.rsqrt(jnp.mean(value * value, axis=-1, keepdims=True) + EPS)
    return value * inverse * gain, inverse


def rms_backward(value, inverse, gain, grad):
    scaled = grad * gain
    inner = jnp.mean(scaled * value, axis=-1, keepdims=True)
    return inverse * scaled - value * inverse * inverse * inverse * inner, grad * value * inverse


def gather_ctx(piece):
    return lax.all_gather(piece, "ctx", axis=0, tiled=True)


def scatter_ctx(partial):
    return lax.psum_scatter(partial.astype(BF16), "ctx", scatter_dimension=0, tiled=True)


def own_columns(array, index, width):
    return lax.dynamic_slice_in_dim(array, index * width, width, axis=1)


def own_rows(array, index, width):
    return lax.dynamic_slice_in_dim(array, index * width, width, axis=0)


def local(
    hidden_in,
    weight_query,
    key_weight_matrix,
    weight_value,
    weight_out,
    weight_gate,
    weight_up,
    weight_down,
    gain_attention,
    gain_feed,
    gain_query,
    gain_key,
    positions,
    token_block_index,
    grad_out,
):
    parts = lax.axis_size("ctx")
    shards = lax.axis_size("fsdp")
    me = lax.axis_index("ctx")
    shard = lax.axis_index("fsdp")
    heads = QUERY_HEADS // parts
    sharers = parts // KEY_VALUE_HEADS
    key_head = me // sharers
    query_width = heads * HEAD_SIZE
    feed_width = FF // parts
    rows = D // shards
    scale = HEAD_SIZE ** (-0.5)

    def gather_rows(piece):
        return lax.all_gather(piece, "fsdp", axis=0, tiled=True)

    def gather_columns(piece):
        return lax.all_gather(piece, "fsdp", axis=1, tiled=True)

    gains = lax.all_gather(
        jnp.concatenate([gain_attention, gain_feed, gain_query, gain_key]), "fsdp", axis=0
    ).astype(F32)
    head_rows = HEAD_SIZE // shards
    norm_attention = gains[:, :rows].reshape(-1)
    norm_feed = gains[:, rows : 2 * rows].reshape(-1)
    norm_query = gains[:, 2 * rows : 2 * rows + head_rows].reshape(-1)
    norm_key = gains[:, 2 * rows + head_rows :].reshape(-1)

    qkv_weight = gather_rows(
        jnp.concatenate(
            [
                own_columns(weight_query, me, query_width),
                own_columns(key_weight_matrix, key_head, HEAD_SIZE),
                own_columns(weight_value, key_head, HEAD_SIZE),
            ],
            axis=1,
        )
    )
    out_weight = gather_columns(own_rows(weight_out, me, query_width))
    gate_weight = gather_rows(own_columns(weight_gate, me, feed_width))
    up_weight = gather_rows(own_columns(weight_up, me, feed_width))
    down_weight = gather_columns(own_rows(weight_down, me, feed_width))

    whole = lax.all_gather(jnp.stack([positions[0], token_block_index[0]]), "ctx", axis=1, tiled=True)
    cosine, sine = tables(whole[0])
    ids = whole[1]
    cosine = cosine[:, None, :]
    sine = sine[:, None, :]
    tokens = ids.shape[0]

    residual = hidden_in[0].astype(F32)
    normed, inverse_one = rms_forward(residual, norm_attention)
    normed_all = gather_ctx(normed.astype(BF16))
    grad_out_all = gather_ctx(grad_out[0])

    projected = dot(normed_all, qkv_weight)
    query_proj = projected[:, :query_width].reshape(tokens, heads, HEAD_SIZE)
    key_proj = projected[:, query_width : query_width + HEAD_SIZE].reshape(tokens, 1, HEAD_SIZE)
    values = projected[:, query_width + HEAD_SIZE :].astype(BF16)
    query_normed, inverse_query = rms_forward(query_proj, norm_query)
    queries = (rotary(query_normed, cosine, sine) * scale).astype(BF16)
    key_normed, inverse_key = rms_forward(key_proj, norm_key)
    keys = rotary(key_normed, cosine, sine).astype(BF16)[:, 0]

    allowed = (ids[None, :] <= ids[:, None])[:, None, :]
    scores = jnp.einsum("qrd,kd->qrk", queries, keys, preferred_element_type=F32)
    expon = jnp.where(allowed, jnp.exp(scores), 0.0)
    total = jnp.sum(expon, axis=-1)
    context = (
        jnp.einsum("qrk,kd->qrd", expon.astype(BF16), values, preferred_element_type=F32)
        / total[..., None]
    ).astype(BF16)

    middle = residual + scatter_ctx(dot(context.reshape(tokens, query_width), out_weight)).astype(F32)
    normed_two, inverse_two = rms_forward(middle, norm_feed)
    normed_two_all = gather_ctx(normed_two.astype(BF16))

    gate = dot(normed_two_all, gate_weight)
    up = dot(normed_two_all, up_weight)
    sigma = jax.nn.sigmoid(gate)
    activation = (gate * sigma * up).astype(BF16)
    grad_act = rdot(grad_out_all, down_weight)
    grad_gate = (grad_act * up * sigma * (1.0 + gate * (1.0 - sigma))).astype(BF16)
    grad_up = (grad_act * gate * sigma).astype(BF16)
    grad_normed_two = scatter_ctx(rdot(grad_gate, gate_weight) + rdot(grad_up, up_weight)).astype(F32)
    hidden_out = (middle + scatter_ctx(dot(activation, down_weight)).astype(F32)).astype(BF16)

    def sum_rows(grad):
        return lax.psum_scatter(grad.astype(BF16), "fsdp", scatter_dimension=0, tiled=True)

    feed_shard = sum_rows(
        jnp.concatenate(
            [
                tdot(normed_two_all, grad_gate),
                tdot(normed_two_all, grad_up),
                tdot(grad_out_all, activation),
            ],
            axis=1,
        )
    )
    feed_all = lax.all_gather(feed_shard, "ctx", axis=0)

    back_two, gain_two_terms = rms_backward(middle, inverse_two, norm_feed, grad_normed_two)
    grad_middle = grad_out[0].astype(F32) + back_two
    grad_attention_all = gather_ctx(grad_middle.astype(BF16))
    context_grad = rdot(grad_attention_all, out_weight).astype(BF16).reshape(tokens, heads, HEAD_SIZE)
    delta = jnp.sum(context_grad.astype(F32) * context.astype(F32), axis=-1)
    probs = expon / total[..., None]
    grad_probs = jnp.einsum("qrd,kd->qrk", context_grad, values, preferred_element_type=F32)
    grad_scores = (probs * (grad_probs - delta[..., None])).astype(BF16)
    grad_values = jnp.einsum(
        "qrk,qrd->kd", probs.astype(BF16), context_grad, preferred_element_type=F32
    )
    grad_keys = jnp.einsum("qrk,qrd->kd", grad_scores, queries, preferred_element_type=F32)
    grad_queries = jnp.einsum("qrk,kd->qrd", grad_scores, keys, preferred_element_type=F32)

    back_query, query_gain_terms = rms_backward(
        query_proj, inverse_query, norm_query, reverse_rotation(grad_queries * scale, cosine, sine)
    )
    back_key, key_gain_terms = rms_backward(
        key_proj, inverse_key, norm_key, reverse_rotation(grad_keys[:, None], cosine, sine)
    )
    grad_qkv = jnp.concatenate(
        [
            back_query.reshape(tokens, query_width).astype(BF16),
            back_key[:, 0].astype(BF16),
            grad_values.astype(BF16),
        ],
        axis=1,
    )
    grad_normed_one = scatter_ctx(rdot(grad_qkv, qkv_weight)).astype(F32)
    back_one, gain_one_terms = rms_backward(residual, inverse_one, norm_attention, grad_normed_one)
    grad_hidden = grad_middle + back_one

    attention_shard = sum_rows(
        jnp.concatenate(
            [
                tdot(normed_all, grad_qkv),
                tdot(grad_attention_all, context.reshape(tokens, query_width)),
            ],
            axis=1,
        )
    )
    attention_all = lax.all_gather(attention_shard, "ctx", axis=0)

    gain_totals = lax.psum(
        jnp.concatenate(
            [
                jnp.sum(gain_one_terms, axis=0),
                jnp.sum(gain_two_terms, axis=0),
                jnp.sum(query_gain_terms, axis=(0, 1)),
                jnp.sum(key_gain_terms, axis=(0, 1)),
            ]
        ),
        ("ctx", "fsdp"),
    )

    def columns(stacked):
        return stacked.astype(F32).transpose(1, 0, 2).reshape(rows, -1)

    def key_columns(stacked):
        summed = stacked.astype(F32).reshape(KEY_VALUE_HEADS, sharers, rows, HEAD_SIZE).sum(axis=1)
        return summed.transpose(1, 0, 2).reshape(rows, -1)

    def as_rows(stacked):
        return stacked.astype(F32).transpose(0, 2, 1).reshape(-1, rows)

    first, second = query_width, query_width + HEAD_SIZE
    third = second + HEAD_SIZE
    return (
        hidden_out[None],
        grad_hidden[None],
        columns(attention_all[:, :, :first]),
        key_columns(attention_all[:, :, first:second]),
        key_columns(attention_all[:, :, second:third]),
        as_rows(attention_all[:, :, third:]),
        columns(feed_all[:, :, :feed_width]),
        columns(feed_all[:, :, feed_width : 2 * feed_width]),
        as_rows(feed_all[:, :, 2 * feed_width :]),
        lax.dynamic_slice_in_dim(gain_totals, shard * rows, rows),
        lax.dynamic_slice_in_dim(gain_totals, D + shard * rows, rows),
        lax.dynamic_slice_in_dim(gain_totals, 2 * D + shard * head_rows, head_rows),
        lax.dynamic_slice_in_dim(gain_totals, 2 * D + HEAD_SIZE + shard * head_rows, head_rows),
    )


def solution(mesh):
    tokens = P("fsdp", "ctx", None)
    by_rows = P("fsdp", None)
    by_columns = P(None, "fsdp")
    per_token = P("fsdp", "ctx")
    vector = P("fsdp")
    weights = (by_rows, by_rows, by_rows, by_columns, by_rows, by_rows, by_columns)
    return jax.shard_map(
        local,
        mesh=mesh,
        in_specs=(tokens, *weights, vector, vector, vector, vector, per_token, per_token, tokens),
        out_specs=(tokens, tokens, *weights, vector, vector, vector, vector),
        check_vma=False,
    )
```

```python
import functools

import jax
import jax.numpy as jnp
from jax import lax
from jax.experimental import pallas as pl
from jax.experimental.pallas import tpu as pltpu
from jax.sharding import PartitionSpec as P

D = 2048
QUERY_HEADS = 16
KEY_VALUE_HEADS = 8
HEAD_SIZE = 128
FF = 6144
EPS = 1e-06
THETA = 1000000.0
F32 = jnp.float32
BF16 = jnp.bfloat16
MESH = pl.DeviceIdType.MESH
VMEM = pltpu.VMEM
WHOLE = pl.BlockSpec(memory_space=pltpu.VMEM)
HBM = pl.BlockSpec(memory_space=pl.ANY)
CHUNKS = 4
WIDE = D // CHUNKS


def dot(left, right):
    return jnp.dot(left, right, preferred_element_type=F32)


def tdot(left, right):
    return lax.dot_general(left, right, (((0,), (0,)), ((), ())), preferred_element_type=F32)


def rdot(left, right):
    return lax.dot_general(left, right, (((1,), (1,)), ((), ())), preferred_element_type=F32)


def loop(count, body):
    def step(index, carry):
        body(index)
        return carry

    lax.fori_loop(0, count, step, 0)


def line_position():
    me = lax.axis_index("ctx")
    return me, me // 2, me % 2, lax.axis_size("ctx") // 2


def send(source, target, send_sem, recv_sem, axis, index):
    return pltpu.make_async_remote_copy(
        src_ref=source,
        dst_ref=target,
        send_sem=send_sem,
        recv_sem=recv_sem,
        device_id={axis: index},
        device_id_type=MESH,
    )


def line_barrier():
    me, chip, core, chips = line_position()
    barrier = pltpu.get_barrier_semaphore()

    def greet(index):
        pl.semaphore_signal(barrier, inc=1, device_id={"ctx": index}, device_id_type=MESH)

    greet(me + 1 - 2 * core)

    @pl.when(chip > 0)
    def _():
        greet(me - 2)

    @pl.when(chip < chips - 1)
    def _():
        greet(me + 2)

    peers = 1 + (chip > 0).astype(jnp.int32) + (chip < chips - 1).astype(jnp.int32)
    pl.semaphore_wait(barrier, peers)


def peers_of(axis):
    me, size = lax.axis_index(axis), lax.axis_size(axis)
    return size - 1, lambda i: (me + i + 1) % size, lambda i: (me + size - i - 1) % size


def full_barrier():
    barrier = pltpu.get_barrier_semaphore()
    total = 0
    for axis in ("fsdp", "ctx"):
        count, ahead, _ = peers_of(axis)
        loop(
            count,
            lambda i, axis=axis, ahead=ahead: pl.semaphore_signal(
                barrier, inc=1, device_id={axis: ahead(i)}, device_id_type=MESH
            ),
        )
        total += count
    pl.semaphore_wait(barrier, total)


def gather_scratch(chips):
    return [pltpu.SemaphoreType.DMA((chips,)) for _ in range(6)]


class Gather:
    def __init__(self, land, sems, consume=None, late=False):
        self.late = late
        self.land = land
        self.sems = sems
        self.consume = consume
        self.me, self.chip, self.core, self.chips = line_position()

    def right(self, step, source):
        ref = self.land.at[2 * source + self.core]
        return send(ref, ref, self.sems[0].at[step], self.sems[1].at[step], "ctx", self.me + 2)

    def left(self, step, source):
        ref = self.land.at[2 * source + self.core]
        return send(ref, ref, self.sems[2].at[step], self.sems[3].at[step], "ctx", self.me - 2)

    def across(self, source, core):
        ref = self.land.at[2 * source + core]
        other = self.me + 1 - 2 * self.core
        return send(ref, ref, self.sems[4].at[source], self.sems[5].at[source], "ctx", other)

    def step(self, step):
        chip, core, chips = self.chip, self.core, self.chips
        low, high = chip - step, chip + step
        has_low = low >= 0
        has_high = jnp.logical_and(high < chips, step > 0)

        @pl.when(jnp.logical_and(has_low, step > 0))
        def _():
            self.right(step - 1, low).wait_recv()

        @pl.when(jnp.logical_and(has_low, chip < chips - 1))
        def _():
            self.right(step, low).start()

        @pl.when(has_high)
        def _():
            self.left(step - 1, high).wait_recv()

        @pl.when(jnp.logical_and(high < chips, chip > 0))
        def _():
            self.left(step, high).start()

        @pl.when(has_low)
        def _():
            self.across(low, core).start()

        @pl.when(has_high)
        def _():
            self.across(high, core).start()

        if not self.late:
            self.use(step)
            return

        @pl.when(step > 0)
        def _():
            self.use(step - 1)

        @pl.when(step == chips - 1)
        def _():
            self.use(step)

    def use(self, step):
        chip, core, chips = self.chip, self.core, self.chips
        low, high = chip - step, chip + step

        def one(kind):
            upward = kind % 2
            crossed = kind // 2
            source = jnp.where(upward == 1, high, low)
            valid = jnp.where(upward == 1, jnp.logical_and(high < chips, step > 0), low >= 0)
            parity = jnp.where(crossed == 1, 1 - core, core)

            @pl.when(valid)
            def _():
                @pl.when(crossed == 1)
                def _():
                    self.across(source, parity).wait_recv()

                if self.consume is not None:
                    self.consume(2 * source + parity)

        loop(4, one)

    def finish(self):
        chip, core, chips = self.chip, self.core, self.chips

        def one(step):
            @pl.when(jnp.logical_and(chip - step >= 0, chip < chips - 1))
            def _():
                self.right(step, chip - step).wait_send()

            @pl.when(jnp.logical_and(chip + step < chips, chip > 0))
            def _():
                self.left(step, chip + step).wait_send()

            self.across(step, core).wait_send()

        loop(chips, one)


def scatter_scratch(chips, rows):
    buffers = [VMEM((count, CHUNKS, rows, WIDE), BF16) for count in (chips + 1, chips, chips)]
    return buffers + [pltpu.SemaphoreType.DMA((chips, CHUNKS)) for _ in range(6)]


class Scatter:
    def __init__(self, scratch, produce, total):
        self.line, self.out, self.other = scratch[:3]
        self.sems = scratch[3:]
        self.produce = produce
        self.total = total
        self.me, self.chip, self.core, self.chips = line_position()


    def right(self, step, chunk):
        ref = self.line.at[step, chunk]
        sems = self.sems
        return send(ref, ref, sems[0].at[step, chunk], sems[1].at[step, chunk], "ctx", self.me + 2)

    def left(self, step, chunk):
        ref = self.line.at[self.chips - step, chunk]
        sems = self.sems
        return send(ref, ref, sems[2].at[step, chunk], sems[3].at[step, chunk], "ctx", self.me - 2)

    def across(self, target, chunk):
        sems = self.sems
        return send(
            self.out.at[target, chunk],
            self.other.at[target, chunk],
            sems[4].at[target, chunk],
            sems[5].at[target, chunk],
            "ctx",
            self.me + 1 - 2 * self.core,
        )

    def begin(self):
        def clear(index):
            slot, chunk = index // CHUNKS, index % CHUNKS
            at_left = jnp.logical_and(self.chip == 0, slot < self.chips)
            at_right = jnp.logical_and(self.chip == self.chips - 1, slot > 0)

            @pl.when(jnp.logical_or(at_left, at_right))
            def _():
                self.line[slot, chunk] = jnp.zeros(self.line.shape[2:], BF16)

        loop((self.chips + 1) * CHUNKS, clear)

    def when_right(self, time):
        return jnp.logical_and(time >= self.chip, time < self.chips - 1)

    def when_left(self, time):
        return jnp.logical_and(time >= self.chips - 1 - self.chip, time < self.chips - 1)

    def prepare(self, time):
        def cross(target):
            def one(chunk):
                piece = 2 * target + 1 - self.core
                self.out[target, chunk] = self.produce(piece, chunk).astype(BF16)
                self.across(target, chunk).start()

            loop(CHUNKS, one)

        @pl.when(self.when_right(time))
        def _():
            cross(self.chips - 1 - time + self.chip)

        @pl.when(self.when_left(time))
        def _():
            cross(time - (self.chips - 1 - self.chip))

        @pl.when(time == self.chips - 1)
        def _():
            cross(self.chip)

    def step(self, time):
        chip, core, chips = self.chip, self.core, self.chips

        @pl.when(self.when_right(time))
        def _():
            step = time - chip
            target = chips - 1 - step

            def one(chunk):
                self.across(target, chunk).wait_recv()

                @pl.when(chip > 0)
                def _():
                    self.right(step, chunk).wait_recv()

                value = self.produce(2 * target + core, chunk) + self.other[target, chunk].astype(F32)
                value = value + self.line[step, chunk].astype(F32)
                self.line[step, chunk] = value.astype(BF16)
                self.right(step, chunk).start()

            loop(CHUNKS, one)

        @pl.when(self.when_left(time))
        def _():
            step = time - (chips - 1 - chip)

            def one(chunk):
                self.across(step, chunk).wait_recv()

                @pl.when(chip < chips - 1)
                def _():
                    self.left(step, chunk).wait_recv()

                value = self.produce(2 * step + core, chunk) + self.other[step, chunk].astype(F32)
                value = value + self.line[chips - step, chunk].astype(F32)
                self.line[chips - step, chunk] = value.astype(BF16)
                self.left(step, chunk).start()

            loop(CHUNKS, one)

    def finish(self):
        chip, core, chips = self.chip, self.core, self.chips
        last = chips - 1 - chip

        def one(chunk):
            self.across(chip, chunk).wait_recv()
            value = self.produce(2 * chip + core, chunk) + self.other[chip, chunk].astype(F32)

            @pl.when(chip > 0)
            def _():
                self.right(last, chunk).wait_recv()

            @pl.when(chip < chips - 1)
            def _():
                self.left(chip, chunk).wait_recv()

            value = value + self.line[last, chunk].astype(F32)
            value = value + self.line[chips - chip, chunk].astype(F32)
            self.total[:, pl.ds(pl.multiple_of(chunk * WIDE, WIDE), WIDE)] = value

        loop(CHUNKS, one)

        def drain(index):
            step, chunk = index // CHUNKS, index % CHUNKS

            @pl.when(step < last)
            def _():
                self.right(step, chunk).wait_send()

            @pl.when(step < chip)
            def _():
                self.left(step, chunk).wait_send()

            self.across(step, chunk).wait_send()

        loop(chips * CHUNKS, drain)


def row_blocks(rows, body, size=32):
    def one(index):
        body(pl.ds(pl.multiple_of(index * size, size), size))

    loop(rows // size, one)


def inverse_norm(value):
    return lax.rsqrt(jnp.mean(value * value, axis=-1, keepdims=True) + EPS)


def params(identity, megabytes):
    return pltpu.CompilerParams(
        collective_id=identity,
        has_side_effects=True,
        vmem_limit_bytes=megabytes * 1024 * 1024,
    )


def copy_in(source, target, sem):
    copy = pltpu.make_async_copy(source, target, sem)
    copy.start()
    return copy


def first_kernel(rows, width, *refs):
    x, gains, tokens, part, land, proj, weights, gain_rows, all_gains, all_tokens = refs[:10]
    sems, small = refs[10:16], refs[16:]
    me, _, _, chips = line_position()
    shard = lax.axis_index("fsdp")
    shards, ahead, behind = peers_of("fsdp")
    parts, next_part, past_part = peers_of("ctx")
    full_barrier()

    def gain_copy(i, slot):
        return send(gains, all_gains.at[slot], small[0].at[i], small[1].at[i], "fsdp", ahead(i))

    def token_copy(i, slot):
        return send(tokens, all_tokens.at[slot], small[2].at[i], small[3].at[i], "ctx", next_part(i))

    def weight_copy(i, owner):
        target = weights.at[pl.ds(pl.multiple_of(owner * rows, rows), rows), :]
        return send(part, target, small[4].at[i], small[5].at[i], "fsdp", ahead(i))

    loop(shards, lambda i: gain_copy(i, shard).start())
    loop(parts, lambda i: token_copy(i, me).start())
    loop(shards, lambda i: weight_copy(i, shard).start())
    all_gains[shard] = gains[...]
    all_tokens[me] = tokens[...]
    weights[pl.ds(pl.multiple_of(shard * rows, rows), rows), :] = part[...]
    loop(shards, lambda i: gain_copy(i, behind(i)).wait_recv())
    lanes = rows // 128
    for kind in range(2):
        for owner in range(shards + 1):
            for j in range(lanes):
                at = owner * rows + j * 128
                gain_rows[kind : kind + 1, at : at + 128] = all_gains[
                    owner, kind * lanes + j : kind * lanes + j + 1, :
                ]

    def norm(block):
        value = x[block, :].astype(F32)
        land[me, block] = (value * inverse_norm(value) * gain_rows[0:1, :]).astype(BF16)

    row_blocks(x.shape[0], norm)

    def consume(piece):
        proj[piece] = dot(land[piece], weights[:, :width])

    gather = Gather(land, sems, consume, late=True)

    def step(index):
        @pl.when(index == 1)
        def _():
            loop(shards, lambda i: weight_copy(i, behind(i)).wait_recv())

        gather.step(index)

    loop(chips, step)
    gather.finish()
    loop(shards, lambda i: gain_copy(i, shard).wait_send())
    loop(shards, lambda i: weight_copy(i, shard).wait_send())
    loop(parts, lambda i: token_copy(i, past_part(i)).wait_recv())
    loop(parts, lambda i: token_copy(i, me).wait_send())


def first(hidden, gains, tokens, part, shards, parts, width):
    count = hidden.shape[0]
    return pl.pallas_call(
        functools.partial(first_kernel, D // shards, width),
        out_shape=(
            jax.ShapeDtypeStruct((parts, count, D), BF16),
            jax.ShapeDtypeStruct((parts, count, width), F32),
            jax.ShapeDtypeStruct((D, part.shape[1]), BF16),
            jax.ShapeDtypeStruct((8, D), F32),
            jax.ShapeDtypeStruct((shards, *gains.shape), F32),
            jax.ShapeDtypeStruct((parts, *tokens.shape), jnp.int32),
        ),
        in_specs=[WHOLE] * 4,
        out_specs=(WHOLE,) * 6,
        scratch_shapes=gather_scratch(parts // 2)
        + [pltpu.SemaphoreType.DMA((shards,))] * 2
        + [pltpu.SemaphoreType.DMA((parts,))] * 2
        + [pltpu.SemaphoreType.DMA((shards,))] * 2,
        compiler_params=params(0, 60),
        name="gather_normed",
    )(hidden, gains, tokens, part)


def out_kernel(columns, *refs):
    context, weights, x, gain_rows, middle, normed = refs[:6]
    weight, weight_sem, total = refs[6:9]
    scratch = refs[9:]
    chips = line_position()[3]
    copy = copy_in(weights.at[:, columns], weight, weight_sem)

    def produce(piece, chunk):
        return rdot(context[piece], weight[pl.ds(pl.multiple_of(chunk * WIDE, WIDE), WIDE), :])

    scatter = Scatter(scratch, produce, total)
    scatter.begin()
    line_barrier()
    copy.wait()
    scatter.prepare(0)

    def step(time):
        scatter.step(time)
        scatter.prepare(time + 1)

    loop(chips - 1, step)
    scatter.finish()

    def norm(block):
        value = x[block, :].astype(F32) + total[block, :]
        middle[block, :] = value
        normed[block, :] = (value * inverse_norm(value) * gain_rows[1:2, :]).astype(BF16)

    row_blocks(x.shape[0], norm)


def attention_out(context, weights, hidden, gain_rows):
    parts, count, width = context.shape
    return pl.pallas_call(
        functools.partial(out_kernel, pl.ds(weights.shape[1] - width, width)),
        out_shape=(
            jax.ShapeDtypeStruct((count, D), F32),
            jax.ShapeDtypeStruct((count, D), BF16),
        ),
        in_specs=[WHOLE, HBM, WHOLE, WHOLE],
        out_specs=(WHOLE,) * 2,
        scratch_shapes=[VMEM((D, width), BF16), pltpu.SemaphoreType.DMA, VMEM((count, D), F32)]
        + scatter_scratch(parts // 2, count),
        compiler_params=params(1, 60),
        name="attention_out",
    )(context, weights, hidden, gain_rows)


def feed_kernel(width, *refs):
    x, grads, weights, land, activation, back = refs[:6]
    weight, weight_sem, grad, grad_sems = refs[6:10]
    sems = refs[10:]
    me, _, _, chips = line_position()
    copy = copy_in(weights, weight, weight_sem)

    def grad_copy(piece):
        return pltpu.make_async_copy(grads.at[piece], grad.at[piece], grad_sems.at[piece])

    loop(2 * chips, lambda piece: grad_copy(piece).start())
    land[me] = x[...]
    size = 256 if width % 256 == 0 else 128

    def consume(piece):
        grad_copy(piece).wait()

        def one(index):
            def columns(kind):
                return pl.ds(pl.multiple_of(kind * width + index * size, 128), size)

            gate = dot(land[piece], weight[:, columns(0)])
            up = dot(land[piece], weight[:, columns(1)])
            grad_act = dot(grad[piece], weight[:, columns(2)])
            sigma = 1.0 / (1.0 + jnp.exp(-gate))
            activation[piece, :, columns(0)] = (gate * sigma * up).astype(BF16)
            back[piece, :, columns(0)] = (
                grad_act * up * sigma * (1.0 + gate * (1.0 - sigma))
            ).astype(BF16)
            back[piece, :, columns(1)] = (grad_act * gate * sigma).astype(BF16)

        loop(width // size, one)

    line_barrier()
    gather = Gather(land, sems, consume)
    copy.wait()
    loop(chips, gather.step)
    gather.finish()


def feed(normed, grads, weights):
    parts, count, _ = grads.shape
    width = weights.shape[1] // 3
    return pl.pallas_call(
        functools.partial(feed_kernel, width),
        out_shape=(
            jax.ShapeDtypeStruct((parts, count, D), BF16),
            jax.ShapeDtypeStruct((parts, count, width), BF16),
            jax.ShapeDtypeStruct((parts, count, 2 * width), BF16),
        ),
        in_specs=[WHOLE, HBM, HBM],
        out_specs=(WHOLE,) * 3,
        scratch_shapes=[
            VMEM(weights.shape, BF16),
            pltpu.SemaphoreType.DMA,
            VMEM(grads.shape, BF16),
            pltpu.SemaphoreType.DMA((parts,)),
        ]
        + gather_scratch(parts // 2),
        compiler_params=params(2, 60),
        name="feed",
    )(normed, grads, weights)


def rms_back(value, gain, grad):
    inverse = inverse_norm(value)
    scaled = grad * gain
    inner = jnp.mean(scaled * value, axis=-1, keepdims=True)
    terms = grad * value * inverse
    return inverse * scaled - value * (inverse * inverse * inverse * inner), terms


def feed_back_kernel(columns, *refs):
    back, weights, middle, grad, gain_rows, grad_middle, low, gain_sum = refs[:8]
    weight, weight_sem, total = refs[8:11]
    scratch = refs[11:]
    chips = line_position()[3]
    copy = copy_in(weights.at[:, columns], weight, weight_sem)

    def produce(piece, chunk):
        return rdot(back[piece], weight[pl.ds(pl.multiple_of(chunk * WIDE, WIDE), WIDE), :])

    scatter = Scatter(scratch, produce, total)
    scatter.begin()
    line_barrier()
    copy.wait()
    scatter.prepare(0)

    def step(time):
        scatter.step(time)
        scatter.prepare(time + 1)

    loop(chips - 1, step)
    scatter.finish()
    gain_sum[...] = jnp.zeros_like(gain_sum)

    def norm(block):
        through, terms = rms_back(middle[block, :], gain_rows[1:2, :], total[block, :])
        value = grad[block, :].astype(F32) + through
        grad_middle[block, :] = value
        low[block, :] = value.astype(BF16)
        gain_sum[0:1, :] += jnp.sum(terms, axis=0, keepdims=True)

    row_blocks(middle.shape[0], norm)


def feed_back(back, weights, middle, grad, gain_rows):
    parts, count, width = back.shape
    return pl.pallas_call(
        functools.partial(feed_back_kernel, pl.ds(0, width)),
        out_shape=(
            jax.ShapeDtypeStruct((count, D), F32),
            jax.ShapeDtypeStruct((count, D), BF16),
            jax.ShapeDtypeStruct((8, D), F32),
        ),
        in_specs=[WHOLE, HBM, WHOLE, WHOLE, WHOLE],
        out_specs=(WHOLE,) * 3,
        scratch_shapes=[VMEM((D, width), BF16), pltpu.SemaphoreType.DMA, VMEM((count, D), F32)]
        + scatter_scratch(parts // 2, count),
        compiler_params=params(3, 60),
        name="feed_back",
    )(back, weights, middle, grad, gain_rows)


def turn_kernel(columns, down_columns, *refs):
    low, weights, activation, feed_weights, middle, land, context_grad, hidden = refs[:8]
    weight, weight_sem, down, down_sem, total = refs[8:13]
    gather_sems, scratch = refs[13:19], refs[19:]
    me, _, _, chips = line_position()
    copy = copy_in(weights.at[:, columns], weight, weight_sem)
    down_copy = copy_in(feed_weights.at[:, down_columns], down, down_sem)
    land[me] = low[...]

    def consume(piece):
        context_grad[piece] = dot(land[piece], weight[...]).astype(BF16)

    def produce(piece, chunk):
        return rdot(activation[piece], down[pl.ds(pl.multiple_of(chunk * WIDE, WIDE), WIDE), :])

    gather = Gather(land, gather_sems, consume)
    scatter = Scatter(scratch, produce, total)
    scatter.begin()
    line_barrier()
    copy.wait()
    down_copy.wait()
    scatter.prepare(0)

    def step(time):
        gather.step(time)
        scatter.step(time)
        scatter.prepare(time + 1)

    loop(chips - 1, step)
    gather.step(chips - 1)
    scatter.finish()
    gather.finish()

    def add(block):
        hidden[block, :] = (middle[block, :] + total[block, :]).astype(BF16)

    row_blocks(middle.shape[0], add)


def turn(low, weights, activation, feed_weights, middle, width):
    parts, count, feed_width = activation.shape
    return pl.pallas_call(
        functools.partial(
            turn_kernel, pl.ds(weights.shape[1] - width, width), pl.ds(2 * feed_width, feed_width)
        ),
        out_shape=(
            jax.ShapeDtypeStruct((parts, count, D), BF16),
            jax.ShapeDtypeStruct((parts, count, width), BF16),
            jax.ShapeDtypeStruct((count, D), BF16),
        ),
        in_specs=[WHOLE, HBM, WHOLE, HBM, WHOLE],
        out_specs=(WHOLE,) * 3,
        scratch_shapes=[
            VMEM((D, width), BF16),
            pltpu.SemaphoreType.DMA,
            VMEM((D, feed_width), BF16),
            pltpu.SemaphoreType.DMA,
            VMEM((count, D), F32),
        ]
        + gather_scratch(parts // 2)
        + scatter_scratch(parts // 2, count),
        compiler_params=params(4, 62),
        name="turn",
    )(low, weights, activation, feed_weights, middle)


def last_kernel(columns, *refs):
    back, weights, x, grad_middle, gain_rows, gain_two, gain_heads, hidden, gain_out = refs[:9]
    weight, weight_sem, total, gain_one, pack, pack_in, shard_sum, shard_in = refs[9:17]
    small, scratch = refs[17:21], refs[21:]
    chips = line_position()[3]
    copy = copy_in(weights.at[:, columns], weight, weight_sem)

    def produce(piece, chunk):
        return rdot(back[piece], weight[pl.ds(pl.multiple_of(chunk * WIDE, WIDE), WIDE), :])

    scatter = Scatter(scratch, produce, total)
    scatter.begin()
    full_barrier()
    copy.wait()
    scatter.prepare(0)

    def step(time):
        scatter.step(time)
        scatter.prepare(time + 1)

    loop(chips - 1, step)
    scatter.finish()
    gain_one[...] = jnp.zeros_like(gain_one)

    def norm(block):
        through, terms = rms_back(x[block, :].astype(F32), gain_rows[0:1, :], total[block, :])
        hidden[block, :] = grad_middle[block, :] + through
        gain_one[0:1, :] += jnp.sum(terms, axis=0, keepdims=True)

    row_blocks(x.shape[0], norm)

    shard = lax.axis_index("fsdp")
    shards, ahead, _ = peers_of("fsdp")
    parts, next_part, _ = peers_of("ctx")
    rows = D // (shards + 1)
    lanes = rows // 128
    pack[...] = jnp.zeros_like(pack)
    for owner in range(shards + 1):
        for j in range(lanes):
            at = owner * rows + j * 128
            pack[owner, j : j + 1, :] = gain_one[0:1, at : at + 128]
            pack[owner, lanes + j : lanes + j + 1, :] = gain_two[0:1, at : at + 128]
        pack[owner, 2 * lanes : 2 * lanes + 2, :] = gain_heads[0:2, :]

    def pack_copy(i):
        return send(pack.at[ahead(i)], pack_in.at[i], small[0].at[i], small[1].at[i], "fsdp", ahead(i))

    def sum_copy(i):
        return send(shard_sum, shard_in.at[i], small[2].at[i], small[3].at[i], "ctx", next_part(i))

    loop(shards, lambda i: pack_copy(i).start())
    shard_sum[...] = pack[shard]

    def add_pack(i):
        pack_copy(i).wait_recv()
        shard_sum[...] += pack_in[i]

    loop(shards, add_pack)
    loop(parts, lambda i: sum_copy(i).start())
    gain_out[...] = shard_sum[...]

    def add_sum(i):
        sum_copy(i).wait_recv()
        gain_out[...] += shard_in[i]

    loop(parts, add_sum)
    loop(shards, lambda i: pack_copy(i).wait_send())
    loop(parts, lambda i: sum_copy(i).wait_send())


def last(back, weights, hidden, grad_middle, gain_rows, gain_two, gain_heads, shards):
    parts, count, width = back.shape
    return pl.pallas_call(
        functools.partial(last_kernel, pl.ds(0, width)),
        out_shape=(
            jax.ShapeDtypeStruct((count, D), F32),
            jax.ShapeDtypeStruct((16, 128), F32),
        ),
        in_specs=[WHOLE, HBM] + [WHOLE] * 5,
        out_specs=(WHOLE,) * 2,
        scratch_shapes=[
            VMEM((D, width), BF16),
            pltpu.SemaphoreType.DMA,
            VMEM((count, D), F32),
            VMEM((8, D), F32),
            VMEM((shards, 16, 128), F32),
            VMEM((shards, 16, 128), F32),
            VMEM((16, 128), F32),
            VMEM((parts, 16, 128), F32),
        ]
        + [pltpu.SemaphoreType.DMA((shards,))] * 2
        + [pltpu.SemaphoreType.DMA((parts,))] * 2
        + scatter_scratch(parts // 2, count),
        compiler_params=params(5, 60),
        name="last",
    )(back, weights, hidden, grad_middle, gain_rows, gain_two, gain_heads)


QUERY_TILE = 256
KEY_TILE = 512


def reach(index, tokens):
    return jnp.minimum((index + 2) * QUERY_TILE + KEY_TILE - 1, tokens) // KEY_TILE


def head_norm(value, gain, cosine, sine):
    normed = value * inverse_norm(value) * gain
    return normed * cosine + pltpu.roll(normed, HEAD_SIZE // 2, 1) * sine


def attention_kernel(heads, proj, cosine, sine, gain, id_column, id_row, *refs):
    queries, keys, values, context, inverse = refs
    tokens = proj.shape[0]
    key_at = heads * HEAD_SIZE

    def prepare(index):
        block = pl.ds(pl.multiple_of(index * QUERY_TILE, QUERY_TILE), QUERY_TILE)
        c, s = cosine[block, :], sine[block, :]
        for h in range(heads):
            lanes = slice(h * HEAD_SIZE, (h + 1) * HEAD_SIZE)
            rotated = head_norm(proj[block, lanes], gain[0:1, :], c, s) * HEAD_SIZE ** (-0.5)
            queries[block, lanes] = rotated.astype(BF16)
        rotated = head_norm(proj[block, key_at : key_at + HEAD_SIZE], gain[1:2, :], c, s)
        keys[block, :] = rotated.astype(BF16)
        values[block, :] = proj[block, key_at + HEAD_SIZE : key_at + 2 * HEAD_SIZE].astype(BF16)

    loop(tokens // QUERY_TILE, prepare)

    def attend(index):
        block = pl.ds(pl.multiple_of(index * QUERY_TILE, QUERY_TILE), QUERY_TILE)
        query_ids = id_column[block, :]
        for h in range(heads):
            lanes = slice(h * HEAD_SIZE, (h + 1) * HEAD_SIZE)
            query = queries[block, lanes]

            def one(tile, carry):
                sums, total = carry
                span = pl.ds(pl.multiple_of(tile * KEY_TILE, KEY_TILE), KEY_TILE)
                scores = rdot(query, keys[span, :])
                expon = jnp.where(id_row[0:1, span] <= query_ids, jnp.exp(scores), 0.0)
                sums = sums + dot(expon.astype(BF16), values[span, :])
                return sums, total + jnp.sum(expon, axis=1, keepdims=True)

            start = (jnp.zeros((QUERY_TILE, HEAD_SIZE), F32), jnp.zeros((QUERY_TILE, 1), F32))
            sums, total = lax.fori_loop(0, reach(index, tokens), one, start)
            scale = 1.0 / total
            context[block, lanes] = (sums * scale).astype(BF16)
            inverse[h : h + 1, block] = jnp.broadcast_to(scale, (QUERY_TILE, HEAD_SIZE)).T[0:1, :]

    loop(tokens // QUERY_TILE, attend)


def attention(proj, cosine, sine, gain, id_column, id_row, heads):
    tokens = proj.shape[0]
    width = heads * HEAD_SIZE
    return pl.pallas_call(
        functools.partial(attention_kernel, heads),
        out_shape=(
            jax.ShapeDtypeStruct((tokens, width), BF16),
            jax.ShapeDtypeStruct((tokens, HEAD_SIZE), BF16),
            jax.ShapeDtypeStruct((tokens, HEAD_SIZE), BF16),
            jax.ShapeDtypeStruct((tokens, width), BF16),
            jax.ShapeDtypeStruct((8, tokens), F32),
        ),
        in_specs=[WHOLE] * 6,
        out_specs=(WHOLE,) * 5,
        compiler_params=pltpu.CompilerParams(vmem_limit_bytes=48 * 1024 * 1024),
        name="attention",
    )(proj, cosine, sine, gain, id_column, id_row)


def attention_back_kernel(heads, *refs):
    queries, keys, values, out_grad, inverse, context, proj, cosine, sine, gain = refs[:10]
    id_column, id_row, back, gain_sum, key_grad, value_grad, query_grad = refs[10:]
    tokens = proj.shape[0]
    key_at = heads * HEAD_SIZE
    key_grad[...] = jnp.zeros_like(key_grad)
    value_grad[...] = jnp.zeros_like(value_grad)
    gain_sum[...] = jnp.zeros_like(gain_sum)

    def through(block, lanes, grad, row):
        turned = pltpu.roll(grad, HEAD_SIZE // 2, 1)
        unrotated = grad * cosine[block, :] - turned * sine[block, :]
        result, terms = rms_back(proj[block, lanes], gain[row : row + 1, :], unrotated)
        back[block, lanes] = result.astype(BF16)
        gain_sum[row : row + 1, :] += jnp.sum(terms, axis=0, keepdims=True)

    def attend(index):
        block = pl.ds(pl.multiple_of(index * QUERY_TILE, QUERY_TILE), QUERY_TILE)
        query_ids = id_row[0:1, block]
        for h in range(heads):
            lanes = slice(h * HEAD_SIZE, (h + 1) * HEAD_SIZE)
            query = queries[block, lanes]
            grad = out_grad[block, lanes]
            scale = inverse[h : h + 1, block]
            products = grad.astype(F32) * context[block, lanes].astype(F32)
            shift = lax.dot_general(
                jnp.ones((8, HEAD_SIZE), F32),
                products,
                (((1,), (1,)), ((), ())),
                precision=lax.Precision.HIGHEST,
                preferred_element_type=F32,
            )[0:1, :]
            query_grad[...] = jnp.zeros_like(query_grad)

            def one(tile):
                span = pl.ds(pl.multiple_of(tile * KEY_TILE, KEY_TILE), KEY_TILE)
                key = keys[span, :]
                scores = rdot(key, query)
                probs = jnp.where(id_column[span, :] <= query_ids, jnp.exp(scores) * scale, 0.0)
                grad_scores = (probs * (rdot(values[span, :], grad) - shift)).astype(BF16)
                value_grad[span, :] += dot(probs.astype(BF16), grad)
                key_grad[span, :] += dot(grad_scores, query)
                query_grad[...] += tdot(grad_scores, key)

            loop(reach(index, tokens), one)
            through(block, lanes, query_grad[...] * HEAD_SIZE ** (-0.5), 0)

    loop(tokens // QUERY_TILE, attend)

    def finish(index):
        block = pl.ds(pl.multiple_of(index * QUERY_TILE, QUERY_TILE), QUERY_TILE)
        through(block, slice(key_at, key_at + HEAD_SIZE), key_grad[block, :], 1)
        back[block, key_at + HEAD_SIZE : key_at + 2 * HEAD_SIZE] = value_grad[block, :].astype(BF16)

    loop(tokens // QUERY_TILE, finish)


def attention_back(heads, *operands):
    tokens = operands[0].shape[0]
    width = heads * HEAD_SIZE
    return pl.pallas_call(
        functools.partial(attention_back_kernel, heads),
        out_shape=(
            jax.ShapeDtypeStruct((tokens, width + 2 * HEAD_SIZE), BF16),
            jax.ShapeDtypeStruct((8, HEAD_SIZE), F32),
        ),
        in_specs=[WHOLE] * len(operands),
        out_specs=(WHOLE,) * 2,
        scratch_shapes=[
            VMEM((tokens, HEAD_SIZE), F32),
            VMEM((tokens, HEAD_SIZE), F32),
            VMEM((QUERY_TILE, HEAD_SIZE), F32),
        ],
        compiler_params=pltpu.CompilerParams(vmem_limit_bytes=48 * 1024 * 1024),
        name="attention_back",
    )(*operands)


def spread_kernel(source, target):
    target[...] = source[0].astype(F32)


def spread_columns(stacked):
    parts, rows, width = stacked.shape
    return pl.pallas_call(
        spread_kernel,
        out_shape=jax.ShapeDtypeStruct((rows, parts * width), F32),
        grid=(parts,),
        in_specs=[pl.BlockSpec((1, rows, width), lambda i: (i, 0, 0))],
        out_specs=pl.BlockSpec((rows, width), lambda i: (0, i)),
        compiler_params=pltpu.CompilerParams(vmem_limit_bytes=32 * 1024 * 1024),
        name="spread",
    )(stacked)


def spread_heads_kernel(width, source, query, key, value):
    query[...] = source[0, :, :width].astype(F32)
    key[...] = source[0, :, width : width + HEAD_SIZE].astype(F32)
    value[...] = source[0, :, width + HEAD_SIZE :].astype(F32)


def spread_heads(stacked, width):
    parts, rows, total = stacked.shape
    widths = (width, HEAD_SIZE, HEAD_SIZE)
    return pl.pallas_call(
        functools.partial(spread_heads_kernel, width),
        out_shape=tuple(jax.ShapeDtypeStruct((rows, parts * w), F32) for w in widths),
        grid=(parts,),
        in_specs=[pl.BlockSpec((1, rows, total), lambda i: (i, 0, 0))],
        out_specs=tuple(pl.BlockSpec((rows, w), lambda i: (0, i)) for w in widths),
        compiler_params=pltpu.CompilerParams(vmem_limit_bytes=32 * 1024 * 1024),
        name="spread_heads",
    )(stacked)


def own_columns(array, index, width):
    return lax.dynamic_slice_in_dim(array, index * width, width, axis=1)


def own_rows(array, index, width):
    return lax.dynamic_slice_in_dim(array, index * width, width, axis=0)


def local(
    hidden_in,
    weight_query,
    key_weight_matrix,
    weight_value,
    weight_out,
    weight_gate,
    weight_up,
    weight_down,
    gain_attention,
    gain_feed,
    gain_query,
    gain_key,
    positions,
    token_block_index,
    grad_out,
):
    parts = lax.axis_size("ctx")
    shards = lax.axis_size("fsdp")
    me = lax.axis_index("ctx")
    shard = lax.axis_index("fsdp")
    heads = QUERY_HEADS // parts
    sharers = parts // KEY_VALUE_HEADS
    key_head = me // sharers
    width = heads * HEAD_SIZE
    feed_width = FF // parts
    rows = D // shards
    head_rows = HEAD_SIZE // shards
    count = hidden_in.shape[1]
    tokens = parts * count

    def gather_rows(piece):
        return lax.all_gather(piece, "fsdp", axis=0, tiled=True)

    def sum_rows(grad):
        return lax.psum_scatter(grad.astype(BF16), "fsdp", scatter_dimension=0, tiled=True)

    def gather_parts(piece):
        return lax.all_gather(piece, "ctx", axis=0)

    own_heads_weight = jnp.concatenate(
        [
            own_columns(weight_query, me, width),
            own_columns(key_weight_matrix, key_head, HEAD_SIZE),
            own_columns(weight_value, key_head, HEAD_SIZE),
            own_rows(weight_out, me, width).T,
        ],
        axis=1,
    )
    feed_weight = gather_rows(
        jnp.concatenate(
            [
                own_columns(weight_gate, me, feed_width),
                own_columns(weight_up, me, feed_width),
                own_rows(weight_down, me, feed_width).T,
            ],
            axis=1,
        )
    )

    own_gains = jnp.concatenate([gain_attention, gain_feed, gain_query, gain_key]).astype(F32)
    own_gains = jnp.pad(own_gains, (0, 2048 - own_gains.shape[0])).reshape(16, 128)
    own_tokens = jnp.pad(jnp.stack([positions[0], token_block_index[0]]), ((0, 6), (0, 0)))
    hidden, grad = hidden_in[0], grad_out[0]
    normed_all, proj, heads_weight, gain_rows, gains, whole = first(
        hidden, own_gains, own_tokens, own_heads_weight, shards, parts, width + 2 * HEAD_SIZE
    )
    grad_late, gains = lax.optimization_barrier((grad, gains))
    grad_all = gather_parts(grad_late)
    flat_gains = gains.reshape(shards, -1)
    norm_query = flat_gains[:, 2 * rows : 2 * rows + head_rows].reshape(1, -1)
    norm_key = flat_gains[:, 2 * rows + head_rows : 2 * rows + 2 * head_rows].reshape(1, -1)
    head_gains = jnp.concatenate([norm_query, norm_key, jnp.zeros((6, HEAD_SIZE), F32)])

    half = HEAD_SIZE // 2
    freq = THETA ** (-(jnp.arange(half).astype(F32) * 2.0 / HEAD_SIZE))
    angle = whole[:, 0].reshape(-1).astype(F32)[:, None] * freq
    cosine, sine = jnp.cos(angle), jnp.sin(angle)
    cosine = jnp.concatenate([cosine, cosine], axis=1)
    sine = jnp.concatenate([-sine, sine], axis=1)
    ids = whole[:, 1].reshape(-1)
    id_row, id_column = ids[None, :], ids[:, None]

    proj = proj.reshape(tokens, width + 2 * HEAD_SIZE)
    queries, keys, values, context, inverse = attention(
        proj, cosine, sine, head_gains, id_column, id_row, heads
    )
    middle, normed_two = attention_out(
        context.reshape(parts, count, width), heads_weight, hidden, gain_rows
    )
    normed_two_all, activation, back = feed(normed_two, grad_all, feed_weight)

    flat_grad = grad_all.reshape(tokens, D)
    flat_back = back.reshape(tokens, 2 * feed_width)
    flat_activation = activation.reshape(tokens, feed_width)
    grad_gate_up = tdot(normed_two_all.reshape(tokens, D), flat_back).astype(BF16)
    grad_down = tdot(flat_activation, flat_grad).astype(BF16)
    back, grad_gate_up, grad_down = lax.optimization_barrier((back, grad_gate_up, grad_down))
    grad_gate_up = sum_rows(grad_gate_up)
    grad_down = sum_rows(
        grad_down.reshape(feed_width, shards, rows).transpose(1, 0, 2).reshape(shards * feed_width, rows)
    )
    gate_parts = gather_parts(grad_gate_up[:, :feed_width])
    up_parts = gather_parts(grad_gate_up[:, feed_width:])
    grad_weight_down = lax.all_gather(grad_down, "ctx", axis=0, tiled=True).astype(F32)

    grad_middle, low, gain_two = feed_back(back, feed_weight, middle, grad, gain_rows)
    low_all, context_grad, hidden_out = turn(low, heads_weight, activation, feed_weight, middle, width)

    context_grad = context_grad.reshape(tokens, width)
    grad_qkv, gain_heads = attention_back(
        heads,
        queries,
        keys,
        values,
        context_grad,
        inverse,
        context,
        proj,
        cosine,
        sine,
        head_gains,
        id_column,
        id_row,
    )
    grad_hidden, gain_sums = last(
        grad_qkv.reshape(parts, count, -1),
        heads_weight,
        hidden,
        grad_middle,
        gain_rows,
        gain_two,
        gain_heads,
        shards,
    )

    grad_heads = sum_rows(tdot(normed_all.reshape(tokens, D), grad_qkv))
    grad_out_weight = sum_rows(
        tdot(context, low_all.reshape(tokens, D))
        .astype(BF16)
        .reshape(width, shards, rows)
        .transpose(1, 0, 2)
        .reshape(shards * width, rows)
    )
    head_parts = gather_parts(grad_heads)
    grad_weight_out = lax.all_gather(grad_out_weight, "ctx", axis=0, tiled=True).astype(F32)

    gain_sums = gain_sums.reshape(-1)
    def columns(stacked):
        return stacked.astype(F32).transpose(1, 0, 2).reshape(rows, -1)

    def key_columns(stacked):
        summed = stacked.astype(F32).reshape(KEY_VALUE_HEADS, sharers, rows, HEAD_SIZE).sum(axis=1)
        return summed.transpose(1, 0, 2).reshape(rows, -1)

    if sharers == 1:
        grad_query, grad_key, grad_value = spread_heads(head_parts, width)
    else:
        grad_query = columns(head_parts[:, :, :width])
        grad_key = key_columns(head_parts[:, :, width : width + HEAD_SIZE])
        grad_value = key_columns(head_parts[:, :, width + HEAD_SIZE :])
    return (
        hidden_out[None],
        grad_hidden[None],
        grad_query,
        grad_key,
        grad_value,
        grad_weight_out,
        spread_columns(gate_parts),
        spread_columns(up_parts),
        grad_weight_down,
        gain_sums[:rows],
        gain_sums[rows : 2 * rows],
        lax.dynamic_slice_in_dim(gain_sums, 2 * rows + shard * head_rows, head_rows),
        lax.dynamic_slice_in_dim(gain_sums, 2 * rows + HEAD_SIZE + shard * head_rows, head_rows),
    )


def solution(mesh):
    tokens = P("fsdp", "ctx", None)
    by_rows = P("fsdp", None)
    by_columns = P(None, "fsdp")
    per_token = P("fsdp", "ctx")
    vector = P("fsdp")
    weights = (by_rows, by_rows, by_rows, by_columns, by_rows, by_rows, by_columns)
    return jax.shard_map(
        local,
        mesh=mesh,
        in_specs=(tokens, *weights, vector, vector, vector, vector, per_token, per_token, tokens),
        out_specs=(tokens, tokens, *weights, vector, vector, vector, vector),
        check_vma=False,
    )
```

```python
import functools

import jax
import jax.numpy as jnp
from jax import lax
from jax.experimental import pallas as pl
from jax.experimental.layout import Layout, with_layout_constraint
from jax.experimental.pallas import tpu as pltpu
from jax.sharding import PartitionSpec as P

D = 2048
QUERY_HEADS = 16
KEY_VALUE_HEADS = 8
HEAD_SIZE = 128
FF = 6144
EPS = 1e-06
THETA = 1000000.0
F32 = jnp.float32
BF16 = jnp.bfloat16
MESH = pl.DeviceIdType.MESH
VMEM = pltpu.VMEM
WHOLE = pl.BlockSpec(memory_space=pltpu.VMEM)
HBM = pl.BlockSpec(memory_space=pl.ANY)
CHUNKS = 4
WIDE = D // CHUNKS


def dot(left, right):
    return jnp.dot(left, right, preferred_element_type=F32)


def tdot(left, right):
    return lax.dot_general(left, right, (((0,), (0,)), ((), ())), preferred_element_type=F32)


def rdot(left, right):
    return lax.dot_general(left, right, (((1,), (1,)), ((), ())), preferred_element_type=F32)


def loop(count, body):
    def step(index, carry):
        body(index)
        return carry

    lax.fori_loop(0, count, step, 0)


def line_position():
    me = lax.axis_index("ctx")
    return me, me // 2, me % 2, lax.axis_size("ctx") // 2


def send(source, target, send_sem, recv_sem, axis, index):
    return pltpu.make_async_remote_copy(
        src_ref=source,
        dst_ref=target,
        send_sem=send_sem,
        recv_sem=recv_sem,
        device_id={axis: index},
        device_id_type=MESH,
    )


def line_barrier():
    me, chip, core, chips = line_position()
    barrier = pltpu.get_barrier_semaphore()

    def greet(index):
        pl.semaphore_signal(barrier, inc=1, device_id={"ctx": index}, device_id_type=MESH)

    greet(me + 1 - 2 * core)

    @pl.when(chip > 0)
    def _():
        greet(me - 2)

    @pl.when(chip < chips - 1)
    def _():
        greet(me + 2)

    peers = 1 + (chip > 0).astype(jnp.int32) + (chip < chips - 1).astype(jnp.int32)
    pl.semaphore_wait(barrier, peers)


def peers_of(axis):
    me, size = lax.axis_index(axis), lax.axis_size(axis)
    return size - 1, lambda i: (me + i + 1) % size, lambda i: (me + size - i - 1) % size


def full_barrier():
    barrier = pltpu.get_barrier_semaphore()
    total = 0
    for axis in ("fsdp", "ctx"):
        count, ahead, _ = peers_of(axis)
        loop(
            count,
            lambda i, axis=axis, ahead=ahead: pl.semaphore_signal(
                barrier, inc=1, device_id={axis: ahead(i)}, device_id_type=MESH
            ),
        )
        total += count
    pl.semaphore_wait(barrier, total)


def gather_scratch(chips):
    return [pltpu.SemaphoreType.DMA((chips,)) for _ in range(6)]


class Gather:
    def __init__(self, land, sems, consume=None, late=False):
        self.late = late
        self.land = land
        self.sems = sems
        self.consume = consume
        self.me, self.chip, self.core, self.chips = line_position()

    def right(self, step, source):
        ref = self.land.at[2 * source + self.core]
        return send(ref, ref, self.sems[0].at[step], self.sems[1].at[step], "ctx", self.me + 2)

    def left(self, step, source):
        ref = self.land.at[2 * source + self.core]
        return send(ref, ref, self.sems[2].at[step], self.sems[3].at[step], "ctx", self.me - 2)

    def across(self, source, core):
        ref = self.land.at[2 * source + core]
        other = self.me + 1 - 2 * self.core
        return send(ref, ref, self.sems[4].at[source], self.sems[5].at[source], "ctx", other)

    def step(self, step):
        chip, core, chips = self.chip, self.core, self.chips
        low, high = chip - step, chip + step
        has_low = low >= 0
        has_high = jnp.logical_and(high < chips, step > 0)

        @pl.when(jnp.logical_and(has_low, step > 0))
        def _():
            self.right(step - 1, low).wait_recv()

        @pl.when(jnp.logical_and(has_low, chip < chips - 1))
        def _():
            self.right(step, low).start()

        @pl.when(has_high)
        def _():
            self.left(step - 1, high).wait_recv()

        @pl.when(jnp.logical_and(high < chips, chip > 0))
        def _():
            self.left(step, high).start()

        @pl.when(has_low)
        def _():
            self.across(low, core).start()

        @pl.when(has_high)
        def _():
            self.across(high, core).start()

        if not self.late:
            self.use(step)
            return

        @pl.when(step > 0)
        def _():
            self.use(step - 1)

        @pl.when(step == chips - 1)
        def _():
            self.use(step)

    def use(self, step):
        chip, core, chips = self.chip, self.core, self.chips
        low, high = chip - step, chip + step

        def one(kind):
            upward = kind % 2
            crossed = kind // 2
            source = jnp.where(upward == 1, high, low)
            valid = jnp.where(upward == 1, jnp.logical_and(high < chips, step > 0), low >= 0)
            parity = jnp.where(crossed == 1, 1 - core, core)

            @pl.when(valid)
            def _():
                @pl.when(crossed == 1)
                def _():
                    self.across(source, parity).wait_recv()

                if self.consume is not None:
                    self.consume(2 * source + parity)

        loop(4, one)

    def finish(self):
        chip, core, chips = self.chip, self.core, self.chips

        def one(step):
            @pl.when(jnp.logical_and(chip - step >= 0, chip < chips - 1))
            def _():
                self.right(step, chip - step).wait_send()

            @pl.when(jnp.logical_and(chip + step < chips, chip > 0))
            def _():
                self.left(step, chip + step).wait_send()

            self.across(step, core).wait_send()

        loop(chips, one)


def scatter_scratch(chips, rows):
    buffers = [VMEM((count, CHUNKS, rows, WIDE), BF16) for count in (chips + 1, chips, chips)]
    return buffers + [pltpu.SemaphoreType.DMA((chips, CHUNKS)) for _ in range(6)]


class Scatter:
    def __init__(self, scratch, produce, total):
        self.line, self.out, self.other = scratch[:3]
        self.sems = scratch[3:]
        self.produce = produce
        self.total = total
        self.me, self.chip, self.core, self.chips = line_position()


    def right(self, step, chunk):
        ref = self.line.at[step, chunk]
        sems = self.sems
        return send(ref, ref, sems[0].at[step, chunk], sems[1].at[step, chunk], "ctx", self.me + 2)

    def left(self, step, chunk):
        ref = self.line.at[self.chips - step, chunk]
        sems = self.sems
        return send(ref, ref, sems[2].at[step, chunk], sems[3].at[step, chunk], "ctx", self.me - 2)

    def across(self, target, chunk):
        sems = self.sems
        return send(
            self.out.at[target, chunk],
            self.other.at[target, chunk],
            sems[4].at[target, chunk],
            sems[5].at[target, chunk],
            "ctx",
            self.me + 1 - 2 * self.core,
        )

    def begin(self):
        def clear(index):
            slot, chunk = index // CHUNKS, index % CHUNKS
            at_left = jnp.logical_and(self.chip == 0, slot < self.chips)
            at_right = jnp.logical_and(self.chip == self.chips - 1, slot > 0)

            @pl.when(jnp.logical_or(at_left, at_right))
            def _():
                self.line[slot, chunk] = jnp.zeros(self.line.shape[2:], BF16)

        loop((self.chips + 1) * CHUNKS, clear)

    def when_right(self, time):
        return jnp.logical_and(time >= self.chip, time < self.chips - 1)

    def when_left(self, time):
        return jnp.logical_and(time >= self.chips - 1 - self.chip, time < self.chips - 1)

    def prepare(self, time):
        def cross(target):
            def one(chunk):
                piece = 2 * target + 1 - self.core
                self.out[target, chunk] = self.produce(piece, chunk).astype(BF16)
                self.across(target, chunk).start()

            loop(CHUNKS, one)

        @pl.when(self.when_right(time))
        def _():
            cross(self.chips - 1 - time + self.chip)

        @pl.when(self.when_left(time))
        def _():
            cross(time - (self.chips - 1 - self.chip))

        @pl.when(time == self.chips - 1)
        def _():
            cross(self.chip)

    def step(self, time):
        chip, core, chips = self.chip, self.core, self.chips

        @pl.when(self.when_right(time))
        def _():
            step = time - chip
            target = chips - 1 - step

            def one(chunk):
                self.across(target, chunk).wait_recv()

                @pl.when(chip > 0)
                def _():
                    self.right(step, chunk).wait_recv()

                value = self.produce(2 * target + core, chunk) + self.other[target, chunk].astype(F32)
                value = value + self.line[step, chunk].astype(F32)
                self.line[step, chunk] = value.astype(BF16)
                self.right(step, chunk).start()

            loop(CHUNKS, one)

        @pl.when(self.when_left(time))
        def _():
            step = time - (chips - 1 - chip)

            def one(chunk):
                self.across(step, chunk).wait_recv()

                @pl.when(chip < chips - 1)
                def _():
                    self.left(step, chunk).wait_recv()

                value = self.produce(2 * step + core, chunk) + self.other[step, chunk].astype(F32)
                value = value + self.line[chips - step, chunk].astype(F32)
                self.line[chips - step, chunk] = value.astype(BF16)
                self.left(step, chunk).start()

            loop(CHUNKS, one)

    def finish(self):
        chip, core, chips = self.chip, self.core, self.chips
        last = chips - 1 - chip

        def one(chunk):
            self.across(chip, chunk).wait_recv()
            value = self.produce(2 * chip + core, chunk) + self.other[chip, chunk].astype(F32)

            @pl.when(chip > 0)
            def _():
                self.right(last, chunk).wait_recv()

            @pl.when(chip < chips - 1)
            def _():
                self.left(chip, chunk).wait_recv()

            value = value + self.line[last, chunk].astype(F32)
            value = value + self.line[chips - chip, chunk].astype(F32)
            self.total[:, pl.ds(pl.multiple_of(chunk * WIDE, WIDE), WIDE)] = value

        loop(CHUNKS, one)

        def drain(index):
            step, chunk = index // CHUNKS, index % CHUNKS

            @pl.when(step < last)
            def _():
                self.right(step, chunk).wait_send()

            @pl.when(step < chip)
            def _():
                self.left(step, chunk).wait_send()

            self.across(step, chunk).wait_send()

        loop(chips * CHUNKS, drain)


def row_blocks(rows, body, size=32):
    def one(index):
        body(pl.ds(pl.multiple_of(index * size, size), size))

    loop(rows // size, one)


def inverse_norm(value):
    return lax.rsqrt(jnp.mean(value * value, axis=-1, keepdims=True) + EPS)


def params(identity, megabytes):
    return pltpu.CompilerParams(
        collective_id=identity,
        has_side_effects=True,
        vmem_limit_bytes=megabytes * 1024 * 1024,
    )


def cost(microseconds):
    return pl.CostEstimate(
        flops=int(microseconds * 1.15e9), bytes_accessed=1024, transcendentals=0
    )


def copy_in(source, target, sem):
    copy = pltpu.make_async_copy(source, target, sem)
    copy.start()
    return copy


def first_kernel(rows, width, *refs):
    x, gains, tokens, part, land, proj, weights, gain_rows, all_gains, all_tokens = refs[:10]
    sems, small = refs[10:16], refs[16:]
    me, _, _, chips = line_position()
    shard = lax.axis_index("fsdp")
    shards, ahead, behind = peers_of("fsdp")
    parts, next_part, past_part = peers_of("ctx")
    full_barrier()

    def gain_copy(i, slot):
        return send(gains, all_gains.at[slot], small[0].at[i], small[1].at[i], "fsdp", ahead(i))

    def token_copy(i, slot):
        return send(tokens, all_tokens.at[slot], small[2].at[i], small[3].at[i], "ctx", next_part(i))

    def weight_copy(i, owner):
        target = weights.at[pl.ds(pl.multiple_of(owner * rows, rows), rows), :]
        return send(part, target, small[4].at[i], small[5].at[i], "fsdp", ahead(i))

    loop(shards, lambda i: gain_copy(i, shard).start())
    loop(parts, lambda i: token_copy(i, me).start())
    loop(shards, lambda i: weight_copy(i, shard).start())
    all_gains[shard] = gains[...]
    all_tokens[me] = tokens[...]
    weights[pl.ds(pl.multiple_of(shard * rows, rows), rows), :] = part[...]
    loop(shards, lambda i: gain_copy(i, behind(i)).wait_recv())
    lanes = rows // 128
    for kind in range(2):
        for owner in range(shards + 1):
            for j in range(lanes):
                at = owner * rows + j * 128
                gain_rows[kind : kind + 1, at : at + 128] = all_gains[
                    owner, kind * lanes + j : kind * lanes + j + 1, :
                ]

    def norm(block):
        value = x[block, :].astype(F32)
        land[me, block] = (value * inverse_norm(value) * gain_rows[0:1, :]).astype(BF16)

    row_blocks(x.shape[0], norm)

    gather = Gather(land, sems)
    loop(chips, gather.step)
    loop(shards, lambda i: weight_copy(i, behind(i)).wait_recv())

    def project(piece):
        proj[piece] = dot(land[piece], weights[:, :width])

    loop(2 * chips, project)
    gather.finish()
    loop(shards, lambda i: gain_copy(i, shard).wait_send())
    loop(shards, lambda i: weight_copy(i, shard).wait_send())
    loop(parts, lambda i: token_copy(i, past_part(i)).wait_recv())
    loop(parts, lambda i: token_copy(i, me).wait_send())


def first(hidden, gains, tokens, part, shards, parts, width):
    count = hidden.shape[0]
    return pl.pallas_call(
        functools.partial(first_kernel, D // shards, width),
        out_shape=(
            jax.ShapeDtypeStruct((parts, count, D), BF16),
            jax.ShapeDtypeStruct((parts, count, width), F32),
            jax.ShapeDtypeStruct((D, part.shape[1]), BF16),
            jax.ShapeDtypeStruct((8, D), F32),
            jax.ShapeDtypeStruct((shards, *gains.shape), F32),
            jax.ShapeDtypeStruct((parts, *tokens.shape), jnp.int32),
        ),
        in_specs=[WHOLE] * 4,
        out_specs=(WHOLE,) * 6,
        scratch_shapes=gather_scratch(parts // 2)
        + [pltpu.SemaphoreType.DMA((shards,))] * 2
        + [pltpu.SemaphoreType.DMA((parts,))] * 2
        + [pltpu.SemaphoreType.DMA((shards,))] * 2,
        compiler_params=params(0, 60),
        cost_estimate=cost(85),
        name="gather_normed",
    )(hidden, gains, tokens, part)


def out_kernel(columns, *refs):
    context, weights, x, gain_rows, middle, normed = refs[:6]
    weight, weight_sem, total = refs[6:9]
    scratch = refs[9:]
    chips = line_position()[3]
    copy = copy_in(weights.at[:, columns], weight, weight_sem)

    def produce(piece, chunk):
        return rdot(context[piece], weight[pl.ds(pl.multiple_of(chunk * WIDE, WIDE), WIDE), :])

    scatter = Scatter(scratch, produce, total)
    scatter.begin()
    line_barrier()
    copy.wait()
    scatter.prepare(0)

    def step(time):
        scatter.step(time)
        scatter.prepare(time + 1)

    loop(chips - 1, step)
    scatter.finish()

    def norm(block):
        value = x[block, :].astype(F32) + total[block, :]
        middle[block, :] = value
        normed[block, :] = (value * inverse_norm(value) * gain_rows[1:2, :]).astype(BF16)

    row_blocks(x.shape[0], norm)


def attention_out(context, weights, hidden, gain_rows):
    parts, count, width = context.shape
    return pl.pallas_call(
        functools.partial(out_kernel, pl.ds(weights.shape[1] - width, width)),
        out_shape=(
            jax.ShapeDtypeStruct((count, D), F32),
            jax.ShapeDtypeStruct((count, D), BF16),
        ),
        in_specs=[WHOLE, HBM, WHOLE, WHOLE],
        out_specs=(WHOLE,) * 2,
        scratch_shapes=[VMEM((D, width), BF16), pltpu.SemaphoreType.DMA, VMEM((count, D), F32)]
        + scatter_scratch(parts // 2, count),
        compiler_params=params(1, 60),
        cost_estimate=cost(90),
        name="attention_out",
    )(context, weights, hidden, gain_rows)


def feed_kernel(width, *refs):
    x, grads, weights, land, activation, back = refs[:6]
    weight, weight_sem, grad, grad_sems = refs[6:10]
    sems = refs[10:]
    me, _, _, chips = line_position()
    copy = copy_in(weights, weight, weight_sem)

    def grad_copy(piece):
        return pltpu.make_async_copy(grads.at[piece], grad.at[piece], grad_sems.at[piece])

    loop(2 * chips, lambda piece: grad_copy(piece).start())
    land[me] = x[...]
    size = 256 if width % 256 == 0 else 128

    def consume(piece):
        grad_copy(piece).wait()

        def one(index):
            def columns(kind):
                return pl.ds(pl.multiple_of(kind * width + index * size, 128), size)

            gate = dot(land[piece], weight[:, columns(0)])
            up = dot(land[piece], weight[:, columns(1)])
            grad_act = dot(grad[piece], weight[:, columns(2)])
            sigma = 1.0 / (1.0 + jnp.exp(-gate))
            activation[piece, :, columns(0)] = (gate * sigma * up).astype(BF16)
            back[piece, :, columns(0)] = (
                grad_act * up * sigma * (1.0 + gate * (1.0 - sigma))
            ).astype(BF16)
            back[piece, :, columns(1)] = (grad_act * gate * sigma).astype(BF16)

        loop(width // size, one)

    line_barrier()
    gather = Gather(land, sems, consume)
    copy.wait()
    loop(chips, gather.step)
    gather.finish()


def feed(normed, grads, weights):
    parts, count, _ = grads.shape
    width = weights.shape[1] // 3
    return pl.pallas_call(
        functools.partial(feed_kernel, width),
        out_shape=(
            jax.ShapeDtypeStruct((parts, count, D), BF16),
            jax.ShapeDtypeStruct((parts, count, width), BF16),
            jax.ShapeDtypeStruct((parts, count, 2 * width), BF16),
        ),
        in_specs=[WHOLE, HBM, HBM],
        out_specs=(WHOLE,) * 3,
        scratch_shapes=[
            VMEM(weights.shape, BF16),
            pltpu.SemaphoreType.DMA,
            VMEM(grads.shape, BF16),
            pltpu.SemaphoreType.DMA((parts,)),
        ]
        + gather_scratch(parts // 2),
        compiler_params=params(2, 60),
        cost_estimate=cost(90),
        name="feed",
    )(normed, grads, weights)


def rms_back(value, gain, grad):
    inverse = inverse_norm(value)
    scaled = grad * gain
    inner = jnp.mean(scaled * value, axis=-1, keepdims=True)
    terms = grad * value * inverse
    return inverse * scaled - value * (inverse * inverse * inverse * inner), terms


def feed_back_kernel(columns, *refs):
    back, weights, middle, grad, gain_rows, grad_middle, low, gain_sum = refs[:8]
    weight, weight_sem, total = refs[8:11]
    scratch = refs[11:]
    chips = line_position()[3]
    copy = copy_in(weights.at[:, columns], weight, weight_sem)

    def produce(piece, chunk):
        return rdot(back[piece], weight[pl.ds(pl.multiple_of(chunk * WIDE, WIDE), WIDE), :])

    scatter = Scatter(scratch, produce, total)
    scatter.begin()
    line_barrier()
    copy.wait()
    scatter.prepare(0)

    def step(time):
        scatter.step(time)
        scatter.prepare(time + 1)

    loop(chips - 1, step)
    scatter.finish()
    gain_sum[...] = jnp.zeros_like(gain_sum)

    def norm(block):
        through, terms = rms_back(middle[block, :], gain_rows[1:2, :], total[block, :])
        value = grad[block, :].astype(F32) + through
        grad_middle[block, :] = value
        low[block, :] = value.astype(BF16)
        gain_sum[0:1, :] += jnp.sum(terms, axis=0, keepdims=True)

    row_blocks(middle.shape[0], norm)


def feed_back(back, weights, middle, grad, gain_rows):
    parts, count, width = back.shape
    return pl.pallas_call(
        functools.partial(feed_back_kernel, pl.ds(0, width)),
        out_shape=(
            jax.ShapeDtypeStruct((count, D), F32),
            jax.ShapeDtypeStruct((count, D), BF16),
            jax.ShapeDtypeStruct((8, D), F32),
        ),
        in_specs=[WHOLE, HBM, WHOLE, WHOLE, WHOLE],
        out_specs=(WHOLE,) * 3,
        scratch_shapes=[VMEM((D, width), BF16), pltpu.SemaphoreType.DMA, VMEM((count, D), F32)]
        + scatter_scratch(parts // 2, count),
        compiler_params=params(3, 60),
        cost_estimate=cost(86),
        name="feed_back",
    )(back, weights, middle, grad, gain_rows)


def turn_kernel(columns, down_columns, *refs):
    low, weights, activation, feed_weights, middle, land, context_grad, hidden = refs[:8]
    weight, weight_sem, down, down_sem, total = refs[8:13]
    gather_sems, scratch = refs[13:19], refs[19:]
    me, _, _, chips = line_position()
    copy = copy_in(weights.at[:, columns], weight, weight_sem)
    down_copy = copy_in(feed_weights.at[:, down_columns], down, down_sem)
    land[me] = low[...]

    def consume(piece):
        context_grad[piece] = dot(land[piece], weight[...]).astype(BF16)

    def produce(piece, chunk):
        return rdot(activation[piece], down[pl.ds(pl.multiple_of(chunk * WIDE, WIDE), WIDE), :])

    gather = Gather(land, gather_sems, consume)
    scatter = Scatter(scratch, produce, total)
    scatter.begin()
    line_barrier()
    copy.wait()
    down_copy.wait()
    scatter.prepare(0)

    def step(time):
        gather.step(time)
        scatter.step(time)
        scatter.prepare(time + 1)

    loop(chips - 1, step)
    gather.step(chips - 1)
    scatter.finish()
    gather.finish()

    def add(block):
        hidden[block, :] = (middle[block, :] + total[block, :]).astype(BF16)

    row_blocks(middle.shape[0], add)


def turn(low, weights, activation, feed_weights, middle, width):
    parts, count, feed_width = activation.shape
    return pl.pallas_call(
        functools.partial(
            turn_kernel, pl.ds(weights.shape[1] - width, width), pl.ds(2 * feed_width, feed_width)
        ),
        out_shape=(
            jax.ShapeDtypeStruct((parts, count, D), BF16),
            jax.ShapeDtypeStruct((parts, count, width), BF16),
            jax.ShapeDtypeStruct((count, D), BF16),
        ),
        in_specs=[WHOLE, HBM, WHOLE, HBM, WHOLE],
        out_specs=(WHOLE,) * 3,
        scratch_shapes=[
            VMEM((D, width), BF16),
            pltpu.SemaphoreType.DMA,
            VMEM((D, feed_width), BF16),
            pltpu.SemaphoreType.DMA,
            VMEM((count, D), F32),
        ]
        + gather_scratch(parts // 2)
        + scatter_scratch(parts // 2, count),
        compiler_params=params(4, 62),
        cost_estimate=cost(107),
        name="turn",
    )(low, weights, activation, feed_weights, middle)


def last_kernel(columns, *refs):
    back, weights, x, grad_middle, gain_rows, gain_two, gain_heads, hidden, gain_out = refs[:9]
    weight, weight_sem, total, gain_one, pack, pack_in, shard_sum, shard_in = refs[9:17]
    small, scratch = refs[17:21], refs[21:]
    chips = line_position()[3]
    copy = copy_in(weights.at[:, columns], weight, weight_sem)

    def produce(piece, chunk):
        return rdot(back[piece], weight[pl.ds(pl.multiple_of(chunk * WIDE, WIDE), WIDE), :])

    scatter = Scatter(scratch, produce, total)
    scatter.begin()
    full_barrier()
    copy.wait()
    scatter.prepare(0)

    def step(time):
        scatter.step(time)
        scatter.prepare(time + 1)

    loop(chips - 1, step)
    scatter.finish()
    gain_one[...] = jnp.zeros_like(gain_one)

    def norm(block):
        through, terms = rms_back(x[block, :].astype(F32), gain_rows[0:1, :], total[block, :])
        hidden[block, :] = grad_middle[block, :] + through
        gain_one[0:1, :] += jnp.sum(terms, axis=0, keepdims=True)

    row_blocks(x.shape[0], norm)

    shard = lax.axis_index("fsdp")
    shards, ahead, _ = peers_of("fsdp")
    parts, next_part, _ = peers_of("ctx")
    rows = D // (shards + 1)
    lanes = rows // 128
    pack[...] = jnp.zeros_like(pack)
    for owner in range(shards + 1):
        for j in range(lanes):
            at = owner * rows + j * 128
            pack[owner, j : j + 1, :] = gain_one[0:1, at : at + 128]
            pack[owner, lanes + j : lanes + j + 1, :] = gain_two[0:1, at : at + 128]
        pack[owner, 2 * lanes : 2 * lanes + 2, :] = gain_heads[0:2, :]

    def pack_copy(i):
        return send(pack.at[ahead(i)], pack_in.at[i], small[0].at[i], small[1].at[i], "fsdp", ahead(i))

    def sum_copy(i):
        return send(shard_sum, shard_in.at[i], small[2].at[i], small[3].at[i], "ctx", next_part(i))

    loop(shards, lambda i: pack_copy(i).start())
    shard_sum[...] = pack[shard]

    def add_pack(i):
        pack_copy(i).wait_recv()
        shard_sum[...] += pack_in[i]

    loop(shards, add_pack)
    loop(parts, lambda i: sum_copy(i).start())
    gain_out[...] = shard_sum[...]

    def add_sum(i):
        sum_copy(i).wait_recv()
        gain_out[...] += shard_in[i]

    loop(parts, add_sum)
    loop(shards, lambda i: pack_copy(i).wait_send())
    loop(parts, lambda i: sum_copy(i).wait_send())


def last(back, weights, hidden, grad_middle, gain_rows, gain_two, gain_heads, shards):
    parts, count, width = back.shape
    return pl.pallas_call(
        functools.partial(last_kernel, pl.ds(0, width)),
        out_shape=(
            jax.ShapeDtypeStruct((count, D), F32),
            jax.ShapeDtypeStruct((16, 128), F32),
        ),
        in_specs=[WHOLE, HBM] + [WHOLE] * 5,
        out_specs=(WHOLE,) * 2,
        scratch_shapes=[
            VMEM((D, width), BF16),
            pltpu.SemaphoreType.DMA,
            VMEM((count, D), F32),
            VMEM((8, D), F32),
            VMEM((shards, 16, 128), F32),
            VMEM((shards, 16, 128), F32),
            VMEM((16, 128), F32),
            VMEM((parts, 16, 128), F32),
        ]
        + [pltpu.SemaphoreType.DMA((shards,))] * 2
        + [pltpu.SemaphoreType.DMA((parts,))] * 2
        + scatter_scratch(parts // 2, count),
        compiler_params=params(5, 60),
        cost_estimate=cost(90),
        name="last",
    )(back, weights, hidden, grad_middle, gain_rows, gain_two, gain_heads)


QUERY_TILE = 256
KEY_TILE = 512


def reach(index, tokens):
    return jnp.minimum((index + 2) * QUERY_TILE + KEY_TILE - 1, tokens) // KEY_TILE


def head_norm(value, gain, cosine, sine):
    normed = value * inverse_norm(value) * gain
    return normed * cosine + pltpu.roll(normed, HEAD_SIZE // 2, 1) * sine


def attention_kernel(heads, proj, cosine, sine, gain, id_column, id_row, *refs):
    queries, keys, values, context, inverse = refs
    tokens = proj.shape[0]
    key_at = heads * HEAD_SIZE

    def prepare(index):
        block = pl.ds(pl.multiple_of(index * QUERY_TILE, QUERY_TILE), QUERY_TILE)
        c, s = cosine[block, :], sine[block, :]
        for h in range(heads):
            lanes = slice(h * HEAD_SIZE, (h + 1) * HEAD_SIZE)
            rotated = head_norm(proj[block, lanes], gain[0:1, :], c, s) * HEAD_SIZE ** (-0.5)
            queries[block, lanes] = rotated.astype(BF16)
        rotated = head_norm(proj[block, key_at : key_at + HEAD_SIZE], gain[1:2, :], c, s)
        keys[block, :] = rotated.astype(BF16)
        values[block, :] = proj[block, key_at + HEAD_SIZE : key_at + 2 * HEAD_SIZE].astype(BF16)

    loop(tokens // QUERY_TILE, prepare)

    def attend(index):
        block = pl.ds(pl.multiple_of(index * QUERY_TILE, QUERY_TILE), QUERY_TILE)
        query_ids = id_column[block, :]
        for h in range(heads):
            lanes = slice(h * HEAD_SIZE, (h + 1) * HEAD_SIZE)
            query = queries[block, lanes]

            def one(tile, carry):
                sums, total = carry
                span = pl.ds(pl.multiple_of(tile * KEY_TILE, KEY_TILE), KEY_TILE)
                scores = rdot(query, keys[span, :])
                expon = jnp.where(id_row[0:1, span] <= query_ids, jnp.exp(scores), 0.0)
                sums = sums + dot(expon.astype(BF16), values[span, :])
                return sums, total + jnp.sum(expon, axis=1, keepdims=True)

            start = (jnp.zeros((QUERY_TILE, HEAD_SIZE), F32), jnp.zeros((QUERY_TILE, 1), F32))
            sums, total = lax.fori_loop(0, reach(index, tokens), one, start)
            scale = 1.0 / total
            context[block, lanes] = (sums * scale).astype(BF16)
            inverse[h : h + 1, block] = jnp.broadcast_to(scale, (QUERY_TILE, HEAD_SIZE)).T[0:1, :]

    loop(tokens // QUERY_TILE, attend)


def attention(proj, cosine, sine, gain, id_column, id_row, heads):
    tokens = proj.shape[0]
    width = heads * HEAD_SIZE
    return pl.pallas_call(
        functools.partial(attention_kernel, heads),
        out_shape=(
            jax.ShapeDtypeStruct((tokens, width), BF16),
            jax.ShapeDtypeStruct((tokens, HEAD_SIZE), BF16),
            jax.ShapeDtypeStruct((tokens, HEAD_SIZE), BF16),
            jax.ShapeDtypeStruct((tokens, width), BF16),
            jax.ShapeDtypeStruct((8, tokens), F32),
        ),
        in_specs=[WHOLE] * 6,
        out_specs=(WHOLE,) * 5,
        compiler_params=pltpu.CompilerParams(vmem_limit_bytes=48 * 1024 * 1024),
        cost_estimate=cost(27),
        name="attention",
    )(proj, cosine, sine, gain, id_column, id_row)


def attention_back_kernel(heads, *refs):
    queries, keys, values, out_grad, inverse, context, proj, cosine, sine, gain = refs[:10]
    id_column, id_row, back, gain_sum, key_grad, value_grad, query_grad = refs[10:]
    tokens = proj.shape[0]
    key_at = heads * HEAD_SIZE
    key_grad[...] = jnp.zeros_like(key_grad)
    value_grad[...] = jnp.zeros_like(value_grad)
    gain_sum[...] = jnp.zeros_like(gain_sum)

    def through(block, lanes, grad, row):
        turned = pltpu.roll(grad, HEAD_SIZE // 2, 1)
        unrotated = grad * cosine[block, :] - turned * sine[block, :]
        result, terms = rms_back(proj[block, lanes], gain[row : row + 1, :], unrotated)
        back[block, lanes] = result.astype(BF16)
        gain_sum[row : row + 1, :] += jnp.sum(terms, axis=0, keepdims=True)

    def attend(index):
        block = pl.ds(pl.multiple_of(index * QUERY_TILE, QUERY_TILE), QUERY_TILE)
        query_ids = id_row[0:1, block]
        for h in range(heads):
            lanes = slice(h * HEAD_SIZE, (h + 1) * HEAD_SIZE)
            query = queries[block, lanes]
            grad = out_grad[block, lanes]
            scale = inverse[h : h + 1, block]
            products = grad.astype(F32) * context[block, lanes].astype(F32)
            shift = lax.dot_general(
                jnp.ones((8, HEAD_SIZE), F32),
                products,
                (((1,), (1,)), ((), ())),
                precision=lax.Precision.HIGHEST,
                preferred_element_type=F32,
            )[0:1, :]
            query_grad[...] = jnp.zeros_like(query_grad)

            def one(tile):
                span = pl.ds(pl.multiple_of(tile * KEY_TILE, KEY_TILE), KEY_TILE)
                key = keys[span, :]
                scores = rdot(key, query)
                probs = jnp.where(id_column[span, :] <= query_ids, jnp.exp(scores) * scale, 0.0)
                grad_scores = (probs * (rdot(values[span, :], grad) - shift)).astype(BF16)
                value_grad[span, :] += dot(probs.astype(BF16), grad)
                key_grad[span, :] += dot(grad_scores, query)
                query_grad[...] += tdot(grad_scores, key)

            loop(reach(index, tokens), one)
            through(block, lanes, query_grad[...] * HEAD_SIZE ** (-0.5), 0)

    loop(tokens // QUERY_TILE, attend)

    def finish(index):
        block = pl.ds(pl.multiple_of(index * QUERY_TILE, QUERY_TILE), QUERY_TILE)
        through(block, slice(key_at, key_at + HEAD_SIZE), key_grad[block, :], 1)
        back[block, key_at + HEAD_SIZE : key_at + 2 * HEAD_SIZE] = value_grad[block, :].astype(BF16)

    loop(tokens // QUERY_TILE, finish)


def attention_back(heads, *operands):
    tokens = operands[0].shape[0]
    width = heads * HEAD_SIZE
    return pl.pallas_call(
        functools.partial(attention_back_kernel, heads),
        out_shape=(
            jax.ShapeDtypeStruct((tokens, width + 2 * HEAD_SIZE), BF16),
            jax.ShapeDtypeStruct((8, HEAD_SIZE), F32),
        ),
        in_specs=[WHOLE] * len(operands),
        out_specs=(WHOLE,) * 2,
        scratch_shapes=[
            VMEM((tokens, HEAD_SIZE), F32),
            VMEM((tokens, HEAD_SIZE), F32),
            VMEM((QUERY_TILE, HEAD_SIZE), F32),
        ],
        compiler_params=pltpu.CompilerParams(vmem_limit_bytes=48 * 1024 * 1024),
        cost_estimate=cost(38),
        name="attention_back",
    )(*operands)


def spread_feed_kernel(width, source, gate, up, down):
    gate[...] = source[0, :, :width].astype(F32)
    up[...] = source[0, :, width : 2 * width].astype(F32)
    down[...] = source[0, :, 2 * width :].astype(F32).T


def spread_feed(stacked):
    parts, rows, total = stacked.shape
    width = total // 3
    across = jax.ShapeDtypeStruct((rows, parts * width), F32)
    return pl.pallas_call(
        functools.partial(spread_feed_kernel, width),
        out_shape=(across, across, jax.ShapeDtypeStruct((parts * width, rows), F32)),
        grid=(parts,),
        in_specs=[pl.BlockSpec((1, rows, total), lambda i: (i, 0, 0))],
        out_specs=(
            pl.BlockSpec((rows, width), lambda i: (0, i)),
            pl.BlockSpec((rows, width), lambda i: (0, i)),
            pl.BlockSpec((width, rows), lambda i: (i, 0)),
        ),
        compiler_params=pltpu.CompilerParams(vmem_limit_bytes=32 * 1024 * 1024),
        name="spread_feed",
    )(stacked)


def spread_heads_kernel(width, source, query, key, value, out):
    second = width + HEAD_SIZE
    third = second + HEAD_SIZE
    query[...] = source[0, :, :width].astype(F32)
    key[...] = source[0, :, width:second].astype(F32)
    value[...] = source[0, :, second:third].astype(F32)
    out[...] = source[0, :, third:].astype(F32).T


def spread_heads(stacked, width):
    parts, rows, total = stacked.shape
    widths = (width, HEAD_SIZE, HEAD_SIZE)
    return pl.pallas_call(
        functools.partial(spread_heads_kernel, width),
        out_shape=tuple(jax.ShapeDtypeStruct((rows, parts * w), F32) for w in widths)
        + (jax.ShapeDtypeStruct((parts * width, rows), F32),),
        grid=(parts,),
        in_specs=[pl.BlockSpec((1, rows, total), lambda i: (i, 0, 0))],
        out_specs=tuple(pl.BlockSpec((rows, w), lambda i: (0, i)) for w in widths)
        + (pl.BlockSpec((width, rows), lambda i: (i, 0)),),
        compiler_params=pltpu.CompilerParams(vmem_limit_bytes=32 * 1024 * 1024),
        name="spread_heads",
    )(stacked)


def by_row(array):
    return with_layout_constraint(array, Layout(major_to_minor=(0, 1)))


def own_columns(array, index, width):
    return lax.dynamic_slice_in_dim(array, index * width, width, axis=1)


def own_rows(array, index, width):
    return lax.dynamic_slice_in_dim(array, index * width, width, axis=0)


def local(
    hidden_in,
    weight_query,
    key_weight_matrix,
    weight_value,
    weight_out,
    weight_gate,
    weight_up,
    weight_down,
    gain_attention,
    gain_feed,
    gain_query,
    gain_key,
    positions,
    token_block_index,
    grad_out,
):
    parts = lax.axis_size("ctx")
    shards = lax.axis_size("fsdp")
    me = lax.axis_index("ctx")
    shard = lax.axis_index("fsdp")
    heads = QUERY_HEADS // parts
    sharers = parts // KEY_VALUE_HEADS
    key_head = me // sharers
    width = heads * HEAD_SIZE
    feed_width = FF // parts
    rows = D // shards
    head_rows = HEAD_SIZE // shards
    count = hidden_in.shape[1]
    tokens = parts * count

    def gather_rows(piece):
        return lax.all_gather(piece, "fsdp", axis=0, tiled=True)

    def sum_rows(grad):
        return lax.psum_scatter(grad.astype(BF16), "fsdp", scatter_dimension=0, tiled=True)

    def gather_parts(piece):
        return lax.all_gather(piece, "ctx", axis=0)

    own_heads_weight = jnp.concatenate(
        [
            own_columns(weight_query, me, width),
            own_columns(key_weight_matrix, key_head, HEAD_SIZE),
            own_columns(weight_value, key_head, HEAD_SIZE),
            own_rows(weight_out, me, width).T,
        ],
        axis=1,
    )
    feed_weight = gather_rows(
        jnp.concatenate(
            [
                own_columns(weight_gate, me, feed_width),
                own_columns(weight_up, me, feed_width),
                own_rows(weight_down, me, feed_width).T,
            ],
            axis=1,
        )
    )

    own_gains = jnp.concatenate([gain_attention, gain_feed, gain_query, gain_key]).astype(F32)
    own_gains = jnp.pad(own_gains, (0, 2048 - own_gains.shape[0])).reshape(16, 128)
    own_tokens = jnp.pad(jnp.stack([positions[0], token_block_index[0]]), ((0, 6), (0, 0)))
    hidden, grad = hidden_in[0], grad_out[0]
    normed_all, proj, heads_weight, gain_rows, gains, whole = first(
        hidden, own_gains, own_tokens, own_heads_weight, shards, parts, width + 2 * HEAD_SIZE
    )
    grad_late, gains = lax.optimization_barrier((grad, gains))
    grad_all = gather_parts(grad_late)
    flat_gains = gains.reshape(shards, -1)
    norm_query = flat_gains[:, 2 * rows : 2 * rows + head_rows].reshape(1, -1)
    norm_key = flat_gains[:, 2 * rows + head_rows : 2 * rows + 2 * head_rows].reshape(1, -1)
    head_gains = jnp.concatenate([norm_query, norm_key, jnp.zeros((6, HEAD_SIZE), F32)])

    half = HEAD_SIZE // 2
    freq = THETA ** (-(jnp.arange(half).astype(F32) * 2.0 / HEAD_SIZE))
    angle = whole[:, 0].reshape(-1).astype(F32)[:, None] * freq
    cosine, sine = jnp.cos(angle), jnp.sin(angle)
    cosine = jnp.concatenate([cosine, cosine], axis=1)
    sine = jnp.concatenate([-sine, sine], axis=1)
    ids = whole[:, 1].reshape(-1)
    id_row, id_column = ids[None, :], ids[:, None]

    proj = proj.reshape(tokens, width + 2 * HEAD_SIZE)
    queries, keys, values, context, inverse = attention(
        proj, cosine, sine, head_gains, id_column, id_row, heads
    )
    middle, normed_two = attention_out(
        context.reshape(parts, count, width), heads_weight, hidden, gain_rows
    )
    normed_two_all, activation, back = feed(normed_two, grad_all, feed_weight)

    flat_grad = grad_all.reshape(tokens, D)
    flat_back = back.reshape(tokens, 2 * feed_width)
    flat_activation = activation.reshape(tokens, feed_width)
    feed_grad = jnp.concatenate(
        [
            by_row(tdot(normed_two_all.reshape(tokens, D), flat_back).astype(BF16)),
            by_row(tdot(flat_grad, flat_activation).astype(BF16)),
        ],
        axis=1,
    )
    back, feed_grad = lax.optimization_barrier((back, feed_grad))
    feed_shard = sum_rows(feed_grad)

    grad_middle, low, gain_two = feed_back(back, feed_weight, middle, grad, gain_rows)
    low, feed_shard = lax.optimization_barrier((low, feed_shard))
    feed_parts = gather_parts(feed_shard)
    low_all, context_grad, hidden_out = turn(low, heads_weight, activation, feed_weight, middle, width)

    context_grad = context_grad.reshape(tokens, width)
    grad_qkv, gain_heads = attention_back(
        heads,
        queries,
        keys,
        values,
        context_grad,
        inverse,
        context,
        proj,
        cosine,
        sine,
        head_gains,
        id_column,
        id_row,
    )
    head_grad = jnp.concatenate(
        [
            by_row(tdot(normed_all.reshape(tokens, D), grad_qkv).astype(BF16)),
            by_row(tdot(low_all.reshape(tokens, D), context).astype(BF16)),
        ],
        axis=1,
    )
    grad_qkv, head_grad, feed_parts = lax.optimization_barrier((grad_qkv, head_grad, feed_parts))
    head_shard = sum_rows(head_grad)
    grad_hidden, gain_sums = last(
        grad_qkv.reshape(parts, count, -1),
        heads_weight,
        hidden,
        grad_middle,
        gain_rows,
        gain_two,
        gain_heads,
        shards,
    )

    head_parts = gather_parts(head_shard)
    gain_sums = gain_sums.reshape(-1)
    grad_gate, grad_up, grad_down = spread_feed(feed_parts)
    grad_query, grad_key, grad_value, grad_out_weight = spread_heads(head_parts, width)
    if sharers > 1:
        grad_key, grad_value = (
            part.reshape(rows, KEY_VALUE_HEADS, sharers, HEAD_SIZE).sum(axis=2).reshape(rows, -1)
            for part in (grad_key, grad_value)
        )
    return (
        hidden_out[None],
        grad_hidden[None],
        grad_query,
        grad_key,
        grad_value,
        grad_out_weight,
        grad_gate,
        grad_up,
        grad_down,
        gain_sums[:rows],
        gain_sums[rows : 2 * rows],
        lax.dynamic_slice_in_dim(gain_sums, 2 * rows + shard * head_rows, head_rows),
        lax.dynamic_slice_in_dim(gain_sums, 2 * rows + HEAD_SIZE + shard * head_rows, head_rows),
    )


def solution(mesh):
    tokens = P("fsdp", "ctx", None)
    by_rows = P("fsdp", None)
    by_columns = P(None, "fsdp")
    per_token = P("fsdp", "ctx")
    vector = P("fsdp")
    weights = (by_rows, by_rows, by_rows, by_columns, by_rows, by_rows, by_columns)
    return jax.shard_map(
        local,
        mesh=mesh,
        in_specs=(tokens, *weights, vector, vector, vector, vector, per_token, per_token, tokens),
        out_specs=(tokens, tokens, *weights, vector, vector, vector, vector),
        check_vma=False,
    )
```

```python
import functools

import jax
import jax.numpy as jnp
from jax import lax
from jax.experimental import pallas as pl
from jax.experimental.layout import Layout, with_layout_constraint
from jax.experimental.pallas import tpu as pltpu
from jax.sharding import PartitionSpec as P

D = 2048
QUERY_HEADS = 16
KEY_VALUE_HEADS = 8
HEAD_SIZE = 128
FF = 6144
EPS = 1e-06
THETA = 1000000.0
F32 = jnp.float32
BF16 = jnp.bfloat16
MESH = pl.DeviceIdType.MESH
VMEM = pltpu.VMEM
WHOLE = pl.BlockSpec(memory_space=pltpu.VMEM)
HBM = pl.BlockSpec(memory_space=pl.ANY)
CHUNKS = 4
WIDE = D // CHUNKS


def dot(left, right):
    return jnp.dot(left, right, preferred_element_type=F32)


def tdot(left, right):
    return lax.dot_general(left, right, (((0,), (0,)), ((), ())), preferred_element_type=F32)


def rdot(left, right):
    return lax.dot_general(left, right, (((1,), (1,)), ((), ())), preferred_element_type=F32)


def loop(count, body):
    def step(index, carry):
        body(index)
        return carry

    lax.fori_loop(0, count, step, 0)


def line_position():
    me = lax.axis_index("ctx")
    return me, me // 2, me % 2, lax.axis_size("ctx") // 2


def send(source, target, send_sem, recv_sem, axis, index):
    return pltpu.make_async_remote_copy(
        src_ref=source,
        dst_ref=target,
        send_sem=send_sem,
        recv_sem=recv_sem,
        device_id={axis: index},
        device_id_type=MESH,
    )


def line_barrier():
    me, chip, core, chips = line_position()
    barrier = pltpu.get_barrier_semaphore()

    def greet(index):
        pl.semaphore_signal(barrier, inc=1, device_id={"ctx": index}, device_id_type=MESH)

    greet(me + 1 - 2 * core)

    @pl.when(chip > 0)
    def _():
        greet(me - 2)

    @pl.when(chip < chips - 1)
    def _():
        greet(me + 2)

    peers = 1 + (chip > 0).astype(jnp.int32) + (chip < chips - 1).astype(jnp.int32)
    pl.semaphore_wait(barrier, peers)


def peers_of(axis):
    me, size = lax.axis_index(axis), lax.axis_size(axis)
    return size - 1, lambda i: (me + i + 1) % size, lambda i: (me + size - i - 1) % size


def full_barrier():
    barrier = pltpu.get_barrier_semaphore()
    total = 0
    for axis in ("fsdp", "ctx"):
        count, ahead, _ = peers_of(axis)
        loop(
            count,
            lambda i, axis=axis, ahead=ahead: pl.semaphore_signal(
                barrier, inc=1, device_id={axis: ahead(i)}, device_id_type=MESH
            ),
        )
        total += count
    pl.semaphore_wait(barrier, total)


def gather_scratch(chips):
    return [pltpu.SemaphoreType.DMA((chips,)) for _ in range(6)]


class Gather:
    def __init__(self, land, sems, consume=None, late=False):
        self.late = late
        self.land = land
        self.sems = sems
        self.consume = consume
        self.me, self.chip, self.core, self.chips = line_position()

    def right(self, step, source):
        ref = self.land.at[2 * source + self.core]
        return send(ref, ref, self.sems[0].at[step], self.sems[1].at[step], "ctx", self.me + 2)

    def left(self, step, source):
        ref = self.land.at[2 * source + self.core]
        return send(ref, ref, self.sems[2].at[step], self.sems[3].at[step], "ctx", self.me - 2)

    def across(self, source, core):
        ref = self.land.at[2 * source + core]
        other = self.me + 1 - 2 * self.core
        return send(ref, ref, self.sems[4].at[source], self.sems[5].at[source], "ctx", other)

    def step(self, step):
        chip, core, chips = self.chip, self.core, self.chips
        low, high = chip - step, chip + step
        has_low = low >= 0
        has_high = jnp.logical_and(high < chips, step > 0)

        @pl.when(jnp.logical_and(has_low, step > 0))
        def _():
            self.right(step - 1, low).wait_recv()

        @pl.when(jnp.logical_and(has_low, chip < chips - 1))
        def _():
            self.right(step, low).start()

        @pl.when(has_high)
        def _():
            self.left(step - 1, high).wait_recv()

        @pl.when(jnp.logical_and(high < chips, chip > 0))
        def _():
            self.left(step, high).start()

        @pl.when(has_low)
        def _():
            self.across(low, core).start()

        @pl.when(has_high)
        def _():
            self.across(high, core).start()

        if not self.late:
            self.use(step)
            return

        @pl.when(step > 0)
        def _():
            self.use(step - 1)

        @pl.when(step == chips - 1)
        def _():
            self.use(step)

    def use(self, step):
        chip, core, chips = self.chip, self.core, self.chips
        low, high = chip - step, chip + step

        def one(kind):
            upward = kind % 2
            crossed = kind // 2
            source = jnp.where(upward == 1, high, low)
            valid = jnp.where(upward == 1, jnp.logical_and(high < chips, step > 0), low >= 0)
            parity = jnp.where(crossed == 1, 1 - core, core)

            @pl.when(valid)
            def _():
                @pl.when(crossed == 1)
                def _():
                    self.across(source, parity).wait_recv()

                if self.consume is not None:
                    self.consume(2 * source + parity)

        loop(4, one)

    def finish(self):
        chip, core, chips = self.chip, self.core, self.chips

        def one(step):
            @pl.when(jnp.logical_and(chip - step >= 0, chip < chips - 1))
            def _():
                self.right(step, chip - step).wait_send()

            @pl.when(jnp.logical_and(chip + step < chips, chip > 0))
            def _():
                self.left(step, chip + step).wait_send()

            self.across(step, core).wait_send()

        loop(chips, one)


def scatter_scratch(chips, rows):
    buffers = [VMEM((count, CHUNKS, rows, WIDE), BF16) for count in (chips + 1, chips, chips)]
    return buffers + [pltpu.SemaphoreType.DMA((chips, CHUNKS)) for _ in range(6)]


class Scatter:
    def __init__(self, scratch, produce, total):
        self.line, self.out, self.other = scratch[:3]
        self.sems = scratch[3:]
        self.produce = produce
        self.total = total
        self.me, self.chip, self.core, self.chips = line_position()


    def right(self, step, chunk):
        ref = self.line.at[step, chunk]
        sems = self.sems
        return send(ref, ref, sems[0].at[step, chunk], sems[1].at[step, chunk], "ctx", self.me + 2)

    def left(self, step, chunk):
        ref = self.line.at[self.chips - step, chunk]
        sems = self.sems
        return send(ref, ref, sems[2].at[step, chunk], sems[3].at[step, chunk], "ctx", self.me - 2)

    def across(self, target, chunk):
        sems = self.sems
        return send(
            self.out.at[target, chunk],
            self.other.at[target, chunk],
            sems[4].at[target, chunk],
            sems[5].at[target, chunk],
            "ctx",
            self.me + 1 - 2 * self.core,
        )

    def begin(self):
        def clear(index):
            slot, chunk = index // CHUNKS, index % CHUNKS
            at_left = jnp.logical_and(self.chip == 0, slot < self.chips)
            at_right = jnp.logical_and(self.chip == self.chips - 1, slot > 0)

            @pl.when(jnp.logical_or(at_left, at_right))
            def _():
                self.line[slot, chunk] = jnp.zeros(self.line.shape[2:], BF16)

        loop((self.chips + 1) * CHUNKS, clear)

    def when_right(self, time):
        return jnp.logical_and(time >= self.chip, time < self.chips - 1)

    def when_left(self, time):
        return jnp.logical_and(time >= self.chips - 1 - self.chip, time < self.chips - 1)

    def prepare(self, time):
        def cross(target):
            def one(chunk):
                piece = 2 * target + 1 - self.core
                self.out[target, chunk] = self.produce(piece, chunk).astype(BF16)
                self.across(target, chunk).start()

            loop(CHUNKS, one)

        @pl.when(self.when_right(time))
        def _():
            cross(self.chips - 1 - time + self.chip)

        @pl.when(self.when_left(time))
        def _():
            cross(time - (self.chips - 1 - self.chip))

        @pl.when(time == self.chips - 1)
        def _():
            cross(self.chip)

    def step(self, time):
        chip, core, chips = self.chip, self.core, self.chips

        @pl.when(self.when_right(time))
        def _():
            step = time - chip
            target = chips - 1 - step

            def one(chunk):
                self.across(target, chunk).wait_recv()

                @pl.when(chip > 0)
                def _():
                    self.right(step, chunk).wait_recv()

                value = self.produce(2 * target + core, chunk) + self.other[target, chunk].astype(F32)
                value = value + self.line[step, chunk].astype(F32)
                self.line[step, chunk] = value.astype(BF16)
                self.right(step, chunk).start()

            loop(CHUNKS, one)

        @pl.when(self.when_left(time))
        def _():
            step = time - (chips - 1 - chip)

            def one(chunk):
                self.across(step, chunk).wait_recv()

                @pl.when(chip < chips - 1)
                def _():
                    self.left(step, chunk).wait_recv()

                value = self.produce(2 * step + core, chunk) + self.other[step, chunk].astype(F32)
                value = value + self.line[chips - step, chunk].astype(F32)
                self.line[chips - step, chunk] = value.astype(BF16)
                self.left(step, chunk).start()

            loop(CHUNKS, one)

    def finish(self):
        chip, core, chips = self.chip, self.core, self.chips
        last = chips - 1 - chip

        def one(chunk):
            self.across(chip, chunk).wait_recv()
            value = self.produce(2 * chip + core, chunk) + self.other[chip, chunk].astype(F32)

            @pl.when(chip > 0)
            def _():
                self.right(last, chunk).wait_recv()

            @pl.when(chip < chips - 1)
            def _():
                self.left(chip, chunk).wait_recv()

            value = value + self.line[last, chunk].astype(F32)
            value = value + self.line[chips - chip, chunk].astype(F32)
            self.total[:, pl.ds(pl.multiple_of(chunk * WIDE, WIDE), WIDE)] = value

        loop(CHUNKS, one)

        def drain(index):
            step, chunk = index // CHUNKS, index % CHUNKS

            @pl.when(step < last)
            def _():
                self.right(step, chunk).wait_send()

            @pl.when(step < chip)
            def _():
                self.left(step, chunk).wait_send()

            self.across(step, chunk).wait_send()

        loop(chips * CHUNKS, drain)


def row_blocks(rows, body, size=32):
    def one(index):
        body(pl.ds(pl.multiple_of(index * size, size), size))

    loop(rows // size, one)


def inverse_norm(value):
    return lax.rsqrt(jnp.mean(value * value, axis=-1, keepdims=True) + EPS)


def params(identity, megabytes):
    return pltpu.CompilerParams(
        collective_id=identity,
        has_side_effects=True,
        vmem_limit_bytes=megabytes * 1024 * 1024,
    )


def cost(microseconds):
    return pl.CostEstimate(
        flops=int(microseconds * 1.15e9), bytes_accessed=1024, transcendentals=0
    )


def copy_in(source, target, sem):
    copy = pltpu.make_async_copy(source, target, sem)
    copy.start()
    return copy


def first_kernel(rows, width, *refs):
    x, gains, tokens, part, land, proj, weights, gain_rows, all_gains, all_tokens = refs[:10]
    sems, small = refs[10:16], refs[16:]
    me, _, _, chips = line_position()
    shard = lax.axis_index("fsdp")
    shards, ahead, behind = peers_of("fsdp")
    parts, next_part, past_part = peers_of("ctx")
    full_barrier()

    def gain_copy(i, slot):
        return send(gains, all_gains.at[slot], small[0].at[i], small[1].at[i], "fsdp", ahead(i))

    def token_copy(i, slot):
        return send(tokens, all_tokens.at[slot], small[2].at[i], small[3].at[i], "ctx", next_part(i))

    def weight_copy(i, owner):
        target = weights.at[pl.ds(pl.multiple_of(owner * rows, rows), rows), :]
        return send(part, target, small[4].at[i], small[5].at[i], "fsdp", ahead(i))

    loop(shards, lambda i: gain_copy(i, shard).start())
    loop(parts, lambda i: token_copy(i, me).start())
    loop(shards, lambda i: weight_copy(i, shard).start())
    all_gains[shard] = gains[...]
    all_tokens[me] = tokens[...]
    weights[pl.ds(pl.multiple_of(shard * rows, rows), rows), :] = part[...]
    loop(shards, lambda i: gain_copy(i, behind(i)).wait_recv())
    lanes = rows // 128
    for kind in range(2):
        for owner in range(shards + 1):
            for j in range(lanes):
                at = owner * rows + j * 128
                gain_rows[kind : kind + 1, at : at + 128] = all_gains[
                    owner, kind * lanes + j : kind * lanes + j + 1, :
                ]

    def norm(block):
        value = x[block, :].astype(F32)
        land[me, block] = (value * inverse_norm(value) * gain_rows[0:1, :]).astype(BF16)

    row_blocks(x.shape[0], norm)

    gather = Gather(land, sems)
    loop(chips, gather.step)
    loop(shards, lambda i: weight_copy(i, behind(i)).wait_recv())

    def project(piece):
        proj[piece] = dot(land[piece], weights[:, :width])

    loop(2 * chips, project)
    gather.finish()
    loop(shards, lambda i: gain_copy(i, shard).wait_send())
    loop(shards, lambda i: weight_copy(i, shard).wait_send())
    loop(parts, lambda i: token_copy(i, past_part(i)).wait_recv())
    loop(parts, lambda i: token_copy(i, me).wait_send())


def first(hidden, gains, tokens, part, shards, parts, width):
    count = hidden.shape[0]
    return pl.pallas_call(
        functools.partial(first_kernel, D // shards, width),
        out_shape=(
            jax.ShapeDtypeStruct((parts, count, D), BF16),
            jax.ShapeDtypeStruct((parts, count, width), F32),
            jax.ShapeDtypeStruct((D, part.shape[1]), BF16),
            jax.ShapeDtypeStruct((8, D), F32),
            jax.ShapeDtypeStruct((shards, *gains.shape), F32),
            jax.ShapeDtypeStruct((parts, *tokens.shape), jnp.int32),
        ),
        in_specs=[WHOLE] * 4,
        out_specs=(WHOLE,) * 6,
        scratch_shapes=gather_scratch(parts // 2)
        + [pltpu.SemaphoreType.DMA((shards,))] * 2
        + [pltpu.SemaphoreType.DMA((parts,))] * 2
        + [pltpu.SemaphoreType.DMA((shards,))] * 2,
        compiler_params=params(0, 60),
        cost_estimate=cost(85),
        name="gather_normed",
    )(hidden, gains, tokens, part)


def out_kernel(columns, *refs):
    context, weights, x, gain_rows, middle, normed = refs[:6]
    weight, weight_sem, total = refs[6:9]
    scratch = refs[9:]
    chips = line_position()[3]
    copy = copy_in(weights.at[:, columns], weight, weight_sem)

    def produce(piece, chunk):
        return rdot(context[piece], weight[pl.ds(pl.multiple_of(chunk * WIDE, WIDE), WIDE), :])

    scatter = Scatter(scratch, produce, total)
    scatter.begin()
    line_barrier()
    copy.wait()
    scatter.prepare(0)

    def step(time):
        scatter.step(time)
        scatter.prepare(time + 1)

    loop(chips - 1, step)
    scatter.finish()

    def norm(block):
        value = x[block, :].astype(F32) + total[block, :]
        middle[block, :] = value
        normed[block, :] = (value * inverse_norm(value) * gain_rows[1:2, :]).astype(BF16)

    row_blocks(x.shape[0], norm)


def attention_out(context, weights, hidden, gain_rows):
    parts, count, width = context.shape
    return pl.pallas_call(
        functools.partial(out_kernel, pl.ds(weights.shape[1] - width, width)),
        out_shape=(
            jax.ShapeDtypeStruct((count, D), F32),
            jax.ShapeDtypeStruct((count, D), BF16),
        ),
        in_specs=[WHOLE, HBM, WHOLE, WHOLE],
        out_specs=(WHOLE,) * 2,
        scratch_shapes=[VMEM((D, width), BF16), pltpu.SemaphoreType.DMA, VMEM((count, D), F32)]
        + scatter_scratch(parts // 2, count),
        compiler_params=params(1, 60),
        cost_estimate=cost(90),
        name="attention_out",
    )(context, weights, hidden, gain_rows)


def feed_kernel(width, *refs):
    x, grads, weights, land, activation, back = refs[:6]
    weight, weight_sem, grad, grad_sems = refs[6:10]
    sems = refs[10:]
    me, _, _, chips = line_position()
    copy = copy_in(weights, weight, weight_sem)

    def grad_copy(piece):
        return pltpu.make_async_copy(grads.at[piece], grad.at[piece], grad_sems.at[piece])

    loop(2 * chips, lambda piece: grad_copy(piece).start())
    land[me] = x[...]
    size = 256 if width % 256 == 0 else 128

    def consume(piece):
        grad_copy(piece).wait()

        def one(index):
            def columns(kind):
                return pl.ds(pl.multiple_of(kind * width + index * size, 128), size)

            gate = dot(land[piece], weight[:, columns(0)])
            up = dot(land[piece], weight[:, columns(1)])
            grad_act = dot(grad[piece], weight[:, columns(2)])
            sigma = 1.0 / (1.0 + jnp.exp(-gate))
            activation[piece, :, columns(0)] = (gate * sigma * up).astype(BF16)
            back[piece, :, columns(0)] = (
                grad_act * up * sigma * (1.0 + gate * (1.0 - sigma))
            ).astype(BF16)
            back[piece, :, columns(1)] = (grad_act * gate * sigma).astype(BF16)

        loop(width // size, one)

    line_barrier()
    gather = Gather(land, sems, consume)
    copy.wait()
    loop(chips, gather.step)
    gather.finish()


def feed(normed, grads, weights):
    parts, count, _ = grads.shape
    width = weights.shape[1] // 3
    return pl.pallas_call(
        functools.partial(feed_kernel, width),
        out_shape=(
            jax.ShapeDtypeStruct((parts, count, D), BF16),
            jax.ShapeDtypeStruct((parts, count, width), BF16),
            jax.ShapeDtypeStruct((parts, count, 2 * width), BF16),
        ),
        in_specs=[WHOLE, HBM, HBM],
        out_specs=(WHOLE,) * 3,
        scratch_shapes=[
            VMEM(weights.shape, BF16),
            pltpu.SemaphoreType.DMA,
            VMEM(grads.shape, BF16),
            pltpu.SemaphoreType.DMA((parts,)),
        ]
        + gather_scratch(parts // 2),
        compiler_params=params(2, 60),
        cost_estimate=cost(90),
        name="feed",
    )(normed, grads, weights)


def rms_back(value, gain, grad):
    inverse = inverse_norm(value)
    scaled = grad * gain
    inner = jnp.mean(scaled * value, axis=-1, keepdims=True)
    terms = grad * value * inverse
    return inverse * scaled - value * (inverse * inverse * inverse * inner), terms


def feed_back_kernel(columns, *refs):
    back, weights, middle, grad, gain_rows, grad_middle, low, gain_sum = refs[:8]
    weight, weight_sem, total = refs[8:11]
    scratch = refs[11:]
    chips = line_position()[3]
    copy = copy_in(weights.at[:, columns], weight, weight_sem)

    def produce(piece, chunk):
        return rdot(back[piece], weight[pl.ds(pl.multiple_of(chunk * WIDE, WIDE), WIDE), :])

    scatter = Scatter(scratch, produce, total)
    scatter.begin()
    line_barrier()
    copy.wait()
    scatter.prepare(0)

    def step(time):
        scatter.step(time)
        scatter.prepare(time + 1)

    loop(chips - 1, step)
    scatter.finish()
    gain_sum[...] = jnp.zeros_like(gain_sum)

    def norm(block):
        through, terms = rms_back(middle[block, :], gain_rows[1:2, :], total[block, :])
        value = grad[block, :].astype(F32) + through
        grad_middle[block, :] = value
        low[block, :] = value.astype(BF16)
        gain_sum[0:1, :] += jnp.sum(terms, axis=0, keepdims=True)

    row_blocks(middle.shape[0], norm)


def feed_back(back, weights, middle, grad, gain_rows):
    parts, count, width = back.shape
    return pl.pallas_call(
        functools.partial(feed_back_kernel, pl.ds(0, width)),
        out_shape=(
            jax.ShapeDtypeStruct((count, D), F32),
            jax.ShapeDtypeStruct((count, D), BF16),
            jax.ShapeDtypeStruct((8, D), F32),
        ),
        in_specs=[WHOLE, HBM, WHOLE, WHOLE, WHOLE],
        out_specs=(WHOLE,) * 3,
        scratch_shapes=[VMEM((D, width), BF16), pltpu.SemaphoreType.DMA, VMEM((count, D), F32)]
        + scatter_scratch(parts // 2, count),
        compiler_params=params(3, 60),
        cost_estimate=cost(86),
        name="feed_back",
    )(back, weights, middle, grad, gain_rows)


def turn_kernel(columns, down_columns, *refs):
    low, weights, activation, feed_weights, middle, land, context_grad, hidden = refs[:8]
    weight, weight_sem, down, down_sem, total = refs[8:13]
    gather_sems, scratch = refs[13:19], refs[19:]
    me, _, _, chips = line_position()
    copy = copy_in(weights.at[:, columns], weight, weight_sem)
    down_copy = copy_in(feed_weights.at[:, down_columns], down, down_sem)
    land[me] = low[...]

    def consume(piece):
        context_grad[piece] = dot(land[piece], weight[...]).astype(BF16)

    def produce(piece, chunk):
        return rdot(activation[piece], down[pl.ds(pl.multiple_of(chunk * WIDE, WIDE), WIDE), :])

    gather = Gather(land, gather_sems, consume)
    scatter = Scatter(scratch, produce, total)
    scatter.begin()
    line_barrier()
    copy.wait()
    down_copy.wait()
    scatter.prepare(0)

    def step(time):
        gather.step(time)
        scatter.step(time)
        scatter.prepare(time + 1)

    loop(chips - 1, step)
    gather.step(chips - 1)
    scatter.finish()
    gather.finish()

    def add(block):
        hidden[block, :] = (middle[block, :] + total[block, :]).astype(BF16)

    row_blocks(middle.shape[0], add)


def turn(low, weights, activation, feed_weights, middle, width):
    parts, count, feed_width = activation.shape
    return pl.pallas_call(
        functools.partial(
            turn_kernel, pl.ds(weights.shape[1] - width, width), pl.ds(2 * feed_width, feed_width)
        ),
        out_shape=(
            jax.ShapeDtypeStruct((parts, count, D), BF16),
            jax.ShapeDtypeStruct((parts, count, width), BF16),
            jax.ShapeDtypeStruct((count, D), BF16),
        ),
        in_specs=[WHOLE, HBM, WHOLE, HBM, WHOLE],
        out_specs=(WHOLE,) * 3,
        scratch_shapes=[
            VMEM((D, width), BF16),
            pltpu.SemaphoreType.DMA,
            VMEM((D, feed_width), BF16),
            pltpu.SemaphoreType.DMA,
            VMEM((count, D), F32),
        ]
        + gather_scratch(parts // 2)
        + scatter_scratch(parts // 2, count),
        compiler_params=params(4, 62),
        cost_estimate=cost(107),
        name="turn",
    )(low, weights, activation, feed_weights, middle)


def last_kernel(columns, *refs):
    back, weights, x, grad_middle, gain_rows, gain_two, gain_heads, head_grad = refs[:8]
    hidden, gain_out, land = refs[8:11]
    weight, weight_sem, total, gain_one, pack, pack_in, shard_sum, shard_in, head_in = refs[11:20]
    small, gather_sems, scratch = refs[20:26], refs[26:32], refs[32:]
    me, _, _, chips = line_position()
    shard = lax.axis_index("fsdp")
    shards, ahead, _ = peers_of("fsdp")
    parts, next_part, _ = peers_of("ctx")
    copy = copy_in(weights.at[:, columns], weight, weight_sem)

    def produce(piece, chunk):
        return rdot(back[piece], weight[pl.ds(pl.multiple_of(chunk * WIDE, WIDE), WIDE), :])

    def head_copy(i):
        return send(head_grad.at[ahead(i)], head_in.at[i], small[4].at[i], small[5].at[i], "fsdp", ahead(i))

    def head_sum(block):
        value = head_grad[shard, block].astype(F32)
        for i in range(shards):
            value = value + head_in[i, block].astype(F32)
        land[me, block] = value.astype(BF16)

    scatter = Scatter(scratch, produce, total)
    gather = Gather(land, gather_sems)
    scatter.begin()
    full_barrier()
    copy.wait()
    scatter.prepare(0)
    loop(shards, lambda i: head_copy(i).start())

    def step(time):
        scatter.step(time)

        @pl.when(time == 1)
        def _():
            loop(shards, lambda i: head_copy(i).wait_recv())
            row_blocks(head_grad.shape[1], head_sum)

        @pl.when(time >= 1)
        def _():
            gather.step(time - 1)

        scatter.prepare(time + 1)

    loop(chips - 1, step)
    scatter.finish()
    gather.step(chips - 2)
    gain_one[...] = jnp.zeros_like(gain_one)

    def norm(block):
        through, terms = rms_back(x[block, :].astype(F32), gain_rows[0:1, :], total[block, :])
        hidden[block, :] = grad_middle[block, :] + through
        gain_one[0:1, :] += jnp.sum(terms, axis=0, keepdims=True)

    row_blocks(x.shape[0], norm)

    rows = D // (shards + 1)
    lanes = rows // 128
    pack[...] = jnp.zeros_like(pack)
    for owner in range(shards + 1):
        for j in range(lanes):
            at = owner * rows + j * 128
            pack[owner, j : j + 1, :] = gain_one[0:1, at : at + 128]
            pack[owner, lanes + j : lanes + j + 1, :] = gain_two[0:1, at : at + 128]
        pack[owner, 2 * lanes : 2 * lanes + 2, :] = gain_heads[0:2, :]

    def pack_copy(i):
        return send(pack.at[ahead(i)], pack_in.at[i], small[0].at[i], small[1].at[i], "fsdp", ahead(i))

    def sum_copy(i):
        return send(shard_sum, shard_in.at[i], small[2].at[i], small[3].at[i], "ctx", next_part(i))

    loop(shards, lambda i: pack_copy(i).start())
    shard_sum[...] = pack[shard]

    def add_pack(i):
        pack_copy(i).wait_recv()
        shard_sum[...] += pack_in[i]

    loop(shards, add_pack)
    loop(parts, lambda i: sum_copy(i).start())
    gain_out[...] = shard_sum[...]

    def add_sum(i):
        sum_copy(i).wait_recv()
        gain_out[...] += shard_in[i]

    loop(parts, add_sum)
    gather.step(chips - 1)
    gather.finish()
    loop(shards, lambda i: head_copy(i).wait_send())
    loop(shards, lambda i: pack_copy(i).wait_send())
    loop(parts, lambda i: sum_copy(i).wait_send())


def last(back, weights, hidden, grad_middle, gain_rows, gain_two, gain_heads, head_grad):
    parts, count, width = back.shape
    shards, rows, head_width = head_grad.shape
    return pl.pallas_call(
        functools.partial(last_kernel, pl.ds(0, width)),
        out_shape=(
            jax.ShapeDtypeStruct((count, D), F32),
            jax.ShapeDtypeStruct((16, 128), F32),
            jax.ShapeDtypeStruct((parts, rows, head_width), BF16),
        ),
        in_specs=[WHOLE, HBM] + [WHOLE] * 6,
        out_specs=(WHOLE,) * 3,
        scratch_shapes=[
            VMEM((D, width), BF16),
            pltpu.SemaphoreType.DMA,
            VMEM((count, D), F32),
            VMEM((8, D), F32),
            VMEM((shards, 16, 128), F32),
            VMEM((shards, 16, 128), F32),
            VMEM((16, 128), F32),
            VMEM((parts, 16, 128), F32),
            VMEM((shards - 1, rows, head_width), BF16),
        ]
        + [pltpu.SemaphoreType.DMA((shards,))] * 2
        + [pltpu.SemaphoreType.DMA((parts,))] * 2
        + [pltpu.SemaphoreType.DMA((shards,))] * 2
        + gather_scratch(parts // 2)
        + scatter_scratch(parts // 2, count),
        compiler_params=params(5, 60),
        cost_estimate=cost(90),
        name="last",
    )(back, weights, hidden, grad_middle, gain_rows, gain_two, gain_heads, head_grad)


QUERY_TILE = 256
KEY_TILE = 512


def reach(index, tokens):
    return jnp.minimum((index + 2) * QUERY_TILE + KEY_TILE - 1, tokens) // KEY_TILE


def head_norm(value, gain, cosine, sine):
    normed = value * inverse_norm(value) * gain
    return normed * cosine + pltpu.roll(normed, HEAD_SIZE // 2, 1) * sine


def attention_kernel(heads, proj, cosine, sine, gain, id_column, id_row, *refs):
    queries, keys, values, context, inverse = refs
    tokens = proj.shape[0]
    key_at = heads * HEAD_SIZE

    def prepare(index):
        block = pl.ds(pl.multiple_of(index * QUERY_TILE, QUERY_TILE), QUERY_TILE)
        c, s = cosine[block, :], sine[block, :]
        for h in range(heads):
            lanes = slice(h * HEAD_SIZE, (h + 1) * HEAD_SIZE)
            rotated = head_norm(proj[block, lanes], gain[0:1, :], c, s) * HEAD_SIZE ** (-0.5)
            queries[block, lanes] = rotated.astype(BF16)
        rotated = head_norm(proj[block, key_at : key_at + HEAD_SIZE], gain[1:2, :], c, s)
        keys[block, :] = rotated.astype(BF16)
        values[block, :] = proj[block, key_at + HEAD_SIZE : key_at + 2 * HEAD_SIZE].astype(BF16)

    loop(tokens // QUERY_TILE, prepare)

    def attend(index):
        block = pl.ds(pl.multiple_of(index * QUERY_TILE, QUERY_TILE), QUERY_TILE)
        query_ids = id_column[block, :]
        for h in range(heads):
            lanes = slice(h * HEAD_SIZE, (h + 1) * HEAD_SIZE)
            query = queries[block, lanes]

            def one(tile, carry):
                sums, total = carry
                span = pl.ds(pl.multiple_of(tile * KEY_TILE, KEY_TILE), KEY_TILE)
                scores = rdot(query, keys[span, :])
                expon = jnp.where(id_row[0:1, span] <= query_ids, jnp.exp(scores), 0.0)
                sums = sums + dot(expon.astype(BF16), values[span, :])
                return sums, total + jnp.sum(expon, axis=1, keepdims=True)

            start = (jnp.zeros((QUERY_TILE, HEAD_SIZE), F32), jnp.zeros((QUERY_TILE, 1), F32))
            sums, total = lax.fori_loop(0, reach(index, tokens), one, start)
            scale = 1.0 / total
            context[block, lanes] = (sums * scale).astype(BF16)
            inverse[h : h + 1, block] = jnp.broadcast_to(scale, (QUERY_TILE, HEAD_SIZE)).T[0:1, :]

    loop(tokens // QUERY_TILE, attend)


def attention(proj, cosine, sine, gain, id_column, id_row, heads):
    tokens = proj.shape[0]
    width = heads * HEAD_SIZE
    return pl.pallas_call(
        functools.partial(attention_kernel, heads),
        out_shape=(
            jax.ShapeDtypeStruct((tokens, width), BF16),
            jax.ShapeDtypeStruct((tokens, HEAD_SIZE), BF16),
            jax.ShapeDtypeStruct((tokens, HEAD_SIZE), BF16),
            jax.ShapeDtypeStruct((tokens, width), BF16),
            jax.ShapeDtypeStruct((8, tokens), F32),
        ),
        in_specs=[WHOLE] * 6,
        out_specs=(WHOLE,) * 5,
        compiler_params=pltpu.CompilerParams(vmem_limit_bytes=48 * 1024 * 1024),
        cost_estimate=cost(27),
        name="attention",
    )(proj, cosine, sine, gain, id_column, id_row)


def attention_back_kernel(heads, *refs):
    queries, keys, values, out_grad, inverse, context, proj, cosine, sine, gain = refs[:10]
    id_column, id_row, back, gain_sum, key_grad, value_grad, query_grad = refs[10:]
    tokens = proj.shape[0]
    key_at = heads * HEAD_SIZE
    key_grad[...] = jnp.zeros_like(key_grad)
    value_grad[...] = jnp.zeros_like(value_grad)
    gain_sum[...] = jnp.zeros_like(gain_sum)

    def through(block, lanes, grad, row):
        turned = pltpu.roll(grad, HEAD_SIZE // 2, 1)
        unrotated = grad * cosine[block, :] - turned * sine[block, :]
        result, terms = rms_back(proj[block, lanes], gain[row : row + 1, :], unrotated)
        back[block, lanes] = result.astype(BF16)
        gain_sum[row : row + 1, :] += jnp.sum(terms, axis=0, keepdims=True)

    def attend(index):
        block = pl.ds(pl.multiple_of(index * QUERY_TILE, QUERY_TILE), QUERY_TILE)
        query_ids = id_row[0:1, block]
        for h in range(heads):
            lanes = slice(h * HEAD_SIZE, (h + 1) * HEAD_SIZE)
            query = queries[block, lanes]
            grad = out_grad[block, lanes]
            scale = inverse[h : h + 1, block]
            products = grad.astype(F32) * context[block, lanes].astype(F32)
            shift = lax.dot_general(
                jnp.ones((8, HEAD_SIZE), F32),
                products,
                (((1,), (1,)), ((), ())),
                precision=lax.Precision.HIGHEST,
                preferred_element_type=F32,
            )[0:1, :]
            query_grad[...] = jnp.zeros_like(query_grad)

            def one(tile):
                span = pl.ds(pl.multiple_of(tile * KEY_TILE, KEY_TILE), KEY_TILE)
                key = keys[span, :]
                scores = rdot(key, query)
                probs = jnp.where(id_column[span, :] <= query_ids, jnp.exp(scores) * scale, 0.0)
                grad_scores = (probs * (rdot(values[span, :], grad) - shift)).astype(BF16)
                value_grad[span, :] += dot(probs.astype(BF16), grad)
                key_grad[span, :] += dot(grad_scores, query)
                query_grad[...] += tdot(grad_scores, key)

            loop(reach(index, tokens), one)
            through(block, lanes, query_grad[...] * HEAD_SIZE ** (-0.5), 0)

    loop(tokens // QUERY_TILE, attend)

    def finish(index):
        block = pl.ds(pl.multiple_of(index * QUERY_TILE, QUERY_TILE), QUERY_TILE)
        through(block, slice(key_at, key_at + HEAD_SIZE), key_grad[block, :], 1)
        back[block, key_at + HEAD_SIZE : key_at + 2 * HEAD_SIZE] = value_grad[block, :].astype(BF16)

    loop(tokens // QUERY_TILE, finish)


def attention_back(heads, *operands):
    tokens = operands[0].shape[0]
    width = heads * HEAD_SIZE
    return pl.pallas_call(
        functools.partial(attention_back_kernel, heads),
        out_shape=(
            jax.ShapeDtypeStruct((tokens, width + 2 * HEAD_SIZE), BF16),
            jax.ShapeDtypeStruct((8, HEAD_SIZE), F32),
        ),
        in_specs=[WHOLE] * len(operands),
        out_specs=(WHOLE,) * 2,
        scratch_shapes=[
            VMEM((tokens, HEAD_SIZE), F32),
            VMEM((tokens, HEAD_SIZE), F32),
            VMEM((QUERY_TILE, HEAD_SIZE), F32),
        ],
        compiler_params=pltpu.CompilerParams(vmem_limit_bytes=48 * 1024 * 1024),
        cost_estimate=cost(38),
        name="attention_back",
    )(*operands)


def spread_feed_kernel(width, source, gate, up, down):
    gate[...] = source[0, :, :width].astype(F32)
    up[...] = source[0, :, width : 2 * width].astype(F32)
    down[...] = source[0, :, 2 * width :].astype(F32).T


def spread_feed(stacked):
    parts, rows, total = stacked.shape
    width = total // 3
    across = jax.ShapeDtypeStruct((rows, parts * width), F32)
    return pl.pallas_call(
        functools.partial(spread_feed_kernel, width),
        out_shape=(across, across, jax.ShapeDtypeStruct((parts * width, rows), F32)),
        grid=(parts,),
        in_specs=[pl.BlockSpec((1, rows, total), lambda i: (i, 0, 0))],
        out_specs=(
            pl.BlockSpec((rows, width), lambda i: (0, i)),
            pl.BlockSpec((rows, width), lambda i: (0, i)),
            pl.BlockSpec((width, rows), lambda i: (i, 0)),
        ),
        compiler_params=pltpu.CompilerParams(vmem_limit_bytes=32 * 1024 * 1024),
        name="spread_feed",
    )(stacked)


def spread_heads_kernel(width, source, query, key, value, out):
    second = width + HEAD_SIZE
    third = second + HEAD_SIZE
    query[...] = source[0, :, :width].astype(F32)
    key[...] = source[0, :, width:second].astype(F32)
    value[...] = source[0, :, second:third].astype(F32)
    out[...] = source[0, :, third:].astype(F32).T


def spread_heads(stacked, width):
    parts, rows, total = stacked.shape
    widths = (width, HEAD_SIZE, HEAD_SIZE)
    return pl.pallas_call(
        functools.partial(spread_heads_kernel, width),
        out_shape=tuple(jax.ShapeDtypeStruct((rows, parts * w), F32) for w in widths)
        + (jax.ShapeDtypeStruct((parts * width, rows), F32),),
        grid=(parts,),
        in_specs=[pl.BlockSpec((1, rows, total), lambda i: (i, 0, 0))],
        out_specs=tuple(pl.BlockSpec((rows, w), lambda i: (0, i)) for w in widths)
        + (pl.BlockSpec((width, rows), lambda i: (i, 0)),),
        compiler_params=pltpu.CompilerParams(vmem_limit_bytes=32 * 1024 * 1024),
        name="spread_heads",
    )(stacked)


def by_row(array):
    return with_layout_constraint(array, Layout(major_to_minor=(0, 1)))


def own_columns(array, index, width):
    return lax.dynamic_slice_in_dim(array, index * width, width, axis=1)


def own_rows(array, index, width):
    return lax.dynamic_slice_in_dim(array, index * width, width, axis=0)


def local(
    hidden_in,
    weight_query,
    key_weight_matrix,
    weight_value,
    weight_out,
    weight_gate,
    weight_up,
    weight_down,
    gain_attention,
    gain_feed,
    gain_query,
    gain_key,
    positions,
    token_block_index,
    grad_out,
):
    parts = lax.axis_size("ctx")
    shards = lax.axis_size("fsdp")
    me = lax.axis_index("ctx")
    shard = lax.axis_index("fsdp")
    heads = QUERY_HEADS // parts
    sharers = parts // KEY_VALUE_HEADS
    key_head = me // sharers
    width = heads * HEAD_SIZE
    feed_width = FF // parts
    rows = D // shards
    head_rows = HEAD_SIZE // shards
    count = hidden_in.shape[1]
    tokens = parts * count

    def gather_rows(piece):
        return lax.all_gather(piece, "fsdp", axis=0, tiled=True)

    def sum_rows(grad):
        return lax.psum_scatter(grad.astype(BF16), "fsdp", scatter_dimension=0, tiled=True)

    def gather_parts(piece):
        return lax.all_gather(piece, "ctx", axis=0)

    own_heads_weight = jnp.concatenate(
        [
            own_columns(weight_query, me, width),
            own_columns(key_weight_matrix, key_head, HEAD_SIZE),
            own_columns(weight_value, key_head, HEAD_SIZE),
            own_rows(weight_out, me, width).T,
        ],
        axis=1,
    )
    feed_weight = gather_rows(
        jnp.concatenate(
            [
                own_columns(weight_gate, me, feed_width),
                own_columns(weight_up, me, feed_width),
                own_rows(weight_down, me, feed_width).T,
            ],
            axis=1,
        )
    )

    own_gains = jnp.concatenate([gain_attention, gain_feed, gain_query, gain_key]).astype(F32)
    own_gains = jnp.pad(own_gains, (0, 2048 - own_gains.shape[0])).reshape(16, 128)
    own_tokens = jnp.pad(jnp.stack([positions[0], token_block_index[0]]), ((0, 6), (0, 0)))
    hidden, grad = hidden_in[0], grad_out[0]
    normed_all, proj, heads_weight, gain_rows, gains, whole = first(
        hidden, own_gains, own_tokens, own_heads_weight, shards, parts, width + 2 * HEAD_SIZE
    )
    grad_late, gains = lax.optimization_barrier((grad, gains))
    grad_all = gather_parts(grad_late)
    flat_gains = gains.reshape(shards, -1)
    norm_query = flat_gains[:, 2 * rows : 2 * rows + head_rows].reshape(1, -1)
    norm_key = flat_gains[:, 2 * rows + head_rows : 2 * rows + 2 * head_rows].reshape(1, -1)
    head_gains = jnp.concatenate([norm_query, norm_key, jnp.zeros((6, HEAD_SIZE), F32)])

    half = HEAD_SIZE // 2
    freq = THETA ** (-(jnp.arange(half).astype(F32) * 2.0 / HEAD_SIZE))
    angle = whole[:, 0].reshape(-1).astype(F32)[:, None] * freq
    cosine, sine = jnp.cos(angle), jnp.sin(angle)
    cosine = jnp.concatenate([cosine, cosine], axis=1)
    sine = jnp.concatenate([-sine, sine], axis=1)
    ids = whole[:, 1].reshape(-1)
    id_row, id_column = ids[None, :], ids[:, None]

    proj = proj.reshape(tokens, width + 2 * HEAD_SIZE)
    queries, keys, values, context, inverse = attention(
        proj, cosine, sine, head_gains, id_column, id_row, heads
    )
    middle, normed_two = attention_out(
        context.reshape(parts, count, width), heads_weight, hidden, gain_rows
    )
    normed_two_all, activation, back = feed(normed_two, grad_all, feed_weight)

    flat_grad = grad_all.reshape(tokens, D)
    flat_back = back.reshape(tokens, 2 * feed_width)
    flat_activation = activation.reshape(tokens, feed_width)
    feed_grad = jnp.concatenate(
        [
            by_row(tdot(normed_two_all.reshape(tokens, D), flat_back).astype(BF16)),
            by_row(tdot(flat_grad, flat_activation).astype(BF16)),
        ],
        axis=1,
    )
    back, feed_grad = lax.optimization_barrier((back, feed_grad))
    feed_shard = sum_rows(feed_grad)

    grad_middle, low, gain_two = feed_back(back, feed_weight, middle, grad, gain_rows)
    low_all, context_grad, hidden_out = turn(low, heads_weight, activation, feed_weight, middle, width)

    context_grad, feed_shard = lax.optimization_barrier((context_grad, feed_shard))
    feed_parts = gather_parts(feed_shard)
    context_grad = context_grad.reshape(tokens, width)
    grad_qkv, gain_heads = attention_back(
        heads,
        queries,
        keys,
        values,
        context_grad,
        inverse,
        context,
        proj,
        cosine,
        sine,
        head_gains,
        id_column,
        id_row,
    )
    head_grad = jnp.concatenate(
        [
            by_row(tdot(normed_all.reshape(tokens, D), grad_qkv).astype(BF16)),
            by_row(tdot(low_all.reshape(tokens, D), context).astype(BF16)),
        ],
        axis=1,
    )
    grad_hidden, gain_sums, head_parts = last(
        grad_qkv.reshape(parts, count, -1),
        heads_weight,
        hidden,
        grad_middle,
        gain_rows,
        gain_two,
        gain_heads,
        head_grad.reshape(shards, rows, -1),
    )

    gain_sums = gain_sums.reshape(-1)
    grad_gate, grad_up, grad_down = spread_feed(feed_parts)
    grad_query, grad_key, grad_value, grad_out_weight = spread_heads(head_parts, width)
    if sharers > 1:
        grad_key, grad_value = (
            part.reshape(rows, KEY_VALUE_HEADS, sharers, HEAD_SIZE).sum(axis=2).reshape(rows, -1)
            for part in (grad_key, grad_value)
        )
    return (
        hidden_out[None],
        grad_hidden[None],
        grad_query,
        grad_key,
        grad_value,
        grad_out_weight,
        grad_gate,
        grad_up,
        grad_down,
        gain_sums[:rows],
        gain_sums[rows : 2 * rows],
        lax.dynamic_slice_in_dim(gain_sums, 2 * rows + shard * head_rows, head_rows),
        lax.dynamic_slice_in_dim(gain_sums, 2 * rows + HEAD_SIZE + shard * head_rows, head_rows),
    )


def solution(mesh):
    tokens = P("fsdp", "ctx", None)
    by_rows = P("fsdp", None)
    by_columns = P(None, "fsdp")
    per_token = P("fsdp", "ctx")
    vector = P("fsdp")
    weights = (by_rows, by_rows, by_rows, by_columns, by_rows, by_rows, by_columns)
    return jax.shard_map(
        local,
        mesh=mesh,
        in_specs=(tokens, *weights, vector, vector, vector, vector, per_token, per_token, tokens),
        out_specs=(tokens, tokens, *weights, vector, vector, vector, vector),
        check_vma=False,
    )
```

```python
import functools

import jax
import jax.numpy as jnp
from jax import lax
from jax.experimental import pallas as pl
from jax.experimental.layout import Layout, with_layout_constraint
from jax.experimental.pallas import tpu as pltpu
from jax.sharding import PartitionSpec as P

D = 2048
QUERY_HEADS = 16
KEY_VALUE_HEADS = 8
HEAD_SIZE = 128
FF = 6144
EPS = 1e-06
THETA = 1000000.0
F32 = jnp.float32
BF16 = jnp.bfloat16
MESH = pl.DeviceIdType.MESH
VMEM = pltpu.VMEM
WHOLE = pl.BlockSpec(memory_space=pltpu.VMEM)
HBM = pl.BlockSpec(memory_space=pl.ANY)
CHUNKS = 4
WIDE = D // CHUNKS


def dot(left, right):
    return jnp.dot(left, right, preferred_element_type=F32)


def tdot(left, right):
    return lax.dot_general(left, right, (((0,), (0,)), ((), ())), preferred_element_type=F32)


def rdot(left, right):
    return lax.dot_general(left, right, (((1,), (1,)), ((), ())), preferred_element_type=F32)


def loop(count, body):
    def step(index, carry):
        body(index)
        return carry

    lax.fori_loop(0, count, step, 0)


def line_position():
    me = lax.axis_index("ctx")
    return me, me // 2, me % 2, lax.axis_size("ctx") // 2


def send(source, target, send_sem, recv_sem, axis, index):
    return pltpu.make_async_remote_copy(
        src_ref=source,
        dst_ref=target,
        send_sem=send_sem,
        recv_sem=recv_sem,
        device_id={axis: index},
        device_id_type=MESH,
    )


def line_barrier():
    me, chip, core, chips = line_position()
    barrier = pltpu.get_barrier_semaphore()

    def greet(index):
        pl.semaphore_signal(barrier, inc=1, device_id={"ctx": index}, device_id_type=MESH)

    greet(me + 1 - 2 * core)

    @pl.when(chip > 0)
    def _():
        greet(me - 2)

    @pl.when(chip < chips - 1)
    def _():
        greet(me + 2)

    peers = 1 + (chip > 0).astype(jnp.int32) + (chip < chips - 1).astype(jnp.int32)
    pl.semaphore_wait(barrier, peers)


def peers_of(axis):
    me, size = lax.axis_index(axis), lax.axis_size(axis)
    return size - 1, lambda i: (me + i + 1) % size, lambda i: (me + size - i - 1) % size


def full_barrier():
    barrier = pltpu.get_barrier_semaphore()
    total = 0
    for axis in ("fsdp", "ctx"):
        count, ahead, _ = peers_of(axis)
        loop(
            count,
            lambda i, axis=axis, ahead=ahead: pl.semaphore_signal(
                barrier, inc=1, device_id={axis: ahead(i)}, device_id_type=MESH
            ),
        )
        total += count
    pl.semaphore_wait(barrier, total)


def gather_scratch(chips):
    return [pltpu.SemaphoreType.DMA((chips,)) for _ in range(6)]


class Gather:
    def __init__(self, land, sems, consume=None, late=False):
        self.late = late
        self.land = land
        self.sems = sems
        self.consume = consume
        self.me, self.chip, self.core, self.chips = line_position()

    def right(self, step, source):
        ref = self.land.at[2 * source + self.core]
        return send(ref, ref, self.sems[0].at[step], self.sems[1].at[step], "ctx", self.me + 2)

    def left(self, step, source):
        ref = self.land.at[2 * source + self.core]
        return send(ref, ref, self.sems[2].at[step], self.sems[3].at[step], "ctx", self.me - 2)

    def across(self, source, core):
        ref = self.land.at[2 * source + core]
        other = self.me + 1 - 2 * self.core
        return send(ref, ref, self.sems[4].at[source], self.sems[5].at[source], "ctx", other)

    def step(self, step):
        chip, core, chips = self.chip, self.core, self.chips
        low, high = chip - step, chip + step
        has_low = low >= 0
        has_high = jnp.logical_and(high < chips, step > 0)

        @pl.when(jnp.logical_and(has_low, step > 0))
        def _():
            self.right(step - 1, low).wait_recv()

        @pl.when(jnp.logical_and(has_low, chip < chips - 1))
        def _():
            self.right(step, low).start()

        @pl.when(has_high)
        def _():
            self.left(step - 1, high).wait_recv()

        @pl.when(jnp.logical_and(high < chips, chip > 0))
        def _():
            self.left(step, high).start()

        @pl.when(has_low)
        def _():
            self.across(low, core).start()

        @pl.when(has_high)
        def _():
            self.across(high, core).start()

        if not self.late:
            self.use(step)
            return

        @pl.when(step > 0)
        def _():
            self.use(step - 1)

        @pl.when(step == chips - 1)
        def _():
            self.use(step)

    def use(self, step):
        chip, core, chips = self.chip, self.core, self.chips
        low, high = chip - step, chip + step

        def one(kind):
            upward = kind % 2
            crossed = kind // 2
            source = jnp.where(upward == 1, high, low)
            valid = jnp.where(upward == 1, jnp.logical_and(high < chips, step > 0), low >= 0)
            parity = jnp.where(crossed == 1, 1 - core, core)

            @pl.when(valid)
            def _():
                @pl.when(crossed == 1)
                def _():
                    self.across(source, parity).wait_recv()

                if self.consume is not None:
                    self.consume(2 * source + parity)

        loop(4, one)

    def finish(self):
        chip, core, chips = self.chip, self.core, self.chips

        def one(step):
            @pl.when(jnp.logical_and(chip - step >= 0, chip < chips - 1))
            def _():
                self.right(step, chip - step).wait_send()

            @pl.when(jnp.logical_and(chip + step < chips, chip > 0))
            def _():
                self.left(step, chip + step).wait_send()

            self.across(step, core).wait_send()

        loop(chips, one)


def scatter_scratch(chips, rows):
    buffers = [VMEM((count, CHUNKS, rows, WIDE), BF16) for count in (chips + 1, chips, chips)]
    return buffers + [pltpu.SemaphoreType.DMA((chips, CHUNKS)) for _ in range(6)]


class Scatter:
    def __init__(self, scratch, produce, total):
        self.line, self.out, self.other = scratch[:3]
        self.sems = scratch[3:]
        self.produce = produce
        self.total = total
        self.me, self.chip, self.core, self.chips = line_position()


    def right(self, step, chunk):
        ref = self.line.at[step, chunk]
        sems = self.sems
        return send(ref, ref, sems[0].at[step, chunk], sems[1].at[step, chunk], "ctx", self.me + 2)

    def left(self, step, chunk):
        ref = self.line.at[self.chips - step, chunk]
        sems = self.sems
        return send(ref, ref, sems[2].at[step, chunk], sems[3].at[step, chunk], "ctx", self.me - 2)

    def across(self, target, chunk):
        sems = self.sems
        return send(
            self.out.at[target, chunk],
            self.other.at[target, chunk],
            sems[4].at[target, chunk],
            sems[5].at[target, chunk],
            "ctx",
            self.me + 1 - 2 * self.core,
        )

    def begin(self):
        def clear(index):
            slot, chunk = index // CHUNKS, index % CHUNKS
            at_left = jnp.logical_and(self.chip == 0, slot < self.chips)
            at_right = jnp.logical_and(self.chip == self.chips - 1, slot > 0)

            @pl.when(jnp.logical_or(at_left, at_right))
            def _():
                self.line[slot, chunk] = jnp.zeros(self.line.shape[2:], BF16)

        loop((self.chips + 1) * CHUNKS, clear)

    def when_right(self, time):
        return jnp.logical_and(time >= self.chip, time < self.chips - 1)

    def when_left(self, time):
        return jnp.logical_and(time >= self.chips - 1 - self.chip, time < self.chips - 1)

    def prepare(self, time):
        def cross(target):
            def one(chunk):
                piece = 2 * target + 1 - self.core
                self.out[target, chunk] = self.produce(piece, chunk).astype(BF16)
                self.across(target, chunk).start()

            loop(CHUNKS, one)

        @pl.when(self.when_right(time))
        def _():
            cross(self.chips - 1 - time + self.chip)

        @pl.when(self.when_left(time))
        def _():
            cross(time - (self.chips - 1 - self.chip))

        @pl.when(time == self.chips - 1)
        def _():
            cross(self.chip)

    def step(self, time):
        chip, core, chips = self.chip, self.core, self.chips

        @pl.when(self.when_right(time))
        def _():
            step = time - chip
            target = chips - 1 - step

            def one(chunk):
                self.across(target, chunk).wait_recv()

                @pl.when(chip > 0)
                def _():
                    self.right(step, chunk).wait_recv()

                value = self.produce(2 * target + core, chunk) + self.other[target, chunk].astype(F32)
                value = value + self.line[step, chunk].astype(F32)
                self.line[step, chunk] = value.astype(BF16)
                self.right(step, chunk).start()

            loop(CHUNKS, one)

        @pl.when(self.when_left(time))
        def _():
            step = time - (chips - 1 - chip)

            def one(chunk):
                self.across(step, chunk).wait_recv()

                @pl.when(chip < chips - 1)
                def _():
                    self.left(step, chunk).wait_recv()

                value = self.produce(2 * step + core, chunk) + self.other[step, chunk].astype(F32)
                value = value + self.line[chips - step, chunk].astype(F32)
                self.line[chips - step, chunk] = value.astype(BF16)
                self.left(step, chunk).start()

            loop(CHUNKS, one)

    def finish(self):
        chip, core, chips = self.chip, self.core, self.chips
        last = chips - 1 - chip

        def one(chunk):
            self.across(chip, chunk).wait_recv()
            value = self.produce(2 * chip + core, chunk) + self.other[chip, chunk].astype(F32)

            @pl.when(chip > 0)
            def _():
                self.right(last, chunk).wait_recv()

            @pl.when(chip < chips - 1)
            def _():
                self.left(chip, chunk).wait_recv()

            value = value + self.line[last, chunk].astype(F32)
            value = value + self.line[chips - chip, chunk].astype(F32)
            self.total[:, pl.ds(pl.multiple_of(chunk * WIDE, WIDE), WIDE)] = value

        loop(CHUNKS, one)

        def drain(index):
            step, chunk = index // CHUNKS, index % CHUNKS

            @pl.when(step < last)
            def _():
                self.right(step, chunk).wait_send()

            @pl.when(step < chip)
            def _():
                self.left(step, chunk).wait_send()

            self.across(step, chunk).wait_send()

        loop(chips * CHUNKS, drain)


def row_blocks(rows, body, size=32):
    def one(index):
        body(pl.ds(pl.multiple_of(index * size, size), size))

    loop(rows // size, one)


def inverse_norm(value):
    return lax.rsqrt(jnp.mean(value * value, axis=-1, keepdims=True) + EPS)


def params(identity, megabytes):
    return pltpu.CompilerParams(
        collective_id=identity,
        has_side_effects=True,
        vmem_limit_bytes=megabytes * 1024 * 1024,
    )


def cost(microseconds):
    return pl.CostEstimate(
        flops=int(microseconds * 1.15e9), bytes_accessed=1024, transcendentals=0
    )


def copy_in(source, target, sem):
    copy = pltpu.make_async_copy(source, target, sem)
    copy.start()
    return copy


def first_kernel(rows, width, *refs):
    x, gains, tokens, part, land, proj, weights, gain_rows, all_gains, all_tokens = refs[:10]
    sems, small = refs[10:16], refs[16:]
    me, _, _, chips = line_position()
    shard = lax.axis_index("fsdp")
    shards, ahead, behind = peers_of("fsdp")
    parts, next_part, past_part = peers_of("ctx")
    full_barrier()

    def gain_copy(i, slot):
        return send(gains, all_gains.at[slot], small[0].at[i], small[1].at[i], "fsdp", ahead(i))

    def token_copy(i, slot):
        return send(tokens, all_tokens.at[slot], small[2].at[i], small[3].at[i], "ctx", next_part(i))

    def weight_copy(i, owner):
        target = weights.at[pl.ds(pl.multiple_of(owner * rows, rows), rows), :]
        return send(part, target, small[4].at[i], small[5].at[i], "fsdp", ahead(i))

    loop(shards, lambda i: gain_copy(i, shard).start())
    loop(parts, lambda i: token_copy(i, me).start())
    loop(shards, lambda i: weight_copy(i, shard).start())
    all_gains[shard] = gains[...]
    all_tokens[me] = tokens[...]
    weights[pl.ds(pl.multiple_of(shard * rows, rows), rows), :] = part[...]
    loop(shards, lambda i: gain_copy(i, behind(i)).wait_recv())
    lanes = rows // 128
    for kind in range(2):
        for owner in range(shards + 1):
            for j in range(lanes):
                at = owner * rows + j * 128
                gain_rows[kind : kind + 1, at : at + 128] = all_gains[
                    owner, kind * lanes + j : kind * lanes + j + 1, :
                ]

    def norm(block):
        value = x[block, :].astype(F32)
        land[me, block] = (value * inverse_norm(value) * gain_rows[0:1, :]).astype(BF16)

    row_blocks(x.shape[0], norm)

    gather = Gather(land, sems)
    loop(chips, gather.step)
    loop(shards, lambda i: weight_copy(i, behind(i)).wait_recv())

    def project(piece):
        proj[piece] = dot(land[piece], weights[:, :width])

    loop(2 * chips, project)
    gather.finish()
    loop(shards, lambda i: gain_copy(i, shard).wait_send())
    loop(shards, lambda i: weight_copy(i, shard).wait_send())
    loop(parts, lambda i: token_copy(i, past_part(i)).wait_recv())
    loop(parts, lambda i: token_copy(i, me).wait_send())


def first(hidden, gains, tokens, part, shards, parts, width):
    count = hidden.shape[0]
    return pl.pallas_call(
        functools.partial(first_kernel, D // shards, width),
        out_shape=(
            jax.ShapeDtypeStruct((parts, count, D), BF16),
            jax.ShapeDtypeStruct((parts, count, width), F32),
            jax.ShapeDtypeStruct((D, part.shape[1]), BF16),
            jax.ShapeDtypeStruct((8, D), F32),
            jax.ShapeDtypeStruct((shards, *gains.shape), F32),
            jax.ShapeDtypeStruct((parts, *tokens.shape), jnp.int32),
        ),
        in_specs=[WHOLE] * 4,
        out_specs=(WHOLE,) * 6,
        scratch_shapes=gather_scratch(parts // 2)
        + [pltpu.SemaphoreType.DMA((shards,))] * 2
        + [pltpu.SemaphoreType.DMA((parts,))] * 2
        + [pltpu.SemaphoreType.DMA((shards,))] * 2,
        compiler_params=params(0, 60),
        cost_estimate=cost(85),
        name="gather_normed",
    )(hidden, gains, tokens, part)


def feed_kernel(width, *refs):
    x, grads, weights, land, activation, back = refs[:6]
    weight, weight_sem, grad, grad_sems = refs[6:10]
    sems = refs[10:]
    me, _, _, chips = line_position()
    copy = copy_in(weights, weight, weight_sem)

    def grad_copy(piece):
        return pltpu.make_async_copy(grads.at[piece], grad.at[piece], grad_sems.at[piece])

    loop(2 * chips, lambda piece: grad_copy(piece).start())
    land[me] = x[...]
    size = 256 if width % 256 == 0 else 128

    def consume(piece):
        grad_copy(piece).wait()

        def one(index):
            def columns(kind):
                return pl.ds(pl.multiple_of(kind * width + index * size, 128), size)

            gate = dot(land[piece], weight[:, columns(0)])
            up = dot(land[piece], weight[:, columns(1)])
            grad_act = dot(grad[piece], weight[:, columns(2)])
            sigma = 1.0 / (1.0 + jnp.exp(-gate))
            activation[piece, :, columns(0)] = (gate * sigma * up).astype(BF16)
            back[piece, :, columns(0)] = (
                grad_act * up * sigma * (1.0 + gate * (1.0 - sigma))
            ).astype(BF16)
            back[piece, :, columns(1)] = (grad_act * gate * sigma).astype(BF16)

        loop(width // size, one)

    line_barrier()
    gather = Gather(land, sems, consume)
    copy.wait()
    loop(chips, gather.step)
    gather.finish()


def feed(normed, grads, weights):
    parts, count, _ = grads.shape
    width = weights.shape[1] // 3
    return pl.pallas_call(
        functools.partial(feed_kernel, width),
        out_shape=(
            jax.ShapeDtypeStruct((parts, count, D), BF16),
            jax.ShapeDtypeStruct((parts, count, width), BF16),
            jax.ShapeDtypeStruct((parts, count, 2 * width), BF16),
        ),
        in_specs=[WHOLE, HBM, HBM],
        out_specs=(WHOLE,) * 3,
        scratch_shapes=[
            VMEM(weights.shape, BF16),
            pltpu.SemaphoreType.DMA,
            VMEM(grads.shape, BF16),
            pltpu.SemaphoreType.DMA((parts,)),
        ]
        + gather_scratch(parts // 2),
        compiler_params=params(2, 60),
        cost_estimate=cost(90),
        name="feed",
    )(normed, grads, weights)


def rms_back(value, gain, grad):
    inverse = inverse_norm(value)
    scaled = grad * gain
    inner = jnp.mean(scaled * value, axis=-1, keepdims=True)
    terms = grad * value * inverse
    return inverse * scaled - value * (inverse * inverse * inverse * inner), terms


def feed_back_kernel(columns, *refs):
    back, weights, middle, grad, gain_rows, grad_middle, low, gain_sum = refs[:8]
    weight, weight_sem, total = refs[8:11]
    scratch = refs[11:]
    chips = line_position()[3]
    copy = copy_in(weights.at[:, columns], weight, weight_sem)

    def produce(piece, chunk):
        return rdot(back[piece], weight[pl.ds(pl.multiple_of(chunk * WIDE, WIDE), WIDE), :])

    scatter = Scatter(scratch, produce, total)
    scatter.begin()
    line_barrier()
    copy.wait()
    scatter.prepare(0)

    def step(time):
        scatter.step(time)
        scatter.prepare(time + 1)

    loop(chips - 1, step)
    scatter.finish()
    gain_sum[...] = jnp.zeros_like(gain_sum)

    def norm(block):
        through, terms = rms_back(middle[block, :], gain_rows[1:2, :], total[block, :])
        value = grad[block, :].astype(F32) + through
        grad_middle[block, :] = value
        low[block, :] = value.astype(BF16)
        gain_sum[0:1, :] += jnp.sum(terms, axis=0, keepdims=True)

    row_blocks(middle.shape[0], norm)


def feed_back(back, weights, middle, grad, gain_rows):
    parts, count, width = back.shape
    return pl.pallas_call(
        functools.partial(feed_back_kernel, pl.ds(0, width)),
        out_shape=(
            jax.ShapeDtypeStruct((count, D), F32),
            jax.ShapeDtypeStruct((count, D), BF16),
            jax.ShapeDtypeStruct((8, D), F32),
        ),
        in_specs=[WHOLE, HBM, WHOLE, WHOLE, WHOLE],
        out_specs=(WHOLE,) * 3,
        scratch_shapes=[VMEM((D, width), BF16), pltpu.SemaphoreType.DMA, VMEM((count, D), F32)]
        + scatter_scratch(parts // 2, count),
        compiler_params=params(3, 60),
        cost_estimate=cost(86),
        name="feed_back",
    )(back, weights, middle, grad, gain_rows)


def turn_kernel(columns, down_columns, *refs):
    low, weights, activation, feed_weights, middle, land, context_grad, hidden = refs[:8]
    weight, weight_sem, down, down_sem, total = refs[8:13]
    gather_sems, scratch = refs[13:19], refs[19:]
    me, _, _, chips = line_position()
    copy = copy_in(weights.at[:, columns], weight, weight_sem)
    down_copy = copy_in(feed_weights.at[:, down_columns], down, down_sem)
    land[me] = low[...]

    def consume(piece):
        context_grad[piece] = dot(land[piece], weight[...]).astype(BF16)

    def produce(piece, chunk):
        return rdot(activation[piece], down[pl.ds(pl.multiple_of(chunk * WIDE, WIDE), WIDE), :])

    gather = Gather(land, gather_sems, consume)
    scatter = Scatter(scratch, produce, total)
    scatter.begin()
    line_barrier()
    copy.wait()
    down_copy.wait()
    scatter.prepare(0)

    def step(time):
        gather.step(time)
        scatter.step(time)
        scatter.prepare(time + 1)

    loop(chips - 1, step)
    gather.step(chips - 1)
    scatter.finish()
    gather.finish()

    def add(block):
        hidden[block, :] = (middle[block, :] + total[block, :]).astype(BF16)

    row_blocks(middle.shape[0], add)


def turn(low, weights, activation, feed_weights, middle, width):
    parts, count, feed_width = activation.shape
    return pl.pallas_call(
        functools.partial(
            turn_kernel, pl.ds(weights.shape[1] - width, width), pl.ds(2 * feed_width, feed_width)
        ),
        out_shape=(
            jax.ShapeDtypeStruct((parts, count, D), BF16),
            jax.ShapeDtypeStruct((parts, count, width), BF16),
            jax.ShapeDtypeStruct((count, D), BF16),
        ),
        in_specs=[WHOLE, HBM, WHOLE, HBM, WHOLE],
        out_specs=(WHOLE,) * 3,
        scratch_shapes=[
            VMEM((D, width), BF16),
            pltpu.SemaphoreType.DMA,
            VMEM((D, feed_width), BF16),
            pltpu.SemaphoreType.DMA,
            VMEM((count, D), F32),
        ]
        + gather_scratch(parts // 2)
        + scatter_scratch(parts // 2, count),
        compiler_params=params(4, 62),
        cost_estimate=cost(107),
        name="turn",
    )(low, weights, activation, feed_weights, middle)


def last_kernel(columns, *refs):
    back, weights, x, grad_middle, gain_rows, gain_two, gain_heads, head_grad = refs[:8]
    hidden, gain_out, land = refs[8:11]
    weight, weight_sem, total, gain_one, pack, pack_in, shard_sum, shard_in, head_in = refs[11:20]
    small, gather_sems, scratch = refs[20:26], refs[26:32], refs[32:]
    me, _, _, chips = line_position()
    shard = lax.axis_index("fsdp")
    shards, ahead, _ = peers_of("fsdp")
    parts, next_part, _ = peers_of("ctx")
    copy = copy_in(weights.at[:, columns], weight, weight_sem)

    def produce(piece, chunk):
        return rdot(back[piece], weight[pl.ds(pl.multiple_of(chunk * WIDE, WIDE), WIDE), :])

    def head_copy(i):
        return send(head_grad.at[ahead(i)], head_in.at[i], small[4].at[i], small[5].at[i], "fsdp", ahead(i))

    def head_sum(block):
        value = head_grad[shard, block].astype(F32)
        for i in range(shards):
            value = value + head_in[i, block].astype(F32)
        land[me, block] = value.astype(BF16)

    scatter = Scatter(scratch, produce, total)
    gather = Gather(land, gather_sems)
    scatter.begin()
    full_barrier()
    copy.wait()
    scatter.prepare(0)
    loop(shards, lambda i: head_copy(i).start())

    def step(time):
        scatter.step(time)

        @pl.when(time == 1)
        def _():
            loop(shards, lambda i: head_copy(i).wait_recv())
            row_blocks(head_grad.shape[1], head_sum)

        @pl.when(time >= 1)
        def _():
            gather.step(time - 1)

        scatter.prepare(time + 1)

    loop(chips - 1, step)
    scatter.finish()
    gather.step(chips - 2)
    gain_one[...] = jnp.zeros_like(gain_one)

    def norm(block):
        through, terms = rms_back(x[block, :].astype(F32), gain_rows[0:1, :], total[block, :])
        hidden[block, :] = grad_middle[block, :] + through
        gain_one[0:1, :] += jnp.sum(terms, axis=0, keepdims=True)

    row_blocks(x.shape[0], norm)

    rows = D // (shards + 1)
    lanes = rows // 128
    pack[...] = jnp.zeros_like(pack)
    for owner in range(shards + 1):
        for j in range(lanes):
            at = owner * rows + j * 128
            pack[owner, j : j + 1, :] = gain_one[0:1, at : at + 128]
            pack[owner, lanes + j : lanes + j + 1, :] = gain_two[0:1, at : at + 128]
        pack[owner, 2 * lanes : 2 * lanes + 2, :] = gain_heads[0:2, :]

    def pack_copy(i):
        return send(pack.at[ahead(i)], pack_in.at[i], small[0].at[i], small[1].at[i], "fsdp", ahead(i))

    def sum_copy(i):
        return send(shard_sum, shard_in.at[i], small[2].at[i], small[3].at[i], "ctx", next_part(i))

    loop(shards, lambda i: pack_copy(i).start())
    shard_sum[...] = pack[shard]

    def add_pack(i):
        pack_copy(i).wait_recv()
        shard_sum[...] += pack_in[i]

    loop(shards, add_pack)
    loop(parts, lambda i: sum_copy(i).start())
    gain_out[...] = shard_sum[...]

    def add_sum(i):
        sum_copy(i).wait_recv()
        gain_out[...] += shard_in[i]

    loop(parts, add_sum)
    gather.step(chips - 1)
    gather.finish()
    loop(shards, lambda i: head_copy(i).wait_send())
    loop(shards, lambda i: pack_copy(i).wait_send())
    loop(parts, lambda i: sum_copy(i).wait_send())


def last(back, weights, hidden, grad_middle, gain_rows, gain_two, gain_heads, head_grad):
    parts, count, width = back.shape
    shards, rows, head_width = head_grad.shape
    return pl.pallas_call(
        functools.partial(last_kernel, pl.ds(0, width)),
        out_shape=(
            jax.ShapeDtypeStruct((count, D), F32),
            jax.ShapeDtypeStruct((16, 128), F32),
            jax.ShapeDtypeStruct((parts, rows, head_width), BF16),
        ),
        in_specs=[WHOLE, HBM] + [WHOLE] * 6,
        out_specs=(WHOLE,) * 3,
        scratch_shapes=[
            VMEM((D, width), BF16),
            pltpu.SemaphoreType.DMA,
            VMEM((count, D), F32),
            VMEM((8, D), F32),
            VMEM((shards, 16, 128), F32),
            VMEM((shards, 16, 128), F32),
            VMEM((16, 128), F32),
            VMEM((parts, 16, 128), F32),
            VMEM((shards - 1, rows, head_width), BF16),
        ]
        + [pltpu.SemaphoreType.DMA((shards,))] * 2
        + [pltpu.SemaphoreType.DMA((parts,))] * 2
        + [pltpu.SemaphoreType.DMA((shards,))] * 2
        + gather_scratch(parts // 2)
        + scatter_scratch(parts // 2, count),
        compiler_params=params(5, 60),
        cost_estimate=cost(90),
        name="last",
    )(back, weights, hidden, grad_middle, gain_rows, gain_two, gain_heads, head_grad)


QUERY_TILE = 256
KEY_TILE = 512


def reach(index, tokens):
    return jnp.minimum((index + 2) * QUERY_TILE + KEY_TILE - 1, tokens) // KEY_TILE


def head_norm(value, gain, cosine, sine):
    normed = value * inverse_norm(value) * gain
    return normed * cosine + pltpu.roll(normed, HEAD_SIZE // 2, 1) * sine


def attend_kernel(heads, columns, *refs):
    proj, cosine, sine, gain, id_column, id_row, weights, x, grad, gain_rows = refs[:10]
    queries, keys, values, context, inverse, middle, normed, land = refs[10:18]
    weight, weight_sem, grad_sem, total = refs[18:22]
    gather_sems, scratch = refs[22:28], refs[28:]
    me, _, _, chips = line_position()
    tokens = proj.shape[0]
    count = x.shape[0]
    key_at = heads * HEAD_SIZE
    copy = copy_in(weights.at[:, columns], weight, weight_sem)
    own = copy_in(grad, land.at[me], grad_sem)
    gather = Gather(land, gather_sems)
    line_barrier()
    own.wait()
    gather.step(0)

    def prepare(index):
        block = pl.ds(pl.multiple_of(index * QUERY_TILE, QUERY_TILE), QUERY_TILE)
        c, s = cosine[block, :], sine[block, :]
        for h in range(heads):
            lanes = slice(h * HEAD_SIZE, (h + 1) * HEAD_SIZE)
            rotated = head_norm(proj[block, lanes], gain[0:1, :], c, s) * HEAD_SIZE ** (-0.5)
            queries[block, lanes] = rotated.astype(BF16)
        rotated = head_norm(proj[block, key_at : key_at + HEAD_SIZE], gain[1:2, :], c, s)
        keys[block, :] = rotated.astype(BF16)
        values[block, :] = proj[block, key_at + HEAD_SIZE : key_at + 2 * HEAD_SIZE].astype(BF16)

    loop(tokens // QUERY_TILE, prepare)

    def attend(index):
        block = pl.ds(pl.multiple_of(index * QUERY_TILE, QUERY_TILE), QUERY_TILE)
        query_ids = id_column[block, :]
        for h in range(heads):
            lanes = slice(h * HEAD_SIZE, (h + 1) * HEAD_SIZE)
            query = queries[block, lanes]

            def one(tile, carry):
                sums, total = carry
                span = pl.ds(pl.multiple_of(tile * KEY_TILE, KEY_TILE), KEY_TILE)
                scores = rdot(query, keys[span, :])
                expon = jnp.where(id_row[0:1, span] <= query_ids, jnp.exp(scores), 0.0)
                sums = sums + dot(expon.astype(BF16), values[span, :])
                return sums, total + jnp.sum(expon, axis=1, keepdims=True)

            start = (jnp.zeros((QUERY_TILE, HEAD_SIZE), F32), jnp.zeros((QUERY_TILE, 1), F32))
            sums, total = lax.fori_loop(0, reach(index, tokens), one, start)
            scale = 1.0 / total
            context[block, lanes] = (sums * scale).astype(BF16)
            inverse[h : h + 1, block] = jnp.broadcast_to(scale, (QUERY_TILE, HEAD_SIZE)).T[0:1, :]

    loop(tokens // QUERY_TILE, attend)

    def produce(piece, chunk):
        block = pl.ds(pl.multiple_of(piece * count, count), count)
        return rdot(context[block, :], weight[pl.ds(pl.multiple_of(chunk * WIDE, WIDE), WIDE), :])

    scatter = Scatter(scratch, produce, total)
    scatter.begin()
    copy.wait()
    scatter.prepare(0)
    gather.step(1)

    def step(time):
        scatter.step(time)

        @pl.when(time + 2 < chips)
        def _():
            gather.step(time + 2)

        scatter.prepare(time + 1)

    loop(chips - 1, step)
    scatter.finish()

    def norm(block):
        value = x[block, :].astype(F32) + total[block, :]
        middle[block, :] = value
        normed[block, :] = (value * inverse_norm(value) * gain_rows[1:2, :]).astype(BF16)

    row_blocks(count, norm)
    gather.finish()


def attend(proj, cosine, sine, gain, id_column, id_row, weights, hidden, grad, gain_rows, heads):
    tokens = proj.shape[0]
    width = heads * HEAD_SIZE
    count = hidden.shape[0]
    parts = tokens // count
    return pl.pallas_call(
        functools.partial(attend_kernel, heads, pl.ds(weights.shape[1] - width, width)),
        out_shape=(
            jax.ShapeDtypeStruct((tokens, width), BF16),
            jax.ShapeDtypeStruct((tokens, HEAD_SIZE), BF16),
            jax.ShapeDtypeStruct((tokens, HEAD_SIZE), BF16),
            jax.ShapeDtypeStruct((tokens, width), BF16),
            jax.ShapeDtypeStruct((8, tokens), F32),
            jax.ShapeDtypeStruct((count, D), F32),
            jax.ShapeDtypeStruct((count, D), BF16),
            jax.ShapeDtypeStruct((parts, count, D), BF16),
        ),
        in_specs=[WHOLE] * 6 + [HBM, WHOLE, HBM, WHOLE],
        out_specs=(WHOLE,) * 7 + (HBM,),
        scratch_shapes=[
            VMEM((D, width), BF16),
            pltpu.SemaphoreType.DMA,
            pltpu.SemaphoreType.DMA,
            VMEM((count, D), F32),
        ]
        + gather_scratch(parts // 2)
        + scatter_scratch(parts // 2, count),
        compiler_params=params(1, 60),
        cost_estimate=cost(110),
        name="attend",
    )(proj, cosine, sine, gain, id_column, id_row, weights, hidden, grad, gain_rows)


def attention_back_kernel(heads, *refs):
    queries, keys, values, out_grad, inverse, context, proj, cosine, sine, gain = refs[:10]
    id_column, id_row, back, gain_sum, key_grad, value_grad, query_grad = refs[10:]
    tokens = proj.shape[0]
    key_at = heads * HEAD_SIZE
    key_grad[...] = jnp.zeros_like(key_grad)
    value_grad[...] = jnp.zeros_like(value_grad)
    gain_sum[...] = jnp.zeros_like(gain_sum)

    def through(block, lanes, grad, row):
        turned = pltpu.roll(grad, HEAD_SIZE // 2, 1)
        unrotated = grad * cosine[block, :] - turned * sine[block, :]
        result, terms = rms_back(proj[block, lanes], gain[row : row + 1, :], unrotated)
        back[block, lanes] = result.astype(BF16)
        gain_sum[row : row + 1, :] += jnp.sum(terms, axis=0, keepdims=True)

    def attend(index):
        block = pl.ds(pl.multiple_of(index * QUERY_TILE, QUERY_TILE), QUERY_TILE)
        query_ids = id_row[0:1, block]
        for h in range(heads):
            lanes = slice(h * HEAD_SIZE, (h + 1) * HEAD_SIZE)
            query = queries[block, lanes]
            grad = out_grad[block, lanes]
            scale = inverse[h : h + 1, block]
            products = grad.astype(F32) * context[block, lanes].astype(F32)
            shift = lax.dot_general(
                jnp.ones((8, HEAD_SIZE), F32),
                products,
                (((1,), (1,)), ((), ())),
                precision=lax.Precision.HIGHEST,
                preferred_element_type=F32,
            )[0:1, :]
            query_grad[...] = jnp.zeros_like(query_grad)

            def one(tile):
                span = pl.ds(pl.multiple_of(tile * KEY_TILE, KEY_TILE), KEY_TILE)
                key = keys[span, :]
                scores = rdot(key, query)
                probs = jnp.where(id_column[span, :] <= query_ids, jnp.exp(scores) * scale, 0.0)
                grad_scores = (probs * (rdot(values[span, :], grad) - shift)).astype(BF16)
                value_grad[span, :] += dot(probs.astype(BF16), grad)
                key_grad[span, :] += dot(grad_scores, query)
                query_grad[...] += tdot(grad_scores, key)

            loop(reach(index, tokens), one)
            through(block, lanes, query_grad[...] * HEAD_SIZE ** (-0.5), 0)

    loop(tokens // QUERY_TILE, attend)

    def finish(index):
        block = pl.ds(pl.multiple_of(index * QUERY_TILE, QUERY_TILE), QUERY_TILE)
        through(block, slice(key_at, key_at + HEAD_SIZE), key_grad[block, :], 1)
        back[block, key_at + HEAD_SIZE : key_at + 2 * HEAD_SIZE] = value_grad[block, :].astype(BF16)

    loop(tokens // QUERY_TILE, finish)


def attention_back(heads, *operands):
    tokens = operands[0].shape[0]
    width = heads * HEAD_SIZE
    return pl.pallas_call(
        functools.partial(attention_back_kernel, heads),
        out_shape=(
            jax.ShapeDtypeStruct((tokens, width + 2 * HEAD_SIZE), BF16),
            jax.ShapeDtypeStruct((8, HEAD_SIZE), F32),
        ),
        in_specs=[WHOLE] * len(operands),
        out_specs=(WHOLE,) * 2,
        scratch_shapes=[
            VMEM((tokens, HEAD_SIZE), F32),
            VMEM((tokens, HEAD_SIZE), F32),
            VMEM((QUERY_TILE, HEAD_SIZE), F32),
        ],
        compiler_params=pltpu.CompilerParams(vmem_limit_bytes=48 * 1024 * 1024),
        cost_estimate=cost(38),
        name="attention_back",
    )(*operands)


def spread_feed_kernel(width, source, gate, up, down):
    gate[...] = source[0, :, :width].astype(F32)
    up[...] = source[0, :, width : 2 * width].astype(F32)
    down[...] = source[0, :, 2 * width :].astype(F32).T


def spread_feed(stacked):
    parts, rows, total = stacked.shape
    width = total // 3
    across = jax.ShapeDtypeStruct((rows, parts * width), F32)
    return pl.pallas_call(
        functools.partial(spread_feed_kernel, width),
        out_shape=(across, across, jax.ShapeDtypeStruct((parts * width, rows), F32)),
        grid=(parts,),
        in_specs=[pl.BlockSpec((1, rows, total), lambda i: (i, 0, 0))],
        out_specs=(
            pl.BlockSpec((rows, width), lambda i: (0, i)),
            pl.BlockSpec((rows, width), lambda i: (0, i)),
            pl.BlockSpec((width, rows), lambda i: (i, 0)),
        ),
        compiler_params=pltpu.CompilerParams(vmem_limit_bytes=32 * 1024 * 1024),
        name="spread_feed",
    )(stacked)


def spread_heads_kernel(width, source, query, key, value, out):
    second = width + HEAD_SIZE
    third = second + HEAD_SIZE
    query[...] = source[0, :, :width].astype(F32)
    key[...] = source[0, :, width:second].astype(F32)
    value[...] = source[0, :, second:third].astype(F32)
    out[...] = source[0, :, third:].astype(F32).T


def spread_heads(stacked, width):
    parts, rows, total = stacked.shape
    widths = (width, HEAD_SIZE, HEAD_SIZE)
    return pl.pallas_call(
        functools.partial(spread_heads_kernel, width),
        out_shape=tuple(jax.ShapeDtypeStruct((rows, parts * w), F32) for w in widths)
        + (jax.ShapeDtypeStruct((parts * width, rows), F32),),
        grid=(parts,),
        in_specs=[pl.BlockSpec((1, rows, total), lambda i: (i, 0, 0))],
        out_specs=tuple(pl.BlockSpec((rows, w), lambda i: (0, i)) for w in widths)
        + (pl.BlockSpec((width, rows), lambda i: (i, 0)),),
        compiler_params=pltpu.CompilerParams(vmem_limit_bytes=32 * 1024 * 1024),
        name="spread_heads",
    )(stacked)


def by_row(array):
    return with_layout_constraint(array, Layout(major_to_minor=(0, 1)))


def own_columns(array, index, width):
    return lax.dynamic_slice_in_dim(array, index * width, width, axis=1)


def own_rows(array, index, width):
    return lax.dynamic_slice_in_dim(array, index * width, width, axis=0)


def local(
    hidden_in,
    weight_query,
    key_weight_matrix,
    weight_value,
    weight_out,
    weight_gate,
    weight_up,
    weight_down,
    gain_attention,
    gain_feed,
    gain_query,
    gain_key,
    positions,
    token_block_index,
    grad_out,
):
    parts = lax.axis_size("ctx")
    shards = lax.axis_size("fsdp")
    me = lax.axis_index("ctx")
    shard = lax.axis_index("fsdp")
    heads = QUERY_HEADS // parts
    sharers = parts // KEY_VALUE_HEADS
    key_head = me // sharers
    width = heads * HEAD_SIZE
    feed_width = FF // parts
    rows = D // shards
    head_rows = HEAD_SIZE // shards
    count = hidden_in.shape[1]
    tokens = parts * count

    def gather_rows(piece):
        return lax.all_gather(piece, "fsdp", axis=0, tiled=True)

    def sum_rows(grad):
        return lax.psum_scatter(grad.astype(BF16), "fsdp", scatter_dimension=0, tiled=True)

    def gather_parts(piece):
        return lax.all_gather(piece, "ctx", axis=0)

    own_heads_weight = jnp.concatenate(
        [
            own_columns(weight_query, me, width),
            own_columns(key_weight_matrix, key_head, HEAD_SIZE),
            own_columns(weight_value, key_head, HEAD_SIZE),
            own_rows(weight_out, me, width).T,
        ],
        axis=1,
    )
    feed_weight = gather_rows(
        jnp.concatenate(
            [
                own_columns(weight_gate, me, feed_width),
                own_columns(weight_up, me, feed_width),
                own_rows(weight_down, me, feed_width).T,
            ],
            axis=1,
        )
    )

    own_gains = jnp.concatenate([gain_attention, gain_feed, gain_query, gain_key]).astype(F32)
    own_gains = jnp.pad(own_gains, (0, 2048 - own_gains.shape[0])).reshape(16, 128)
    own_tokens = jnp.pad(jnp.stack([positions[0], token_block_index[0]]), ((0, 6), (0, 0)))
    hidden, grad = hidden_in[0], grad_out[0]
    normed_all, proj, heads_weight, gain_rows, gains, whole = first(
        hidden, own_gains, own_tokens, own_heads_weight, shards, parts, width + 2 * HEAD_SIZE
    )
    flat_gains = gains.reshape(shards, -1)
    norm_query = flat_gains[:, 2 * rows : 2 * rows + head_rows].reshape(1, -1)
    norm_key = flat_gains[:, 2 * rows + head_rows : 2 * rows + 2 * head_rows].reshape(1, -1)
    head_gains = jnp.concatenate([norm_query, norm_key, jnp.zeros((6, HEAD_SIZE), F32)])

    half = HEAD_SIZE // 2
    freq = THETA ** (-(jnp.arange(half).astype(F32) * 2.0 / HEAD_SIZE))
    angle = whole[:, 0].reshape(-1).astype(F32)[:, None] * freq
    cosine, sine = jnp.cos(angle), jnp.sin(angle)
    cosine = jnp.concatenate([cosine, cosine], axis=1)
    sine = jnp.concatenate([-sine, sine], axis=1)
    ids = whole[:, 1].reshape(-1)
    id_row, id_column = ids[None, :], ids[:, None]

    proj = proj.reshape(tokens, width + 2 * HEAD_SIZE)
    queries, keys, values, context, inverse, middle, normed_two, grad_all = attend(
        proj, cosine, sine, head_gains, id_column, id_row, heads_weight, hidden, grad, gain_rows, heads
    )
    normed_two_all, activation, back = feed(normed_two, grad_all, feed_weight)

    flat_grad = grad_all.reshape(tokens, D)
    flat_back = back.reshape(tokens, 2 * feed_width)
    flat_activation = activation.reshape(tokens, feed_width)
    feed_grad = jnp.concatenate(
        [
            by_row(tdot(normed_two_all.reshape(tokens, D), flat_back).astype(BF16)),
            by_row(tdot(flat_grad, flat_activation).astype(BF16)),
        ],
        axis=1,
    )
    back, feed_grad = lax.optimization_barrier((back, feed_grad))
    feed_shard = sum_rows(feed_grad)

    grad_middle, low, gain_two = feed_back(back, feed_weight, middle, grad, gain_rows)
    low_all, context_grad, hidden_out = turn(low, heads_weight, activation, feed_weight, middle, width)

    context_grad, feed_shard = lax.optimization_barrier((context_grad, feed_shard))
    feed_parts = gather_parts(feed_shard)
    context_grad = context_grad.reshape(tokens, width)
    grad_qkv, gain_heads = attention_back(
        heads,
        queries,
        keys,
        values,
        context_grad,
        inverse,
        context,
        proj,
        cosine,
        sine,
        head_gains,
        id_column,
        id_row,
    )
    head_grad = jnp.concatenate(
        [
            by_row(tdot(normed_all.reshape(tokens, D), grad_qkv).astype(BF16)),
            by_row(tdot(low_all.reshape(tokens, D), context).astype(BF16)),
        ],
        axis=1,
    )
    grad_hidden, gain_sums, head_parts = last(
        grad_qkv.reshape(parts, count, -1),
        heads_weight,
        hidden,
        grad_middle,
        gain_rows,
        gain_two,
        gain_heads,
        head_grad.reshape(shards, rows, -1),
    )

    gain_sums = gain_sums.reshape(-1)
    grad_gate, grad_up, grad_down = spread_feed(feed_parts)
    grad_query, grad_key, grad_value, grad_out_weight = spread_heads(head_parts, width)
    if sharers > 1:
        grad_key, grad_value = (
            part.reshape(rows, KEY_VALUE_HEADS, sharers, HEAD_SIZE).sum(axis=2).reshape(rows, -1)
            for part in (grad_key, grad_value)
        )
    return (
        hidden_out[None],
        grad_hidden[None],
        grad_query,
        grad_key,
        grad_value,
        grad_out_weight,
        grad_gate,
        grad_up,
        grad_down,
        gain_sums[:rows],
        gain_sums[rows : 2 * rows],
        lax.dynamic_slice_in_dim(gain_sums, 2 * rows + shard * head_rows, head_rows),
        lax.dynamic_slice_in_dim(gain_sums, 2 * rows + HEAD_SIZE + shard * head_rows, head_rows),
    )


def solution(mesh):
    tokens = P("fsdp", "ctx", None)
    by_rows = P("fsdp", None)
    by_columns = P(None, "fsdp")
    per_token = P("fsdp", "ctx")
    vector = P("fsdp")
    weights = (by_rows, by_rows, by_rows, by_columns, by_rows, by_rows, by_columns)
    return jax.shard_map(
        local,
        mesh=mesh,
        in_specs=(tokens, *weights, vector, vector, vector, vector, per_token, per_token, tokens),
        out_specs=(tokens, tokens, *weights, vector, vector, vector, vector),
        check_vma=False,
    )
```

```python
import functools

import jax
import jax.numpy as jnp
from jax import lax
from jax.experimental import pallas as pl
from jax.experimental.layout import Layout, with_layout_constraint
from jax.experimental.pallas import tpu as pltpu
from jax.sharding import PartitionSpec as P

D = 2048
QUERY_HEADS = 16
KEY_VALUE_HEADS = 8
HEAD_SIZE = 128
FF = 6144
EPS = 1e-06
THETA = 1000000.0
F32 = jnp.float32
BF16 = jnp.bfloat16
MESH = pl.DeviceIdType.MESH
VMEM = pltpu.VMEM
WHOLE = pl.BlockSpec(memory_space=pltpu.VMEM)
HBM = pl.BlockSpec(memory_space=pl.ANY)
CHUNKS = 4
WIDE = D // CHUNKS


def dot(left, right):
    return jnp.dot(left, right, preferred_element_type=F32)


def tdot(left, right):
    return lax.dot_general(left, right, (((0,), (0,)), ((), ())), preferred_element_type=F32)


def rdot(left, right):
    return lax.dot_general(left, right, (((1,), (1,)), ((), ())), preferred_element_type=F32)


def loop(count, body):
    def step(index, carry):
        body(index)
        return carry

    lax.fori_loop(0, count, step, 0)


def line_position():
    me = lax.axis_index("ctx")
    return me, me // 2, me % 2, lax.axis_size("ctx") // 2


def send(source, target, send_sem, recv_sem, axis, index):
    return pltpu.make_async_remote_copy(
        src_ref=source,
        dst_ref=target,
        send_sem=send_sem,
        recv_sem=recv_sem,
        device_id={axis: index},
        device_id_type=MESH,
    )


def line_barrier():
    me, chip, core, chips = line_position()
    barrier = pltpu.get_barrier_semaphore()

    def greet(index):
        pl.semaphore_signal(barrier, inc=1, device_id={"ctx": index}, device_id_type=MESH)

    greet(me + 1 - 2 * core)

    @pl.when(chip > 0)
    def _():
        greet(me - 2)

    @pl.when(chip < chips - 1)
    def _():
        greet(me + 2)

    peers = 1 + (chip > 0).astype(jnp.int32) + (chip < chips - 1).astype(jnp.int32)
    pl.semaphore_wait(barrier, peers)


def peers_of(axis):
    me, size = lax.axis_index(axis), lax.axis_size(axis)
    return size - 1, lambda i: (me + i + 1) % size, lambda i: (me + size - i - 1) % size


def full_barrier():
    barrier = pltpu.get_barrier_semaphore()
    total = 0
    for axis in ("fsdp", "ctx"):
        count, ahead, _ = peers_of(axis)
        loop(
            count,
            lambda i, axis=axis, ahead=ahead: pl.semaphore_signal(
                barrier, inc=1, device_id={axis: ahead(i)}, device_id_type=MESH
            ),
        )
        total += count
    pl.semaphore_wait(barrier, total)


def gather_scratch(chips):
    return [pltpu.SemaphoreType.DMA((chips,)) for _ in range(6)]


class Gather:
    def __init__(self, land, sems, consume=None, late=False):
        self.late = late
        self.land = land
        self.sems = sems
        self.consume = consume
        self.me, self.chip, self.core, self.chips = line_position()

    def right(self, step, source):
        ref = self.land.at[2 * source + self.core]
        return send(ref, ref, self.sems[0].at[step], self.sems[1].at[step], "ctx", self.me + 2)

    def left(self, step, source):
        ref = self.land.at[2 * source + self.core]
        return send(ref, ref, self.sems[2].at[step], self.sems[3].at[step], "ctx", self.me - 2)

    def across(self, source, core):
        ref = self.land.at[2 * source + core]
        other = self.me + 1 - 2 * self.core
        return send(ref, ref, self.sems[4].at[source], self.sems[5].at[source], "ctx", other)

    def step(self, step):
        chip, core, chips = self.chip, self.core, self.chips
        low, high = chip - step, chip + step
        has_low = low >= 0
        has_high = jnp.logical_and(high < chips, step > 0)

        @pl.when(jnp.logical_and(has_low, step > 0))
        def _():
            self.right(step - 1, low).wait_recv()

        @pl.when(jnp.logical_and(has_low, chip < chips - 1))
        def _():
            self.right(step, low).start()

        @pl.when(has_high)
        def _():
            self.left(step - 1, high).wait_recv()

        @pl.when(jnp.logical_and(high < chips, chip > 0))
        def _():
            self.left(step, high).start()

        @pl.when(has_low)
        def _():
            self.across(low, core).start()

        @pl.when(has_high)
        def _():
            self.across(high, core).start()

        if not self.late:
            self.use(step)
            return

        @pl.when(step > 0)
        def _():
            self.use(step - 1)

        @pl.when(step == chips - 1)
        def _():
            self.use(step)

    def use(self, step):
        chip, core, chips = self.chip, self.core, self.chips
        low, high = chip - step, chip + step

        def one(kind):
            upward = kind % 2
            crossed = kind // 2
            source = jnp.where(upward == 1, high, low)
            valid = jnp.where(upward == 1, jnp.logical_and(high < chips, step > 0), low >= 0)
            parity = jnp.where(crossed == 1, 1 - core, core)

            @pl.when(valid)
            def _():
                @pl.when(crossed == 1)
                def _():
                    self.across(source, parity).wait_recv()

                if self.consume is not None:
                    self.consume(2 * source + parity)

        loop(4, one)

    def finish(self):
        chip, core, chips = self.chip, self.core, self.chips

        def one(step):
            @pl.when(jnp.logical_and(chip - step >= 0, chip < chips - 1))
            def _():
                self.right(step, chip - step).wait_send()

            @pl.when(jnp.logical_and(chip + step < chips, chip > 0))
            def _():
                self.left(step, chip + step).wait_send()

            self.across(step, core).wait_send()

        loop(chips, one)


def scatter_scratch(chips, rows):
    buffers = [VMEM((count, CHUNKS, rows, WIDE), BF16) for count in (chips + 1, chips, chips)]
    return buffers + [pltpu.SemaphoreType.DMA((chips, CHUNKS)) for _ in range(6)]


class Scatter:
    def __init__(self, scratch, produce, total):
        self.line, self.out, self.other = scratch[:3]
        self.sems = scratch[3:]
        self.produce = produce
        self.total = total
        self.me, self.chip, self.core, self.chips = line_position()


    def right(self, step, chunk):
        ref = self.line.at[step, chunk]
        sems = self.sems
        return send(ref, ref, sems[0].at[step, chunk], sems[1].at[step, chunk], "ctx", self.me + 2)

    def left(self, step, chunk):
        ref = self.line.at[self.chips - step, chunk]
        sems = self.sems
        return send(ref, ref, sems[2].at[step, chunk], sems[3].at[step, chunk], "ctx", self.me - 2)

    def across(self, target, chunk):
        sems = self.sems
        return send(
            self.out.at[target, chunk],
            self.other.at[target, chunk],
            sems[4].at[target, chunk],
            sems[5].at[target, chunk],
            "ctx",
            self.me + 1 - 2 * self.core,
        )

    def begin(self):
        def clear(index):
            slot, chunk = index // CHUNKS, index % CHUNKS
            at_left = jnp.logical_and(self.chip == 0, slot < self.chips)
            at_right = jnp.logical_and(self.chip == self.chips - 1, slot > 0)

            @pl.when(jnp.logical_or(at_left, at_right))
            def _():
                self.line[slot, chunk] = jnp.zeros(self.line.shape[2:], BF16)

        loop((self.chips + 1) * CHUNKS, clear)

    def when_right(self, time):
        return jnp.logical_and(time >= self.chip, time < self.chips - 1)

    def when_left(self, time):
        return jnp.logical_and(time >= self.chips - 1 - self.chip, time < self.chips - 1)

    def prepare(self, time):
        def cross(target):
            def one(chunk):
                piece = 2 * target + 1 - self.core
                self.out[target, chunk] = self.produce(piece, chunk).astype(BF16)
                self.across(target, chunk).start()

            loop(CHUNKS, one)

        @pl.when(self.when_right(time))
        def _():
            cross(self.chips - 1 - time + self.chip)

        @pl.when(self.when_left(time))
        def _():
            cross(time - (self.chips - 1 - self.chip))

        @pl.when(time == self.chips - 1)
        def _():
            cross(self.chip)

    def step(self, time):
        chip, core, chips = self.chip, self.core, self.chips

        @pl.when(self.when_right(time))
        def _():
            step = time - chip
            target = chips - 1 - step

            def one(chunk):
                self.across(target, chunk).wait_recv()

                @pl.when(chip > 0)
                def _():
                    self.right(step, chunk).wait_recv()

                value = self.produce(2 * target + core, chunk) + self.other[target, chunk].astype(F32)
                value = value + self.line[step, chunk].astype(F32)
                self.line[step, chunk] = value.astype(BF16)
                self.right(step, chunk).start()

            loop(CHUNKS, one)

        @pl.when(self.when_left(time))
        def _():
            step = time - (chips - 1 - chip)

            def one(chunk):
                self.across(step, chunk).wait_recv()

                @pl.when(chip < chips - 1)
                def _():
                    self.left(step, chunk).wait_recv()

                value = self.produce(2 * step + core, chunk) + self.other[step, chunk].astype(F32)
                value = value + self.line[chips - step, chunk].astype(F32)
                self.line[chips - step, chunk] = value.astype(BF16)
                self.left(step, chunk).start()

            loop(CHUNKS, one)

    def finish(self):
        chip, core, chips = self.chip, self.core, self.chips
        last = chips - 1 - chip

        def one(chunk):
            self.across(chip, chunk).wait_recv()
            value = self.produce(2 * chip + core, chunk) + self.other[chip, chunk].astype(F32)

            @pl.when(chip > 0)
            def _():
                self.right(last, chunk).wait_recv()

            @pl.when(chip < chips - 1)
            def _():
                self.left(chip, chunk).wait_recv()

            value = value + self.line[last, chunk].astype(F32)
            value = value + self.line[chips - chip, chunk].astype(F32)
            self.total[:, pl.ds(pl.multiple_of(chunk * WIDE, WIDE), WIDE)] = value

        loop(CHUNKS, one)

        def drain(index):
            step, chunk = index // CHUNKS, index % CHUNKS

            @pl.when(step < last)
            def _():
                self.right(step, chunk).wait_send()

            @pl.when(step < chip)
            def _():
                self.left(step, chunk).wait_send()

            self.across(step, chunk).wait_send()

        loop(chips * CHUNKS, drain)


def row_blocks(rows, body, size=32):
    def one(index):
        body(pl.ds(pl.multiple_of(index * size, size), size))

    loop(rows // size, one)


def inverse_norm(value):
    return lax.rsqrt(jnp.mean(value * value, axis=-1, keepdims=True) + EPS)


def params(identity, megabytes):
    return pltpu.CompilerParams(
        collective_id=identity,
        has_side_effects=True,
        vmem_limit_bytes=megabytes * 1024 * 1024,
    )


def cost(microseconds):
    return pl.CostEstimate(
        flops=int(microseconds * 1.15e9), bytes_accessed=1024, transcendentals=0
    )


class FsdpSum:
    def __init__(self, grad, arrived, send_sems, recv_sems):
        self.grad, self.arrived = grad, arrived
        self.sems = send_sems, recv_sems
        self.peers, self.ahead, _ = peers_of("fsdp")

    def copy(self, i):
        target = self.ahead(i)
        return send(
            self.grad.at[target], self.arrived.at[i], self.sems[0].at[i], self.sems[1].at[i], "fsdp", target
        )

    def start(self):
        loop(self.peers, lambda i: self.copy(i).start())

    def collect(self, land, slot):
        shard = lax.axis_index("fsdp")
        loop(self.peers, lambda i: self.copy(i).wait_recv())

        def add(block):
            value = self.grad[shard, block].astype(F32)
            for i in range(self.peers):
                value = value + self.arrived[i, block].astype(F32)
            land[slot, block] = value.astype(BF16)

        row_blocks(self.grad.shape[1], add)

    def finish(self):
        loop(self.peers, lambda i: self.copy(i).wait_send())


def fsdp_scratch(shards, rows, width):
    return [VMEM((shards - 1, rows, width), BF16)] + [pltpu.SemaphoreType.DMA((shards,))] * 2


def copy_in(source, target, sem):
    copy = pltpu.make_async_copy(source, target, sem)
    copy.start()
    return copy


def first_kernel(rows, width, *refs):
    x, gains, tokens, part, land, proj, weights, gain_rows, all_gains, all_tokens = refs[:10]
    sems, small = refs[10:16], refs[16:]
    me, _, _, chips = line_position()
    shard = lax.axis_index("fsdp")
    shards, ahead, behind = peers_of("fsdp")
    parts, next_part, past_part = peers_of("ctx")
    full_barrier()

    def gain_copy(i, slot):
        return send(gains, all_gains.at[slot], small[0].at[i], small[1].at[i], "fsdp", ahead(i))

    def token_copy(i, slot):
        return send(tokens, all_tokens.at[slot], small[2].at[i], small[3].at[i], "ctx", next_part(i))

    def weight_copy(i, owner):
        target = weights.at[pl.ds(pl.multiple_of(owner * rows, rows), rows), :]
        return send(part, target, small[4].at[i], small[5].at[i], "fsdp", ahead(i))

    loop(shards, lambda i: gain_copy(i, shard).start())
    loop(parts, lambda i: token_copy(i, me).start())
    loop(shards, lambda i: weight_copy(i, shard).start())
    all_gains[shard] = gains[...]
    all_tokens[me] = tokens[...]
    weights[pl.ds(pl.multiple_of(shard * rows, rows), rows), :] = part[...]
    loop(shards, lambda i: gain_copy(i, behind(i)).wait_recv())
    lanes = rows // 128
    for kind in range(2):
        for owner in range(shards + 1):
            for j in range(lanes):
                at = owner * rows + j * 128
                gain_rows[kind : kind + 1, at : at + 128] = all_gains[
                    owner, kind * lanes + j : kind * lanes + j + 1, :
                ]

    def norm(block):
        value = x[block, :].astype(F32)
        land[me, block] = (value * inverse_norm(value) * gain_rows[0:1, :]).astype(BF16)

    row_blocks(x.shape[0], norm)

    gather = Gather(land, sems)
    loop(chips, gather.step)
    loop(shards, lambda i: weight_copy(i, behind(i)).wait_recv())

    def project(piece):
        proj[piece] = dot(land[piece], weights[:, :width])

    loop(2 * chips, project)
    gather.finish()
    loop(shards, lambda i: gain_copy(i, shard).wait_send())
    loop(shards, lambda i: weight_copy(i, shard).wait_send())
    loop(parts, lambda i: token_copy(i, past_part(i)).wait_recv())
    loop(parts, lambda i: token_copy(i, me).wait_send())


def first(hidden, gains, tokens, part, shards, parts, width):
    count = hidden.shape[0]
    return pl.pallas_call(
        functools.partial(first_kernel, D // shards, width),
        out_shape=(
            jax.ShapeDtypeStruct((parts, count, D), BF16),
            jax.ShapeDtypeStruct((parts, count, width), F32),
            jax.ShapeDtypeStruct((D, part.shape[1]), BF16),
            jax.ShapeDtypeStruct((8, D), F32),
            jax.ShapeDtypeStruct((shards, *gains.shape), F32),
            jax.ShapeDtypeStruct((parts, *tokens.shape), jnp.int32),
        ),
        in_specs=[WHOLE] * 4,
        out_specs=(WHOLE,) * 6,
        scratch_shapes=gather_scratch(parts // 2)
        + [pltpu.SemaphoreType.DMA((shards,))] * 2
        + [pltpu.SemaphoreType.DMA((parts,))] * 2
        + [pltpu.SemaphoreType.DMA((shards,))] * 2,
        compiler_params=params(0, 60),
        cost_estimate=cost(85),
        name="gather_normed",
    )(hidden, gains, tokens, part)


def feed_kernel(width, *refs):
    x, grads, weights, land, activation, back = refs[:6]
    weight, weight_sem, grad, grad_sems = refs[6:10]
    sems = refs[10:]
    me, _, _, chips = line_position()
    copy = copy_in(weights, weight, weight_sem)

    def grad_copy(piece):
        return pltpu.make_async_copy(grads.at[piece], grad.at[piece], grad_sems.at[piece])

    loop(2 * chips, lambda piece: grad_copy(piece).start())
    land[me] = x[...]
    size = 256 if width % 256 == 0 else 128

    def consume(piece):
        grad_copy(piece).wait()

        def one(index):
            def columns(kind):
                return pl.ds(pl.multiple_of(kind * width + index * size, 128), size)

            gate = dot(land[piece], weight[:, columns(0)])
            up = dot(land[piece], weight[:, columns(1)])
            grad_act = dot(grad[piece], weight[:, columns(2)])
            sigma = 1.0 / (1.0 + jnp.exp(-gate))
            activation[piece, :, columns(0)] = (gate * sigma * up).astype(BF16)
            back[piece, :, columns(0)] = (
                grad_act * up * sigma * (1.0 + gate * (1.0 - sigma))
            ).astype(BF16)
            back[piece, :, columns(1)] = (grad_act * gate * sigma).astype(BF16)

        loop(width // size, one)

    line_barrier()
    gather = Gather(land, sems, consume)
    copy.wait()
    loop(chips, gather.step)
    gather.finish()


def feed(normed, grads, weights):
    parts, count, _ = grads.shape
    width = weights.shape[1] // 3
    return pl.pallas_call(
        functools.partial(feed_kernel, width),
        out_shape=(
            jax.ShapeDtypeStruct((parts, count, D), BF16),
            jax.ShapeDtypeStruct((parts, count, width), BF16),
            jax.ShapeDtypeStruct((parts, count, 2 * width), BF16),
        ),
        in_specs=[WHOLE, HBM, HBM],
        out_specs=(WHOLE,) * 3,
        scratch_shapes=[
            VMEM(weights.shape, BF16),
            pltpu.SemaphoreType.DMA,
            VMEM(grads.shape, BF16),
            pltpu.SemaphoreType.DMA((parts,)),
        ]
        + gather_scratch(parts // 2),
        compiler_params=params(2, 60),
        cost_estimate=cost(90),
        name="feed",
    )(normed, grads, weights)


def rms_back(value, gain, grad):
    inverse = inverse_norm(value)
    scaled = grad * gain
    inner = jnp.mean(scaled * value, axis=-1, keepdims=True)
    terms = grad * value * inverse
    return inverse * scaled - value * (inverse * inverse * inverse * inner), terms


def feed_back_kernel(columns, *refs):
    back, weights, middle, grad, gain_rows, down_grad, grad_middle, low, gain_sum, land = refs[:10]
    weight, weight_sem, total = refs[10:13]
    down_refs, gather_sems, scratch = refs[13:16], refs[16:22], refs[22:]
    me, _, _, chips = line_position()
    copy = copy_in(weights.at[:, columns], weight, weight_sem)

    def produce(piece, chunk):
        return rdot(back[piece], weight[pl.ds(pl.multiple_of(chunk * WIDE, WIDE), WIDE), :])

    down = FsdpSum(down_grad, *down_refs)
    gather = Gather(land, gather_sems)
    scatter = Scatter(scratch, produce, total)
    scatter.begin()
    full_barrier()
    down.start()
    copy.wait()
    scatter.prepare(0)

    def step(time):
        scatter.step(time)
        scatter.prepare(time + 1)

        @pl.when(time == 1)
        def _():
            down.collect(land, me)

        @pl.when(time >= 1)
        def _():
            gather.step(time - 1)

    loop(chips - 1, step)
    scatter.finish()
    gather.step(chips - 2)
    gain_sum[...] = jnp.zeros_like(gain_sum)

    def norm(block):
        through, terms = rms_back(middle[block, :], gain_rows[1:2, :], total[block, :])
        value = grad[block, :].astype(F32) + through
        grad_middle[block, :] = value
        low[block, :] = value.astype(BF16)
        gain_sum[0:1, :] += jnp.sum(terms, axis=0, keepdims=True)

    row_blocks(middle.shape[0], norm)
    gather.step(chips - 1)
    gather.finish()
    down.finish()


def feed_back(back, weights, middle, grad, gain_rows, down_grad):
    parts, count, width = back.shape
    shards, rows, down_width = down_grad.shape
    return pl.pallas_call(
        functools.partial(feed_back_kernel, pl.ds(0, width)),
        out_shape=(
            jax.ShapeDtypeStruct((count, D), F32),
            jax.ShapeDtypeStruct((count, D), BF16),
            jax.ShapeDtypeStruct((8, D), F32),
            jax.ShapeDtypeStruct((parts, rows, down_width), BF16),
        ),
        in_specs=[WHOLE, HBM, WHOLE, WHOLE, WHOLE, WHOLE],
        out_specs=(WHOLE,) * 4,
        scratch_shapes=[VMEM((D, width), BF16), pltpu.SemaphoreType.DMA, VMEM((count, D), F32)]
        + fsdp_scratch(shards, rows, down_width)
        + gather_scratch(parts // 2)
        + scatter_scratch(parts // 2, count),
        compiler_params=params(3, 62),
        cost_estimate=cost(100),
        name="feed_back",
    )(back, weights, middle, grad, gain_rows, down_grad)


def turn_kernel(columns, down_columns, *refs):
    low, weights, activation, feed_weights, middle, land, context_grad, hidden = refs[:8]
    weight, weight_sem, down, down_sem, total = refs[8:13]
    gather_sems, scratch = refs[13:19], refs[19:]
    me, _, _, chips = line_position()
    copy = copy_in(weights.at[:, columns], weight, weight_sem)
    down_copy = copy_in(feed_weights.at[:, down_columns], down, down_sem)
    land[me] = low[...]

    def consume(piece):
        context_grad[piece] = dot(land[piece], weight[...]).astype(BF16)

    def produce(piece, chunk):
        return rdot(activation[piece], down[pl.ds(pl.multiple_of(chunk * WIDE, WIDE), WIDE), :])

    gather = Gather(land, gather_sems, consume)
    scatter = Scatter(scratch, produce, total)
    scatter.begin()
    line_barrier()
    copy.wait()
    down_copy.wait()
    scatter.prepare(0)

    def step(time):
        gather.step(time)
        scatter.step(time)
        scatter.prepare(time + 1)

    loop(chips - 1, step)
    gather.step(chips - 1)
    scatter.finish()
    gather.finish()

    def add(block):
        hidden[block, :] = (middle[block, :] + total[block, :]).astype(BF16)

    row_blocks(middle.shape[0], add)


def turn(low, weights, activation, feed_weights, middle, width):
    parts, count, feed_width = activation.shape
    return pl.pallas_call(
        functools.partial(
            turn_kernel, pl.ds(weights.shape[1] - width, width), pl.ds(2 * feed_width, feed_width)
        ),
        out_shape=(
            jax.ShapeDtypeStruct((parts, count, D), BF16),
            jax.ShapeDtypeStruct((parts, count, width), BF16),
            jax.ShapeDtypeStruct((count, D), BF16),
        ),
        in_specs=[WHOLE, HBM, WHOLE, HBM, WHOLE],
        out_specs=(WHOLE,) * 3,
        scratch_shapes=[
            VMEM((D, width), BF16),
            pltpu.SemaphoreType.DMA,
            VMEM((D, feed_width), BF16),
            pltpu.SemaphoreType.DMA,
            VMEM((count, D), F32),
        ]
        + gather_scratch(parts // 2)
        + scatter_scratch(parts // 2, count),
        compiler_params=params(4, 62),
        cost_estimate=cost(107),
        name="turn",
    )(low, weights, activation, feed_weights, middle)


def last_kernel(columns, *refs):
    back, weights, x, grad_middle, gain_rows, gain_two, gain_heads, head_grad = refs[:8]
    hidden, gain_out, land = refs[8:11]
    weight, weight_sem, total, gain_one, pack, pack_in, shard_sum, shard_in = refs[11:19]
    small, head_refs, gather_sems, scratch = refs[19:23], refs[23:26], refs[26:32], refs[32:]
    me, _, _, chips = line_position()
    shard = lax.axis_index("fsdp")
    shards, ahead, _ = peers_of("fsdp")
    parts, next_part, _ = peers_of("ctx")
    copy = copy_in(weights.at[:, columns], weight, weight_sem)

    def produce(piece, chunk):
        return rdot(back[piece], weight[pl.ds(pl.multiple_of(chunk * WIDE, WIDE), WIDE), :])

    heads = FsdpSum(head_grad, *head_refs)
    scatter = Scatter(scratch, produce, total)
    gather = Gather(land, gather_sems)
    scatter.begin()
    full_barrier()
    copy.wait()
    scatter.prepare(0)
    heads.start()

    def step(time):
        scatter.step(time)

        @pl.when(time == 1)
        def _():
            heads.collect(land, me)

        @pl.when(time >= 1)
        def _():
            gather.step(time - 1)

        scatter.prepare(time + 1)

    loop(chips - 1, step)
    scatter.finish()
    gather.step(chips - 2)
    gain_one[...] = jnp.zeros_like(gain_one)

    def norm(block):
        through, terms = rms_back(x[block, :].astype(F32), gain_rows[0:1, :], total[block, :])
        hidden[block, :] = grad_middle[block, :] + through
        gain_one[0:1, :] += jnp.sum(terms, axis=0, keepdims=True)

    row_blocks(x.shape[0], norm)

    rows = D // (shards + 1)
    lanes = rows // 128
    pack[...] = jnp.zeros_like(pack)
    for owner in range(shards + 1):
        for j in range(lanes):
            at = owner * rows + j * 128
            pack[owner, j : j + 1, :] = gain_one[0:1, at : at + 128]
            pack[owner, lanes + j : lanes + j + 1, :] = gain_two[0:1, at : at + 128]
        pack[owner, 2 * lanes : 2 * lanes + 2, :] = gain_heads[0:2, :]

    def pack_copy(i):
        return send(pack.at[ahead(i)], pack_in.at[i], small[0].at[i], small[1].at[i], "fsdp", ahead(i))

    def sum_copy(i):
        return send(shard_sum, shard_in.at[i], small[2].at[i], small[3].at[i], "ctx", next_part(i))

    loop(shards, lambda i: pack_copy(i).start())
    shard_sum[...] = pack[shard]

    def add_pack(i):
        pack_copy(i).wait_recv()
        shard_sum[...] += pack_in[i]

    loop(shards, add_pack)
    loop(parts, lambda i: sum_copy(i).start())
    gain_out[...] = shard_sum[...]

    def add_sum(i):
        sum_copy(i).wait_recv()
        gain_out[...] += shard_in[i]

    loop(parts, add_sum)
    gather.step(chips - 1)
    gather.finish()
    heads.finish()
    loop(shards, lambda i: pack_copy(i).wait_send())
    loop(parts, lambda i: sum_copy(i).wait_send())


def last(back, weights, hidden, grad_middle, gain_rows, gain_two, gain_heads, head_grad):
    parts, count, width = back.shape
    shards, rows, head_width = head_grad.shape
    return pl.pallas_call(
        functools.partial(last_kernel, pl.ds(0, width)),
        out_shape=(
            jax.ShapeDtypeStruct((count, D), F32),
            jax.ShapeDtypeStruct((16, 128), F32),
            jax.ShapeDtypeStruct((parts, rows, head_width), BF16),
        ),
        in_specs=[WHOLE, HBM] + [WHOLE] * 6,
        out_specs=(WHOLE,) * 3,
        scratch_shapes=[
            VMEM((D, width), BF16),
            pltpu.SemaphoreType.DMA,
            VMEM((count, D), F32),
            VMEM((8, D), F32),
            VMEM((shards, 16, 128), F32),
            VMEM((shards, 16, 128), F32),
            VMEM((16, 128), F32),
            VMEM((parts, 16, 128), F32),
        ]
        + [pltpu.SemaphoreType.DMA((shards,))] * 2
        + [pltpu.SemaphoreType.DMA((parts,))] * 2
        + fsdp_scratch(shards, rows, head_width)
        + gather_scratch(parts // 2)
        + scatter_scratch(parts // 2, count),
        compiler_params=params(5, 60),
        cost_estimate=cost(90),
        name="last",
    )(back, weights, hidden, grad_middle, gain_rows, gain_two, gain_heads, head_grad)


QUERY_TILE = 256
KEY_TILE = 512


def reach(index, tokens):
    return jnp.minimum((index + 2) * QUERY_TILE + KEY_TILE - 1, tokens) // KEY_TILE


def head_norm(value, gain, cosine, sine):
    normed = value * inverse_norm(value) * gain
    return normed * cosine + pltpu.roll(normed, HEAD_SIZE // 2, 1) * sine


def attend_kernel(heads, columns, *refs):
    proj, cosine, sine, gain, id_column, id_row, weights, x, grad, gain_rows = refs[:10]
    queries, keys, values, context, inverse, middle, normed, land = refs[10:18]
    weight, weight_sem, grad_sem, total = refs[18:22]
    gather_sems, scratch = refs[22:28], refs[28:]
    me, _, _, chips = line_position()
    tokens = proj.shape[0]
    count = x.shape[0]
    key_at = heads * HEAD_SIZE
    copy = copy_in(weights.at[:, columns], weight, weight_sem)
    own = copy_in(grad, land.at[me], grad_sem)
    gather = Gather(land, gather_sems)
    line_barrier()
    own.wait()
    gather.step(0)

    def prepare(index):
        block = pl.ds(pl.multiple_of(index * QUERY_TILE, QUERY_TILE), QUERY_TILE)
        c, s = cosine[block, :], sine[block, :]
        for h in range(heads):
            lanes = slice(h * HEAD_SIZE, (h + 1) * HEAD_SIZE)
            rotated = head_norm(proj[block, lanes], gain[0:1, :], c, s) * HEAD_SIZE ** (-0.5)
            queries[block, lanes] = rotated.astype(BF16)
        rotated = head_norm(proj[block, key_at : key_at + HEAD_SIZE], gain[1:2, :], c, s)
        keys[block, :] = rotated.astype(BF16)
        values[block, :] = proj[block, key_at + HEAD_SIZE : key_at + 2 * HEAD_SIZE].astype(BF16)

    loop(tokens // QUERY_TILE, prepare)

    def attend(index):
        block = pl.ds(pl.multiple_of(index * QUERY_TILE, QUERY_TILE), QUERY_TILE)
        query_ids = id_column[block, :]
        for h in range(heads):
            lanes = slice(h * HEAD_SIZE, (h + 1) * HEAD_SIZE)
            query = queries[block, lanes]

            def one(tile, carry):
                sums, total = carry
                span = pl.ds(pl.multiple_of(tile * KEY_TILE, KEY_TILE), KEY_TILE)
                scores = rdot(query, keys[span, :])
                expon = jnp.where(id_row[0:1, span] <= query_ids, jnp.exp(scores), 0.0)
                sums = sums + dot(expon.astype(BF16), values[span, :])
                return sums, total + jnp.sum(expon, axis=1, keepdims=True)

            start = (jnp.zeros((QUERY_TILE, HEAD_SIZE), F32), jnp.zeros((QUERY_TILE, 1), F32))
            sums, total = lax.fori_loop(0, reach(index, tokens), one, start)
            scale = 1.0 / total
            context[block, lanes] = (sums * scale).astype(BF16)
            inverse[h : h + 1, block] = jnp.broadcast_to(scale, (QUERY_TILE, HEAD_SIZE)).T[0:1, :]

    loop(tokens // QUERY_TILE, attend)

    def produce(piece, chunk):
        block = pl.ds(pl.multiple_of(piece * count, count), count)
        return rdot(context[block, :], weight[pl.ds(pl.multiple_of(chunk * WIDE, WIDE), WIDE), :])

    scatter = Scatter(scratch, produce, total)
    scatter.begin()
    copy.wait()
    scatter.prepare(0)
    gather.step(1)

    def step(time):
        scatter.step(time)
        scatter.prepare(time + 1)

        @pl.when(time >= 1)
        def _():
            gather.step(time + 1)

    loop(chips - 1, step)
    scatter.finish()

    def norm(block):
        value = x[block, :].astype(F32) + total[block, :]
        middle[block, :] = value
        normed[block, :] = (value * inverse_norm(value) * gain_rows[1:2, :]).astype(BF16)

    row_blocks(count, norm)
    gather.finish()


def attend(proj, cosine, sine, gain, id_column, id_row, weights, hidden, grad, gain_rows, heads):
    tokens = proj.shape[0]
    width = heads * HEAD_SIZE
    count = hidden.shape[0]
    parts = tokens // count
    return pl.pallas_call(
        functools.partial(attend_kernel, heads, pl.ds(weights.shape[1] - width, width)),
        out_shape=(
            jax.ShapeDtypeStruct((tokens, width), BF16),
            jax.ShapeDtypeStruct((tokens, HEAD_SIZE), BF16),
            jax.ShapeDtypeStruct((tokens, HEAD_SIZE), BF16),
            jax.ShapeDtypeStruct((tokens, width), BF16),
            jax.ShapeDtypeStruct((8, tokens), F32),
            jax.ShapeDtypeStruct((count, D), F32),
            jax.ShapeDtypeStruct((count, D), BF16),
            jax.ShapeDtypeStruct((parts, count, D), BF16),
        ),
        in_specs=[WHOLE] * 6 + [HBM, WHOLE, HBM, WHOLE],
        out_specs=(WHOLE,) * 7 + (HBM,),
        scratch_shapes=[
            VMEM((D, width), BF16),
            pltpu.SemaphoreType.DMA,
            pltpu.SemaphoreType.DMA,
            VMEM((count, D), F32),
        ]
        + gather_scratch(parts // 2)
        + scatter_scratch(parts // 2, count),
        compiler_params=params(1, 60),
        cost_estimate=cost(110),
        name="attend",
    )(proj, cosine, sine, gain, id_column, id_row, weights, hidden, grad, gain_rows)


def attention_back_kernel(heads, *refs):
    queries, keys, values, out_grad, inverse, context, proj, cosine, sine, gain = refs[:10]
    id_column, id_row, back, gain_sum, key_grad, value_grad, query_grad = refs[10:]
    tokens = proj.shape[0]
    key_at = heads * HEAD_SIZE
    key_grad[...] = jnp.zeros_like(key_grad)
    value_grad[...] = jnp.zeros_like(value_grad)
    gain_sum[...] = jnp.zeros_like(gain_sum)

    def through(block, lanes, grad, row):
        turned = pltpu.roll(grad, HEAD_SIZE // 2, 1)
        unrotated = grad * cosine[block, :] - turned * sine[block, :]
        result, terms = rms_back(proj[block, lanes], gain[row : row + 1, :], unrotated)
        back[block, lanes] = result.astype(BF16)
        gain_sum[row : row + 1, :] += jnp.sum(terms, axis=0, keepdims=True)

    def attend(index):
        block = pl.ds(pl.multiple_of(index * QUERY_TILE, QUERY_TILE), QUERY_TILE)
        query_ids = id_row[0:1, block]
        for h in range(heads):
            lanes = slice(h * HEAD_SIZE, (h + 1) * HEAD_SIZE)
            query = queries[block, lanes]
            grad = out_grad[block, lanes]
            scale = inverse[h : h + 1, block]
            products = grad.astype(F32) * context[block, lanes].astype(F32)
            shift = lax.dot_general(
                jnp.ones((8, HEAD_SIZE), F32),
                products,
                (((1,), (1,)), ((), ())),
                precision=lax.Precision.HIGHEST,
                preferred_element_type=F32,
            )[0:1, :]
            query_grad[...] = jnp.zeros_like(query_grad)

            def one(tile):
                span = pl.ds(pl.multiple_of(tile * KEY_TILE, KEY_TILE), KEY_TILE)
                key = keys[span, :]
                scores = rdot(key, query)
                probs = jnp.where(id_column[span, :] <= query_ids, jnp.exp(scores) * scale, 0.0)
                grad_scores = (probs * (rdot(values[span, :], grad) - shift)).astype(BF16)
                value_grad[span, :] += dot(probs.astype(BF16), grad)
                key_grad[span, :] += dot(grad_scores, query)
                query_grad[...] += tdot(grad_scores, key)

            loop(reach(index, tokens), one)
            through(block, lanes, query_grad[...] * HEAD_SIZE ** (-0.5), 0)

    loop(tokens // QUERY_TILE, attend)

    def finish(index):
        block = pl.ds(pl.multiple_of(index * QUERY_TILE, QUERY_TILE), QUERY_TILE)
        through(block, slice(key_at, key_at + HEAD_SIZE), key_grad[block, :], 1)
        back[block, key_at + HEAD_SIZE : key_at + 2 * HEAD_SIZE] = value_grad[block, :].astype(BF16)

    loop(tokens // QUERY_TILE, finish)


def attention_back(heads, *operands):
    tokens = operands[0].shape[0]
    width = heads * HEAD_SIZE
    return pl.pallas_call(
        functools.partial(attention_back_kernel, heads),
        out_shape=(
            jax.ShapeDtypeStruct((tokens, width + 2 * HEAD_SIZE), BF16),
            jax.ShapeDtypeStruct((8, HEAD_SIZE), F32),
        ),
        in_specs=[WHOLE] * len(operands),
        out_specs=(WHOLE,) * 2,
        scratch_shapes=[
            VMEM((tokens, HEAD_SIZE), F32),
            VMEM((tokens, HEAD_SIZE), F32),
            VMEM((QUERY_TILE, HEAD_SIZE), F32),
        ],
        compiler_params=pltpu.CompilerParams(vmem_limit_bytes=48 * 1024 * 1024),
        cost_estimate=cost(38),
        name="attention_back",
    )(*operands)


def spread_pair_kernel(width, source, gate, up):
    gate[...] = source[0, :, :width].astype(F32)
    up[...] = source[0, :, width:].astype(F32)


def spread_pair(stacked):
    parts, rows, total = stacked.shape
    width = total // 2
    across = jax.ShapeDtypeStruct((rows, parts * width), F32)
    return pl.pallas_call(
        functools.partial(spread_pair_kernel, width),
        out_shape=(across, across),
        grid=(parts,),
        in_specs=[pl.BlockSpec((1, rows, total), lambda i: (i, 0, 0))],
        out_specs=(pl.BlockSpec((rows, width), lambda i: (0, i)),) * 2,
        compiler_params=pltpu.CompilerParams(vmem_limit_bytes=60 * 1024 * 1024),
        name="spread_pair",
    )(stacked)


def spread_turned_kernel(source, target):
    target[...] = source[0].astype(F32).T


def spread_turned(stacked):
    parts, rows, width = stacked.shape
    return pl.pallas_call(
        spread_turned_kernel,
        out_shape=jax.ShapeDtypeStruct((parts * width, rows), F32),
        grid=(parts,),
        in_specs=[pl.BlockSpec((1, rows, width), lambda i: (i, 0, 0))],
        out_specs=pl.BlockSpec((width, rows), lambda i: (i, 0)),
        compiler_params=pltpu.CompilerParams(vmem_limit_bytes=60 * 1024 * 1024),
        name="spread_turned",
    )(stacked)


def spread_heads_kernel(width, source, query, key, value, out):
    second = width + HEAD_SIZE
    third = second + HEAD_SIZE
    query[...] = source[0, :, :width].astype(F32)
    key[...] = source[0, :, width:second].astype(F32)
    value[...] = source[0, :, second:third].astype(F32)
    out[...] = source[0, :, third:].astype(F32).T


def spread_heads(stacked, width):
    parts, rows, total = stacked.shape
    widths = (width, HEAD_SIZE, HEAD_SIZE)
    return pl.pallas_call(
        functools.partial(spread_heads_kernel, width),
        out_shape=tuple(jax.ShapeDtypeStruct((rows, parts * w), F32) for w in widths)
        + (jax.ShapeDtypeStruct((parts * width, rows), F32),),
        grid=(parts,),
        in_specs=[pl.BlockSpec((1, rows, total), lambda i: (i, 0, 0))],
        out_specs=tuple(pl.BlockSpec((rows, w), lambda i: (0, i)) for w in widths)
        + (pl.BlockSpec((width, rows), lambda i: (i, 0)),),
        compiler_params=pltpu.CompilerParams(vmem_limit_bytes=60 * 1024 * 1024),
        name="spread_heads",
    )(stacked)


def by_row(array):
    return with_layout_constraint(array, Layout(major_to_minor=(0, 1)))


def own_columns(array, index, width):
    return lax.dynamic_slice_in_dim(array, index * width, width, axis=1)


def own_rows(array, index, width):
    return lax.dynamic_slice_in_dim(array, index * width, width, axis=0)


def local(
    hidden_in,
    weight_query,
    key_weight_matrix,
    weight_value,
    weight_out,
    weight_gate,
    weight_up,
    weight_down,
    gain_attention,
    gain_feed,
    gain_query,
    gain_key,
    positions,
    token_block_index,
    grad_out,
):
    parts = lax.axis_size("ctx")
    shards = lax.axis_size("fsdp")
    me = lax.axis_index("ctx")
    shard = lax.axis_index("fsdp")
    heads = QUERY_HEADS // parts
    sharers = parts // KEY_VALUE_HEADS
    key_head = me // sharers
    width = heads * HEAD_SIZE
    feed_width = FF // parts
    rows = D // shards
    head_rows = HEAD_SIZE // shards
    count = hidden_in.shape[1]
    tokens = parts * count

    def gather_rows(piece):
        return lax.all_gather(piece, "fsdp", axis=0, tiled=True)

    def sum_rows(grad):
        return lax.psum_scatter(grad.astype(BF16), "fsdp", scatter_dimension=0, tiled=True)

    def gather_parts(piece):
        return lax.all_gather(piece, "ctx", axis=0)

    own_heads_weight = jnp.concatenate(
        [
            own_columns(weight_query, me, width),
            own_columns(key_weight_matrix, key_head, HEAD_SIZE),
            own_columns(weight_value, key_head, HEAD_SIZE),
            own_rows(weight_out, me, width).T,
        ],
        axis=1,
    )
    feed_weight = gather_rows(
        jnp.concatenate(
            [
                own_columns(weight_gate, me, feed_width),
                own_columns(weight_up, me, feed_width),
                own_rows(weight_down, me, feed_width).T,
            ],
            axis=1,
        )
    )

    own_gains = jnp.concatenate([gain_attention, gain_feed, gain_query, gain_key]).astype(F32)
    own_gains = jnp.pad(own_gains, (0, 2048 - own_gains.shape[0])).reshape(16, 128)
    own_tokens = jnp.pad(jnp.stack([positions[0], token_block_index[0]]), ((0, 6), (0, 0)))
    hidden, grad = hidden_in[0], grad_out[0]
    normed_all, proj, heads_weight, gain_rows, gains, whole = first(
        hidden, own_gains, own_tokens, own_heads_weight, shards, parts, width + 2 * HEAD_SIZE
    )
    flat_gains = gains.reshape(shards, -1)
    norm_query = flat_gains[:, 2 * rows : 2 * rows + head_rows].reshape(1, -1)
    norm_key = flat_gains[:, 2 * rows + head_rows : 2 * rows + 2 * head_rows].reshape(1, -1)
    head_gains = jnp.concatenate([norm_query, norm_key, jnp.zeros((6, HEAD_SIZE), F32)])

    half = HEAD_SIZE // 2
    freq = THETA ** (-(jnp.arange(half).astype(F32) * 2.0 / HEAD_SIZE))
    angle = whole[:, 0].reshape(-1).astype(F32)[:, None] * freq
    cosine, sine = jnp.cos(angle), jnp.sin(angle)
    cosine = jnp.concatenate([cosine, cosine], axis=1)
    sine = jnp.concatenate([-sine, sine], axis=1)
    ids = whole[:, 1].reshape(-1)
    id_row, id_column = ids[None, :], ids[:, None]

    proj = proj.reshape(tokens, width + 2 * HEAD_SIZE)
    queries, keys, values, context, inverse, middle, normed_two, grad_all = attend(
        proj, cosine, sine, head_gains, id_column, id_row, heads_weight, hidden, grad, gain_rows, heads
    )
    normed_two_all, activation, back = feed(normed_two, grad_all, feed_weight)

    flat_grad = grad_all.reshape(tokens, D)
    flat_back = back.reshape(tokens, 2 * feed_width)
    flat_activation = activation.reshape(tokens, feed_width)
    feed_grad = by_row(tdot(normed_two_all.reshape(tokens, D), flat_back).astype(BF16))
    down_grad = by_row(tdot(flat_grad, flat_activation).astype(BF16))
    back, feed_grad, down_grad = lax.optimization_barrier((back, feed_grad, down_grad))
    feed_shard = sum_rows(feed_grad)

    grad_middle, low, gain_two, down_parts = feed_back(
        back, feed_weight, middle, grad, gain_rows, down_grad.reshape(shards, rows, feed_width)
    )
    low_all, context_grad, hidden_out = turn(low, heads_weight, activation, feed_weight, middle, width)

    context_grad, feed_shard, down_parts = lax.optimization_barrier(
        (context_grad, feed_shard, down_parts)
    )
    feed_parts = gather_parts(feed_shard)
    context_grad = context_grad.reshape(tokens, width)
    grad_qkv, gain_heads = attention_back(
        heads,
        queries,
        keys,
        values,
        context_grad,
        inverse,
        context,
        proj,
        cosine,
        sine,
        head_gains,
        id_column,
        id_row,
    )
    head_grad = jnp.concatenate(
        [
            by_row(tdot(normed_all.reshape(tokens, D), grad_qkv).astype(BF16)),
            by_row(tdot(low_all.reshape(tokens, D), context).astype(BF16)),
        ],
        axis=1,
    )
    grad_down = spread_turned(down_parts)
    grad_qkv, grad_down = lax.optimization_barrier((grad_qkv, grad_down))
    grad_hidden, gain_sums, head_parts = last(
        grad_qkv.reshape(parts, count, -1),
        heads_weight,
        hidden,
        grad_middle,
        gain_rows,
        gain_two,
        gain_heads,
        head_grad.reshape(shards, rows, -1),
    )

    gain_sums = gain_sums.reshape(-1)
    grad_gate, grad_up = spread_pair(feed_parts)
    grad_query, grad_key, grad_value, grad_out_weight = spread_heads(head_parts, width)
    if sharers > 1:
        grad_key, grad_value = (
            part.reshape(rows, KEY_VALUE_HEADS, sharers, HEAD_SIZE).sum(axis=2).reshape(rows, -1)
            for part in (grad_key, grad_value)
        )
    return (
        hidden_out[None],
        grad_hidden[None],
        grad_query,
        grad_key,
        grad_value,
        grad_out_weight,
        grad_gate,
        grad_up,
        grad_down,
        gain_sums[:rows],
        gain_sums[rows : 2 * rows],
        lax.dynamic_slice_in_dim(gain_sums, 2 * rows + shard * head_rows, head_rows),
        lax.dynamic_slice_in_dim(gain_sums, 2 * rows + HEAD_SIZE + shard * head_rows, head_rows),
    )


def solution(mesh):
    tokens = P("fsdp", "ctx", None)
    by_rows = P("fsdp", None)
    by_columns = P(None, "fsdp")
    per_token = P("fsdp", "ctx")
    vector = P("fsdp")
    weights = (by_rows, by_rows, by_rows, by_columns, by_rows, by_rows, by_columns)
    return jax.shard_map(
        local,
        mesh=mesh,
        in_specs=(tokens, *weights, vector, vector, vector, vector, per_token, per_token, tokens),
        out_specs=(tokens, tokens, *weights, vector, vector, vector, vector),
        check_vma=False,
    )
```

```python
import functools

import jax
import jax.numpy as jnp
from jax import lax
from jax.experimental import pallas as pl
from jax.experimental.layout import Layout, with_layout_constraint
from jax.experimental.pallas import tpu as pltpu
from jax.sharding import PartitionSpec as P

D = 2048
QUERY_HEADS = 16
KEY_VALUE_HEADS = 8
HEAD_SIZE = 128
FF = 6144
EPS = 1e-06
THETA = 1000000.0
F32 = jnp.float32
BF16 = jnp.bfloat16
MESH = pl.DeviceIdType.MESH
VMEM = pltpu.VMEM
WHOLE = pl.BlockSpec(memory_space=pltpu.VMEM)
HBM = pl.BlockSpec(memory_space=pl.ANY)
CHUNKS = 4
WIDE = D // CHUNKS


def dot(left, right):
    return jnp.dot(left, right, preferred_element_type=F32)


def tdot(left, right):
    return lax.dot_general(left, right, (((0,), (0,)), ((), ())), preferred_element_type=F32)


def rdot(left, right):
    return lax.dot_general(left, right, (((1,), (1,)), ((), ())), preferred_element_type=F32)


def loop(count, body):
    def step(index, carry):
        body(index)
        return carry

    lax.fori_loop(0, count, step, 0)


def line_position():
    me = lax.axis_index("ctx")
    return me, me // 2, me % 2, lax.axis_size("ctx") // 2


def send(source, target, send_sem, recv_sem, axis, index):
    return pltpu.make_async_remote_copy(
        src_ref=source,
        dst_ref=target,
        send_sem=send_sem,
        recv_sem=recv_sem,
        device_id={axis: index},
        device_id_type=MESH,
    )


def line_barrier():
    me, chip, core, chips = line_position()
    barrier = pltpu.get_barrier_semaphore()

    def greet(index):
        pl.semaphore_signal(barrier, inc=1, device_id={"ctx": index}, device_id_type=MESH)

    greet(me + 1 - 2 * core)

    @pl.when(chip > 0)
    def _():
        greet(me - 2)

    @pl.when(chip < chips - 1)
    def _():
        greet(me + 2)

    peers = 1 + (chip > 0).astype(jnp.int32) + (chip < chips - 1).astype(jnp.int32)
    pl.semaphore_wait(barrier, peers)


def peers_of(axis):
    me, size = lax.axis_index(axis), lax.axis_size(axis)
    return size - 1, lambda i: (me + i + 1) % size, lambda i: (me + size - i - 1) % size


def full_barrier():
    barrier = pltpu.get_barrier_semaphore()
    total = 0
    for axis in ("fsdp", "ctx"):
        count, ahead, _ = peers_of(axis)
        loop(
            count,
            lambda i, axis=axis, ahead=ahead: pl.semaphore_signal(
                barrier, inc=1, device_id={axis: ahead(i)}, device_id_type=MESH
            ),
        )
        total += count
    pl.semaphore_wait(barrier, total)


def gather_scratch(chips):
    return [pltpu.SemaphoreType.DMA((chips,)) for _ in range(6)]


class Gather:
    def __init__(self, land, sems, consume=None, late=False):
        self.late = late
        self.land = land
        self.sems = sems
        self.consume = consume
        self.me, self.chip, self.core, self.chips = line_position()

    def right(self, step, source):
        ref = self.land.at[2 * source + self.core]
        return send(ref, ref, self.sems[0].at[step], self.sems[1].at[step], "ctx", self.me + 2)

    def left(self, step, source):
        ref = self.land.at[2 * source + self.core]
        return send(ref, ref, self.sems[2].at[step], self.sems[3].at[step], "ctx", self.me - 2)

    def across(self, source, core):
        ref = self.land.at[2 * source + core]
        other = self.me + 1 - 2 * self.core
        return send(ref, ref, self.sems[4].at[source], self.sems[5].at[source], "ctx", other)

    def step(self, step):
        chip, core, chips = self.chip, self.core, self.chips
        low, high = chip - step, chip + step
        has_low = low >= 0
        has_high = jnp.logical_and(high < chips, step > 0)

        @pl.when(jnp.logical_and(has_low, step > 0))
        def _():
            self.right(step - 1, low).wait_recv()

        @pl.when(jnp.logical_and(has_low, chip < chips - 1))
        def _():
            self.right(step, low).start()

        @pl.when(has_high)
        def _():
            self.left(step - 1, high).wait_recv()

        @pl.when(jnp.logical_and(high < chips, chip > 0))
        def _():
            self.left(step, high).start()

        @pl.when(has_low)
        def _():
            self.across(low, core).start()

        @pl.when(has_high)
        def _():
            self.across(high, core).start()

        if not self.late:
            self.use(step)
            return

        @pl.when(step > 0)
        def _():
            self.use(step - 1)

        @pl.when(step == chips - 1)
        def _():
            self.use(step)

    def use(self, step):
        chip, core, chips = self.chip, self.core, self.chips
        low, high = chip - step, chip + step

        def one(kind):
            upward = kind % 2
            crossed = kind // 2
            source = jnp.where(upward == 1, high, low)
            valid = jnp.where(upward == 1, jnp.logical_and(high < chips, step > 0), low >= 0)
            parity = jnp.where(crossed == 1, 1 - core, core)

            @pl.when(valid)
            def _():
                @pl.when(crossed == 1)
                def _():
                    self.across(source, parity).wait_recv()

                if self.consume is not None:
                    self.consume(2 * source + parity)

        loop(4, one)

    def finish(self):
        chip, core, chips = self.chip, self.core, self.chips

        def one(step):
            @pl.when(jnp.logical_and(chip - step >= 0, chip < chips - 1))
            def _():
                self.right(step, chip - step).wait_send()

            @pl.when(jnp.logical_and(chip + step < chips, chip > 0))
            def _():
                self.left(step, chip + step).wait_send()

            self.across(step, core).wait_send()

        loop(chips, one)


def scatter_scratch(chips, rows):
    buffers = [VMEM((count, CHUNKS, rows, WIDE), BF16) for count in (chips + 1, chips, chips)]
    return buffers + [pltpu.SemaphoreType.DMA((chips, CHUNKS)) for _ in range(6)]


class Scatter:
    def __init__(self, scratch, produce, total):
        self.line, self.out, self.other = scratch[:3]
        self.sems = scratch[3:]
        self.produce = produce
        self.total = total
        self.me, self.chip, self.core, self.chips = line_position()


    def right(self, step, chunk):
        ref = self.line.at[step, chunk]
        sems = self.sems
        return send(ref, ref, sems[0].at[step, chunk], sems[1].at[step, chunk], "ctx", self.me + 2)

    def left(self, step, chunk):
        ref = self.line.at[self.chips - step, chunk]
        sems = self.sems
        return send(ref, ref, sems[2].at[step, chunk], sems[3].at[step, chunk], "ctx", self.me - 2)

    def across(self, target, chunk):
        sems = self.sems
        return send(
            self.out.at[target, chunk],
            self.other.at[target, chunk],
            sems[4].at[target, chunk],
            sems[5].at[target, chunk],
            "ctx",
            self.me + 1 - 2 * self.core,
        )

    def begin(self):
        def clear(index):
            slot, chunk = index // CHUNKS, index % CHUNKS
            at_left = jnp.logical_and(self.chip == 0, slot < self.chips)
            at_right = jnp.logical_and(self.chip == self.chips - 1, slot > 0)

            @pl.when(jnp.logical_or(at_left, at_right))
            def _():
                self.line[slot, chunk] = jnp.zeros(self.line.shape[2:], BF16)

        loop((self.chips + 1) * CHUNKS, clear)

    def when_right(self, time):
        return jnp.logical_and(time >= self.chip, time < self.chips - 1)

    def when_left(self, time):
        return jnp.logical_and(time >= self.chips - 1 - self.chip, time < self.chips - 1)

    def prepare(self, time):
        def cross(target):
            def one(chunk):
                piece = 2 * target + 1 - self.core
                self.out[target, chunk] = self.produce(piece, chunk).astype(BF16)
                self.across(target, chunk).start()

            loop(CHUNKS, one)

        @pl.when(self.when_right(time))
        def _():
            cross(self.chips - 1 - time + self.chip)

        @pl.when(self.when_left(time))
        def _():
            cross(time - (self.chips - 1 - self.chip))

        @pl.when(time == self.chips - 1)
        def _():
            cross(self.chip)

    def step(self, time):
        chip, core, chips = self.chip, self.core, self.chips

        @pl.when(self.when_right(time))
        def _():
            step = time - chip
            target = chips - 1 - step

            def one(chunk):
                self.across(target, chunk).wait_recv()

                @pl.when(chip > 0)
                def _():
                    self.right(step, chunk).wait_recv()

                value = self.produce(2 * target + core, chunk) + self.other[target, chunk].astype(F32)
                value = value + self.line[step, chunk].astype(F32)
                self.line[step, chunk] = value.astype(BF16)
                self.right(step, chunk).start()

            loop(CHUNKS, one)

        @pl.when(self.when_left(time))
        def _():
            step = time - (chips - 1 - chip)

            def one(chunk):
                self.across(step, chunk).wait_recv()

                @pl.when(chip < chips - 1)
                def _():
                    self.left(step, chunk).wait_recv()

                value = self.produce(2 * step + core, chunk) + self.other[step, chunk].astype(F32)
                value = value + self.line[chips - step, chunk].astype(F32)
                self.line[chips - step, chunk] = value.astype(BF16)
                self.left(step, chunk).start()

            loop(CHUNKS, one)

    def finish(self):
        chip, core, chips = self.chip, self.core, self.chips
        last = chips - 1 - chip

        def one(chunk):
            self.across(chip, chunk).wait_recv()
            value = self.produce(2 * chip + core, chunk) + self.other[chip, chunk].astype(F32)

            @pl.when(chip > 0)
            def _():
                self.right(last, chunk).wait_recv()

            @pl.when(chip < chips - 1)
            def _():
                self.left(chip, chunk).wait_recv()

            value = value + self.line[last, chunk].astype(F32)
            value = value + self.line[chips - chip, chunk].astype(F32)
            self.total[:, pl.ds(pl.multiple_of(chunk * WIDE, WIDE), WIDE)] = value

        loop(CHUNKS, one)

        def drain(index):
            step, chunk = index // CHUNKS, index % CHUNKS

            @pl.when(step < last)
            def _():
                self.right(step, chunk).wait_send()

            @pl.when(step < chip)
            def _():
                self.left(step, chunk).wait_send()

            self.across(step, chunk).wait_send()

        loop(chips * CHUNKS, drain)


def row_blocks(rows, body, size=32):
    def one(index):
        body(pl.ds(pl.multiple_of(index * size, size), size))

    loop(rows // size, one)


def inverse_norm(value):
    return lax.rsqrt(jnp.mean(value * value, axis=-1, keepdims=True) + EPS)


def params(identity, megabytes):
    return pltpu.CompilerParams(
        collective_id=identity,
        has_side_effects=True,
        vmem_limit_bytes=megabytes * 1024 * 1024,
    )


def cost(microseconds):
    return pl.CostEstimate(
        flops=int(microseconds * 1.15e9), bytes_accessed=1024, transcendentals=0
    )


class FsdpSum:
    def __init__(self, grad, arrived, send_sems, recv_sems):
        self.grad, self.arrived = grad, arrived
        self.sems = send_sems, recv_sems
        self.peers, self.ahead, _ = peers_of("fsdp")

    def copy(self, i):
        target = self.ahead(i)
        return send(
            self.grad.at[target], self.arrived.at[i], self.sems[0].at[i], self.sems[1].at[i], "fsdp", target
        )

    def start(self):
        loop(self.peers, lambda i: self.copy(i).start())

    def collect(self, land, slot):
        shard = lax.axis_index("fsdp")
        loop(self.peers, lambda i: self.copy(i).wait_recv())

        def add(block):
            value = self.grad[shard, block].astype(F32)
            for i in range(self.peers):
                value = value + self.arrived[i, block].astype(F32)
            land[slot, block] = value.astype(BF16)

        row_blocks(self.grad.shape[1], add)

    def finish(self):
        loop(self.peers, lambda i: self.copy(i).wait_send())


def fsdp_scratch(shards, rows, width):
    return [VMEM((shards - 1, rows, width), BF16)] + [pltpu.SemaphoreType.DMA((shards,))] * 2


def copy_in(source, target, sem):
    copy = pltpu.make_async_copy(source, target, sem)
    copy.start()
    return copy


def first_kernel(rows, width, *refs):
    x, gains, tokens, part, land, proj, weights, gain_rows, all_gains, all_tokens = refs[:10]
    sems, small = refs[10:16], refs[16:]
    me, _, _, chips = line_position()
    shard = lax.axis_index("fsdp")
    shards, ahead, behind = peers_of("fsdp")
    parts, next_part, past_part = peers_of("ctx")
    full_barrier()

    def gain_copy(i, slot):
        return send(gains, all_gains.at[slot], small[0].at[i], small[1].at[i], "fsdp", ahead(i))

    def token_copy(i, slot):
        return send(tokens, all_tokens.at[slot], small[2].at[i], small[3].at[i], "ctx", next_part(i))

    def weight_copy(i, owner):
        target = weights.at[pl.ds(pl.multiple_of(owner * rows, rows), rows), :]
        return send(part, target, small[4].at[i], small[5].at[i], "fsdp", ahead(i))

    loop(shards, lambda i: gain_copy(i, shard).start())
    loop(parts, lambda i: token_copy(i, me).start())
    loop(shards, lambda i: weight_copy(i, shard).start())
    all_gains[shard] = gains[...]
    all_tokens[me] = tokens[...]
    weights[pl.ds(pl.multiple_of(shard * rows, rows), rows), :] = part[...]
    loop(shards, lambda i: gain_copy(i, behind(i)).wait_recv())
    lanes = rows // 128
    for kind in range(2):
        for owner in range(shards + 1):
            for j in range(lanes):
                at = owner * rows + j * 128
                gain_rows[kind : kind + 1, at : at + 128] = all_gains[
                    owner, kind * lanes + j : kind * lanes + j + 1, :
                ]

    def norm(block):
        value = x[block, :].astype(F32)
        land[me, block] = (value * inverse_norm(value) * gain_rows[0:1, :]).astype(BF16)

    row_blocks(x.shape[0], norm)

    gather = Gather(land, sems)
    loop(chips, gather.step)
    loop(shards, lambda i: weight_copy(i, behind(i)).wait_recv())

    def project(piece):
        proj[piece] = dot(land[piece], weights[:, :width])

    loop(2 * chips, project)
    gather.finish()
    loop(shards, lambda i: gain_copy(i, shard).wait_send())
    loop(shards, lambda i: weight_copy(i, shard).wait_send())
    loop(parts, lambda i: token_copy(i, past_part(i)).wait_recv())
    loop(parts, lambda i: token_copy(i, me).wait_send())


def first(hidden, gains, tokens, part, shards, parts, width):
    count = hidden.shape[0]
    return pl.pallas_call(
        functools.partial(first_kernel, D // shards, width),
        out_shape=(
            jax.ShapeDtypeStruct((parts, count, D), BF16),
            jax.ShapeDtypeStruct((parts, count, width), F32),
            jax.ShapeDtypeStruct((D, part.shape[1]), BF16),
            jax.ShapeDtypeStruct((8, D), F32),
            jax.ShapeDtypeStruct((shards, *gains.shape), F32),
            jax.ShapeDtypeStruct((parts, *tokens.shape), jnp.int32),
        ),
        in_specs=[WHOLE] * 4,
        out_specs=(WHOLE,) * 6,
        scratch_shapes=gather_scratch(parts // 2)
        + [pltpu.SemaphoreType.DMA((shards,))] * 2
        + [pltpu.SemaphoreType.DMA((parts,))] * 2
        + [pltpu.SemaphoreType.DMA((shards,))] * 2,
        compiler_params=params(0, 60),
        cost_estimate=cost(85),
        name="gather_normed",
    )(hidden, gains, tokens, part)


def feed_kernel(width, *refs):
    x, grads, weights, land, activation, back = refs[:6]
    weight, weight_sem, grad, grad_sems = refs[6:10]
    sems = refs[10:]
    me, _, _, chips = line_position()
    copy = copy_in(weights, weight, weight_sem)

    def grad_copy(piece):
        return pltpu.make_async_copy(grads.at[piece], grad.at[piece], grad_sems.at[piece])

    loop(2 * chips, lambda piece: grad_copy(piece).start())
    land[me] = x[...]
    size = 256 if width % 256 == 0 else 128

    def consume(piece):
        grad_copy(piece).wait()

        def one(index):
            def columns(kind):
                return pl.ds(pl.multiple_of(kind * width + index * size, 128), size)

            gate = dot(land[piece], weight[:, columns(0)])
            up = dot(land[piece], weight[:, columns(1)])
            grad_act = dot(grad[piece], weight[:, columns(2)])
            sigma = 1.0 / (1.0 + jnp.exp(-gate))
            activation[piece, :, columns(0)] = (gate * sigma * up).astype(BF16)
            back[piece, :, columns(0)] = (
                grad_act * up * sigma * (1.0 + gate * (1.0 - sigma))
            ).astype(BF16)
            back[piece, :, columns(1)] = (grad_act * gate * sigma).astype(BF16)

        loop(width // size, one)

    line_barrier()
    gather = Gather(land, sems, consume)
    copy.wait()
    loop(chips, gather.step)
    gather.finish()


def feed(normed, grads, weights):
    parts, count, _ = grads.shape
    width = weights.shape[1] // 3
    return pl.pallas_call(
        functools.partial(feed_kernel, width),
        out_shape=(
            jax.ShapeDtypeStruct((parts, count, D), BF16),
            jax.ShapeDtypeStruct((parts, count, width), BF16),
            jax.ShapeDtypeStruct((parts, count, 2 * width), BF16),
        ),
        in_specs=[WHOLE, HBM, HBM],
        out_specs=(WHOLE,) * 3,
        scratch_shapes=[
            VMEM(weights.shape, BF16),
            pltpu.SemaphoreType.DMA,
            VMEM(grads.shape, BF16),
            pltpu.SemaphoreType.DMA((parts,)),
        ]
        + gather_scratch(parts // 2),
        compiler_params=params(2, 60),
        cost_estimate=cost(90),
        name="feed",
    )(normed, grads, weights)


def rms_back(value, gain, grad):
    inverse = inverse_norm(value)
    scaled = grad * gain
    inner = jnp.mean(scaled * value, axis=-1, keepdims=True)
    terms = grad * value * inverse
    return inverse * scaled - value * (inverse * inverse * inverse * inner), terms


def feed_back_kernel(columns, *refs):
    back, weights, middle, grad, gain_rows, down_grad, grad_middle, low, gain_sum, land = refs[:10]
    weight, weight_sem, total = refs[10:13]
    down_refs, gather_sems, scratch = refs[13:16], refs[16:22], refs[22:]
    me, _, _, chips = line_position()
    copy = copy_in(weights.at[:, columns], weight, weight_sem)

    def produce(piece, chunk):
        return rdot(back[piece], weight[pl.ds(pl.multiple_of(chunk * WIDE, WIDE), WIDE), :])

    down = FsdpSum(down_grad, *down_refs)
    gather = Gather(land, gather_sems)
    scatter = Scatter(scratch, produce, total)
    scatter.begin()
    full_barrier()
    down.start()
    copy.wait()
    scatter.prepare(0)

    def step(time):
        scatter.step(time)
        scatter.prepare(time + 1)

        @pl.when(time == 1)
        def _():
            down.collect(land, me)

        @pl.when(time >= 1)
        def _():
            gather.step(time - 1)

    loop(chips - 1, step)
    scatter.finish()
    gather.step(chips - 2)
    gain_sum[...] = jnp.zeros_like(gain_sum)

    def norm(block):
        through, terms = rms_back(middle[block, :], gain_rows[1:2, :], total[block, :])
        value = grad[block, :].astype(F32) + through
        grad_middle[block, :] = value
        low[block, :] = value.astype(BF16)
        gain_sum[0:1, :] += jnp.sum(terms, axis=0, keepdims=True)

    row_blocks(middle.shape[0], norm)
    gather.step(chips - 1)
    gather.finish()
    down.finish()


def feed_back(back, weights, middle, grad, gain_rows, down_grad):
    parts, count, width = back.shape
    shards, rows, down_width = down_grad.shape
    return pl.pallas_call(
        functools.partial(feed_back_kernel, pl.ds(0, width)),
        out_shape=(
            jax.ShapeDtypeStruct((count, D), F32),
            jax.ShapeDtypeStruct((count, D), BF16),
            jax.ShapeDtypeStruct((8, D), F32),
            jax.ShapeDtypeStruct((parts, rows, down_width), BF16),
        ),
        in_specs=[WHOLE, HBM, WHOLE, WHOLE, WHOLE, WHOLE],
        out_specs=(WHOLE,) * 4,
        scratch_shapes=[VMEM((D, width), BF16), pltpu.SemaphoreType.DMA, VMEM((count, D), F32)]
        + fsdp_scratch(shards, rows, down_width)
        + gather_scratch(parts // 2)
        + scatter_scratch(parts // 2, count),
        compiler_params=params(3, 62),
        cost_estimate=cost(100),
        name="feed_back",
    )(back, weights, middle, grad, gain_rows, down_grad)


def turn_kernel(columns, down_columns, *refs):
    low, weights, activation, feed_weights, middle, land, context_grad, hidden = refs[:8]
    weight, weight_sem, down, down_sem, total = refs[8:13]
    gather_sems, scratch = refs[13:19], refs[19:]
    me, _, _, chips = line_position()
    copy = copy_in(weights.at[:, columns], weight, weight_sem)
    down_copy = copy_in(feed_weights.at[:, down_columns], down, down_sem)
    land[me] = low[...]

    def consume(piece):
        context_grad[piece] = dot(land[piece], weight[...]).astype(BF16)

    def produce(piece, chunk):
        return rdot(activation[piece], down[pl.ds(pl.multiple_of(chunk * WIDE, WIDE), WIDE), :])

    gather = Gather(land, gather_sems, consume)
    scatter = Scatter(scratch, produce, total)
    scatter.begin()
    line_barrier()
    copy.wait()
    down_copy.wait()
    scatter.prepare(0)

    def step(time):
        gather.step(time)
        scatter.step(time)
        scatter.prepare(time + 1)

    loop(chips - 1, step)
    gather.step(chips - 1)
    scatter.finish()
    gather.finish()

    def add(block):
        hidden[block, :] = (middle[block, :] + total[block, :]).astype(BF16)

    row_blocks(middle.shape[0], add)


def turn(low, weights, activation, feed_weights, middle, width):
    parts, count, feed_width = activation.shape
    return pl.pallas_call(
        functools.partial(
            turn_kernel, pl.ds(weights.shape[1] - width, width), pl.ds(2 * feed_width, feed_width)
        ),
        out_shape=(
            jax.ShapeDtypeStruct((parts, count, D), BF16),
            jax.ShapeDtypeStruct((parts, count, width), BF16),
            jax.ShapeDtypeStruct((count, D), BF16),
        ),
        in_specs=[WHOLE, HBM, WHOLE, HBM, WHOLE],
        out_specs=(WHOLE,) * 3,
        scratch_shapes=[
            VMEM((D, width), BF16),
            pltpu.SemaphoreType.DMA,
            VMEM((D, feed_width), BF16),
            pltpu.SemaphoreType.DMA,
            VMEM((count, D), F32),
        ]
        + gather_scratch(parts // 2)
        + scatter_scratch(parts // 2, count),
        compiler_params=params(4, 62),
        cost_estimate=cost(107),
        name="turn",
    )(low, weights, activation, feed_weights, middle)


def last_kernel(columns, *refs):
    back, weights, x, grad_middle, gain_rows, gain_two, gain_heads, head_grad = refs[:8]
    hidden, gain_out, land = refs[8:11]
    weight, weight_sem, total, gain_one, pack, pack_in, shard_sum, shard_in = refs[11:19]
    small, head_refs, gather_sems, scratch = refs[19:23], refs[23:26], refs[26:32], refs[32:]
    me, _, _, chips = line_position()
    shard = lax.axis_index("fsdp")
    shards, ahead, _ = peers_of("fsdp")
    parts, next_part, _ = peers_of("ctx")
    copy = copy_in(weights.at[:, columns], weight, weight_sem)

    def produce(piece, chunk):
        return rdot(back[piece], weight[pl.ds(pl.multiple_of(chunk * WIDE, WIDE), WIDE), :])

    heads = FsdpSum(head_grad, *head_refs)
    scatter = Scatter(scratch, produce, total)
    gather = Gather(land, gather_sems)
    scatter.begin()
    full_barrier()
    copy.wait()
    scatter.prepare(0)
    heads.start()

    def step(time):
        scatter.step(time)

        @pl.when(time == 1)
        def _():
            heads.collect(land, me)

        @pl.when(time >= 1)
        def _():
            gather.step(time - 1)

        scatter.prepare(time + 1)

    loop(chips - 1, step)
    scatter.finish()
    gather.step(chips - 2)
    gain_one[...] = jnp.zeros_like(gain_one)

    def norm(block):
        through, terms = rms_back(x[block, :].astype(F32), gain_rows[0:1, :], total[block, :])
        hidden[block, :] = grad_middle[block, :] + through
        gain_one[0:1, :] += jnp.sum(terms, axis=0, keepdims=True)

    row_blocks(x.shape[0], norm)

    rows = D // (shards + 1)
    lanes = rows // 128
    pack[...] = jnp.zeros_like(pack)
    for owner in range(shards + 1):
        for j in range(lanes):
            at = owner * rows + j * 128
            pack[owner, j : j + 1, :] = gain_one[0:1, at : at + 128]
            pack[owner, lanes + j : lanes + j + 1, :] = gain_two[0:1, at : at + 128]
        pack[owner, 2 * lanes : 2 * lanes + 2, :] = gain_heads[0:2, :]

    def pack_copy(i):
        return send(pack.at[ahead(i)], pack_in.at[i], small[0].at[i], small[1].at[i], "fsdp", ahead(i))

    def sum_copy(i):
        return send(shard_sum, shard_in.at[i], small[2].at[i], small[3].at[i], "ctx", next_part(i))

    loop(shards, lambda i: pack_copy(i).start())
    shard_sum[...] = pack[shard]

    def add_pack(i):
        pack_copy(i).wait_recv()
        shard_sum[...] += pack_in[i]

    loop(shards, add_pack)
    loop(parts, lambda i: sum_copy(i).start())
    gain_out[...] = shard_sum[...]

    def add_sum(i):
        sum_copy(i).wait_recv()
        gain_out[...] += shard_in[i]

    loop(parts, add_sum)
    gather.step(chips - 1)
    gather.finish()
    heads.finish()
    loop(shards, lambda i: pack_copy(i).wait_send())
    loop(parts, lambda i: sum_copy(i).wait_send())


def last(back, weights, hidden, grad_middle, gain_rows, gain_two, gain_heads, head_grad):
    parts, count, width = back.shape
    shards, rows, head_width = head_grad.shape
    return pl.pallas_call(
        functools.partial(last_kernel, pl.ds(0, width)),
        out_shape=(
            jax.ShapeDtypeStruct((count, D), F32),
            jax.ShapeDtypeStruct((16, 128), F32),
            jax.ShapeDtypeStruct((parts, rows, head_width), BF16),
        ),
        in_specs=[WHOLE, HBM] + [WHOLE] * 6,
        out_specs=(WHOLE,) * 3,
        scratch_shapes=[
            VMEM((D, width), BF16),
            pltpu.SemaphoreType.DMA,
            VMEM((count, D), F32),
            VMEM((8, D), F32),
            VMEM((shards, 16, 128), F32),
            VMEM((shards, 16, 128), F32),
            VMEM((16, 128), F32),
            VMEM((parts, 16, 128), F32),
        ]
        + [pltpu.SemaphoreType.DMA((shards,))] * 2
        + [pltpu.SemaphoreType.DMA((parts,))] * 2
        + fsdp_scratch(shards, rows, head_width)
        + gather_scratch(parts // 2)
        + scatter_scratch(parts // 2, count),
        compiler_params=params(5, 60),
        cost_estimate=cost(90),
        name="last",
    )(back, weights, hidden, grad_middle, gain_rows, gain_two, gain_heads, head_grad)


QUERY_TILE = 256
KEY_TILE = 512


def reach(index, tokens):
    return jnp.minimum((index + 2) * QUERY_TILE + KEY_TILE - 1, tokens) // KEY_TILE


def head_norm(value, gain, cosine, sine):
    normed = value * inverse_norm(value) * gain
    return normed * cosine + pltpu.roll(normed, HEAD_SIZE // 2, 1) * sine


def attend_kernel(heads, columns, *refs):
    proj, cosine, sine, gain, id_column, id_row, weights, x, grad, gain_rows = refs[:10]
    queries, keys, values, context, inverse, middle, normed, land = refs[10:18]
    weight, weight_sem, grad_sem, total = refs[18:22]
    gather_sems, scratch = refs[22:28], refs[28:]
    me, _, _, chips = line_position()
    tokens = proj.shape[0]
    count = x.shape[0]
    key_at = heads * HEAD_SIZE
    copy = copy_in(weights.at[:, columns], weight, weight_sem)
    own = copy_in(grad, land.at[me], grad_sem)
    gather = Gather(land, gather_sems)
    line_barrier()
    own.wait()
    gather.step(0)

    def prepare(index):
        block = pl.ds(pl.multiple_of(index * QUERY_TILE, QUERY_TILE), QUERY_TILE)
        c, s = cosine[block, :], sine[block, :]
        for h in range(heads):
            lanes = slice(h * HEAD_SIZE, (h + 1) * HEAD_SIZE)
            rotated = head_norm(proj[block, lanes], gain[0:1, :], c, s) * HEAD_SIZE ** (-0.5)
            queries[block, lanes] = rotated.astype(BF16)
        rotated = head_norm(proj[block, key_at : key_at + HEAD_SIZE], gain[1:2, :], c, s)
        keys[block, :] = rotated.astype(BF16)
        values[block, :] = proj[block, key_at + HEAD_SIZE : key_at + 2 * HEAD_SIZE].astype(BF16)

    loop(tokens // QUERY_TILE, prepare)

    def attend(index):
        block = pl.ds(pl.multiple_of(index * QUERY_TILE, QUERY_TILE), QUERY_TILE)
        query_ids = id_column[block, :]
        for h in range(heads):
            lanes = slice(h * HEAD_SIZE, (h + 1) * HEAD_SIZE)
            query = queries[block, lanes]

            def one(tile, carry):
                sums, total = carry
                span = pl.ds(pl.multiple_of(tile * KEY_TILE, KEY_TILE), KEY_TILE)
                scores = rdot(query, keys[span, :])
                expon = jnp.where(id_row[0:1, span] <= query_ids, jnp.exp(scores), 0.0)
                sums = sums + dot(expon.astype(BF16), values[span, :])
                return sums, total + jnp.sum(expon, axis=1, keepdims=True)

            start = (jnp.zeros((QUERY_TILE, HEAD_SIZE), F32), jnp.zeros((QUERY_TILE, 1), F32))
            sums, total = lax.fori_loop(0, reach(index, tokens), one, start)
            scale = 1.0 / total
            context[block, lanes] = (sums * scale).astype(BF16)
            inverse[h : h + 1, block] = jnp.broadcast_to(scale, (QUERY_TILE, HEAD_SIZE)).T[0:1, :]

    loop(tokens // QUERY_TILE, attend)

    def produce(piece, chunk):
        block = pl.ds(pl.multiple_of(piece * count, count), count)
        return rdot(context[block, :], weight[pl.ds(pl.multiple_of(chunk * WIDE, WIDE), WIDE), :])

    scatter = Scatter(scratch, produce, total)
    scatter.begin()
    copy.wait()
    scatter.prepare(0)
    gather.step(1)

    def step(time):
        scatter.step(time)
        scatter.prepare(time + 1)

        @pl.when(time >= 1)
        def _():
            gather.step(time + 1)

    loop(chips - 1, step)
    scatter.finish()

    def norm(block):
        value = x[block, :].astype(F32) + total[block, :]
        middle[block, :] = value
        normed[block, :] = (value * inverse_norm(value) * gain_rows[1:2, :]).astype(BF16)

    row_blocks(count, norm)
    gather.finish()


def attend(proj, cosine, sine, gain, id_column, id_row, weights, hidden, grad, gain_rows, heads):
    tokens = proj.shape[0]
    width = heads * HEAD_SIZE
    count = hidden.shape[0]
    parts = tokens // count
    return pl.pallas_call(
        functools.partial(attend_kernel, heads, pl.ds(weights.shape[1] - width, width)),
        out_shape=(
            jax.ShapeDtypeStruct((tokens, width), BF16),
            jax.ShapeDtypeStruct((tokens, HEAD_SIZE), BF16),
            jax.ShapeDtypeStruct((tokens, HEAD_SIZE), BF16),
            jax.ShapeDtypeStruct((tokens, width), BF16),
            jax.ShapeDtypeStruct((8, tokens), F32),
            jax.ShapeDtypeStruct((count, D), F32),
            jax.ShapeDtypeStruct((count, D), BF16),
            jax.ShapeDtypeStruct((parts, count, D), BF16),
        ),
        in_specs=[WHOLE] * 6 + [HBM, WHOLE, WHOLE, WHOLE],
        out_specs=(WHOLE,) * 7 + (HBM,),
        scratch_shapes=[
            VMEM((D, width), BF16),
            pltpu.SemaphoreType.DMA,
            pltpu.SemaphoreType.DMA,
            VMEM((count, D), F32),
        ]
        + gather_scratch(parts // 2)
        + scatter_scratch(parts // 2, count),
        compiler_params=params(1, 60),
        cost_estimate=cost(110),
        name="attend",
    )(proj, cosine, sine, gain, id_column, id_row, weights, hidden, grad, gain_rows)


def attention_back_kernel(heads, *refs):
    queries, keys, values, out_grad, inverse, context, proj, cosine, sine, gain = refs[:10]
    id_column, id_row, back, gain_sum, key_grad, value_grad, query_grad = refs[10:]
    tokens = proj.shape[0]
    key_at = heads * HEAD_SIZE
    key_grad[...] = jnp.zeros_like(key_grad)
    value_grad[...] = jnp.zeros_like(value_grad)
    gain_sum[...] = jnp.zeros_like(gain_sum)

    def through(block, lanes, grad, row):
        turned = pltpu.roll(grad, HEAD_SIZE // 2, 1)
        unrotated = grad * cosine[block, :] - turned * sine[block, :]
        result, terms = rms_back(proj[block, lanes], gain[row : row + 1, :], unrotated)
        back[block, lanes] = result.astype(BF16)
        gain_sum[row : row + 1, :] += jnp.sum(terms, axis=0, keepdims=True)

    def attend(index):
        block = pl.ds(pl.multiple_of(index * QUERY_TILE, QUERY_TILE), QUERY_TILE)
        query_ids = id_row[0:1, block]
        for h in range(heads):
            lanes = slice(h * HEAD_SIZE, (h + 1) * HEAD_SIZE)
            query = queries[block, lanes]
            grad = out_grad[block, lanes]
            scale = inverse[h : h + 1, block]
            products = grad.astype(F32) * context[block, lanes].astype(F32)
            shift = lax.dot_general(
                jnp.ones((8, HEAD_SIZE), F32),
                products,
                (((1,), (1,)), ((), ())),
                precision=lax.Precision.HIGHEST,
                preferred_element_type=F32,
            )[0:1, :]
            query_grad[...] = jnp.zeros_like(query_grad)

            def one(tile):
                span = pl.ds(pl.multiple_of(tile * KEY_TILE, KEY_TILE), KEY_TILE)
                key = keys[span, :]
                scores = rdot(key, query)
                probs = jnp.where(id_column[span, :] <= query_ids, jnp.exp(scores) * scale, 0.0)
                grad_scores = (probs * (rdot(values[span, :], grad) - shift)).astype(BF16)
                value_grad[span, :] += dot(probs.astype(BF16), grad)
                key_grad[span, :] += dot(grad_scores, query)
                query_grad[...] += tdot(grad_scores, key)

            loop(reach(index, tokens), one)
            through(block, lanes, query_grad[...] * HEAD_SIZE ** (-0.5), 0)

    loop(tokens // QUERY_TILE, attend)

    def finish(index):
        block = pl.ds(pl.multiple_of(index * QUERY_TILE, QUERY_TILE), QUERY_TILE)
        through(block, slice(key_at, key_at + HEAD_SIZE), key_grad[block, :], 1)
        back[block, key_at + HEAD_SIZE : key_at + 2 * HEAD_SIZE] = value_grad[block, :].astype(BF16)

    loop(tokens // QUERY_TILE, finish)


def attention_back(heads, *operands):
    tokens = operands[0].shape[0]
    width = heads * HEAD_SIZE
    return pl.pallas_call(
        functools.partial(attention_back_kernel, heads),
        out_shape=(
            jax.ShapeDtypeStruct((tokens, width + 2 * HEAD_SIZE), BF16),
            jax.ShapeDtypeStruct((8, HEAD_SIZE), F32),
        ),
        in_specs=[WHOLE] * len(operands),
        out_specs=(WHOLE,) * 2,
        scratch_shapes=[
            VMEM((tokens, HEAD_SIZE), F32),
            VMEM((tokens, HEAD_SIZE), F32),
            VMEM((QUERY_TILE, HEAD_SIZE), F32),
        ],
        compiler_params=pltpu.CompilerParams(vmem_limit_bytes=48 * 1024 * 1024),
        cost_estimate=cost(38),
        name="attention_back",
    )(*operands)


def spread_pair_kernel(width, source, gate, up):
    gate[...] = source[0, :, :width].astype(F32)
    up[...] = source[0, :, width:].astype(F32)


def spread_pair(stacked):
    parts, rows, total = stacked.shape
    width = total // 2
    across = jax.ShapeDtypeStruct((rows, parts * width), F32)
    return pl.pallas_call(
        functools.partial(spread_pair_kernel, width),
        out_shape=(across, across),
        grid=(parts,),
        in_specs=[pl.BlockSpec((1, rows, total), lambda i: (i, 0, 0))],
        out_specs=(pl.BlockSpec((rows, width), lambda i: (0, i)),) * 2,
        compiler_params=pltpu.CompilerParams(vmem_limit_bytes=60 * 1024 * 1024),
        name="spread_pair",
    )(stacked)


def spread_turned_kernel(source, target):
    target[...] = source[0].astype(F32).T


def spread_turned(stacked):
    parts, rows, width = stacked.shape
    return pl.pallas_call(
        spread_turned_kernel,
        out_shape=jax.ShapeDtypeStruct((parts * width, rows), F32),
        grid=(parts,),
        in_specs=[pl.BlockSpec((1, rows, width), lambda i: (i, 0, 0))],
        out_specs=pl.BlockSpec((width, rows), lambda i: (i, 0)),
        compiler_params=pltpu.CompilerParams(vmem_limit_bytes=60 * 1024 * 1024),
        name="spread_turned",
    )(stacked)


def spread_heads_kernel(width, source, query, key, value, out):
    second = width + HEAD_SIZE
    third = second + HEAD_SIZE
    query[...] = source[0, :, :width].astype(F32)
    key[...] = source[0, :, width:second].astype(F32)
    value[...] = source[0, :, second:third].astype(F32)
    out[...] = source[0, :, third:].astype(F32).T


def spread_heads(stacked, width):
    parts, rows, total = stacked.shape
    widths = (width, HEAD_SIZE, HEAD_SIZE)
    return pl.pallas_call(
        functools.partial(spread_heads_kernel, width),
        out_shape=tuple(jax.ShapeDtypeStruct((rows, parts * w), F32) for w in widths)
        + (jax.ShapeDtypeStruct((parts * width, rows), F32),),
        grid=(parts,),
        in_specs=[pl.BlockSpec((1, rows, total), lambda i: (i, 0, 0))],
        out_specs=tuple(pl.BlockSpec((rows, w), lambda i: (0, i)) for w in widths)
        + (pl.BlockSpec((width, rows), lambda i: (i, 0)),),
        compiler_params=pltpu.CompilerParams(vmem_limit_bytes=60 * 1024 * 1024),
        name="spread_heads",
    )(stacked)


def by_row(array):
    return with_layout_constraint(array, Layout(major_to_minor=(0, 1)))


def own_columns(array, index, width):
    return lax.dynamic_slice_in_dim(array, index * width, width, axis=1)


def own_rows(array, index, width):
    return lax.dynamic_slice_in_dim(array, index * width, width, axis=0)


def local(
    hidden_in,
    weight_query,
    key_weight_matrix,
    weight_value,
    weight_out,
    weight_gate,
    weight_up,
    weight_down,
    gain_attention,
    gain_feed,
    gain_query,
    gain_key,
    positions,
    token_block_index,
    grad_out,
):
    parts = lax.axis_size("ctx")
    shards = lax.axis_size("fsdp")
    me = lax.axis_index("ctx")
    shard = lax.axis_index("fsdp")
    heads = QUERY_HEADS // parts
    sharers = parts // KEY_VALUE_HEADS
    key_head = me // sharers
    width = heads * HEAD_SIZE
    feed_width = FF // parts
    rows = D // shards
    head_rows = HEAD_SIZE // shards
    count = hidden_in.shape[1]
    tokens = parts * count

    def gather_rows(piece):
        return lax.all_gather(piece, "fsdp", axis=0, tiled=True)

    def sum_rows(grad):
        return lax.psum_scatter(grad.astype(BF16), "fsdp", scatter_dimension=0, tiled=True)

    def gather_parts(piece):
        return lax.all_gather(piece, "ctx", axis=0)

    own_heads_weight = jnp.concatenate(
        [
            own_columns(weight_query, me, width),
            own_columns(key_weight_matrix, key_head, HEAD_SIZE),
            own_columns(weight_value, key_head, HEAD_SIZE),
            own_rows(weight_out, me, width).T,
        ],
        axis=1,
    )
    feed_weight = gather_rows(
        jnp.concatenate(
            [
                own_columns(weight_gate, me, feed_width),
                own_columns(weight_up, me, feed_width),
                own_rows(weight_down, me, feed_width).T,
            ],
            axis=1,
        )
    )

    own_gains = jnp.concatenate([gain_attention, gain_feed, gain_query, gain_key]).astype(F32)
    own_gains = jnp.pad(own_gains, (0, 2048 - own_gains.shape[0])).reshape(16, 128)
    own_tokens = jnp.pad(jnp.stack([positions[0], token_block_index[0]]), ((0, 6), (0, 0)))
    hidden, grad = hidden_in[0], grad_out[0]
    normed_all, proj, heads_weight, gain_rows, gains, whole = first(
        hidden, own_gains, own_tokens, own_heads_weight, shards, parts, width + 2 * HEAD_SIZE
    )
    flat_gains = gains.reshape(shards, -1)
    norm_query = flat_gains[:, 2 * rows : 2 * rows + head_rows].reshape(1, -1)
    norm_key = flat_gains[:, 2 * rows + head_rows : 2 * rows + 2 * head_rows].reshape(1, -1)
    head_gains = jnp.concatenate([norm_query, norm_key, jnp.zeros((6, HEAD_SIZE), F32)])

    half = HEAD_SIZE // 2
    freq = THETA ** (-(jnp.arange(half).astype(F32) * 2.0 / HEAD_SIZE))
    angle = whole[:, 0].reshape(-1).astype(F32)[:, None] * freq
    cosine, sine = jnp.cos(angle), jnp.sin(angle)
    cosine = jnp.concatenate([cosine, cosine], axis=1)
    sine = jnp.concatenate([-sine, sine], axis=1)
    ids = whole[:, 1].reshape(-1)
    id_row, id_column = ids[None, :], ids[:, None]

    proj = proj.reshape(tokens, width + 2 * HEAD_SIZE)
    queries, keys, values, context, inverse, middle, normed_two, grad_all = attend(
        proj, cosine, sine, head_gains, id_column, id_row, heads_weight, hidden, grad, gain_rows, heads
    )
    normed_two_all, activation, back = feed(normed_two, grad_all, feed_weight)

    flat_grad = grad_all.reshape(tokens, D)
    flat_back = back.reshape(tokens, 2 * feed_width)
    flat_activation = activation.reshape(tokens, feed_width)
    feed_grad = by_row(tdot(normed_two_all.reshape(tokens, D), flat_back).astype(BF16))
    down_grad = by_row(tdot(flat_grad, flat_activation).astype(BF16))
    back, feed_grad, down_grad = lax.optimization_barrier((back, feed_grad, down_grad))

    grad_middle, low, gain_two, down_parts = feed_back(
        back, feed_weight, middle, grad, gain_rows, down_grad.reshape(shards, rows, feed_width)
    )
    low, feed_grad = lax.optimization_barrier((low, feed_grad))
    feed_shard = sum_rows(feed_grad)
    low_all, context_grad, hidden_out = turn(low, heads_weight, activation, feed_weight, middle, width)

    context_grad, feed_shard, down_parts = lax.optimization_barrier(
        (context_grad, feed_shard, down_parts)
    )
    feed_parts = gather_parts(feed_shard)
    context_grad = context_grad.reshape(tokens, width)
    grad_qkv, gain_heads = attention_back(
        heads,
        queries,
        keys,
        values,
        context_grad,
        inverse,
        context,
        proj,
        cosine,
        sine,
        head_gains,
        id_column,
        id_row,
    )
    head_grad = jnp.concatenate(
        [
            by_row(tdot(normed_all.reshape(tokens, D), grad_qkv).astype(BF16)),
            by_row(tdot(low_all.reshape(tokens, D), context).astype(BF16)),
        ],
        axis=1,
    )
    grad_down = spread_turned(down_parts)
    grad_qkv, grad_down = lax.optimization_barrier((grad_qkv, grad_down))
    grad_hidden, gain_sums, head_parts = last(
        grad_qkv.reshape(parts, count, -1),
        heads_weight,
        hidden,
        grad_middle,
        gain_rows,
        gain_two,
        gain_heads,
        head_grad.reshape(shards, rows, -1),
    )

    gain_sums = gain_sums.reshape(-1)
    grad_gate, grad_up = spread_pair(feed_parts)
    grad_query, grad_key, grad_value, grad_out_weight = spread_heads(head_parts, width)
    if sharers > 1:
        grad_key, grad_value = (
            part.reshape(rows, KEY_VALUE_HEADS, sharers, HEAD_SIZE).sum(axis=2).reshape(rows, -1)
            for part in (grad_key, grad_value)
        )
    return (
        hidden_out[None],
        grad_hidden[None],
        grad_query,
        grad_key,
        grad_value,
        grad_out_weight,
        grad_gate,
        grad_up,
        grad_down,
        gain_sums[:rows],
        gain_sums[rows : 2 * rows],
        lax.dynamic_slice_in_dim(gain_sums, 2 * rows + shard * head_rows, head_rows),
        lax.dynamic_slice_in_dim(gain_sums, 2 * rows + HEAD_SIZE + shard * head_rows, head_rows),
    )


def solution(mesh):
    tokens = P("fsdp", "ctx", None)
    by_rows = P("fsdp", None)
    by_columns = P(None, "fsdp")
    per_token = P("fsdp", "ctx")
    vector = P("fsdp")
    weights = (by_rows, by_rows, by_rows, by_columns, by_rows, by_rows, by_columns)
    return jax.shard_map(
        local,
        mesh=mesh,
        in_specs=(tokens, *weights, vector, vector, vector, vector, per_token, per_token, tokens),
        out_specs=(tokens, tokens, *weights, vector, vector, vector, vector),
        check_vma=False,
    )
```

```python
import functools

import jax
import jax.numpy as jnp
from jax import lax
from jax.experimental import pallas as pl
from jax.experimental.layout import Layout, with_layout_constraint
from jax.experimental.pallas import tpu as pltpu
from jax.sharding import PartitionSpec as P

D = 2048
QUERY_HEADS = 16
KEY_VALUE_HEADS = 8
HEAD_SIZE = 128
FF = 6144
EPS = 1e-06
THETA = 1000000.0
F32 = jnp.float32
BF16 = jnp.bfloat16
MESH = pl.DeviceIdType.MESH
VMEM = pltpu.VMEM
WHOLE = pl.BlockSpec(memory_space=pltpu.VMEM)
HBM = pl.BlockSpec(memory_space=pl.ANY)
CHUNKS = 4
WIDE = D // CHUNKS


def dot(left, right):
    return jnp.dot(left, right, preferred_element_type=F32)


def tdot(left, right):
    return lax.dot_general(left, right, (((0,), (0,)), ((), ())), preferred_element_type=F32)


def rdot(left, right):
    return lax.dot_general(left, right, (((1,), (1,)), ((), ())), preferred_element_type=F32)


def loop(count, body):
    def step(index, carry):
        body(index)
        return carry

    lax.fori_loop(0, count, step, 0)


def line_position():
    me = lax.axis_index("ctx")
    return me, me // 2, me % 2, lax.axis_size("ctx") // 2


def send(source, target, send_sem, recv_sem, axis, index):
    return pltpu.make_async_remote_copy(
        src_ref=source,
        dst_ref=target,
        send_sem=send_sem,
        recv_sem=recv_sem,
        device_id={axis: index},
        device_id_type=MESH,
    )


def line_barrier():
    me, chip, core, chips = line_position()
    barrier = pltpu.get_barrier_semaphore()

    def greet(index):
        pl.semaphore_signal(barrier, inc=1, device_id={"ctx": index}, device_id_type=MESH)

    greet(me + 1 - 2 * core)

    @pl.when(chip > 0)
    def _():
        greet(me - 2)

    @pl.when(chip < chips - 1)
    def _():
        greet(me + 2)

    peers = 1 + (chip > 0).astype(jnp.int32) + (chip < chips - 1).astype(jnp.int32)
    pl.semaphore_wait(barrier, peers)


def peers_of(axis):
    me, size = lax.axis_index(axis), lax.axis_size(axis)
    return size - 1, lambda i: (me + i + 1) % size, lambda i: (me + size - i - 1) % size


def full_barrier():
    barrier = pltpu.get_barrier_semaphore()
    total = 0
    for axis in ("fsdp", "ctx"):
        count, ahead, _ = peers_of(axis)
        loop(
            count,
            lambda i, axis=axis, ahead=ahead: pl.semaphore_signal(
                barrier, inc=1, device_id={axis: ahead(i)}, device_id_type=MESH
            ),
        )
        total += count
    pl.semaphore_wait(barrier, total)


def gather_scratch(chips):
    return [pltpu.SemaphoreType.DMA((chips,)) for _ in range(6)]


class Gather:
    def __init__(self, land, sems, consume=None, late=False):
        self.late = late
        self.land = land
        self.sems = sems
        self.consume = consume
        self.me, self.chip, self.core, self.chips = line_position()

    def right(self, step, source):
        ref = self.land.at[2 * source + self.core]
        return send(ref, ref, self.sems[0].at[step], self.sems[1].at[step], "ctx", self.me + 2)

    def left(self, step, source):
        ref = self.land.at[2 * source + self.core]
        return send(ref, ref, self.sems[2].at[step], self.sems[3].at[step], "ctx", self.me - 2)

    def across(self, source, core):
        ref = self.land.at[2 * source + core]
        other = self.me + 1 - 2 * self.core
        return send(ref, ref, self.sems[4].at[source], self.sems[5].at[source], "ctx", other)

    def step(self, step):
        chip, core, chips = self.chip, self.core, self.chips
        low, high = chip - step, chip + step
        has_low = low >= 0
        has_high = jnp.logical_and(high < chips, step > 0)

        @pl.when(jnp.logical_and(has_low, step > 0))
        def _():
            self.right(step - 1, low).wait_recv()

        @pl.when(jnp.logical_and(has_low, chip < chips - 1))
        def _():
            self.right(step, low).start()

        @pl.when(has_high)
        def _():
            self.left(step - 1, high).wait_recv()

        @pl.when(jnp.logical_and(high < chips, chip > 0))
        def _():
            self.left(step, high).start()

        @pl.when(has_low)
        def _():
            self.across(low, core).start()

        @pl.when(has_high)
        def _():
            self.across(high, core).start()

        if not self.late:
            self.use(step)
            return

        @pl.when(step > 0)
        def _():
            self.use(step - 1)

        @pl.when(step == chips - 1)
        def _():
            self.use(step)

    def use(self, step):
        chip, core, chips = self.chip, self.core, self.chips
        low, high = chip - step, chip + step

        def one(kind):
            upward = kind % 2
            crossed = kind // 2
            source = jnp.where(upward == 1, high, low)
            valid = jnp.where(upward == 1, jnp.logical_and(high < chips, step > 0), low >= 0)
            parity = jnp.where(crossed == 1, 1 - core, core)

            @pl.when(valid)
            def _():
                @pl.when(crossed == 1)
                def _():
                    self.across(source, parity).wait_recv()

                if self.consume is not None:
                    self.consume(2 * source + parity)

        loop(4, one)

    def finish(self):
        chip, core, chips = self.chip, self.core, self.chips

        def one(step):
            @pl.when(jnp.logical_and(chip - step >= 0, chip < chips - 1))
            def _():
                self.right(step, chip - step).wait_send()

            @pl.when(jnp.logical_and(chip + step < chips, chip > 0))
            def _():
                self.left(step, chip + step).wait_send()

            self.across(step, core).wait_send()

        loop(chips, one)


def scatter_scratch(chips, rows):
    buffers = [VMEM((count, CHUNKS, rows, WIDE), BF16) for count in (chips + 1, 2, chips)]
    return buffers + [pltpu.SemaphoreType.DMA((chips, CHUNKS)) for _ in range(6)]


class Scatter:
    def __init__(self, scratch, produce, total):
        self.line, self.out, self.other = scratch[:3]
        self.sems = scratch[3:]
        self.produce = produce
        self.total = total
        self.me, self.chip, self.core, self.chips = line_position()


    def right(self, step, chunk):
        ref = self.line.at[step, chunk]
        sems = self.sems
        return send(ref, ref, sems[0].at[step, chunk], sems[1].at[step, chunk], "ctx", self.me + 2)

    def left(self, step, chunk):
        ref = self.line.at[self.chips - step, chunk]
        sems = self.sems
        return send(ref, ref, sems[2].at[step, chunk], sems[3].at[step, chunk], "ctx", self.me - 2)

    def across(self, target, chunk, slot=0):
        sems = self.sems
        return send(
            self.out.at[slot, chunk],
            self.other.at[target, chunk],
            sems[4].at[target, chunk],
            sems[5].at[target, chunk],
            "ctx",
            self.me + 1 - 2 * self.core,
        )

    def begin(self):
        def clear(index):
            slot, chunk = index // CHUNKS, index % CHUNKS
            at_left = jnp.logical_and(self.chip == 0, slot < self.chips)
            at_right = jnp.logical_and(self.chip == self.chips - 1, slot > 0)

            @pl.when(jnp.logical_or(at_left, at_right))
            def _():
                self.line[slot, chunk] = jnp.zeros(self.line.shape[2:], BF16)

        loop((self.chips + 1) * CHUNKS, clear)

    def when_right(self, time):
        return jnp.logical_and(time >= self.chip, time < self.chips - 1)

    def when_left(self, time):
        return jnp.logical_and(time >= self.chips - 1 - self.chip, time < self.chips - 1)

    def prepare(self, time):
        chip, chips = self.chip, self.chips

        def cross(target, slot, before, used):
            def one(chunk):
                @pl.when(used)
                def _():
                    self.across(before, chunk, slot).wait_send()

                piece = 2 * target + 1 - self.core
                self.out[slot, chunk] = self.produce(piece, chunk).astype(BF16)
                self.across(target, chunk, slot).start()

            loop(CHUNKS, one)

        @pl.when(self.when_right(time))
        def _():
            target = chips - 1 - time + chip
            cross(target, 0, target + 1, time > chip)

        @pl.when(self.when_left(time))
        def _():
            target = time - (chips - 1 - chip)
            cross(target, 1, target - 1, target > 0)

        @pl.when(time == chips - 1)
        def _():
            cross(chip, 0, chip + 1, chip < chips - 1)

    def step(self, time):
        chip, core, chips = self.chip, self.core, self.chips

        @pl.when(self.when_right(time))
        def _():
            step = time - chip
            target = chips - 1 - step

            def one(chunk):
                self.across(target, chunk).wait_recv()

                @pl.when(chip > 0)
                def _():
                    self.right(step, chunk).wait_recv()

                value = self.produce(2 * target + core, chunk) + self.other[target, chunk].astype(F32)
                value = value + self.line[step, chunk].astype(F32)
                self.line[step, chunk] = value.astype(BF16)
                self.right(step, chunk).start()

            loop(CHUNKS, one)

        @pl.when(self.when_left(time))
        def _():
            step = time - (chips - 1 - chip)

            def one(chunk):
                self.across(step, chunk).wait_recv()

                @pl.when(chip < chips - 1)
                def _():
                    self.left(step, chunk).wait_recv()

                value = self.produce(2 * step + core, chunk) + self.other[step, chunk].astype(F32)
                value = value + self.line[chips - step, chunk].astype(F32)
                self.line[chips - step, chunk] = value.astype(BF16)
                self.left(step, chunk).start()

            loop(CHUNKS, one)

    def finish(self):
        chip, core, chips = self.chip, self.core, self.chips
        last = chips - 1 - chip

        def one(chunk):
            self.across(chip, chunk).wait_recv()
            value = self.produce(2 * chip + core, chunk) + self.other[chip, chunk].astype(F32)

            @pl.when(chip > 0)
            def _():
                self.right(last, chunk).wait_recv()

            @pl.when(chip < chips - 1)
            def _():
                self.left(chip, chunk).wait_recv()

            value = value + self.line[last, chunk].astype(F32)
            value = value + self.line[chips - chip, chunk].astype(F32)
            self.total[:, pl.ds(pl.multiple_of(chunk * WIDE, WIDE), WIDE)] = value

        loop(CHUNKS, one)

        def drain(index):
            step, chunk = index // CHUNKS, index % CHUNKS

            @pl.when(step < last)
            def _():
                self.right(step, chunk).wait_send()

            @pl.when(step < chip)
            def _():
                self.left(step, chunk).wait_send()

            @pl.when(jnp.logical_or(step == chip, step == chip - 1))
            def _():
                self.across(step, chunk, jnp.where(step == chip, 0, 1)).wait_send()

        loop(chips * CHUNKS, drain)


def row_blocks(rows, body, size=32):
    def one(index):
        body(pl.ds(pl.multiple_of(index * size, size), size))

    loop(rows // size, one)


def inverse_norm(value):
    return lax.rsqrt(jnp.mean(value * value, axis=-1, keepdims=True) + EPS)


def params(identity, megabytes):
    return pltpu.CompilerParams(
        collective_id=identity,
        has_side_effects=True,
        vmem_limit_bytes=megabytes * 1024 * 1024,
    )


def cost(microseconds):
    return pl.CostEstimate(
        flops=int(microseconds * 1.15e9), bytes_accessed=1024, transcendentals=0
    )


class FsdpSum:
    def __init__(self, grad, arrived, send_sems, recv_sems, own=None):
        self.grad, self.arrived = grad, arrived
        self.own = grad.at[lax.axis_index("fsdp")] if own is None else own
        self.sems = send_sems, recv_sems
        self.peers, self.ahead, _ = peers_of("fsdp")

    def copy(self, i):
        target = self.ahead(i)
        return send(
            self.grad.at[target], self.arrived.at[i], self.sems[0].at[i], self.sems[1].at[i], "fsdp", target
        )

    def start(self):
        loop(self.peers, lambda i: self.copy(i).start())

    def arrive(self):
        loop(self.peers, lambda i: self.copy(i).wait_recv())

    def collect(self, target):
        self.arrive()

        def add(block):
            value = self.own[block, :].astype(F32)
            for i in range(self.peers):
                value = value + self.arrived[i, block].astype(F32)
            target[block, :] = value.astype(BF16)

        row_blocks(self.own.shape[0], add)

    def finish(self):
        loop(self.peers, lambda i: self.copy(i).wait_send())


def fsdp_scratch(shards, rows, width):
    return [VMEM((shards - 1, rows, width), BF16)] + [pltpu.SemaphoreType.DMA((shards,))] * 2


def copy_in(source, target, sem):
    copy = pltpu.make_async_copy(source, target, sem)
    copy.start()
    return copy


def first_kernel(rows, width, *refs):
    x, gains, tokens, part, land, proj, weights, gain_rows, all_gains, all_tokens = refs[:10]
    sems, small = refs[10:16], refs[16:]
    me, _, _, chips = line_position()
    shard = lax.axis_index("fsdp")
    shards, ahead, behind = peers_of("fsdp")
    parts, next_part, past_part = peers_of("ctx")
    full_barrier()

    def gain_copy(i, slot):
        return send(gains, all_gains.at[slot], small[0].at[i], small[1].at[i], "fsdp", ahead(i))

    def token_copy(i, slot):
        return send(tokens, all_tokens.at[slot], small[2].at[i], small[3].at[i], "ctx", next_part(i))

    def weight_copy(i, owner):
        target = weights.at[pl.ds(pl.multiple_of(owner * rows, rows), rows), :]
        return send(part, target, small[4].at[i], small[5].at[i], "fsdp", ahead(i))

    loop(shards, lambda i: gain_copy(i, shard).start())
    loop(parts, lambda i: token_copy(i, me).start())
    loop(shards, lambda i: weight_copy(i, shard).start())
    all_gains[shard] = gains[...]
    all_tokens[me] = tokens[...]
    weights[pl.ds(pl.multiple_of(shard * rows, rows), rows), :] = part[...]
    loop(shards, lambda i: gain_copy(i, behind(i)).wait_recv())
    lanes = rows // 128
    for kind in range(2):
        for owner in range(shards + 1):
            for j in range(lanes):
                at = owner * rows + j * 128
                gain_rows[kind : kind + 1, at : at + 128] = all_gains[
                    owner, kind * lanes + j : kind * lanes + j + 1, :
                ]

    def norm(block):
        value = x[block, :].astype(F32)
        land[me, block] = (value * inverse_norm(value) * gain_rows[0:1, :]).astype(BF16)

    row_blocks(x.shape[0], norm)

    gather = Gather(land, sems)
    loop(chips, gather.step)
    loop(shards, lambda i: weight_copy(i, behind(i)).wait_recv())

    def project(piece):
        proj[piece] = dot(land[piece], weights[:, :width])

    loop(2 * chips, project)
    gather.finish()
    loop(shards, lambda i: gain_copy(i, shard).wait_send())
    loop(shards, lambda i: weight_copy(i, shard).wait_send())
    loop(parts, lambda i: token_copy(i, past_part(i)).wait_recv())
    loop(parts, lambda i: token_copy(i, me).wait_send())


def first(hidden, gains, tokens, part, shards, parts, width):
    count = hidden.shape[0]
    return pl.pallas_call(
        functools.partial(first_kernel, D // shards, width),
        out_shape=(
            jax.ShapeDtypeStruct((parts, count, D), BF16),
            jax.ShapeDtypeStruct((parts, count, width), F32),
            jax.ShapeDtypeStruct((D, part.shape[1]), BF16),
            jax.ShapeDtypeStruct((8, D), F32),
            jax.ShapeDtypeStruct((shards, *gains.shape), F32),
            jax.ShapeDtypeStruct((parts, *tokens.shape), jnp.int32),
        ),
        in_specs=[WHOLE] * 4,
        out_specs=(WHOLE,) * 6,
        scratch_shapes=gather_scratch(parts // 2)
        + [pltpu.SemaphoreType.DMA((shards,))] * 2
        + [pltpu.SemaphoreType.DMA((parts,))] * 2
        + [pltpu.SemaphoreType.DMA((shards,))] * 2,
        compiler_params=params(0, 60),
        cost_estimate=cost(85),
        name="gather_normed",
    )(hidden, gains, tokens, part)


def feed_kernel(width, *refs):
    x, grads, weights, land, activation, back = refs[:6]
    weight, weight_sem, grad, grad_sems = refs[6:10]
    sems = refs[10:]
    me, _, _, chips = line_position()
    copy = copy_in(weights, weight, weight_sem)

    def grad_copy(piece):
        return pltpu.make_async_copy(grads.at[piece], grad.at[piece], grad_sems.at[piece])

    loop(2 * chips, lambda piece: grad_copy(piece).start())
    land[me] = x[...]
    size = 256 if width % 256 == 0 else 128

    def consume(piece):
        grad_copy(piece).wait()

        def one(index):
            def columns(kind):
                return pl.ds(pl.multiple_of(kind * width + index * size, 128), size)

            gate = dot(land[piece], weight[:, columns(0)])
            up = dot(land[piece], weight[:, columns(1)])
            grad_act = dot(grad[piece], weight[:, columns(2)])
            sigma = 1.0 / (1.0 + jnp.exp(-gate))
            activation[piece, :, columns(0)] = (gate * sigma * up).astype(BF16)
            back[piece, :, columns(0)] = (
                grad_act * up * sigma * (1.0 + gate * (1.0 - sigma))
            ).astype(BF16)
            back[piece, :, columns(1)] = (grad_act * gate * sigma).astype(BF16)

        loop(width // size, one)

    line_barrier()
    gather = Gather(land, sems, consume)
    copy.wait()
    loop(chips, gather.step)
    gather.finish()


def feed(normed, grads, weights):
    parts, count, _ = grads.shape
    width = weights.shape[1] // 3
    return pl.pallas_call(
        functools.partial(feed_kernel, width),
        out_shape=(
            jax.ShapeDtypeStruct((parts, count, D), BF16),
            jax.ShapeDtypeStruct((parts, count, width), BF16),
            jax.ShapeDtypeStruct((parts, count, 2 * width), BF16),
        ),
        in_specs=[WHOLE, HBM, HBM],
        out_specs=(WHOLE,) * 3,
        scratch_shapes=[
            VMEM(weights.shape, BF16),
            pltpu.SemaphoreType.DMA,
            VMEM(grads.shape, BF16),
            pltpu.SemaphoreType.DMA((parts,)),
        ]
        + gather_scratch(parts // 2),
        compiler_params=params(2, 60),
        cost_estimate=cost(90),
        name="feed",
    )(normed, grads, weights)


def rms_back(value, gain, grad):
    inverse = inverse_norm(value)
    scaled = grad * gain
    inner = jnp.mean(scaled * value, axis=-1, keepdims=True)
    terms = grad * value * inverse
    return inverse * scaled - value * (inverse * inverse * inverse * inner), terms


def turn_kernel(columns, *refs):
    back, feed_weights, activation, weights, middle, grad, gain_rows, down_grad, pair_grad = refs[:9]
    grad_middle, land, gain_sum, down_land, context_grad, hidden, pair_in = refs[9:16]
    weight, data, head_weight, total, low, piece_in, own_down, down_sum, sems = refs[16:25]
    down_refs, down_sems, gather_sems = refs[25:28], refs[28:34], refs[34:40]
    pair_sems, first_scratch, second_scratch = refs[40:42], refs[42:51], refs[51:]
    me, _, _, chips = line_position()
    width = back.shape[2] // 2
    weight_copy = copy_in(feed_weights.at[:, pl.ds(0, 2 * width)], weight, sems.at[0])
    data_copy = copy_in(back, data, sems.at[1])
    head_copy = copy_in(weights.at[:, columns], head_weight, sems.at[2])
    own_copy = copy_in(down_grad.at[lax.axis_index("fsdp")], own_down, sems.at[3])

    def produce(piece, chunk):
        return rdot(data[piece], weight[pl.ds(pl.multiple_of(chunk * WIDE, WIDE), WIDE), :])

    def produce_hidden(piece, chunk):
        block = pl.ds(pl.multiple_of(chunk * WIDE, WIDE), WIDE)
        return rdot(data[piece, :, :width], weight[block, :width])

    def consume(piece):
        copy = copy_in(land.at[piece], piece_in, sems.at[4])
        copy.wait()
        context_grad[piece] = dot(piece_in[...], head_weight[...]).astype(BF16)

    down = FsdpSum(down_grad, *down_refs, own=own_down)
    pair = FsdpSum(pair_grad, pair_in, *pair_sems, own=own_down)
    down_gather = Gather(down_land, down_sems)
    gather = Gather(land, gather_sems, consume)
    scatter = Scatter(first_scratch, produce, total)
    hidden_scatter = Scatter(second_scratch, produce_hidden, total)
    scatter.begin()
    hidden_scatter.begin()
    full_barrier()
    down.start()
    weight_copy.wait()
    data_copy.wait()
    scatter.prepare(0)

    def step(time):
        scatter.step(time)
        scatter.prepare(time + 1)

        @pl.when(time == 1)
        def _():
            own_copy.wait()
            down.collect(down_sum)
            pair.start()
            copy = copy_in(down_sum, down_land.at[me], sems.at[3])
            copy.wait()

        @pl.when(time >= 1)
        def _():
            down_gather.step(time - 1)

    loop(chips - 1, step)
    scatter.finish()
    down_copy = copy_in(
        feed_weights.at[:, pl.ds(2 * width, width)], weight.at[:, pl.ds(0, width)], sems.at[0]
    )
    act_copy = copy_in(activation, data.at[:, :, pl.ds(0, width)], sems.at[1])
    gain_sum[...] = jnp.zeros_like(gain_sum)

    def norm(block):
        through, terms = rms_back(middle[block, :], gain_rows[1:2, :], total[block, :])
        value = grad[block, :].astype(F32) + through
        grad_middle[block, :] = value
        low[block, :] = value.astype(BF16)
        gain_sum[0:1, :] += jnp.sum(terms, axis=0, keepdims=True)

    row_blocks(middle.shape[0], norm)
    low_copy = copy_in(low, land.at[me], sems.at[3])
    low_copy.wait()
    head_copy.wait()
    gather.step(0)
    down_copy.wait()
    act_copy.wait()
    hidden_scatter.prepare(0)

    def turn_step(time):
        hidden_scatter.step(time)
        hidden_scatter.prepare(time + 1)
        gather.step(time + 1)

        @pl.when(time < 2)
        def _():
            down_gather.step(chips - 2 + time)

    loop(chips - 1, turn_step)
    hidden_scatter.finish()
    gather.finish()
    down_gather.finish()
    down.finish()
    pair.arrive()
    pair.finish()

    def add(block):
        hidden[block, :] = (middle[block, :] + total[block, :]).astype(BF16)

    row_blocks(middle.shape[0], add)


def turn(back, feed_weights, activation, weights, middle, grad, gain_rows, down_grad, pair_grad, width):
    parts, count, feed_width = activation.shape
    shards, rows, _ = down_grad.shape
    return pl.pallas_call(
        functools.partial(turn_kernel, pl.ds(weights.shape[1] - width, width)),
        out_shape=(
            jax.ShapeDtypeStruct((count, D), F32),
            jax.ShapeDtypeStruct((parts, count, D), BF16),
            jax.ShapeDtypeStruct((8, D), F32),
            jax.ShapeDtypeStruct((parts, rows, feed_width), BF16),
            jax.ShapeDtypeStruct((parts, count, width), BF16),
            jax.ShapeDtypeStruct((count, D), BF16),
            jax.ShapeDtypeStruct((shards - 1, rows, 2 * feed_width), BF16),
        ),
        in_specs=[HBM, HBM, HBM, HBM, WHOLE, WHOLE, WHOLE, HBM, HBM],
        out_specs=(WHOLE, HBM, WHOLE, HBM, WHOLE, WHOLE, HBM),
        scratch_shapes=[
            VMEM((D, 2 * feed_width), BF16),
            VMEM((parts, count, 2 * feed_width), BF16),
            VMEM((D, width), BF16),
            VMEM((count, D), F32),
            VMEM((count, D), BF16),
            VMEM((count, D), BF16),
            VMEM((rows, feed_width), BF16),
            VMEM((rows, feed_width), BF16),
            pltpu.SemaphoreType.DMA((5,)),
        ]
        + fsdp_scratch(shards, rows, feed_width)
        + gather_scratch(parts // 2)
        + gather_scratch(parts // 2)
        + [pltpu.SemaphoreType.DMA((shards,))] * 2
        + scatter_scratch(parts // 2, count)
        + scatter_scratch(parts // 2, count),
        compiler_params=params(3, 63),
        cost_estimate=cost(185),
        name="turn",
    )(back, feed_weights, activation, weights, middle, grad, gain_rows, down_grad, pair_grad)


def last_kernel(columns, *refs):
    back, weights, x, grad_middle, gain_rows, gain_two, gain_heads, head_grad = refs[:8]
    hidden, gain_out, land = refs[8:11]
    weight, weight_sem, total, gain_one, pack, pack_in, shard_sum, shard_in = refs[11:19]
    small, head_refs, gather_sems, scratch = refs[19:23], refs[23:26], refs[26:32], refs[32:]
    me, _, _, chips = line_position()
    shard = lax.axis_index("fsdp")
    shards, ahead, _ = peers_of("fsdp")
    parts, next_part, _ = peers_of("ctx")
    copy = copy_in(weights.at[:, columns], weight, weight_sem)

    def produce(piece, chunk):
        return rdot(back[piece], weight[pl.ds(pl.multiple_of(chunk * WIDE, WIDE), WIDE), :])

    heads = FsdpSum(head_grad, *head_refs)
    scatter = Scatter(scratch, produce, total)
    gather = Gather(land, gather_sems)
    scatter.begin()
    full_barrier()
    copy.wait()
    scatter.prepare(0)
    heads.start()

    def step(time):
        scatter.step(time)

        @pl.when(time == 1)
        def _():
            heads.collect(land.at[me])

        @pl.when(time >= 1)
        def _():
            gather.step(time - 1)

        scatter.prepare(time + 1)

    loop(chips - 1, step)
    scatter.finish()
    gather.step(chips - 2)
    gain_one[...] = jnp.zeros_like(gain_one)

    def norm(block):
        through, terms = rms_back(x[block, :].astype(F32), gain_rows[0:1, :], total[block, :])
        hidden[block, :] = grad_middle[block, :] + through
        gain_one[0:1, :] += jnp.sum(terms, axis=0, keepdims=True)

    row_blocks(x.shape[0], norm)

    rows = D // (shards + 1)
    lanes = rows // 128
    pack[...] = jnp.zeros_like(pack)
    for owner in range(shards + 1):
        for j in range(lanes):
            at = owner * rows + j * 128
            pack[owner, j : j + 1, :] = gain_one[0:1, at : at + 128]
            pack[owner, lanes + j : lanes + j + 1, :] = gain_two[0:1, at : at + 128]
        pack[owner, 2 * lanes : 2 * lanes + 2, :] = gain_heads[0:2, :]

    def pack_copy(i):
        return send(pack.at[ahead(i)], pack_in.at[i], small[0].at[i], small[1].at[i], "fsdp", ahead(i))

    def sum_copy(i):
        return send(shard_sum, shard_in.at[i], small[2].at[i], small[3].at[i], "ctx", next_part(i))

    loop(shards, lambda i: pack_copy(i).start())
    shard_sum[...] = pack[shard]

    def add_pack(i):
        pack_copy(i).wait_recv()
        shard_sum[...] += pack_in[i]

    loop(shards, add_pack)
    loop(parts, lambda i: sum_copy(i).start())
    gain_out[...] = shard_sum[...]

    def add_sum(i):
        sum_copy(i).wait_recv()
        gain_out[...] += shard_in[i]

    loop(parts, add_sum)
    gather.step(chips - 1)
    gather.finish()
    heads.finish()
    loop(shards, lambda i: pack_copy(i).wait_send())
    loop(parts, lambda i: sum_copy(i).wait_send())


def last(back, weights, hidden, grad_middle, gain_rows, gain_two, gain_heads, head_grad):
    parts, count, width = back.shape
    shards, rows, head_width = head_grad.shape
    return pl.pallas_call(
        functools.partial(last_kernel, pl.ds(0, width)),
        out_shape=(
            jax.ShapeDtypeStruct((count, D), F32),
            jax.ShapeDtypeStruct((16, 128), F32),
            jax.ShapeDtypeStruct((parts, rows, head_width), BF16),
        ),
        in_specs=[WHOLE, HBM] + [WHOLE] * 6,
        out_specs=(WHOLE,) * 3,
        scratch_shapes=[
            VMEM((D, width), BF16),
            pltpu.SemaphoreType.DMA,
            VMEM((count, D), F32),
            VMEM((8, D), F32),
            VMEM((shards, 16, 128), F32),
            VMEM((shards, 16, 128), F32),
            VMEM((16, 128), F32),
            VMEM((parts, 16, 128), F32),
        ]
        + [pltpu.SemaphoreType.DMA((shards,))] * 2
        + [pltpu.SemaphoreType.DMA((parts,))] * 2
        + fsdp_scratch(shards, rows, head_width)
        + gather_scratch(parts // 2)
        + scatter_scratch(parts // 2, count),
        compiler_params=params(5, 60),
        cost_estimate=cost(90),
        name="last",
    )(back, weights, hidden, grad_middle, gain_rows, gain_two, gain_heads, head_grad)


QUERY_TILE = 256
KEY_TILE = 512


def reach(index, tokens):
    return jnp.minimum((index + 2) * QUERY_TILE + KEY_TILE - 1, tokens) // KEY_TILE


def head_norm(value, gain, cosine, sine):
    normed = value * inverse_norm(value) * gain
    return normed * cosine + pltpu.roll(normed, HEAD_SIZE // 2, 1) * sine


def attend_kernel(heads, columns, *refs):
    proj, cosine, sine, gain, id_column, id_row, weights, x, grad, gain_rows = refs[:10]
    queries, keys, values, context, inverse, middle, normed, land = refs[10:18]
    weight, weight_sem, grad_sem, total = refs[18:22]
    gather_sems, scratch = refs[22:28], refs[28:]
    me, _, _, chips = line_position()
    tokens = proj.shape[0]
    count = x.shape[0]
    key_at = heads * HEAD_SIZE
    copy = copy_in(weights.at[:, columns], weight, weight_sem)
    own = copy_in(grad, land.at[me], grad_sem)
    gather = Gather(land, gather_sems)
    line_barrier()
    own.wait()
    gather.step(0)

    def prepare(index):
        block = pl.ds(pl.multiple_of(index * QUERY_TILE, QUERY_TILE), QUERY_TILE)
        c, s = cosine[block, :], sine[block, :]
        for h in range(heads):
            lanes = slice(h * HEAD_SIZE, (h + 1) * HEAD_SIZE)
            rotated = head_norm(proj[block, lanes], gain[0:1, :], c, s) * HEAD_SIZE ** (-0.5)
            queries[block, lanes] = rotated.astype(BF16)
        rotated = head_norm(proj[block, key_at : key_at + HEAD_SIZE], gain[1:2, :], c, s)
        keys[block, :] = rotated.astype(BF16)
        values[block, :] = proj[block, key_at + HEAD_SIZE : key_at + 2 * HEAD_SIZE].astype(BF16)

    loop(tokens // QUERY_TILE, prepare)

    def attend(index):
        block = pl.ds(pl.multiple_of(index * QUERY_TILE, QUERY_TILE), QUERY_TILE)
        query_ids = id_column[block, :]
        for h in range(heads):
            lanes = slice(h * HEAD_SIZE, (h + 1) * HEAD_SIZE)
            query = queries[block, lanes]

            def one(tile, carry):
                sums, total = carry
                span = pl.ds(pl.multiple_of(tile * KEY_TILE, KEY_TILE), KEY_TILE)
                scores = rdot(query, keys[span, :])
                expon = jnp.where(id_row[0:1, span] <= query_ids, jnp.exp(scores), 0.0)
                sums = sums + dot(expon.astype(BF16), values[span, :])
                return sums, total + jnp.sum(expon, axis=1, keepdims=True)

            start = (jnp.zeros((QUERY_TILE, HEAD_SIZE), F32), jnp.zeros((QUERY_TILE, 1), F32))
            sums, total = lax.fori_loop(0, reach(index, tokens), one, start)
            scale = 1.0 / total
            context[block, lanes] = (sums * scale).astype(BF16)
            inverse[h : h + 1, block] = jnp.broadcast_to(scale, (QUERY_TILE, HEAD_SIZE)).T[0:1, :]

    loop(tokens // QUERY_TILE, attend)

    def produce(piece, chunk):
        block = pl.ds(pl.multiple_of(piece * count, count), count)
        return rdot(context[block, :], weight[pl.ds(pl.multiple_of(chunk * WIDE, WIDE), WIDE), :])

    scatter = Scatter(scratch, produce, total)
    scatter.begin()
    copy.wait()
    scatter.prepare(0)
    gather.step(1)

    def step(time):
        scatter.step(time)
        scatter.prepare(time + 1)

        @pl.when(time >= 1)
        def _():
            gather.step(time + 1)

    loop(chips - 1, step)
    scatter.finish()

    def norm(block):
        value = x[block, :].astype(F32) + total[block, :]
        middle[block, :] = value
        normed[block, :] = (value * inverse_norm(value) * gain_rows[1:2, :]).astype(BF16)

    row_blocks(count, norm)
    gather.finish()


def attend(proj, cosine, sine, gain, id_column, id_row, weights, hidden, grad, gain_rows, heads):
    tokens = proj.shape[0]
    width = heads * HEAD_SIZE
    count = hidden.shape[0]
    parts = tokens // count
    return pl.pallas_call(
        functools.partial(attend_kernel, heads, pl.ds(weights.shape[1] - width, width)),
        out_shape=(
            jax.ShapeDtypeStruct((tokens, width), BF16),
            jax.ShapeDtypeStruct((tokens, HEAD_SIZE), BF16),
            jax.ShapeDtypeStruct((tokens, HEAD_SIZE), BF16),
            jax.ShapeDtypeStruct((tokens, width), BF16),
            jax.ShapeDtypeStruct((8, tokens), F32),
            jax.ShapeDtypeStruct((count, D), F32),
            jax.ShapeDtypeStruct((count, D), BF16),
            jax.ShapeDtypeStruct((parts, count, D), BF16),
        ),
        in_specs=[WHOLE] * 6 + [HBM, WHOLE, WHOLE, WHOLE],
        out_specs=(WHOLE,) * 7 + (HBM,),
        scratch_shapes=[
            VMEM((D, width), BF16),
            pltpu.SemaphoreType.DMA,
            pltpu.SemaphoreType.DMA,
            VMEM((count, D), F32),
        ]
        + gather_scratch(parts // 2)
        + scatter_scratch(parts // 2, count),
        compiler_params=params(1, 60),
        cost_estimate=cost(110),
        name="attend",
    )(proj, cosine, sine, gain, id_column, id_row, weights, hidden, grad, gain_rows)


def attention_back_kernel(heads, *refs):
    queries, keys, values, out_grad, inverse, context, proj, cosine, sine, gain = refs[:10]
    id_column, id_row, back, gain_sum, key_grad, value_grad, query_grad = refs[10:]
    tokens = proj.shape[0]
    key_at = heads * HEAD_SIZE
    key_grad[...] = jnp.zeros_like(key_grad)
    value_grad[...] = jnp.zeros_like(value_grad)
    gain_sum[...] = jnp.zeros_like(gain_sum)

    def through(block, lanes, grad, row):
        turned = pltpu.roll(grad, HEAD_SIZE // 2, 1)
        unrotated = grad * cosine[block, :] - turned * sine[block, :]
        result, terms = rms_back(proj[block, lanes], gain[row : row + 1, :], unrotated)
        back[block, lanes] = result.astype(BF16)
        gain_sum[row : row + 1, :] += jnp.sum(terms, axis=0, keepdims=True)

    def attend(index):
        block = pl.ds(pl.multiple_of(index * QUERY_TILE, QUERY_TILE), QUERY_TILE)
        query_ids = id_row[0:1, block]
        for h in range(heads):
            lanes = slice(h * HEAD_SIZE, (h + 1) * HEAD_SIZE)
            query = queries[block, lanes]
            grad = out_grad[block, lanes]
            scale = inverse[h : h + 1, block]
            products = grad.astype(F32) * context[block, lanes].astype(F32)
            shift = lax.dot_general(
                jnp.ones((8, HEAD_SIZE), F32),
                products,
                (((1,), (1,)), ((), ())),
                precision=lax.Precision.HIGHEST,
                preferred_element_type=F32,
            )[0:1, :]
            query_grad[...] = jnp.zeros_like(query_grad)

            def one(tile):
                span = pl.ds(pl.multiple_of(tile * KEY_TILE, KEY_TILE), KEY_TILE)
                key = keys[span, :]
                scores = rdot(key, query)
                probs = jnp.where(id_column[span, :] <= query_ids, jnp.exp(scores) * scale, 0.0)
                grad_scores = (probs * (rdot(values[span, :], grad) - shift)).astype(BF16)
                value_grad[span, :] += dot(probs.astype(BF16), grad)
                key_grad[span, :] += dot(grad_scores, query)
                query_grad[...] += tdot(grad_scores, key)

            loop(reach(index, tokens), one)
            through(block, lanes, query_grad[...] * HEAD_SIZE ** (-0.5), 0)

    loop(tokens // QUERY_TILE, attend)

    def finish(index):
        block = pl.ds(pl.multiple_of(index * QUERY_TILE, QUERY_TILE), QUERY_TILE)
        through(block, slice(key_at, key_at + HEAD_SIZE), key_grad[block, :], 1)
        back[block, key_at + HEAD_SIZE : key_at + 2 * HEAD_SIZE] = value_grad[block, :].astype(BF16)

    loop(tokens // QUERY_TILE, finish)


def attention_back(heads, *operands):
    tokens = operands[0].shape[0]
    width = heads * HEAD_SIZE
    return pl.pallas_call(
        functools.partial(attention_back_kernel, heads),
        out_shape=(
            jax.ShapeDtypeStruct((tokens, width + 2 * HEAD_SIZE), BF16),
            jax.ShapeDtypeStruct((8, HEAD_SIZE), F32),
        ),
        in_specs=[WHOLE] * len(operands),
        out_specs=(WHOLE,) * 2,
        scratch_shapes=[
            VMEM((tokens, HEAD_SIZE), F32),
            VMEM((tokens, HEAD_SIZE), F32),
            VMEM((QUERY_TILE, HEAD_SIZE), F32),
        ],
        compiler_params=pltpu.CompilerParams(vmem_limit_bytes=48 * 1024 * 1024),
        cost_estimate=cost(38),
        name="attention_back",
    )(*operands)


def spread_pair_kernel(width, source, gate, up):
    gate[...] = source[0, :, :width].astype(F32)
    up[...] = source[0, :, width:].astype(F32)


def spread_pair(stacked):
    parts, rows, total = stacked.shape
    width = total // 2
    across = jax.ShapeDtypeStruct((rows, parts * width), F32)
    return pl.pallas_call(
        functools.partial(spread_pair_kernel, width),
        out_shape=(across, across),
        grid=(parts,),
        in_specs=[pl.BlockSpec((1, rows, total), lambda i: (i, 0, 0))],
        out_specs=(pl.BlockSpec((rows, width), lambda i: (0, i)),) * 2,
        compiler_params=pltpu.CompilerParams(vmem_limit_bytes=60 * 1024 * 1024),
        name="spread_pair",
    )(stacked)


def spread_turned_kernel(source, target):
    target[...] = source[0].astype(F32).T


def spread_turned(stacked):
    parts, rows, width = stacked.shape
    return pl.pallas_call(
        spread_turned_kernel,
        out_shape=jax.ShapeDtypeStruct((parts * width, rows), F32),
        grid=(parts,),
        in_specs=[pl.BlockSpec((1, rows, width), lambda i: (i, 0, 0))],
        out_specs=pl.BlockSpec((width, rows), lambda i: (i, 0)),
        compiler_params=pltpu.CompilerParams(vmem_limit_bytes=60 * 1024 * 1024),
        name="spread_turned",
    )(stacked)


def spread_heads_kernel(width, source, query, key, value, out):
    second = width + HEAD_SIZE
    third = second + HEAD_SIZE
    query[...] = source[0, :, :width].astype(F32)
    key[...] = source[0, :, width:second].astype(F32)
    value[...] = source[0, :, second:third].astype(F32)
    out[...] = source[0, :, third:].astype(F32).T


def spread_heads(stacked, width):
    parts, rows, total = stacked.shape
    widths = (width, HEAD_SIZE, HEAD_SIZE)
    return pl.pallas_call(
        functools.partial(spread_heads_kernel, width),
        out_shape=tuple(jax.ShapeDtypeStruct((rows, parts * w), F32) for w in widths)
        + (jax.ShapeDtypeStruct((parts * width, rows), F32),),
        grid=(parts,),
        in_specs=[pl.BlockSpec((1, rows, total), lambda i: (i, 0, 0))],
        out_specs=tuple(pl.BlockSpec((rows, w), lambda i: (0, i)) for w in widths)
        + (pl.BlockSpec((width, rows), lambda i: (i, 0)),),
        compiler_params=pltpu.CompilerParams(vmem_limit_bytes=60 * 1024 * 1024),
        name="spread_heads",
    )(stacked)


def by_row(array):
    return with_layout_constraint(array, Layout(major_to_minor=(0, 1)))


def own_columns(array, index, width):
    return lax.dynamic_slice_in_dim(array, index * width, width, axis=1)


def own_rows(array, index, width):
    return lax.dynamic_slice_in_dim(array, index * width, width, axis=0)


def local(
    hidden_in,
    weight_query,
    key_weight_matrix,
    weight_value,
    weight_out,
    weight_gate,
    weight_up,
    weight_down,
    gain_attention,
    gain_feed,
    gain_query,
    gain_key,
    positions,
    token_block_index,
    grad_out,
):
    parts = lax.axis_size("ctx")
    shards = lax.axis_size("fsdp")
    me = lax.axis_index("ctx")
    shard = lax.axis_index("fsdp")
    heads = QUERY_HEADS // parts
    sharers = parts // KEY_VALUE_HEADS
    key_head = me // sharers
    width = heads * HEAD_SIZE
    feed_width = FF // parts
    rows = D // shards
    head_rows = HEAD_SIZE // shards
    count = hidden_in.shape[1]
    tokens = parts * count

    def gather_rows(piece):
        return lax.all_gather(piece, "fsdp", axis=0, tiled=True)

    def gather_parts(piece):
        return lax.all_gather(piece, "ctx", axis=0)

    own_heads_weight = jnp.concatenate(
        [
            own_columns(weight_query, me, width),
            own_columns(key_weight_matrix, key_head, HEAD_SIZE),
            own_columns(weight_value, key_head, HEAD_SIZE),
            own_rows(weight_out, me, width).T,
        ],
        axis=1,
    )
    feed_weight = gather_rows(
        jnp.concatenate(
            [
                own_columns(weight_gate, me, feed_width),
                own_columns(weight_up, me, feed_width),
                own_rows(weight_down, me, feed_width).T,
            ],
            axis=1,
        )
    )

    own_gains = jnp.concatenate([gain_attention, gain_feed, gain_query, gain_key]).astype(F32)
    own_gains = jnp.pad(own_gains, (0, 2048 - own_gains.shape[0])).reshape(16, 128)
    own_tokens = jnp.pad(jnp.stack([positions[0], token_block_index[0]]), ((0, 6), (0, 0)))
    hidden, grad = hidden_in[0], grad_out[0]
    normed_all, proj, heads_weight, gain_rows, gains, whole = first(
        hidden, own_gains, own_tokens, own_heads_weight, shards, parts, width + 2 * HEAD_SIZE
    )
    flat_gains = gains.reshape(shards, -1)
    norm_query = flat_gains[:, 2 * rows : 2 * rows + head_rows].reshape(1, -1)
    norm_key = flat_gains[:, 2 * rows + head_rows : 2 * rows + 2 * head_rows].reshape(1, -1)
    head_gains = jnp.concatenate([norm_query, norm_key, jnp.zeros((6, HEAD_SIZE), F32)])

    half = HEAD_SIZE // 2
    freq = THETA ** (-(jnp.arange(half).astype(F32) * 2.0 / HEAD_SIZE))
    angle = whole[:, 0].reshape(-1).astype(F32)[:, None] * freq
    cosine, sine = jnp.cos(angle), jnp.sin(angle)
    cosine = jnp.concatenate([cosine, cosine], axis=1)
    sine = jnp.concatenate([-sine, sine], axis=1)
    ids = whole[:, 1].reshape(-1)
    id_row, id_column = ids[None, :], ids[:, None]

    proj = proj.reshape(tokens, width + 2 * HEAD_SIZE)
    queries, keys, values, context, inverse, middle, normed_two, grad_all = attend(
        proj, cosine, sine, head_gains, id_column, id_row, heads_weight, hidden, grad, gain_rows, heads
    )
    normed_two_all, activation, back = feed(normed_two, grad_all, feed_weight)

    flat_grad = grad_all.reshape(tokens, D)
    flat_back = back.reshape(tokens, 2 * feed_width)
    flat_activation = activation.reshape(tokens, feed_width)
    feed_grad = by_row(tdot(normed_two_all.reshape(tokens, D), flat_back).astype(BF16))
    down_grad = by_row(tdot(flat_grad, flat_activation).astype(BF16))
    back, feed_grad, down_grad = lax.optimization_barrier((back, feed_grad, down_grad))
    feed_grad = feed_grad.reshape(shards, rows, 2 * feed_width)
    grad_middle, low_all, gain_two, down_parts, context_grad, hidden_out, pair_in = turn(
        back,
        feed_weight,
        activation,
        heads_weight,
        middle,
        grad,
        gain_rows,
        down_grad.reshape(shards, rows, feed_width),
        feed_grad,
        width,
    )
    own_pair = lax.dynamic_index_in_dim(feed_grad, shard, keepdims=False)
    feed_shard = (own_pair.astype(F32) + jnp.sum(pair_in.astype(F32), axis=0)).astype(BF16)
    context_grad, feed_shard, down_parts = lax.optimization_barrier(
        (context_grad, feed_shard, down_parts)
    )
    feed_parts = gather_parts(feed_shard)
    context_grad = context_grad.reshape(tokens, width)
    grad_qkv, gain_heads = attention_back(
        heads,
        queries,
        keys,
        values,
        context_grad,
        inverse,
        context,
        proj,
        cosine,
        sine,
        head_gains,
        id_column,
        id_row,
    )
    head_grad = jnp.concatenate(
        [
            by_row(tdot(normed_all.reshape(tokens, D), grad_qkv).astype(BF16)),
            by_row(tdot(low_all.reshape(tokens, D), context).astype(BF16)),
        ],
        axis=1,
    )
    grad_down = spread_turned(down_parts)
    grad_qkv, grad_down = lax.optimization_barrier((grad_qkv, grad_down))
    grad_hidden, gain_sums, head_parts = last(
        grad_qkv.reshape(parts, count, -1),
        heads_weight,
        hidden,
        grad_middle,
        gain_rows,
        gain_two,
        gain_heads,
        head_grad.reshape(shards, rows, -1),
    )

    gain_sums = gain_sums.reshape(-1)
    grad_gate, grad_up = spread_pair(feed_parts)
    grad_query, grad_key, grad_value, grad_out_weight = spread_heads(head_parts, width)
    if sharers > 1:
        grad_key, grad_value = (
            part.reshape(rows, KEY_VALUE_HEADS, sharers, HEAD_SIZE).sum(axis=2).reshape(rows, -1)
            for part in (grad_key, grad_value)
        )
    return (
        hidden_out[None],
        grad_hidden[None],
        grad_query,
        grad_key,
        grad_value,
        grad_out_weight,
        grad_gate,
        grad_up,
        grad_down,
        gain_sums[:rows],
        gain_sums[rows : 2 * rows],
        lax.dynamic_slice_in_dim(gain_sums, 2 * rows + shard * head_rows, head_rows),
        lax.dynamic_slice_in_dim(gain_sums, 2 * rows + HEAD_SIZE + shard * head_rows, head_rows),
    )


def solution(mesh):
    tokens = P("fsdp", "ctx", None)
    by_rows = P("fsdp", None)
    by_columns = P(None, "fsdp")
    per_token = P("fsdp", "ctx")
    vector = P("fsdp")
    weights = (by_rows, by_rows, by_rows, by_columns, by_rows, by_rows, by_columns)
    return jax.shard_map(
        local,
        mesh=mesh,
        in_specs=(tokens, *weights, vector, vector, vector, vector, per_token, per_token, tokens),
        out_specs=(tokens, tokens, *weights, vector, vector, vector, vector),
        check_vma=False,
    )
```

```python
import functools

import jax
import jax.numpy as jnp
from jax import lax
from jax.experimental import pallas as pl
from jax.experimental.layout import Layout, with_layout_constraint
from jax.experimental.pallas import tpu as pltpu
from jax.sharding import PartitionSpec as P

D = 2048
QUERY_HEADS = 16
KEY_VALUE_HEADS = 8
HEAD_SIZE = 128
FF = 6144
EPS = 1e-06
THETA = 1000000.0
F32 = jnp.float32
BF16 = jnp.bfloat16
MESH = pl.DeviceIdType.MESH
VMEM = pltpu.VMEM
WHOLE = pl.BlockSpec(memory_space=pltpu.VMEM)
HBM = pl.BlockSpec(memory_space=pl.ANY)
CHUNKS = 4
WIDE = D // CHUNKS


def dot(left, right):
    return jnp.dot(left, right, preferred_element_type=F32)


def tdot(left, right):
    return lax.dot_general(left, right, (((0,), (0,)), ((), ())), preferred_element_type=F32)


def rdot(left, right):
    return lax.dot_general(left, right, (((1,), (1,)), ((), ())), preferred_element_type=F32)


def loop(count, body):
    def step(index, carry):
        body(index)
        return carry

    lax.fori_loop(0, count, step, 0)


def line_position():
    me = lax.axis_index("ctx")
    return me, me // 2, me % 2, lax.axis_size("ctx") // 2


def send(source, target, send_sem, recv_sem, axis, index):
    return pltpu.make_async_remote_copy(
        src_ref=source,
        dst_ref=target,
        send_sem=send_sem,
        recv_sem=recv_sem,
        device_id={axis: index},
        device_id_type=MESH,
    )


def line_barrier():
    me, chip, core, chips = line_position()
    barrier = pltpu.get_barrier_semaphore()

    def greet(index):
        pl.semaphore_signal(barrier, inc=1, device_id={"ctx": index}, device_id_type=MESH)

    greet(me + 1 - 2 * core)

    @pl.when(chip > 0)
    def _():
        greet(me - 2)

    @pl.when(chip < chips - 1)
    def _():
        greet(me + 2)

    peers = 1 + (chip > 0).astype(jnp.int32) + (chip < chips - 1).astype(jnp.int32)
    pl.semaphore_wait(barrier, peers)


def peers_of(axis):
    me, size = lax.axis_index(axis), lax.axis_size(axis)
    return size - 1, lambda i: (me + i + 1) % size, lambda i: (me + size - i - 1) % size


def full_barrier():
    barrier = pltpu.get_barrier_semaphore()
    total = 0
    for axis in ("fsdp", "ctx"):
        count, ahead, _ = peers_of(axis)
        loop(
            count,
            lambda i, axis=axis, ahead=ahead: pl.semaphore_signal(
                barrier, inc=1, device_id={axis: ahead(i)}, device_id_type=MESH
            ),
        )
        total += count
    pl.semaphore_wait(barrier, total)


def gather_scratch(chips):
    return [pltpu.SemaphoreType.DMA((chips,)) for _ in range(6)]


class Gather:
    def __init__(self, land, sems, consume=None):
        self.land = land
        self.sems = sems
        self.consume = consume
        self.me, self.chip, self.core, self.chips = line_position()

    def right(self, step, source):
        ref = self.land.at[2 * source + self.core]
        return send(ref, ref, self.sems[0].at[step], self.sems[1].at[step], "ctx", self.me + 2)

    def left(self, step, source):
        ref = self.land.at[2 * source + self.core]
        return send(ref, ref, self.sems[2].at[step], self.sems[3].at[step], "ctx", self.me - 2)

    def across(self, source, core):
        ref = self.land.at[2 * source + core]
        other = self.me + 1 - 2 * self.core
        return send(ref, ref, self.sems[4].at[source], self.sems[5].at[source], "ctx", other)

    def step(self, step):
        self.move(step)
        self.use(step)

    def move(self, step):
        chip, core, chips = self.chip, self.core, self.chips
        low, high = chip - step, chip + step
        has_low = low >= 0
        has_high = jnp.logical_and(high < chips, step > 0)

        @pl.when(jnp.logical_and(has_low, step > 0))
        def _():
            self.right(step - 1, low).wait_recv()

        @pl.when(jnp.logical_and(has_low, chip < chips - 1))
        def _():
            self.right(step, low).start()

        @pl.when(has_high)
        def _():
            self.left(step - 1, high).wait_recv()

        @pl.when(jnp.logical_and(high < chips, chip > 0))
        def _():
            self.left(step, high).start()

        @pl.when(has_low)
        def _():
            self.across(low, core).start()

        @pl.when(has_high)
        def _():
            self.across(high, core).start()

    def use(self, step):
        chip, core, chips = self.chip, self.core, self.chips
        low, high = chip - step, chip + step

        def one(kind):
            upward = kind % 2
            crossed = kind // 2
            source = jnp.where(upward == 1, high, low)
            valid = jnp.where(upward == 1, jnp.logical_and(high < chips, step > 0), low >= 0)
            parity = jnp.where(crossed == 1, 1 - core, core)

            @pl.when(valid)
            def _():
                @pl.when(crossed == 1)
                def _():
                    self.across(source, parity).wait_recv()

                if self.consume is not None:
                    self.consume(2 * source + parity)

        loop(4, one)

    def finish(self):
        chip, core, chips = self.chip, self.core, self.chips

        def one(step):
            @pl.when(jnp.logical_and(chip - step >= 0, chip < chips - 1))
            def _():
                self.right(step, chip - step).wait_send()

            @pl.when(jnp.logical_and(chip + step < chips, chip > 0))
            def _():
                self.left(step, chip + step).wait_send()

            self.across(step, core).wait_send()

        loop(chips, one)


def scatter_scratch(chips, rows):
    buffers = [VMEM((count, CHUNKS, rows, WIDE), BF16) for count in (chips + 1, 2, chips)]
    return buffers + [pltpu.SemaphoreType.DMA((chips, CHUNKS)) for _ in range(6)]


class Scatter:
    def __init__(self, scratch, produce, total):
        self.line, self.out, self.other = scratch[:3]
        self.sems = scratch[3:]
        self.produce = produce
        self.total = total
        self.me, self.chip, self.core, self.chips = line_position()


    def right(self, step, chunk):
        ref = self.line.at[step, chunk]
        sems = self.sems
        return send(ref, ref, sems[0].at[step, chunk], sems[1].at[step, chunk], "ctx", self.me + 2)

    def left(self, step, chunk):
        ref = self.line.at[self.chips - step, chunk]
        sems = self.sems
        return send(ref, ref, sems[2].at[step, chunk], sems[3].at[step, chunk], "ctx", self.me - 2)

    def across(self, target, chunk, slot=0):
        sems = self.sems
        return send(
            self.out.at[slot, chunk],
            self.other.at[target, chunk],
            sems[4].at[target, chunk],
            sems[5].at[target, chunk],
            "ctx",
            self.me + 1 - 2 * self.core,
        )

    def begin(self):
        def clear(index):
            slot, chunk = index // CHUNKS, index % CHUNKS
            at_left = jnp.logical_and(self.chip == 0, slot < self.chips)
            at_right = jnp.logical_and(self.chip == self.chips - 1, slot > 0)

            @pl.when(jnp.logical_or(at_left, at_right))
            def _():
                self.line[slot, chunk] = jnp.zeros(self.line.shape[2:], BF16)

        loop((self.chips + 1) * CHUNKS, clear)

    def when_right(self, time):
        return jnp.logical_and(time >= self.chip, time < self.chips - 1)

    def when_left(self, time):
        return jnp.logical_and(time >= self.chips - 1 - self.chip, time < self.chips - 1)

    def prepare(self, time):
        chip, chips = self.chip, self.chips

        def cross(target, slot, before, used):
            def one(chunk):
                @pl.when(used)
                def _():
                    self.across(before, chunk, slot).wait_send()

                piece = 2 * target + 1 - self.core
                self.out[slot, chunk] = self.produce(piece, chunk).astype(BF16)
                self.across(target, chunk, slot).start()

            loop(CHUNKS, one)

        @pl.when(self.when_right(time))
        def _():
            target = chips - 1 - time + chip
            cross(target, 0, target + 1, time > chip)

        @pl.when(self.when_left(time))
        def _():
            target = time - (chips - 1 - chip)
            cross(target, 1, target - 1, target > 0)

        @pl.when(time == chips - 1)
        def _():
            cross(chip, 0, chip + 1, chip < chips - 1)

    def step(self, time):
        chip, core, chips = self.chip, self.core, self.chips

        @pl.when(self.when_right(time))
        def _():
            step = time - chip
            target = chips - 1 - step

            def one(chunk):
                self.across(target, chunk).wait_recv()

                @pl.when(chip > 0)
                def _():
                    self.right(step, chunk).wait_recv()

                value = self.produce(2 * target + core, chunk) + self.other[target, chunk].astype(F32)
                value = value + self.line[step, chunk].astype(F32)
                self.line[step, chunk] = value.astype(BF16)
                self.right(step, chunk).start()

            loop(CHUNKS, one)

        @pl.when(self.when_left(time))
        def _():
            step = time - (chips - 1 - chip)

            def one(chunk):
                self.across(step, chunk).wait_recv()

                @pl.when(chip < chips - 1)
                def _():
                    self.left(step, chunk).wait_recv()

                value = self.produce(2 * step + core, chunk) + self.other[step, chunk].astype(F32)
                value = value + self.line[chips - step, chunk].astype(F32)
                self.line[chips - step, chunk] = value.astype(BF16)
                self.left(step, chunk).start()

            loop(CHUNKS, one)

    def finish(self):
        chip, core, chips = self.chip, self.core, self.chips
        last = chips - 1 - chip

        def one(chunk):
            self.across(chip, chunk).wait_recv()
            value = self.produce(2 * chip + core, chunk) + self.other[chip, chunk].astype(F32)

            @pl.when(chip > 0)
            def _():
                self.right(last, chunk).wait_recv()

            @pl.when(chip < chips - 1)
            def _():
                self.left(chip, chunk).wait_recv()

            value = value + self.line[last, chunk].astype(F32)
            value = value + self.line[chips - chip, chunk].astype(F32)
            self.total[:, pl.ds(pl.multiple_of(chunk * WIDE, WIDE), WIDE)] = value

        loop(CHUNKS, one)

        def drain(index):
            step, chunk = index // CHUNKS, index % CHUNKS

            @pl.when(step < last)
            def _():
                self.right(step, chunk).wait_send()

            @pl.when(step < chip)
            def _():
                self.left(step, chunk).wait_send()

            @pl.when(jnp.logical_or(step == chip, step == chip - 1))
            def _():
                self.across(step, chunk, jnp.where(step == chip, 0, 1)).wait_send()

        loop(chips * CHUNKS, drain)


def tile(index, size):
    return pl.ds(pl.multiple_of(index * size, size), size)


def row_blocks(rows, body, size=32):
    def one(index):
        body(pl.ds(pl.multiple_of(index * size, size), size))

    loop(rows // size, one)


def inverse_norm(value):
    return lax.rsqrt(jnp.mean(value * value, axis=-1, keepdims=True) + EPS)


def params(identity, megabytes):
    return pltpu.CompilerParams(
        collective_id=identity,
        has_side_effects=True,
        vmem_limit_bytes=megabytes * 1024 * 1024,
    )


def cost(microseconds):
    return pl.CostEstimate(
        flops=int(microseconds * 1.15e9), bytes_accessed=1024, transcendentals=0
    )


class FsdpSum:
    def __init__(self, grad, arrived, send_sems, recv_sems, own=None):
        self.grad, self.arrived = grad, arrived
        self.own = grad.at[lax.axis_index("fsdp")] if own is None else own
        self.sems = send_sems, recv_sems
        self.peers, self.ahead, _ = peers_of("fsdp")

    def copy(self, i):
        target = self.ahead(i)
        return send(
            self.grad.at[target], self.arrived.at[i], self.sems[0].at[i], self.sems[1].at[i], "fsdp", target
        )

    def start(self):
        loop(self.peers, lambda i: self.copy(i).start())

    def arrive(self):
        loop(self.peers, lambda i: self.copy(i).wait_recv())

    def collect(self, target):
        self.arrive()

        def add(block):
            value = self.own[block, :].astype(F32)
            for i in range(self.peers):
                value = value + self.arrived[i, block].astype(F32)
            target[block, :] = value.astype(BF16)

        row_blocks(self.own.shape[0], add)

    def finish(self):
        loop(self.peers, lambda i: self.copy(i).wait_send())


def fsdp_scratch(shards, rows, width):
    return [VMEM((shards - 1, rows, width), BF16)] + [pltpu.SemaphoreType.DMA((shards,))] * 2


def sine_cosine(angle):
    count = jnp.floor(angle * 0.6366197723675814 + 0.5)
    rest = angle - count * 1.5703125
    rest = rest - count * 4.837512969970703e-4
    rest = rest - count * 7.549789948768648e-8
    square = rest * rest
    sine = -1.9515295891e-4 * square + 8.3321608736e-3
    sine = rest + rest * square * (sine * square - 1.6666654611e-1)
    cosine = 2.443315711809948e-5 * square - 1.388731625493765e-3
    cosine = 1.0 - 0.5 * square + square * square * (cosine * square + 4.166664568298827e-2)
    quarter = jnp.bitwise_and(count.astype(jnp.int32), 3)
    odd = jnp.bitwise_and(quarter, 1) == 1
    sine, cosine = jnp.where(odd, cosine, sine), jnp.where(odd, sine, cosine)
    sine = jnp.where(quarter >= 2, -sine, sine)
    cosine = jnp.where(jnp.logical_or(quarter == 1, quarter == 2), -cosine, cosine)
    return sine, cosine


class Shares:
    def __init__(self, source, target_of, own_sem, sems):
        self.source, self.target_of = source, target_of
        self.own_sem, self.sems = own_sem, sems
        self.peers, self.ahead, self.behind = peers_of("fsdp")
        self.shard = lax.axis_index("fsdp")

    def copy(self, i, owner):
        sems = self.sems
        target = self.target_of(owner)
        return send(self.source, target, sems[0].at[i], sems[1].at[i], "fsdp", self.ahead(i))

    def own(self):
        return pltpu.make_async_copy(self.source, self.target_of(self.shard), self.own_sem)

    def start(self):
        loop(self.peers, lambda i: self.copy(i, self.shard).start())
        self.own().start()

    def arrive(self):
        self.own().wait()
        loop(self.peers, lambda i: self.copy(i, self.behind(i)).wait_recv())

    def finish(self):
        loop(self.peers, lambda i: self.copy(i, self.shard).wait_send())


def shares_scratch(count, shards):
    return [pltpu.SemaphoreType.DMA((count,))] + [pltpu.SemaphoreType.DMA((shards,))] * (2 * count)


def copy_in(source, target, sem):
    copy = pltpu.make_async_copy(source, target, sem)
    copy.start()
    return copy


QUERY_TILE = 256
KEY_TILE = 512


def reach(index, tokens):
    return jnp.minimum((index + 2) * QUERY_TILE + KEY_TILE - 1, tokens) // KEY_TILE


def head_norm(value, gain, cosine, sine):
    normed = value * inverse_norm(value) * gain
    return normed * cosine + pltpu.roll(normed, HEAD_SIZE // 2, 1) * sine


def forward_kernel(heads, *refs):
    x, grad, gains, token_info, freq = refs[:5]
    sources, refs = refs[5:12], refs[12:]
    normed_land, grad_land, two_land, activation, back = refs[:5]
    proj, cosine, sine, queries, keys, values, context, inverse = refs[5:13]
    middle, gain_rows, all_gains, all_tokens = refs[13:17]
    head_weight, out_weight, pair_weight, down_weight = refs[17:21]
    refs = refs[21:]
    pair, down, own, piece_in, grad_in, act_out, back_out, total, sems = refs[:9]
    small, refs = refs[9:13], refs[13:]
    share_own, share_sems, refs = refs[0], refs[1:15], refs[15:]
    first_sems, grad_sems, two_sems, scratch = refs[:6], refs[6:12], refs[12:18], refs[18:]
    me, _, _, chips = line_position()
    shard = lax.axis_index("fsdp")
    shards, ahead, behind = peers_of("fsdp")
    parts, next_part, past_part = peers_of("ctx")
    count = x.shape[0]
    tokens = 2 * chips * count
    width = heads * HEAD_SIZE
    feed_width = down.shape[0]
    rows = D // (shards + 1)
    lanes = rows // 128
    key_head = me // (2 * chips // KEY_VALUE_HEADS)

    def gain_copy(i, slot):
        return send(gains, all_gains.at[slot], small[0].at[i], small[1].at[i], "fsdp", ahead(i))

    def token_copy(i, slot):
        return send(token_info, all_tokens.at[slot], small[2].at[i], small[3].at[i], "ctx", next_part(i))

    def by_row(target, at, size):
        return lambda owner: target.at[tile(owner, rows), pl.ds(at, size)]

    def by_column(target):
        return lambda owner: target.at[:, tile(owner, rows)]

    places = (
        (sources[0].at[:, tile(me, width)], by_row(head_weight, 0, width)),
        (sources[1].at[:, tile(key_head, HEAD_SIZE)], by_row(head_weight, width, HEAD_SIZE)),
        (sources[2].at[:, tile(key_head, HEAD_SIZE)], by_row(head_weight, width + HEAD_SIZE, HEAD_SIZE)),
        (sources[3].at[tile(me, width), :], by_column(out_weight)),
        (sources[4].at[:, tile(me, feed_width)], by_row(pair, 0, feed_width)),
        (sources[5].at[:, tile(me, feed_width)], by_row(pair, feed_width, feed_width)),
        (sources[6].at[tile(me, feed_width), :], by_column(down)),
    )
    shares = [
        Shares(source, target_of, share_own.at[i], share_sems[2 * i : 2 * i + 2])
        for i, (source, target_of) in enumerate(places)
    ]

    full_barrier()
    loop(shards, lambda i: gain_copy(i, shard).start())
    loop(parts, lambda i: token_copy(i, me).start())
    for share in shares[:4]:
        share.start()
    grad_copy = copy_in(grad, grad_land.at[me], sems.at[0])
    all_gains[shard] = gains[...]
    all_tokens[me] = token_info[...]
    loop(shards, lambda i: gain_copy(i, behind(i)).wait_recv())
    for kind in range(2):
        for owner in range(shards + 1):
            for j in range(lanes):
                at = owner * rows + j * 128
                gain_rows[kind : kind + 1, at : at + 128] = all_gains[
                    owner, kind * lanes + j : kind * lanes + j + 1, :
                ]
    size = HEAD_SIZE // (shards + 1)
    for kind in range(2):
        gain_rows[2 + kind : 3 + kind, 0:HEAD_SIZE] = jnp.concatenate(
            [
                all_gains[
                    owner, 2 * lanes : 2 * lanes + 1, kind * size : (kind + 1) * size
                ]
                for owner in range(shards + 1)
            ],
            axis=1,
        )

    def norm(block):
        value = x[block, :].astype(F32)
        own[block, :] = (value * inverse_norm(value) * gain_rows[0:1, :]).astype(BF16)

    row_blocks(count, norm)
    own_copy = copy_in(own, normed_land.at[me], sems.at[1])
    own_copy.wait()

    def column(piece, row):
        values_in_lanes = all_tokens[piece, row : row + 1, :].astype(F32)
        return jnp.broadcast_to(values_in_lanes, (128, count)).T

    def project(piece):
        copy = copy_in(normed_land.at[piece], piece_in, sems.at[1])
        block = tile(piece, count)
        s, c = sine_cosine(column(piece, 0) * freq[0:1, :])
        lane = lax.broadcasted_iota(jnp.int32, s.shape, 1)
        s = jnp.where(lane < HEAD_SIZE // 2, -s, s)
        cosine[block, :] = c
        sine[block, :] = s
        copy.wait()
        proj[piece] = dot(piece_in[...], head_weight[...])

        def turned(at, row):
            return head_norm(proj[piece, :, at : at + HEAD_SIZE], gain_rows[row : row + 1, 0:HEAD_SIZE], c, s)

        for h in range(heads):
            at = h * HEAD_SIZE
            queries[block, at : at + HEAD_SIZE] = (turned(at, 2) * HEAD_SIZE ** (-0.5)).astype(BF16)
        keys[block, :] = turned(width, 3).astype(BF16)
        values[block, :] = proj[piece, :, width + HEAD_SIZE : width + 2 * HEAD_SIZE].astype(BF16)

    first_gather = Gather(normed_land, first_sems, project)
    grad_gather = Gather(grad_land, grad_sems)
    first_gather.move(0)
    loop(parts, lambda i: token_copy(i, past_part(i)).wait_recv())

    def first_step(step):
        first_gather.move(step + 1)

        @pl.when(step == 0)
        def _():
            for share in shares[:4]:
                share.arrive()
            for share in shares[4:]:
                share.start()

        first_gather.use(step)

    loop(chips - 1, first_step)
    grad_copy.wait()
    grad_gather.step(0)
    first_gather.use(chips - 1)

    def attend(index):
        block = tile(index, QUERY_TILE)
        query_ids = column(index, 1)[:, 0:1]
        for h in range(heads):
            head = slice(h * HEAD_SIZE, (h + 1) * HEAD_SIZE)
            query = queries[block, head]

            def one(key_tile, carry):
                sums, total = carry
                span = tile(key_tile, KEY_TILE)
                scores = rdot(query, keys[span, :])
                key_ids = jnp.concatenate(
                    [all_tokens[key_tile * each + j, 1:2, :] for j in range(each)], axis=1
                ).astype(F32)
                expon = jnp.where(key_ids <= query_ids, jnp.exp(scores), 0.0)
                sums = sums + dot(expon.astype(BF16), values[span, :])
                return sums, total + jnp.sum(expon, axis=1, keepdims=True)

            each = KEY_TILE // count
            start = (jnp.zeros((QUERY_TILE, HEAD_SIZE), F32), jnp.zeros((QUERY_TILE, 1), F32))
            sums, total = lax.fori_loop(0, reach(index, tokens), one, start)
            scale = 1.0 / total
            context[block, head] = (sums * scale).astype(BF16)
            inverse[h : h + 1, block] = jnp.broadcast_to(scale, (QUERY_TILE, HEAD_SIZE)).T[0:1, :]

    loop(tokens // QUERY_TILE, attend)

    def produce(piece, chunk):
        return dot(context[tile(piece, count), :], out_weight[:, tile(chunk, WIDE)])

    scatter = Scatter(scratch, produce, total)
    scatter.begin()
    scatter.prepare(0)
    grad_gather.step(1)

    def scatter_step(time):
        scatter.step(time)
        scatter.prepare(time + 1)

        @pl.when(time >= 1)
        def _():
            grad_gather.step(time + 1)

    loop(chips - 1, scatter_step)
    scatter.finish()

    def norm_two(block):
        value = x[block, :].astype(F32) + total[block, :]
        middle[block, :] = value
        own[block, :] = (value * inverse_norm(value) * gain_rows[1:2, :]).astype(BF16)

    row_blocks(count, norm_two)
    two_copy = copy_in(own, two_land.at[me], sems.at[1])
    two_copy.wait()
    for share in shares[4:]:
        share.arrive()
    outs = [
        copy_in(head_weight, refs_out, sems.at[2 + i])
        for i, (head_weight, refs_out) in enumerate(((pair, pair_weight), (down, down_weight)))
    ]
    feed_size = 256 if feed_width % 256 == 0 else 128

    def act_copy(piece):
        return pltpu.make_async_copy(act_out, activation.at[piece], sems.at[6])

    def back_copy(piece):
        return pltpu.make_async_copy(back_out, back.at[piece], sems.at[7])

    def feed(piece):
        copies = (
            copy_in(two_land.at[piece], piece_in, sems.at[4]),
            copy_in(grad_land.at[piece], grad_in, sems.at[5]),
        )
        for copy in copies:
            copy.wait()

        @pl.when(piece != me)
        def _():
            act_copy(piece).wait()
            back_copy(piece).wait()

        def one(index):
            def columns(kind):
                return pl.ds(pl.multiple_of(kind * feed_width + index * feed_size, 128), feed_size)

            gate = dot(piece_in[...], pair[:, columns(0)])
            up = dot(piece_in[...], pair[:, columns(1)])
            grad_act = rdot(grad_in[...], down[tile(index, feed_size), :])
            sigma = 1.0 / (1.0 + jnp.exp(-gate))
            act_out[:, columns(0)] = (gate * sigma * up).astype(BF16)
            back_out[:, columns(0)] = (
                grad_act * up * sigma * (1.0 + gate * (1.0 - sigma))
            ).astype(BF16)
            back_out[:, columns(1)] = (grad_act * gate * sigma).astype(BF16)

        loop(feed_width // feed_size, one)
        act_copy(piece).start()
        back_copy(piece).start()

    two_gather = Gather(two_land, two_sems, feed)
    loop(chips, two_gather.step)
    act_copy(0).wait()
    back_copy(0).wait()
    first_gather.finish()
    grad_gather.finish()
    two_gather.finish()
    for out in outs:
        out.wait()
    for share in shares:
        share.finish()
    loop(shards, lambda i: gain_copy(i, shard).wait_send())
    loop(parts, lambda i: token_copy(i, me).wait_send())


def forward(hidden, grad, gains, token_info, freq, weights, shards, parts, heads):
    count = hidden.shape[0]
    tokens = parts * count
    width = heads * HEAD_SIZE
    total_width = width + 2 * HEAD_SIZE
    feed_width = FF // parts
    chips = parts // 2
    shape = jax.ShapeDtypeStruct
    return pl.pallas_call(
        functools.partial(forward_kernel, heads),
        out_shape=(
            shape((parts, count, D), BF16),
            shape((parts, count, D), BF16),
            shape((parts, count, D), BF16),
            shape((parts, count, feed_width), BF16),
            shape((parts, count, 2 * feed_width), BF16),
            shape((parts, count, total_width), F32),
            shape((tokens, HEAD_SIZE), F32),
            shape((tokens, HEAD_SIZE), F32),
            shape((tokens, width), BF16),
            shape((tokens, HEAD_SIZE), BF16),
            shape((tokens, HEAD_SIZE), BF16),
            shape((tokens, width), BF16),
            shape((8, tokens), F32),
            shape((count, D), F32),
            shape((8, D), F32),
            shape((shards, *gains.shape), F32),
            shape((parts, *token_info.shape), jnp.int32),
            shape((D, total_width), BF16),
            shape((width, D), BF16),
            shape((D, 2 * feed_width), BF16),
            shape((feed_width, D), BF16),
        ),
        in_specs=[WHOLE] * 5 + [HBM] * 7,
        out_specs=(HBM,) * 5 + (WHOLE,) * 14 + (HBM,) * 2,
        scratch_shapes=[
            VMEM((D, 2 * feed_width), BF16),
            VMEM((feed_width, D), BF16),
            VMEM((count, D), BF16),
            VMEM((count, D), BF16),
            VMEM((count, D), BF16),
            VMEM((count, feed_width), BF16),
            VMEM((count, 2 * feed_width), BF16),
            VMEM((count, D), F32),
            pltpu.SemaphoreType.DMA((8,)),
        ]
        + [pltpu.SemaphoreType.DMA((shards,))] * 2
        + [pltpu.SemaphoreType.DMA((parts,))] * 2
        + shares_scratch(7, shards)
        + gather_scratch(chips)
        + gather_scratch(chips)
        + gather_scratch(chips)
        + scatter_scratch(chips, count),
        compiler_params=params(0, 63),
        cost_estimate=cost(280),
        name="forward",
    )(hidden, grad, gains, token_info, freq, *weights)


def rms_back(value, gain, grad):
    inverse = inverse_norm(value)
    scaled = grad * gain
    inner = jnp.mean(scaled * value, axis=-1, keepdims=True)
    terms = grad * value * inverse
    return inverse * scaled - value * (inverse * inverse * inverse * inner), terms


def turn_kernel(*refs):
    back, pair_weight, down_weight, activation, out_weight = refs[:5]
    middle, grad, gain_rows, down_grad, pair_grad = refs[5:10]
    grad_middle, land, gain_sum, down_land, context_grad, hidden, pair_in = refs[10:17]
    weight, data, total, low, piece_in, own_down, down_sum, sems = refs[17:25]
    down_refs, down_sems, gather_sems = refs[25:28], refs[28:34], refs[34:40]
    pair_sems, first_scratch, second_scratch = refs[40:42], refs[42:51], refs[51:]
    me, _, _, chips = line_position()
    width = back.shape[2] // 2
    weight_copy = copy_in(pair_weight, weight, sems.at[0])
    data_copy = copy_in(back, data, sems.at[1])
    own_copy = copy_in(down_grad.at[lax.axis_index("fsdp")], own_down, sems.at[3])

    def produce(piece, chunk):
        return rdot(data[piece], weight[pl.ds(pl.multiple_of(chunk * WIDE, WIDE), WIDE), :])

    each = 2 * width // WIDE

    def down_block(chunk):
        return tile(chunk // each, width), tile(chunk % each, WIDE)

    def down_copy(chunk):
        source = down_weight.at[:, tile(chunk, WIDE)]
        return pltpu.make_async_copy(source, weight.at[down_block(chunk)], sems.at[5 + chunk])

    def produce_hidden(piece, chunk):
        return dot(data[piece, :, :width], weight[down_block(chunk)])

    def consume(piece):
        copy = copy_in(land.at[piece], piece_in, sems.at[4])
        copy.wait()
        context_grad[piece] = rdot(piece_in[...], out_weight[...]).astype(BF16)

    down = FsdpSum(down_grad, *down_refs, own=own_down)
    pair = FsdpSum(pair_grad, pair_in, *pair_sems, own=own_down)
    down_gather = Gather(down_land, down_sems)
    gather = Gather(land, gather_sems, consume)
    scatter = Scatter(first_scratch, produce, total)
    hidden_scatter = Scatter(second_scratch, produce_hidden, total)
    scatter.begin()
    hidden_scatter.begin()
    full_barrier()
    down.start()
    weight_copy.wait()
    data_copy.wait()
    scatter.prepare(0)

    def step(time):
        scatter.step(time)
        scatter.prepare(time + 1)

        @pl.when(time == 1)
        def _():
            own_copy.wait()
            down.collect(down_sum)
            pair.start()
            copy = copy_in(down_sum, down_land.at[me], sems.at[3])
            copy.wait()

        @pl.when(time >= 1)
        def _():
            down_gather.step(time - 1)

    loop(chips - 1, step)
    scatter.finish()
    for chunk in range(CHUNKS):
        down_copy(chunk).start()
    act_copy = copy_in(activation, data.at[:, :, pl.ds(0, width)], sems.at[1])
    gain_sum[...] = jnp.zeros_like(gain_sum)

    def norm(block):
        through, terms = rms_back(middle[block, :], gain_rows[1:2, :], total[block, :])
        value = grad[block, :].astype(F32) + through
        grad_middle[block, :] = value
        low[block, :] = value.astype(BF16)
        gain_sum[0:1, :] += jnp.sum(terms, axis=0, keepdims=True)

    row_blocks(middle.shape[0], norm)
    low_copy = copy_in(low, land.at[me], sems.at[3])
    low_copy.wait()
    gather.step(0)
    for chunk in range(CHUNKS):
        down_copy(chunk).wait()
    act_copy.wait()
    hidden_scatter.prepare(0)

    def turn_step(time):
        hidden_scatter.step(time)
        hidden_scatter.prepare(time + 1)
        gather.step(time + 1)

        @pl.when(time < 2)
        def _():
            down_gather.step(chips - 2 + time)

    loop(chips - 1, turn_step)
    hidden_scatter.finish()
    gather.finish()
    down_gather.finish()
    down.finish()
    pair.arrive()
    pair.finish()

    def add(block):
        hidden[block, :] = (middle[block, :] + total[block, :]).astype(BF16)

    row_blocks(middle.shape[0], add)


def turn(back, pair_weight, down_weight, activation, out_weight, middle, grad, gain_rows, down_grad, pair_grad):
    parts, count, feed_width = activation.shape
    shards, rows, _ = down_grad.shape
    width = out_weight.shape[0]
    return pl.pallas_call(
        turn_kernel,
        out_shape=(
            jax.ShapeDtypeStruct((count, D), F32),
            jax.ShapeDtypeStruct((parts, count, D), BF16),
            jax.ShapeDtypeStruct((8, D), F32),
            jax.ShapeDtypeStruct((parts, rows, feed_width), BF16),
            jax.ShapeDtypeStruct((parts, count, width), BF16),
            jax.ShapeDtypeStruct((count, D), BF16),
            jax.ShapeDtypeStruct((shards - 1, rows, 2 * feed_width), BF16),
        ),
        in_specs=[HBM] * 4 + [WHOLE] * 4 + [HBM] * 2,
        out_specs=(WHOLE, HBM, WHOLE, HBM, WHOLE, WHOLE, HBM),
        scratch_shapes=[
            VMEM((D, 2 * feed_width), BF16),
            VMEM((parts, count, 2 * feed_width), BF16),
            VMEM((count, D), F32),
            VMEM((count, D), BF16),
            VMEM((count, D), BF16),
            VMEM((rows, feed_width), BF16),
            VMEM((rows, feed_width), BF16),
            pltpu.SemaphoreType.DMA((5 + CHUNKS,)),
        ]
        + fsdp_scratch(shards, rows, feed_width)
        + gather_scratch(parts // 2)
        + gather_scratch(parts // 2)
        + [pltpu.SemaphoreType.DMA((shards,))] * 2
        + scatter_scratch(parts // 2, count)
        + scatter_scratch(parts // 2, count),
        compiler_params=params(3, 63),
        cost_estimate=cost(185),
        name="turn",
    )(
        back,
        pair_weight,
        down_weight,
        activation,
        out_weight,
        middle,
        grad,
        gain_rows,
        down_grad,
        pair_grad,
    )


def last_kernel(*refs):
    back, weights, x, grad_middle, gain_rows, gain_two, gain_heads, head_grad = refs[:8]
    hidden, gain_out, land = refs[8:11]
    weight, weight_sem, total, gain_one, pack, pack_in, shard_sum, shard_in = refs[11:19]
    small, head_refs, gather_sems, scratch = refs[19:23], refs[23:26], refs[26:32], refs[32:]
    me, _, _, chips = line_position()
    shard = lax.axis_index("fsdp")
    shards, ahead, _ = peers_of("fsdp")
    parts, next_part, _ = peers_of("ctx")
    copy = copy_in(weights, weight, weight_sem)

    def produce(piece, chunk):
        return rdot(back[piece], weight[pl.ds(pl.multiple_of(chunk * WIDE, WIDE), WIDE), :])

    heads = FsdpSum(head_grad, *head_refs)
    scatter = Scatter(scratch, produce, total)
    gather = Gather(land, gather_sems)
    scatter.begin()
    full_barrier()
    copy.wait()
    scatter.prepare(0)
    heads.start()

    def step(time):
        scatter.step(time)

        @pl.when(time == 1)
        def _():
            heads.collect(land.at[me])

        @pl.when(time >= 1)
        def _():
            gather.step(time - 1)

        scatter.prepare(time + 1)

    loop(chips - 1, step)
    scatter.finish()
    gather.step(chips - 2)
    gain_one[...] = jnp.zeros_like(gain_one)

    def norm(block):
        through, terms = rms_back(x[block, :].astype(F32), gain_rows[0:1, :], total[block, :])
        hidden[block, :] = grad_middle[block, :] + through
        gain_one[0:1, :] += jnp.sum(terms, axis=0, keepdims=True)

    row_blocks(x.shape[0], norm)

    rows = D // (shards + 1)
    lanes = rows // 128
    pack[...] = jnp.zeros_like(pack)
    for owner in range(shards + 1):
        for j in range(lanes):
            at = owner * rows + j * 128
            pack[owner, j : j + 1, :] = gain_one[0:1, at : at + 128]
            pack[owner, lanes + j : lanes + j + 1, :] = gain_two[0:1, at : at + 128]
        pack[owner, 2 * lanes : 2 * lanes + 2, :] = gain_heads[0:2, :]

    def pack_copy(i):
        return send(pack.at[ahead(i)], pack_in.at[i], small[0].at[i], small[1].at[i], "fsdp", ahead(i))

    def sum_copy(i):
        return send(shard_sum, shard_in.at[i], small[2].at[i], small[3].at[i], "ctx", next_part(i))

    loop(shards, lambda i: pack_copy(i).start())
    shard_sum[...] = pack[shard]

    def add_pack(i):
        pack_copy(i).wait_recv()
        shard_sum[...] += pack_in[i]

    loop(shards, add_pack)
    loop(parts, lambda i: sum_copy(i).start())
    gain_out[...] = shard_sum[...]

    def add_sum(i):
        sum_copy(i).wait_recv()
        gain_out[...] += shard_in[i]

    loop(parts, add_sum)
    gather.step(chips - 1)
    gather.finish()
    heads.finish()
    loop(shards, lambda i: pack_copy(i).wait_send())
    loop(parts, lambda i: sum_copy(i).wait_send())


def last(back, weights, hidden, grad_middle, gain_rows, gain_two, gain_heads, head_grad):
    parts, count, width = back.shape
    shards, rows, head_width = head_grad.shape
    return pl.pallas_call(
        last_kernel,
        out_shape=(
            jax.ShapeDtypeStruct((count, D), F32),
            jax.ShapeDtypeStruct((16, 128), F32),
            jax.ShapeDtypeStruct((parts, rows, head_width), BF16),
        ),
        in_specs=[WHOLE, HBM] + [WHOLE] * 6,
        out_specs=(WHOLE,) * 3,
        scratch_shapes=[
            VMEM((D, width), BF16),
            pltpu.SemaphoreType.DMA,
            VMEM((count, D), F32),
            VMEM((8, D), F32),
            VMEM((shards, 16, 128), F32),
            VMEM((shards, 16, 128), F32),
            VMEM((16, 128), F32),
            VMEM((parts, 16, 128), F32),
        ]
        + [pltpu.SemaphoreType.DMA((shards,))] * 2
        + [pltpu.SemaphoreType.DMA((parts,))] * 2
        + fsdp_scratch(shards, rows, head_width)
        + gather_scratch(parts // 2)
        + scatter_scratch(parts // 2, count),
        compiler_params=params(5, 60),
        cost_estimate=cost(90),
        name="last",
    )(back, weights, hidden, grad_middle, gain_rows, gain_two, gain_heads, head_grad)


def attention_back_kernel(heads, *refs):
    queries, keys, values, out_grad, inverse, context, proj, cosine, sine, gain = refs[:10]
    id_column, id_row, back, gain_sum, key_grad, value_grad, query_grad = refs[10:]
    tokens = proj.shape[0]
    key_at = heads * HEAD_SIZE
    key_grad[...] = jnp.zeros_like(key_grad)
    value_grad[...] = jnp.zeros_like(value_grad)
    gain_sum[...] = jnp.zeros_like(gain_sum)

    def through(block, lanes, grad, row):
        turned = pltpu.roll(grad, HEAD_SIZE // 2, 1)
        unrotated = grad * cosine[block, :] - turned * sine[block, :]
        result, terms = rms_back(proj[block, lanes], gain[row : row + 1, :], unrotated)
        back[block, lanes] = result.astype(BF16)
        gain_sum[row : row + 1, :] += jnp.sum(terms, axis=0, keepdims=True)

    def attend(index):
        block = pl.ds(pl.multiple_of(index * QUERY_TILE, QUERY_TILE), QUERY_TILE)
        query_ids = id_row[0:1, block]
        for h in range(heads):
            lanes = slice(h * HEAD_SIZE, (h + 1) * HEAD_SIZE)
            query = queries[block, lanes]
            grad = out_grad[block, lanes]
            scale = inverse[h : h + 1, block]
            products = grad.astype(F32) * context[block, lanes].astype(F32)
            shift = lax.dot_general(
                jnp.ones((8, HEAD_SIZE), F32),
                products,
                (((1,), (1,)), ((), ())),
                precision=lax.Precision.HIGHEST,
                preferred_element_type=F32,
            )[0:1, :]
            query_grad[...] = jnp.zeros_like(query_grad)

            def one(tile):
                span = pl.ds(pl.multiple_of(tile * KEY_TILE, KEY_TILE), KEY_TILE)
                key = keys[span, :]
                scores = rdot(key, query)
                probs = jnp.where(id_column[span, :] <= query_ids, jnp.exp(scores) * scale, 0.0)
                grad_scores = (probs * (rdot(values[span, :], grad) - shift)).astype(BF16)
                value_grad[span, :] += dot(probs.astype(BF16), grad)
                key_grad[span, :] += dot(grad_scores, query)
                query_grad[...] += tdot(grad_scores, key)

            loop(reach(index, tokens), one)
            through(block, lanes, query_grad[...] * HEAD_SIZE ** (-0.5), 0)

    loop(tokens // QUERY_TILE, attend)

    def finish(index):
        block = pl.ds(pl.multiple_of(index * QUERY_TILE, QUERY_TILE), QUERY_TILE)
        through(block, slice(key_at, key_at + HEAD_SIZE), key_grad[block, :], 1)
        back[block, key_at + HEAD_SIZE : key_at + 2 * HEAD_SIZE] = value_grad[block, :].astype(BF16)

    loop(tokens // QUERY_TILE, finish)


def attention_back(heads, *operands):
    tokens = operands[0].shape[0]
    width = heads * HEAD_SIZE
    return pl.pallas_call(
        functools.partial(attention_back_kernel, heads),
        out_shape=(
            jax.ShapeDtypeStruct((tokens, width + 2 * HEAD_SIZE), BF16),
            jax.ShapeDtypeStruct((8, HEAD_SIZE), F32),
        ),
        in_specs=[WHOLE] * len(operands),
        out_specs=(WHOLE,) * 2,
        scratch_shapes=[
            VMEM((tokens, HEAD_SIZE), F32),
            VMEM((tokens, HEAD_SIZE), F32),
            VMEM((QUERY_TILE, HEAD_SIZE), F32),
        ],
        compiler_params=pltpu.CompilerParams(vmem_limit_bytes=48 * 1024 * 1024),
        cost_estimate=cost(38),
        name="attention_back",
    )(*operands)


def spread_pair_kernel(width, source, gate, up):
    gate[...] = source[0, :, :width].astype(F32)
    up[...] = source[0, :, width:].astype(F32)


def spread_pair(stacked):
    parts, rows, total = stacked.shape
    width = total // 2
    across = jax.ShapeDtypeStruct((rows, parts * width), F32)
    return pl.pallas_call(
        functools.partial(spread_pair_kernel, width),
        out_shape=(across, across),
        grid=(parts,),
        in_specs=[pl.BlockSpec((1, rows, total), lambda i: (i, 0, 0))],
        out_specs=(pl.BlockSpec((rows, width), lambda i: (0, i)),) * 2,
        compiler_params=pltpu.CompilerParams(vmem_limit_bytes=60 * 1024 * 1024),
        name="spread_pair",
    )(stacked)


def spread_turned_kernel(source, target):
    target[...] = source[0].astype(F32).T


def spread_turned(stacked):
    parts, rows, width = stacked.shape
    return pl.pallas_call(
        spread_turned_kernel,
        out_shape=jax.ShapeDtypeStruct((parts * width, rows), F32),
        grid=(parts,),
        in_specs=[pl.BlockSpec((1, rows, width), lambda i: (i, 0, 0))],
        out_specs=pl.BlockSpec((width, rows), lambda i: (i, 0)),
        compiler_params=pltpu.CompilerParams(vmem_limit_bytes=60 * 1024 * 1024),
        name="spread_turned",
    )(stacked)


def spread_heads_kernel(width, source, query, key, value, out):
    second = width + HEAD_SIZE
    third = second + HEAD_SIZE
    query[...] = source[0, :, :width].astype(F32)
    key[...] = source[0, :, width:second].astype(F32)
    value[...] = source[0, :, second:third].astype(F32)
    out[...] = source[0, :, third:].astype(F32).T


def spread_heads(stacked, width):
    parts, rows, total = stacked.shape
    widths = (width, HEAD_SIZE, HEAD_SIZE)
    return pl.pallas_call(
        functools.partial(spread_heads_kernel, width),
        out_shape=tuple(jax.ShapeDtypeStruct((rows, parts * w), F32) for w in widths)
        + (jax.ShapeDtypeStruct((parts * width, rows), F32),),
        grid=(parts,),
        in_specs=[pl.BlockSpec((1, rows, total), lambda i: (i, 0, 0))],
        out_specs=tuple(pl.BlockSpec((rows, w), lambda i: (0, i)) for w in widths)
        + (pl.BlockSpec((width, rows), lambda i: (i, 0)),),
        compiler_params=pltpu.CompilerParams(vmem_limit_bytes=60 * 1024 * 1024),
        name="spread_heads",
    )(stacked)


def by_row(array):
    return with_layout_constraint(array, Layout(major_to_minor=(0, 1)))


def local(
    hidden_in,
    weight_query,
    key_weight_matrix,
    weight_value,
    weight_out,
    weight_gate,
    weight_up,
    weight_down,
    gain_attention,
    gain_feed,
    gain_query,
    gain_key,
    positions,
    token_block_index,
    grad_out,
):
    parts = lax.axis_size("ctx")
    shards = lax.axis_size("fsdp")
    shard = lax.axis_index("fsdp")
    heads = QUERY_HEADS // parts
    sharers = parts // KEY_VALUE_HEADS
    width = heads * HEAD_SIZE
    feed_width = FF // parts
    rows = D // shards
    head_rows = HEAD_SIZE // shards
    count = hidden_in.shape[1]
    tokens = parts * count

    def gather_parts(piece):
        return lax.all_gather(piece, "ctx", axis=0)

    own_gains = jnp.concatenate([gain_attention, gain_feed, gain_query, gain_key]).astype(F32)
    own_gains = jnp.pad(own_gains, (0, 2048 - own_gains.shape[0])).reshape(16, 128)
    own_tokens = jnp.pad(jnp.stack([positions[0], token_block_index[0]]), ((0, 6), (0, 0)))
    half = HEAD_SIZE // 2
    freq = THETA ** (-(jnp.arange(half).astype(F32) * 2.0 / HEAD_SIZE))
    freq = jnp.broadcast_to(jnp.concatenate([freq, freq]), (8, HEAD_SIZE))
    hidden, grad = hidden_in[0], grad_out[0]
    weights = (
        weight_query,
        key_weight_matrix,
        weight_value,
        weight_out,
        weight_gate,
        weight_up,
        weight_down,
    )
    (
        normed_all,
        grad_all,
        normed_two_all,
        activation,
        back,
        proj,
        cosine,
        sine,
        queries,
        keys,
        values,
        context,
        inverse,
        middle,
        gain_rows,
        gains,
        whole,
        heads_weight,
        out_weight,
        pair_weight,
        down_weight,
    ) = forward(hidden, grad, own_gains, own_tokens, freq, weights, shards, parts, heads)
    head_gains = gain_rows[2:4, :HEAD_SIZE]
    ids = whole[:, 1].reshape(-1)
    id_row, id_column = ids[None, :], ids[:, None]
    proj = proj.reshape(tokens, width + 2 * HEAD_SIZE)

    flat_grad = grad_all.reshape(tokens, D)
    flat_back = back.reshape(tokens, 2 * feed_width)
    flat_activation = activation.reshape(tokens, feed_width)
    feed_grad = by_row(tdot(normed_two_all.reshape(tokens, D), flat_back).astype(BF16))
    down_grad = by_row(tdot(flat_grad, flat_activation).astype(BF16))
    back, feed_grad, down_grad = lax.optimization_barrier((back, feed_grad, down_grad))
    feed_grad = feed_grad.reshape(shards, rows, 2 * feed_width)
    grad_middle, low_all, gain_two, down_parts, context_grad, hidden_out, pair_in = turn(
        back,
        pair_weight,
        down_weight,
        activation,
        out_weight,
        middle,
        grad,
        gain_rows,
        down_grad.reshape(shards, rows, feed_width),
        feed_grad,
    )
    own_pair = lax.dynamic_index_in_dim(feed_grad, shard, keepdims=False)
    feed_shard = (own_pair.astype(F32) + jnp.sum(pair_in.astype(F32), axis=0)).astype(BF16)
    context_grad, feed_shard, down_parts = lax.optimization_barrier(
        (context_grad, feed_shard, down_parts)
    )
    feed_parts = gather_parts(feed_shard)
    context_grad = context_grad.reshape(tokens, width)
    grad_qkv, gain_heads = attention_back(
        heads,
        queries,
        keys,
        values,
        context_grad,
        inverse,
        context,
        proj,
        cosine,
        sine,
        head_gains,
        id_column,
        id_row,
    )
    head_grad = jnp.concatenate(
        [
            by_row(tdot(normed_all.reshape(tokens, D), grad_qkv).astype(BF16)),
            by_row(tdot(low_all.reshape(tokens, D), context).astype(BF16)),
        ],
        axis=1,
    )
    grad_down = spread_turned(down_parts)
    grad_qkv, grad_down = lax.optimization_barrier((grad_qkv, grad_down))
    grad_hidden, gain_sums, head_parts = last(
        grad_qkv.reshape(parts, count, -1),
        heads_weight,
        hidden,
        grad_middle,
        gain_rows,
        gain_two,
        gain_heads,
        head_grad.reshape(shards, rows, -1),
    )

    gain_sums = gain_sums.reshape(-1)
    grad_gate, grad_up = spread_pair(feed_parts)
    grad_query, grad_key, grad_value, grad_out_weight = spread_heads(head_parts, width)
    if sharers > 1:
        grad_key, grad_value = (
            part.reshape(rows, KEY_VALUE_HEADS, sharers, HEAD_SIZE).sum(axis=2).reshape(rows, -1)
            for part in (grad_key, grad_value)
        )
    return (
        hidden_out[None],
        grad_hidden[None],
        grad_query,
        grad_key,
        grad_value,
        grad_out_weight,
        grad_gate,
        grad_up,
        grad_down,
        gain_sums[:rows],
        gain_sums[rows : 2 * rows],
        lax.dynamic_slice_in_dim(gain_sums, 2 * rows + shard * head_rows, head_rows),
        lax.dynamic_slice_in_dim(gain_sums, 2 * rows + HEAD_SIZE + shard * head_rows, head_rows),
    )


def solution(mesh):
    tokens = P("fsdp", "ctx", None)
    by_rows = P("fsdp", None)
    by_columns = P(None, "fsdp")
    per_token = P("fsdp", "ctx")
    vector = P("fsdp")
    weights = (by_rows, by_rows, by_rows, by_columns, by_rows, by_rows, by_columns)
    return jax.shard_map(
        local,
        mesh=mesh,
        in_specs=(tokens, *weights, vector, vector, vector, vector, per_token, per_token, tokens),
        out_specs=(tokens, tokens, *weights, vector, vector, vector, vector),
        check_vma=False,
    )
```

```python
import functools

import jax
import jax.numpy as jnp
from jax import lax
from jax.experimental import pallas as pl
from jax.experimental.layout import Layout, with_layout_constraint
from jax.experimental.pallas import tpu as pltpu
from jax.sharding import PartitionSpec as P

D = 2048
QUERY_HEADS = 16
KEY_VALUE_HEADS = 8
HEAD_SIZE = 128
FF = 6144
EPS = 1e-06
THETA = 1000000.0
F32 = jnp.float32
BF16 = jnp.bfloat16
MESH = pl.DeviceIdType.MESH
VMEM = pltpu.VMEM
WHOLE = pl.BlockSpec(memory_space=pltpu.VMEM)
HBM = pl.BlockSpec(memory_space=pl.ANY)
CHUNKS = 4
WIDE = D // CHUNKS


def dot(left, right):
    return jnp.dot(left, right, preferred_element_type=F32)


def tdot(left, right):
    return lax.dot_general(left, right, (((0,), (0,)), ((), ())), preferred_element_type=F32)


def rdot(left, right):
    return lax.dot_general(left, right, (((1,), (1,)), ((), ())), preferred_element_type=F32)


def loop(count, body):
    def step(index, carry):
        body(index)
        return carry

    lax.fori_loop(0, count, step, 0)


def line_position():
    me = lax.axis_index("ctx")
    return me, me // 2, me % 2, lax.axis_size("ctx") // 2


def send(source, target, send_sem, recv_sem, axis, index):
    return pltpu.make_async_remote_copy(
        src_ref=source,
        dst_ref=target,
        send_sem=send_sem,
        recv_sem=recv_sem,
        device_id={axis: index},
        device_id_type=MESH,
    )


def line_barrier():
    me, chip, core, chips = line_position()
    barrier = pltpu.get_barrier_semaphore()

    def greet(index):
        pl.semaphore_signal(barrier, inc=1, device_id={"ctx": index}, device_id_type=MESH)

    greet(me + 1 - 2 * core)

    @pl.when(chip > 0)
    def _():
        greet(me - 2)

    @pl.when(chip < chips - 1)
    def _():
        greet(me + 2)

    peers = 1 + (chip > 0).astype(jnp.int32) + (chip < chips - 1).astype(jnp.int32)
    pl.semaphore_wait(barrier, peers)


def peers_of(axis):
    me, size = lax.axis_index(axis), lax.axis_size(axis)
    return size - 1, lambda i: (me + i + 1) % size, lambda i: (me + size - i - 1) % size


def full_barrier():
    barrier = pltpu.get_barrier_semaphore()
    total = 0
    for axis in ("fsdp", "ctx"):
        count, ahead, _ = peers_of(axis)
        loop(
            count,
            lambda i, axis=axis, ahead=ahead: pl.semaphore_signal(
                barrier, inc=1, device_id={axis: ahead(i)}, device_id_type=MESH
            ),
        )
        total += count
    pl.semaphore_wait(barrier, total)


def gather_scratch(chips):
    return [pltpu.SemaphoreType.DMA((chips,)) for _ in range(6)]


class Gather:
    def __init__(self, land, sems, consume=None):
        self.land = land
        self.sems = sems
        self.consume = consume
        self.me, self.chip, self.core, self.chips = line_position()

    def right(self, step, source):
        ref = self.land.at[2 * source + self.core]
        return send(ref, ref, self.sems[0].at[step], self.sems[1].at[step], "ctx", self.me + 2)

    def left(self, step, source):
        ref = self.land.at[2 * source + self.core]
        return send(ref, ref, self.sems[2].at[step], self.sems[3].at[step], "ctx", self.me - 2)

    def across(self, source, core):
        ref = self.land.at[2 * source + core]
        other = self.me + 1 - 2 * self.core
        return send(ref, ref, self.sems[4].at[source], self.sems[5].at[source], "ctx", other)

    def step(self, step):
        self.move(step)
        self.use(step)

    def move(self, step):
        chip, core, chips = self.chip, self.core, self.chips
        low, high = chip - step, chip + step
        has_low = low >= 0
        has_high = jnp.logical_and(high < chips, step > 0)

        @pl.when(jnp.logical_and(has_low, step > 0))
        def _():
            self.right(step - 1, low).wait_recv()

        @pl.when(jnp.logical_and(has_low, chip < chips - 1))
        def _():
            self.right(step, low).start()

        @pl.when(has_high)
        def _():
            self.left(step - 1, high).wait_recv()

        @pl.when(jnp.logical_and(high < chips, chip > 0))
        def _():
            self.left(step, high).start()

        @pl.when(has_low)
        def _():
            self.across(low, core).start()

        @pl.when(has_high)
        def _():
            self.across(high, core).start()

    def use(self, step):
        chip, core, chips = self.chip, self.core, self.chips
        low, high = chip - step, chip + step

        def one(kind):
            upward = kind % 2
            crossed = kind // 2
            source = jnp.where(upward == 1, high, low)
            valid = jnp.where(upward == 1, jnp.logical_and(high < chips, step > 0), low >= 0)
            parity = jnp.where(crossed == 1, 1 - core, core)

            @pl.when(valid)
            def _():
                @pl.when(crossed == 1)
                def _():
                    self.across(source, parity).wait_recv()

                if self.consume is not None:
                    self.consume(2 * source + parity)

        loop(4, one)

    def finish(self):
        chip, core, chips = self.chip, self.core, self.chips

        def one(step):
            @pl.when(jnp.logical_and(chip - step >= 0, chip < chips - 1))
            def _():
                self.right(step, chip - step).wait_send()

            @pl.when(jnp.logical_and(chip + step < chips, chip > 0))
            def _():
                self.left(step, chip + step).wait_send()

            self.across(step, core).wait_send()

        loop(chips, one)


def scatter_scratch(chips, rows):
    buffers = [VMEM((count, CHUNKS, rows, WIDE), BF16) for count in (chips + 1, 2, chips)]
    return buffers + [pltpu.SemaphoreType.DMA((chips, CHUNKS)) for _ in range(6)]


class Scatter:
    def __init__(self, scratch, produce, total, ready=None):
        self.ready = ready
        self.line, self.out, self.other = scratch[:3]
        self.sems = scratch[3:]
        self.produce = produce
        self.total = total
        self.me, self.chip, self.core, self.chips = line_position()


    def right(self, step, chunk):
        ref = self.line.at[step, chunk]
        sems = self.sems
        return send(ref, ref, sems[0].at[step, chunk], sems[1].at[step, chunk], "ctx", self.me + 2)

    def left(self, step, chunk):
        ref = self.line.at[self.chips - step, chunk]
        sems = self.sems
        return send(ref, ref, sems[2].at[step, chunk], sems[3].at[step, chunk], "ctx", self.me - 2)

    def across(self, target, chunk, slot=0):
        sems = self.sems
        return send(
            self.out.at[slot, chunk],
            self.other.at[target, chunk],
            sems[4].at[target, chunk],
            sems[5].at[target, chunk],
            "ctx",
            self.me + 1 - 2 * self.core,
        )

    def begin(self):
        def clear(index):
            slot, chunk = index // CHUNKS, index % CHUNKS
            at_left = jnp.logical_and(self.chip == 0, slot < self.chips)
            at_right = jnp.logical_and(self.chip == self.chips - 1, slot > 0)

            @pl.when(jnp.logical_or(at_left, at_right))
            def _():
                self.line[slot, chunk] = jnp.zeros(self.line.shape[2:], BF16)

        loop((self.chips + 1) * CHUNKS, clear)

    def when_right(self, time):
        return jnp.logical_and(time >= self.chip, time < self.chips - 1)

    def when_left(self, time):
        return jnp.logical_and(time >= self.chips - 1 - self.chip, time < self.chips - 1)

    def prepare(self, time):
        chip, chips = self.chip, self.chips

        def cross(target, slot, before, used):
            if self.ready is not None:
                self.ready(target)

            def one(chunk):
                @pl.when(used)
                def _():
                    self.across(before, chunk, slot).wait_send()

                piece = 2 * target + 1 - self.core
                self.out[slot, chunk] = self.produce(piece, chunk).astype(BF16)
                self.across(target, chunk, slot).start()

            loop(CHUNKS, one)

        @pl.when(self.when_right(time))
        def _():
            target = chips - 1 - time + chip
            cross(target, 0, target + 1, time > chip)

        @pl.when(self.when_left(time))
        def _():
            target = time - (chips - 1 - chip)
            cross(target, 1, target - 1, target > 0)

        @pl.when(time == chips - 1)
        def _():
            cross(chip, 0, chip + 1, chip < chips - 1)

    def step(self, time):
        chip, core, chips = self.chip, self.core, self.chips

        @pl.when(self.when_right(time))
        def _():
            step = time - chip
            target = chips - 1 - step

            def one(chunk):
                self.across(target, chunk).wait_recv()

                @pl.when(chip > 0)
                def _():
                    self.right(step, chunk).wait_recv()

                value = self.produce(2 * target + core, chunk) + self.other[target, chunk].astype(F32)
                value = value + self.line[step, chunk].astype(F32)
                self.line[step, chunk] = value.astype(BF16)
                self.right(step, chunk).start()

            loop(CHUNKS, one)

        @pl.when(self.when_left(time))
        def _():
            step = time - (chips - 1 - chip)

            def one(chunk):
                self.across(step, chunk).wait_recv()

                @pl.when(chip < chips - 1)
                def _():
                    self.left(step, chunk).wait_recv()

                value = self.produce(2 * step + core, chunk) + self.other[step, chunk].astype(F32)
                value = value + self.line[chips - step, chunk].astype(F32)
                self.line[chips - step, chunk] = value.astype(BF16)
                self.left(step, chunk).start()

            loop(CHUNKS, one)

    def finish(self):
        chip, core, chips = self.chip, self.core, self.chips
        last = chips - 1 - chip

        def one(chunk):
            self.across(chip, chunk).wait_recv()
            value = self.produce(2 * chip + core, chunk) + self.other[chip, chunk].astype(F32)

            @pl.when(chip > 0)
            def _():
                self.right(last, chunk).wait_recv()

            @pl.when(chip < chips - 1)
            def _():
                self.left(chip, chunk).wait_recv()

            value = value + self.line[last, chunk].astype(F32)
            value = value + self.line[chips - chip, chunk].astype(F32)
            self.total[:, pl.ds(pl.multiple_of(chunk * WIDE, WIDE), WIDE)] = value

        loop(CHUNKS, one)

        def drain(index):
            step, chunk = index // CHUNKS, index % CHUNKS

            @pl.when(step < last)
            def _():
                self.right(step, chunk).wait_send()

            @pl.when(step < chip)
            def _():
                self.left(step, chunk).wait_send()

            @pl.when(jnp.logical_or(step == chip, step == chip - 1))
            def _():
                self.across(step, chunk, jnp.where(step == chip, 0, 1)).wait_send()

        loop(chips * CHUNKS, drain)


def tile(index, size):
    return pl.ds(pl.multiple_of(index * size, size), size)


def row_blocks(rows, body, size=32):
    def one(index):
        body(pl.ds(pl.multiple_of(index * size, size), size))

    loop(rows // size, one)


def inverse_norm(value):
    return lax.rsqrt(jnp.mean(value * value, axis=-1, keepdims=True) + EPS)


def params(identity, megabytes):
    return pltpu.CompilerParams(
        collective_id=identity,
        has_side_effects=True,
        vmem_limit_bytes=megabytes * 1024 * 1024,
    )


def cost(microseconds):
    return pl.CostEstimate(
        flops=int(microseconds * 1.15e9), bytes_accessed=1024, transcendentals=0
    )


class FsdpSum:
    def __init__(self, grad, arrived, send_sems, recv_sems, own=None):
        self.grad, self.arrived = grad, arrived
        self.own = grad.at[lax.axis_index("fsdp")] if own is None else own
        self.sems = send_sems, recv_sems
        self.peers, self.ahead, _ = peers_of("fsdp")

    def copy(self, i):
        target = self.ahead(i)
        return send(
            self.grad.at[target], self.arrived.at[i], self.sems[0].at[i], self.sems[1].at[i], "fsdp", target
        )

    def start(self):
        loop(self.peers, lambda i: self.copy(i).start())

    def arrive(self):
        loop(self.peers, lambda i: self.copy(i).wait_recv())

    def collect(self, target):
        self.arrive()

        def add(block):
            value = self.own[block, :].astype(F32)
            for i in range(self.peers):
                value = value + self.arrived[i, block].astype(F32)
            target[block, :] = value.astype(BF16)

        row_blocks(self.own.shape[0], add)

    def finish(self):
        loop(self.peers, lambda i: self.copy(i).wait_send())


def fsdp_scratch(shards, rows, width):
    return [VMEM((shards - 1, rows, width), BF16)] + [pltpu.SemaphoreType.DMA((shards,))] * 2


def sine_cosine(angle):
    count = jnp.floor(angle * 0.6366197723675814 + 0.5)
    rest = angle - count * 1.5703125
    rest = rest - count * 4.837512969970703e-4
    rest = rest - count * 7.549789948768648e-8
    square = rest * rest
    sine = -1.9515295891e-4 * square + 8.3321608736e-3
    sine = rest + rest * square * (sine * square - 1.6666654611e-1)
    cosine = 2.443315711809948e-5 * square - 1.388731625493765e-3
    cosine = 1.0 - 0.5 * square + square * square * (cosine * square + 4.166664568298827e-2)
    quarter = jnp.bitwise_and(count.astype(jnp.int32), 3)
    odd = jnp.bitwise_and(quarter, 1) == 1
    sine, cosine = jnp.where(odd, cosine, sine), jnp.where(odd, sine, cosine)
    sine = jnp.where(quarter >= 2, -sine, sine)
    cosine = jnp.where(jnp.logical_or(quarter == 1, quarter == 2), -cosine, cosine)
    return sine, cosine


class Shares:
    def __init__(self, source, target_of, own_sem, sems):
        self.source, self.target_of = source, target_of
        self.own_sem, self.sems = own_sem, sems
        self.peers, self.ahead, self.behind = peers_of("fsdp")
        self.shard = lax.axis_index("fsdp")

    def copy(self, i, owner):
        sems = self.sems
        target = self.target_of(owner)
        return send(self.source, target, sems[0].at[i], sems[1].at[i], "fsdp", self.ahead(i))

    def own(self):
        return pltpu.make_async_copy(self.source, self.target_of(self.shard), self.own_sem)

    def start(self):
        loop(self.peers, lambda i: self.copy(i, self.shard).start())
        self.own().start()

    def arrive(self):
        self.own().wait()
        loop(self.peers, lambda i: self.copy(i, self.behind(i)).wait_recv())

    def finish(self):
        loop(self.peers, lambda i: self.copy(i, self.shard).wait_send())


def shares_scratch(count, shards):
    return [pltpu.SemaphoreType.DMA((count,))] + [pltpu.SemaphoreType.DMA((shards,))] * (2 * count)


def copy_in(source, target, sem):
    copy = pltpu.make_async_copy(source, target, sem)
    copy.start()
    return copy


QUERY_TILE = 256
KEY_TILE = 512


def reach(index, tokens):
    return jnp.minimum((index + 2) * QUERY_TILE + KEY_TILE - 1, tokens) // KEY_TILE


def head_norm(value, gain, cosine, sine):
    normed = value * inverse_norm(value) * gain
    return normed * cosine + pltpu.roll(normed, HEAD_SIZE // 2, 1) * sine


def forward_kernel(heads, *refs):
    x, grad, gains, token_info, freq = refs[:5]
    sources, refs = refs[5:12], refs[12:]
    normed_land, grad_land, two_land, activation, back = refs[:5]
    proj, cosine, sine, queries, keys, values, context, inverse = refs[5:13]
    middle, gain_rows, all_gains, all_tokens = refs[13:17]
    head_weight, out_weight, pair_weight, down_weight = refs[17:21]
    refs = refs[21:]
    pair, down, own, piece_in, grad_in, act_out, back_out, total, sems = refs[:9]
    small, refs = refs[9:13], refs[13:]
    share_own, share_sems, refs = refs[0], refs[1:15], refs[15:]
    first_sems, grad_sems, two_sems, scratch = refs[:6], refs[6:12], refs[12:18], refs[18:]
    me, _, _, chips = line_position()
    shard = lax.axis_index("fsdp")
    shards, ahead, behind = peers_of("fsdp")
    parts, next_part, past_part = peers_of("ctx")
    count = x.shape[0]
    tokens = 2 * chips * count
    width = heads * HEAD_SIZE
    feed_width = down.shape[0]
    rows = D // (shards + 1)
    lanes = rows // 128
    key_head = me // (2 * chips // KEY_VALUE_HEADS)

    def gain_copy(i, slot):
        return send(gains, all_gains.at[slot], small[0].at[i], small[1].at[i], "fsdp", ahead(i))

    def token_copy(i, slot):
        return send(token_info, all_tokens.at[slot], small[2].at[i], small[3].at[i], "ctx", next_part(i))

    def by_row(target, at, size):
        return lambda owner: target.at[tile(owner, rows), pl.ds(at, size)]

    def by_column(target):
        return lambda owner: target.at[:, tile(owner, rows)]

    places = (
        (sources[0].at[:, tile(me, width)], by_row(head_weight, 0, width)),
        (sources[1].at[:, tile(key_head, HEAD_SIZE)], by_row(head_weight, width, HEAD_SIZE)),
        (sources[2].at[:, tile(key_head, HEAD_SIZE)], by_row(head_weight, width + HEAD_SIZE, HEAD_SIZE)),
        (sources[3].at[tile(me, width), :], by_column(out_weight)),
        (sources[4].at[:, tile(me, feed_width)], by_row(pair, 0, feed_width)),
        (sources[5].at[:, tile(me, feed_width)], by_row(pair, feed_width, feed_width)),
        (sources[6].at[tile(me, feed_width), :], by_column(down)),
    )
    shares = [
        Shares(source, target_of, share_own.at[i], share_sems[2 * i : 2 * i + 2])
        for i, (source, target_of) in enumerate(places)
    ]

    full_barrier()
    loop(shards, lambda i: gain_copy(i, shard).start())
    loop(parts, lambda i: token_copy(i, me).start())
    for share in shares[:4]:
        share.start()
    grad_copy = copy_in(grad, grad_land.at[me], sems.at[0])
    all_gains[shard] = gains[...]
    all_tokens[me] = token_info[...]
    loop(shards, lambda i: gain_copy(i, behind(i)).wait_recv())
    for kind in range(2):
        for owner in range(shards + 1):
            for j in range(lanes):
                at = owner * rows + j * 128
                gain_rows[kind : kind + 1, at : at + 128] = all_gains[
                    owner, kind * lanes + j : kind * lanes + j + 1, :
                ]
    size = HEAD_SIZE // (shards + 1)
    for kind in range(2):
        gain_rows[2 + kind : 3 + kind, 0:HEAD_SIZE] = jnp.concatenate(
            [
                all_gains[
                    owner, 2 * lanes : 2 * lanes + 1, kind * size : (kind + 1) * size
                ]
                for owner in range(shards + 1)
            ],
            axis=1,
        )

    def norm(block):
        value = x[block, :].astype(F32)
        own[block, :] = (value * inverse_norm(value) * gain_rows[0:1, :]).astype(BF16)

    row_blocks(count, norm)
    own_copy = copy_in(own, normed_land.at[me], sems.at[1])
    own_copy.wait()

    def column(piece, row):
        values_in_lanes = all_tokens[piece, row : row + 1, :].astype(F32)
        return jnp.broadcast_to(values_in_lanes, (128, count)).T

    def project(piece):
        copy = copy_in(normed_land.at[piece], piece_in, sems.at[1])
        block = tile(piece, count)
        s, c = sine_cosine(column(piece, 0) * freq[0:1, :])
        lane = lax.broadcasted_iota(jnp.int32, s.shape, 1)
        s = jnp.where(lane < HEAD_SIZE // 2, -s, s)
        cosine[block, :] = c
        sine[block, :] = s
        copy.wait()
        proj[piece] = dot(piece_in[...], head_weight[...])

        def turned(at, row):
            return head_norm(proj[piece, :, at : at + HEAD_SIZE], gain_rows[row : row + 1, 0:HEAD_SIZE], c, s)

        for h in range(heads):
            at = h * HEAD_SIZE
            queries[block, at : at + HEAD_SIZE] = (turned(at, 2) * HEAD_SIZE ** (-0.5)).astype(BF16)
        keys[block, :] = turned(width, 3).astype(BF16)
        values[block, :] = proj[piece, :, width + HEAD_SIZE : width + 2 * HEAD_SIZE].astype(BF16)

    first_gather = Gather(normed_land, first_sems, project)
    grad_gather = Gather(grad_land, grad_sems)
    first_gather.move(0)
    loop(parts, lambda i: token_copy(i, past_part(i)).wait_recv())

    def first_step(step):
        first_gather.move(step + 1)

        @pl.when(step == 0)
        def _():
            for share in shares[:4]:
                share.arrive()
            for share in shares[4:]:
                share.start()

        first_gather.use(step)

    loop(chips - 1, first_step)
    grad_copy.wait()
    grad_gather.step(0)
    first_gather.use(chips - 1)

    def attend(index):
        block = tile(index, QUERY_TILE)
        query_ids = column(index, 1)[:, 0:1]
        for h in range(heads):
            head = slice(h * HEAD_SIZE, (h + 1) * HEAD_SIZE)
            query = queries[block, head]

            def one(key_tile, carry):
                sums, total = carry
                span = tile(key_tile, KEY_TILE)
                scores = rdot(query, keys[span, :])
                key_ids = jnp.concatenate(
                    [all_tokens[key_tile * each + j, 1:2, :] for j in range(each)], axis=1
                ).astype(F32)
                expon = jnp.where(key_ids <= query_ids, jnp.exp(scores), 0.0)
                sums = sums + dot(expon.astype(BF16), values[span, :])
                return sums, total + jnp.sum(expon, axis=1, keepdims=True)

            each = KEY_TILE // count
            start = (jnp.zeros((QUERY_TILE, HEAD_SIZE), F32), jnp.zeros((QUERY_TILE, 1), F32))
            sums, total = lax.fori_loop(0, reach(index, tokens), one, start)
            scale = 1.0 / total
            context[block, head] = (sums * scale).astype(BF16)
            inverse[h : h + 1, block] = jnp.broadcast_to(scale, (QUERY_TILE, HEAD_SIZE)).T[0:1, :]

    def ready(target):
        each = 2 * count // QUERY_TILE
        loop(each, lambda i: attend(target * each + i))

    def produce(piece, chunk):
        return dot(context[tile(piece, count), :], out_weight[:, tile(chunk, WIDE)])

    scatter = Scatter(scratch, produce, total, ready)
    scatter.begin()
    scatter.prepare(0)

    def scatter_step(time):
        scatter.step(time)
        scatter.prepare(time + 1)
        grad_gather.step(time + 1)

    loop(chips - 1, scatter_step)
    scatter.finish()

    def norm_two(block):
        value = x[block, :].astype(F32) + total[block, :]
        middle[block, :] = value
        own[block, :] = (value * inverse_norm(value) * gain_rows[1:2, :]).astype(BF16)

    row_blocks(count, norm_two)
    two_copy = copy_in(own, two_land.at[me], sems.at[1])
    two_copy.wait()
    for share in shares[4:]:
        share.arrive()
    outs = [
        copy_in(head_weight, refs_out, sems.at[2 + i])
        for i, (head_weight, refs_out) in enumerate(((pair, pair_weight), (down, down_weight)))
    ]
    feed_size = 256 if feed_width % 256 == 0 else 128

    def act_copy(piece):
        return pltpu.make_async_copy(act_out, activation.at[piece], sems.at[6])

    def back_copy(piece):
        return pltpu.make_async_copy(back_out, back.at[piece], sems.at[7])

    def feed(piece):
        copies = (
            copy_in(two_land.at[piece], piece_in, sems.at[4]),
            copy_in(grad_land.at[piece], grad_in, sems.at[5]),
        )
        for copy in copies:
            copy.wait()

        @pl.when(piece != me)
        def _():
            act_copy(piece).wait()
            back_copy(piece).wait()

        def one(index):
            def columns(kind):
                return pl.ds(pl.multiple_of(kind * feed_width + index * feed_size, 128), feed_size)

            gate = dot(piece_in[...], pair[:, columns(0)])
            up = dot(piece_in[...], pair[:, columns(1)])
            grad_act = rdot(grad_in[...], down[tile(index, feed_size), :])
            sigma = 1.0 / (1.0 + jnp.exp(-gate))
            act_out[:, columns(0)] = (gate * sigma * up).astype(BF16)
            back_out[:, columns(0)] = (
                grad_act * up * sigma * (1.0 + gate * (1.0 - sigma))
            ).astype(BF16)
            back_out[:, columns(1)] = (grad_act * gate * sigma).astype(BF16)

        loop(feed_width // feed_size, one)
        act_copy(piece).start()
        back_copy(piece).start()

    two_gather = Gather(two_land, two_sems, feed)
    loop(chips, two_gather.step)
    act_copy(0).wait()
    back_copy(0).wait()
    first_gather.finish()
    grad_gather.finish()
    two_gather.finish()
    for out in outs:
        out.wait()
    for share in shares:
        share.finish()
    loop(shards, lambda i: gain_copy(i, shard).wait_send())
    loop(parts, lambda i: token_copy(i, me).wait_send())


def forward(hidden, grad, gains, token_info, freq, weights, shards, parts, heads):
    count = hidden.shape[0]
    tokens = parts * count
    width = heads * HEAD_SIZE
    total_width = width + 2 * HEAD_SIZE
    feed_width = FF // parts
    chips = parts // 2
    shape = jax.ShapeDtypeStruct
    return pl.pallas_call(
        functools.partial(forward_kernel, heads),
        out_shape=(
            shape((parts, count, D), BF16),
            shape((parts, count, D), BF16),
            shape((parts, count, D), BF16),
            shape((parts, count, feed_width), BF16),
            shape((parts, count, 2 * feed_width), BF16),
            shape((parts, count, total_width), F32),
            shape((tokens, HEAD_SIZE), F32),
            shape((tokens, HEAD_SIZE), F32),
            shape((tokens, width), BF16),
            shape((tokens, HEAD_SIZE), BF16),
            shape((tokens, HEAD_SIZE), BF16),
            shape((tokens, width), BF16),
            shape((8, tokens), F32),
            shape((count, D), F32),
            shape((8, D), F32),
            shape((shards, *gains.shape), F32),
            shape((parts, *token_info.shape), jnp.int32),
            shape((D, total_width), BF16),
            shape((width, D), BF16),
            shape((D, 2 * feed_width), BF16),
            shape((feed_width, D), BF16),
        ),
        in_specs=[WHOLE] * 5 + [HBM] * 7,
        out_specs=(HBM,) * 5 + (WHOLE,) * 14 + (HBM,) * 2,
        scratch_shapes=[
            VMEM((D, 2 * feed_width), BF16),
            VMEM((feed_width, D), BF16),
            VMEM((count, D), BF16),
            VMEM((count, D), BF16),
            VMEM((count, D), BF16),
            VMEM((count, feed_width), BF16),
            VMEM((count, 2 * feed_width), BF16),
            VMEM((count, D), F32),
            pltpu.SemaphoreType.DMA((8,)),
        ]
        + [pltpu.SemaphoreType.DMA((shards,))] * 2
        + [pltpu.SemaphoreType.DMA((parts,))] * 2
        + shares_scratch(7, shards)
        + gather_scratch(chips)
        + gather_scratch(chips)
        + gather_scratch(chips)
        + scatter_scratch(chips, count),
        compiler_params=params(0, 63),
        cost_estimate=cost(280),
        name="forward",
    )(hidden, grad, gains, token_info, freq, *weights)


def slab_size(parts):
    return 256 if parts <= 8 else 128


class Slabs:
    def __init__(self, sources, buffers, out, target, sems, products):
        self.sources, self.buffers, self.out, self.target = sources, buffers, out, target
        self.sems, self.products = sems, products
        self.size = out.shape[0]
        self.count = D // self.size

    def copies(self, index):
        slot = index % 2
        return [
            pltpu.make_async_copy(
                source.at[:, :, tile(index, self.size)], buffer.at[slot], self.sems.at[2 * i + slot]
            )
            for i, (source, buffer) in enumerate(zip(self.sources, self.buffers))
        ]

    def fetch(self, index):
        for copy in self.copies(index):
            copy.start()

    def leave(self, index):
        each = self.target.shape[1] // self.size
        target = self.target.at[index // each, tile(index % each, self.size), :]
        return pltpu.make_async_copy(self.out, target, self.sems.at[2 * len(self.sources)])

    def run(self, begin, end):
        def one(index, carry):
            for copy in self.copies(index):
                copy.wait()

            @pl.when(index + 1 < self.count)
            def _():
                self.fetch(index + 1)

            @pl.when(index > 0)
            def _():
                self.leave(index - 1).wait()

            at = 0
            for left, right in self.products(index % 2):
                left = left.reshape(-1, self.size)
                right = right.reshape(left.shape[0], -1)
                width = right.shape[1]
                self.out[:, at : at + width] = tdot(left, right).astype(BF16)
                at += width
            self.leave(index).start()

            @pl.when(index == self.count - 1)
            def _():
                self.leave(index).wait()

            return carry

        lax.fori_loop(begin, end, one, 0)


def rms_back(value, gain, grad):
    inverse = inverse_norm(value)
    scaled = grad * gain
    inner = jnp.mean(scaled * value, axis=-1, keepdims=True)
    terms = grad * value * inverse
    return inverse * scaled - value * (inverse * inverse * inverse * inner), terms


def turn_kernel(*refs):
    back, pair_weight, down_weight, activation, out_weight = refs[:5]
    middle, grad, gain_rows, down_grad, normed = refs[5:10]
    grad_middle, land, gain_sum, down_land, context_grad, hidden, pair_in, pair_grad = refs[10:18]
    weight, data, total, low, own_down, sems = refs[18:24]
    slab, slab_out, slab_sems = refs[24:27]
    down_refs, down_sems, gather_sems = refs[27:30], refs[30:36], refs[36:42]
    pair_sems, first_scratch, second_scratch = refs[42:44], refs[44:53], refs[53:]
    me, _, _, chips = line_position()
    width = back.shape[2] // 2
    weight_copy = copy_in(pair_weight, weight, sems.at[0])
    data_copy = copy_in(back, data, sems.at[1])
    own_copy = copy_in(down_grad.at[lax.axis_index("fsdp")], own_down, sems.at[3])

    def produce(piece, chunk):
        return rdot(data[piece], weight[pl.ds(pl.multiple_of(chunk * WIDE, WIDE), WIDE), :])

    each = 2 * width // WIDE

    def down_block(chunk):
        return tile(chunk // each, width), tile(chunk % each, WIDE)

    def down_copy(chunk):
        source = down_weight.at[:, tile(chunk, WIDE)]
        return pltpu.make_async_copy(source, weight.at[down_block(chunk)], sems.at[5 + chunk])

    def produce_hidden(piece, chunk):
        return dot(data[piece, :, :width], weight[down_block(chunk)])

    def consume(piece):
        copy = copy_in(land.at[piece], low, sems.at[4])
        copy.wait()
        context_grad[piece] = rdot(low[...], out_weight[...]).astype(BF16)

    def products(slot):
        return ((slab[slot], data[...]),)

    slabs = Slabs((normed,), (slab,), slab_out, pair_grad, slab_sems, products)
    down = FsdpSum(down_grad, *down_refs, own=own_down)
    pair = FsdpSum(pair_grad, pair_in, *pair_sems, own=own_down)
    down_gather = Gather(down_land, down_sems)
    gather = Gather(land, gather_sems, consume)
    scatter = Scatter(first_scratch, produce, total)
    hidden_scatter = Scatter(second_scratch, produce_hidden, total)
    scatter.begin()
    hidden_scatter.begin()
    full_barrier()
    down.start()
    slabs.fetch(0)
    weight_copy.wait()
    data_copy.wait()
    scatter.prepare(0)

    def step(time):
        scatter.step(time)
        scatter.prepare(time + 1)

        @pl.when(time == 1)
        def _():
            own_copy.wait()
            down.collect(own_down)
            copy = copy_in(own_down, down_land.at[me], sems.at[3])
            copy.wait()

        @pl.when(time >= 1)
        def _():
            down_gather.step(time - 1)

        @pl.when(time < 3)
        def _():
            slabs.run(time * slabs.count // 3, (time + 1) * slabs.count // 3)

        @pl.when(time == 2)
        def _():
            pair.start()

    loop(chips - 1, step)
    scatter.finish()
    for chunk in range(CHUNKS):
        down_copy(chunk).start()
    act_copy = copy_in(activation, data.at[:, :, pl.ds(0, width)], sems.at[1])
    gain_sum[...] = jnp.zeros_like(gain_sum)

    def norm(block):
        through, terms = rms_back(middle[block, :], gain_rows[1:2, :], total[block, :])
        value = grad[block, :].astype(F32) + through
        grad_middle[block, :] = value
        low[block, :] = value.astype(BF16)
        gain_sum[0:1, :] += jnp.sum(terms, axis=0, keepdims=True)

    row_blocks(middle.shape[0], norm)
    low_copy = copy_in(low, land.at[me], sems.at[3])
    low_copy.wait()
    gather.step(0)
    for chunk in range(CHUNKS):
        down_copy(chunk).wait()
    act_copy.wait()
    hidden_scatter.prepare(0)

    def turn_step(time):
        hidden_scatter.step(time)
        hidden_scatter.prepare(time + 1)
        gather.step(time + 1)

        @pl.when(time < 2)
        def _():
            down_gather.step(chips - 2 + time)

    loop(chips - 1, turn_step)
    hidden_scatter.finish()
    gather.finish()
    down_gather.finish()
    down.finish()
    pair.arrive()
    pair.finish()

    def add(block):
        hidden[block, :] = (middle[block, :] + total[block, :]).astype(BF16)

    row_blocks(middle.shape[0], add)


def turn(back, pair_weight, down_weight, activation, out_weight, middle, grad, gain_rows, down_grad, normed):
    parts, count, feed_width = activation.shape
    shards, rows, _ = down_grad.shape
    width = out_weight.shape[0]
    return pl.pallas_call(
        turn_kernel,
        out_shape=(
            jax.ShapeDtypeStruct((count, D), F32),
            jax.ShapeDtypeStruct((parts, count, D), BF16),
            jax.ShapeDtypeStruct((8, D), F32),
            jax.ShapeDtypeStruct((parts, rows, feed_width), BF16),
            jax.ShapeDtypeStruct((parts, count, width), BF16),
            jax.ShapeDtypeStruct((count, D), BF16),
            jax.ShapeDtypeStruct((shards - 1, rows, 2 * feed_width), BF16),
            jax.ShapeDtypeStruct((shards, rows, 2 * feed_width), BF16),
        ),
        in_specs=[HBM] * 4 + [WHOLE] * 4 + [HBM] * 2,
        out_specs=(WHOLE, HBM, WHOLE, HBM, WHOLE, WHOLE, HBM, HBM),
        scratch_shapes=[
            VMEM((D, 2 * feed_width), BF16),
            VMEM((parts, count, 2 * feed_width), BF16),
            VMEM((count, D), F32),
            VMEM((count, D), BF16),
            VMEM((rows, feed_width), BF16),
            pltpu.SemaphoreType.DMA((5 + CHUNKS,)),
            VMEM((2, parts, count, slab_size(parts)), BF16),
            VMEM((slab_size(parts), 2 * feed_width), BF16),
            pltpu.SemaphoreType.DMA((3,)),
        ]
        + fsdp_scratch(shards, rows, feed_width)
        + gather_scratch(parts // 2)
        + gather_scratch(parts // 2)
        + [pltpu.SemaphoreType.DMA((shards,))] * 2
        + scatter_scratch(parts // 2, count)
        + scatter_scratch(parts // 2, count),
        compiler_params=params(3, 63),
        cost_estimate=cost(185),
        name="turn",
    )(
        back,
        pair_weight,
        down_weight,
        activation,
        out_weight,
        middle,
        grad,
        gain_rows,
        down_grad,
        normed,
    )


def last_kernel(*refs):
    back, weights, x, grad_middle, gain_rows, gain_two, gain_heads, context, normed, low = refs[:10]
    hidden, gain_out, head_grad, query_out, key_out, value_out, out_out = refs[10:17]
    weight, weight_sem, total, gain_one, pack, pack_in, shard_sum, shard_in, land = refs[17:26]
    slabs_in, slab_out, slab_sems, own_head = refs[26:28], refs[28], refs[29], refs[30]
    stages, stage_sems, refs = refs[31:35], refs[35], refs[36:]
    small, head_refs, gather_sems, scratch = refs[:4], refs[4:7], refs[7:13], refs[13:]
    me, _, _, chips = line_position()
    shard = lax.axis_index("fsdp")
    shards, ahead, _ = peers_of("fsdp")
    parts, next_part, _ = peers_of("ctx")
    copy = copy_in(weights, weight, weight_sem)

    def produce(piece, chunk):
        return rdot(back[piece], weight[pl.ds(pl.multiple_of(chunk * WIDE, WIDE), WIDE), :])

    def products(slot):
        return (slabs_in[0][slot], back[...]), (slabs_in[1][slot], context[...])

    width = context.shape[2]

    def stage_copies(piece):
        targets = (
            query_out.at[:, tile(piece, width)],
            key_out.at[:, tile(piece, HEAD_SIZE)],
            value_out.at[:, tile(piece, HEAD_SIZE)],
            out_out.at[tile(piece, width), :],
        )
        return [
            pltpu.make_async_copy(stage, target, stage_sems.at[i])
            for i, (stage, target) in enumerate(zip(stages, targets))
        ]

    def consume(piece):
        @pl.when(piece != me)
        def _():
            for copy in stage_copies(piece):
                copy.wait()

        second = width + HEAD_SIZE
        third = second + HEAD_SIZE
        stages[0][...] = land[piece, :, :width].astype(F32)
        stages[1][...] = land[piece, :, width:second].astype(F32)
        stages[2][...] = land[piece, :, second:third].astype(F32)
        stages[3][...] = land[piece, :, third:].astype(F32).T
        for copy in stage_copies(piece):
            copy.start()

    slabs = Slabs((normed, low), slabs_in, slab_out, head_grad, slab_sems, products)
    heads = FsdpSum(head_grad, *head_refs, own=own_head)
    scatter = Scatter(scratch, produce, total)
    gather = Gather(land, gather_sems, consume)
    scatter.begin()
    slabs.fetch(0)
    full_barrier()
    copy.wait()
    scatter.prepare(0)

    def step(time):
        scatter.step(time)
        scatter.prepare(time + 1)

        @pl.when(time == 0)
        def _():
            slabs.run(0, slabs.count)
            heads.start()
            own = copy_in(head_grad.at[shard], own_head, weight_sem)
            own.wait()

        @pl.when(time == 1)
        def _():
            heads.collect(land.at[me])

        @pl.when(time >= 1)
        def _():
            gather.step(time - 1)

    loop(chips - 1, step)
    scatter.finish()
    gather.step(chips - 2)
    gain_one[...] = jnp.zeros_like(gain_one)

    def norm(block):
        through, terms = rms_back(x[block, :].astype(F32), gain_rows[0:1, :], total[block, :])
        hidden[block, :] = grad_middle[block, :] + through
        gain_one[0:1, :] += jnp.sum(terms, axis=0, keepdims=True)

    row_blocks(x.shape[0], norm)

    rows = D // (shards + 1)
    lanes = rows // 128
    pack[...] = jnp.zeros_like(pack)
    for owner in range(shards + 1):
        for j in range(lanes):
            at = owner * rows + j * 128
            pack[owner, j : j + 1, :] = gain_one[0:1, at : at + 128]
            pack[owner, lanes + j : lanes + j + 1, :] = gain_two[0:1, at : at + 128]
        pack[owner, 2 * lanes : 2 * lanes + 2, :] = gain_heads[0:2, :]

    def pack_copy(i):
        return send(pack.at[ahead(i)], pack_in.at[i], small[0].at[i], small[1].at[i], "fsdp", ahead(i))

    def sum_copy(i):
        return send(shard_sum, shard_in.at[i], small[2].at[i], small[3].at[i], "ctx", next_part(i))

    loop(shards, lambda i: pack_copy(i).start())
    shard_sum[...] = pack[shard]

    def add_pack(i):
        pack_copy(i).wait_recv()
        shard_sum[...] += pack_in[i]

    loop(shards, add_pack)
    loop(parts, lambda i: sum_copy(i).start())
    gain_out[...] = shard_sum[...]

    def add_sum(i):
        sum_copy(i).wait_recv()
        gain_out[...] += shard_in[i]

    loop(parts, add_sum)
    gather.step(chips - 1)
    gather.finish()
    for stage in stage_copies(0):
        stage.wait()
    heads.finish()
    loop(shards, lambda i: pack_copy(i).wait_send())
    loop(parts, lambda i: sum_copy(i).wait_send())


def last(back, weights, hidden, grad_middle, gain_rows, gain_two, gain_heads, context, normed, low, shards):
    parts, count, width = back.shape
    rows = D // shards
    query_width = context.shape[2]
    head_width = width + query_width
    return pl.pallas_call(
        last_kernel,
        out_shape=(
            jax.ShapeDtypeStruct((count, D), F32),
            jax.ShapeDtypeStruct((16, 128), F32),
            jax.ShapeDtypeStruct((shards, rows, head_width), BF16),
            jax.ShapeDtypeStruct((rows, parts * query_width), F32),
            jax.ShapeDtypeStruct((rows, parts * HEAD_SIZE), F32),
            jax.ShapeDtypeStruct((rows, parts * HEAD_SIZE), F32),
            jax.ShapeDtypeStruct((parts * query_width, rows), F32),
        ),
        in_specs=[WHOLE, HBM] + [WHOLE] * 6 + [HBM] * 2,
        out_specs=(WHOLE,) * 2 + (HBM,) * 5,
        scratch_shapes=[
            VMEM((D, width), BF16),
            pltpu.SemaphoreType.DMA,
            VMEM((count, D), F32),
            VMEM((8, D), F32),
            VMEM((shards, 16, 128), F32),
            VMEM((shards, 16, 128), F32),
            VMEM((16, 128), F32),
            VMEM((parts, 16, 128), F32),
            VMEM((parts, rows, head_width), BF16),
            VMEM((2, parts, count, slab_size(parts)), BF16),
            VMEM((2, parts, count, slab_size(parts)), BF16),
            VMEM((slab_size(parts), head_width), BF16),
            pltpu.SemaphoreType.DMA((5,)),
            VMEM((rows, head_width), BF16),
            VMEM((rows, query_width), F32),
            VMEM((rows, HEAD_SIZE), F32),
            VMEM((rows, HEAD_SIZE), F32),
            VMEM((query_width, rows), F32),
            pltpu.SemaphoreType.DMA((4,)),
        ]
        + [pltpu.SemaphoreType.DMA((shards,))] * 2
        + [pltpu.SemaphoreType.DMA((parts,))] * 2
        + fsdp_scratch(shards, rows, head_width)
        + gather_scratch(parts // 2)
        + scatter_scratch(parts // 2, count),
        compiler_params=params(5, 60),
        cost_estimate=cost(90),
        name="last",
    )(back, weights, hidden, grad_middle, gain_rows, gain_two, gain_heads, context, normed, low)


def attention_back_kernel(heads, *refs):
    queries, keys, values, out_grad, inverse, context, proj, cosine, sine, gain = refs[:10]
    id_column, id_row, back, gain_sum, key_grad, value_grad, query_grad = refs[10:]
    tokens = proj.shape[0]
    key_at = heads * HEAD_SIZE
    key_grad[...] = jnp.zeros_like(key_grad)
    value_grad[...] = jnp.zeros_like(value_grad)
    gain_sum[...] = jnp.zeros_like(gain_sum)

    def through(block, lanes, grad, row):
        turned = pltpu.roll(grad, HEAD_SIZE // 2, 1)
        unrotated = grad * cosine[block, :] - turned * sine[block, :]
        result, terms = rms_back(proj[block, lanes], gain[row : row + 1, :], unrotated)
        back[block, lanes] = result.astype(BF16)
        gain_sum[row : row + 1, :] += jnp.sum(terms, axis=0, keepdims=True)

    def attend(index):
        block = pl.ds(pl.multiple_of(index * QUERY_TILE, QUERY_TILE), QUERY_TILE)
        query_ids = id_row[0:1, block]
        for h in range(heads):
            lanes = slice(h * HEAD_SIZE, (h + 1) * HEAD_SIZE)
            query = queries[block, lanes]
            grad = out_grad[block, lanes]
            scale = inverse[h : h + 1, block]
            products = grad.astype(F32) * context[block, lanes].astype(F32)
            shift = lax.dot_general(
                jnp.ones((8, HEAD_SIZE), F32),
                products,
                (((1,), (1,)), ((), ())),
                precision=lax.Precision.HIGHEST,
                preferred_element_type=F32,
            )[0:1, :]
            query_grad[...] = jnp.zeros_like(query_grad)

            def one(tile):
                span = pl.ds(pl.multiple_of(tile * KEY_TILE, KEY_TILE), KEY_TILE)
                key = keys[span, :]
                scores = rdot(key, query)
                probs = jnp.where(id_column[span, :] <= query_ids, jnp.exp(scores) * scale, 0.0)
                grad_scores = (probs * (rdot(values[span, :], grad) - shift)).astype(BF16)
                value_grad[span, :] += dot(probs.astype(BF16), grad)
                key_grad[span, :] += dot(grad_scores, query)
                query_grad[...] += tdot(grad_scores, key)

            loop(reach(index, tokens), one)
            through(block, lanes, query_grad[...] * HEAD_SIZE ** (-0.5), 0)

    loop(tokens // QUERY_TILE, attend)

    def finish(index):
        block = pl.ds(pl.multiple_of(index * QUERY_TILE, QUERY_TILE), QUERY_TILE)
        through(block, slice(key_at, key_at + HEAD_SIZE), key_grad[block, :], 1)
        back[block, key_at + HEAD_SIZE : key_at + 2 * HEAD_SIZE] = value_grad[block, :].astype(BF16)

    loop(tokens // QUERY_TILE, finish)


def attention_back(heads, *operands):
    tokens = operands[0].shape[0]
    width = heads * HEAD_SIZE
    return pl.pallas_call(
        functools.partial(attention_back_kernel, heads),
        out_shape=(
            jax.ShapeDtypeStruct((tokens, width + 2 * HEAD_SIZE), BF16),
            jax.ShapeDtypeStruct((8, HEAD_SIZE), F32),
        ),
        in_specs=[WHOLE] * len(operands),
        out_specs=(WHOLE,) * 2,
        scratch_shapes=[
            VMEM((tokens, HEAD_SIZE), F32),
            VMEM((tokens, HEAD_SIZE), F32),
            VMEM((QUERY_TILE, HEAD_SIZE), F32),
        ],
        compiler_params=pltpu.CompilerParams(vmem_limit_bytes=48 * 1024 * 1024),
        cost_estimate=cost(38),
        name="attention_back",
    )(*operands)


def spread_pair_kernel(width, source, gate, up):
    gate[...] = source[0, :, :width].astype(F32)
    up[...] = source[0, :, width:].astype(F32)


def spread_pair(stacked):
    parts, rows, total = stacked.shape
    width = total // 2
    across = jax.ShapeDtypeStruct((rows, parts * width), F32)
    return pl.pallas_call(
        functools.partial(spread_pair_kernel, width),
        out_shape=(across, across),
        grid=(parts,),
        in_specs=[pl.BlockSpec((1, rows, total), lambda i: (i, 0, 0))],
        out_specs=(pl.BlockSpec((rows, width), lambda i: (0, i)),) * 2,
        compiler_params=pltpu.CompilerParams(vmem_limit_bytes=60 * 1024 * 1024),
        name="spread_pair",
    )(stacked)


def spread_turned_kernel(source, target):
    target[...] = source[0].astype(F32).T


def spread_turned(stacked):
    parts, rows, width = stacked.shape
    return pl.pallas_call(
        spread_turned_kernel,
        out_shape=jax.ShapeDtypeStruct((parts * width, rows), F32),
        grid=(parts,),
        in_specs=[pl.BlockSpec((1, rows, width), lambda i: (i, 0, 0))],
        out_specs=pl.BlockSpec((width, rows), lambda i: (i, 0)),
        compiler_params=pltpu.CompilerParams(vmem_limit_bytes=60 * 1024 * 1024),
        name="spread_turned",
    )(stacked)


def by_row(array):
    return with_layout_constraint(array, Layout(major_to_minor=(0, 1)))


def local(
    hidden_in,
    weight_query,
    key_weight_matrix,
    weight_value,
    weight_out,
    weight_gate,
    weight_up,
    weight_down,
    gain_attention,
    gain_feed,
    gain_query,
    gain_key,
    positions,
    token_block_index,
    grad_out,
):
    parts = lax.axis_size("ctx")
    shards = lax.axis_size("fsdp")
    shard = lax.axis_index("fsdp")
    heads = QUERY_HEADS // parts
    sharers = parts // KEY_VALUE_HEADS
    width = heads * HEAD_SIZE
    feed_width = FF // parts
    rows = D // shards
    head_rows = HEAD_SIZE // shards
    count = hidden_in.shape[1]
    tokens = parts * count

    def gather_parts(piece):
        return lax.all_gather(piece, "ctx", axis=0)

    own_gains = jnp.concatenate([gain_attention, gain_feed, gain_query, gain_key]).astype(F32)
    own_gains = jnp.pad(own_gains, (0, 2048 - own_gains.shape[0])).reshape(16, 128)
    own_tokens = jnp.pad(jnp.stack([positions[0], token_block_index[0]]), ((0, 6), (0, 0)))
    half = HEAD_SIZE // 2
    freq = THETA ** (-(jnp.arange(half).astype(F32) * 2.0 / HEAD_SIZE))
    freq = jnp.broadcast_to(jnp.concatenate([freq, freq]), (8, HEAD_SIZE))
    hidden, grad = hidden_in[0], grad_out[0]
    weights = (
        weight_query,
        key_weight_matrix,
        weight_value,
        weight_out,
        weight_gate,
        weight_up,
        weight_down,
    )
    (
        normed_all,
        grad_all,
        normed_two_all,
        activation,
        back,
        proj,
        cosine,
        sine,
        queries,
        keys,
        values,
        context,
        inverse,
        middle,
        gain_rows,
        gains,
        whole,
        heads_weight,
        out_weight,
        pair_weight,
        down_weight,
    ) = forward(hidden, grad, own_gains, own_tokens, freq, weights, shards, parts, heads)
    head_gains = gain_rows[2:4, :HEAD_SIZE]
    ids = whole[:, 1].reshape(-1)
    id_row, id_column = ids[None, :], ids[:, None]
    proj = proj.reshape(tokens, width + 2 * HEAD_SIZE)

    flat_grad = grad_all.reshape(tokens, D)
    flat_activation = activation.reshape(tokens, feed_width)
    down_grad = by_row(tdot(flat_grad, flat_activation).astype(BF16))
    grad_middle, low_all, gain_two, down_parts, context_grad, hidden_out, pair_in, pair_grad = turn(
        back,
        pair_weight,
        down_weight,
        activation,
        out_weight,
        middle,
        grad,
        gain_rows,
        down_grad.reshape(shards, rows, feed_width),
        normed_two_all,
    )
    own_pair = lax.dynamic_index_in_dim(pair_grad, shard, keepdims=False)
    feed_shard = (own_pair.astype(F32) + jnp.sum(pair_in.astype(F32), axis=0)).astype(BF16)
    context_grad, feed_shard, down_parts = lax.optimization_barrier(
        (context_grad, feed_shard, down_parts)
    )
    feed_parts = gather_parts(feed_shard)
    context_grad = context_grad.reshape(tokens, width)
    grad_qkv, gain_heads = attention_back(
        heads,
        queries,
        keys,
        values,
        context_grad,
        inverse,
        context,
        proj,
        cosine,
        sine,
        head_gains,
        id_column,
        id_row,
    )
    grad_down = spread_turned(down_parts)
    grad_qkv, grad_down = lax.optimization_barrier((grad_qkv, grad_down))
    grad_hidden, gain_sums, _, grad_query, grad_key, grad_value, grad_out_weight = last(
        grad_qkv.reshape(parts, count, -1),
        heads_weight,
        hidden,
        grad_middle,
        gain_rows,
        gain_two,
        gain_heads,
        context.reshape(parts, count, width),
        normed_all,
        low_all,
        shards,
    )

    gain_sums = gain_sums.reshape(-1)
    grad_gate, grad_up = spread_pair(feed_parts)
    if sharers > 1:
        grad_key, grad_value = (
            part.reshape(rows, KEY_VALUE_HEADS, sharers, HEAD_SIZE).sum(axis=2).reshape(rows, -1)
            for part in (grad_key, grad_value)
        )
    return (
        hidden_out[None],
        grad_hidden[None],
        grad_query,
        grad_key,
        grad_value,
        grad_out_weight,
        grad_gate,
        grad_up,
        grad_down,
        gain_sums[:rows],
        gain_sums[rows : 2 * rows],
        lax.dynamic_slice_in_dim(gain_sums, 2 * rows + shard * head_rows, head_rows),
        lax.dynamic_slice_in_dim(gain_sums, 2 * rows + HEAD_SIZE + shard * head_rows, head_rows),
    )


def solution(mesh):
    tokens = P("fsdp", "ctx", None)
    by_rows = P("fsdp", None)
    by_columns = P(None, "fsdp")
    per_token = P("fsdp", "ctx")
    vector = P("fsdp")
    weights = (by_rows, by_rows, by_rows, by_columns, by_rows, by_rows, by_columns)
    return jax.shard_map(
        local,
        mesh=mesh,
        in_specs=(tokens, *weights, vector, vector, vector, vector, per_token, per_token, tokens),
        out_specs=(tokens, tokens, *weights, vector, vector, vector, vector),
        check_vma=False,
    )
```

```python
import functools

import jax
import jax.numpy as jnp
from jax import lax
from jax.experimental import pallas as pl
from jax.experimental.layout import Layout, with_layout_constraint
from jax.experimental.pallas import tpu as pltpu
from jax.sharding import PartitionSpec as P

D = 2048
QUERY_HEADS = 16
KEY_VALUE_HEADS = 8
HEAD_SIZE = 128
FF = 6144
EPS = 1e-06
THETA = 1000000.0
F32 = jnp.float32
BF16 = jnp.bfloat16
MESH = pl.DeviceIdType.MESH
VMEM = pltpu.VMEM
WHOLE = pl.BlockSpec(memory_space=pltpu.VMEM)
HBM = pl.BlockSpec(memory_space=pl.ANY)
CHUNKS = 4
WIDE = D // CHUNKS


def dot(left, right):
    return jnp.dot(left, right, preferred_element_type=F32)


def tdot(left, right):
    return lax.dot_general(left, right, (((0,), (0,)), ((), ())), preferred_element_type=F32)


def rdot(left, right):
    return lax.dot_general(left, right, (((1,), (1,)), ((), ())), preferred_element_type=F32)


def loop(count, body):
    def step(index, carry):
        body(index)
        return carry

    lax.fori_loop(0, count, step, 0)


def line_position():
    me = lax.axis_index("ctx")
    return me, me // 2, me % 2, lax.axis_size("ctx") // 2


def send(source, target, send_sem, recv_sem, axis, index):
    return pltpu.make_async_remote_copy(
        src_ref=source,
        dst_ref=target,
        send_sem=send_sem,
        recv_sem=recv_sem,
        device_id={axis: index},
        device_id_type=MESH,
    )


def line_barrier():
    me, chip, core, chips = line_position()
    barrier = pltpu.get_barrier_semaphore()

    def greet(index):
        pl.semaphore_signal(barrier, inc=1, device_id={"ctx": index}, device_id_type=MESH)

    greet(me + 1 - 2 * core)

    @pl.when(chip > 0)
    def _():
        greet(me - 2)

    @pl.when(chip < chips - 1)
    def _():
        greet(me + 2)

    peers = 1 + (chip > 0).astype(jnp.int32) + (chip < chips - 1).astype(jnp.int32)
    pl.semaphore_wait(barrier, peers)


def peers_of(axis):
    me, size = lax.axis_index(axis), lax.axis_size(axis)
    return size - 1, lambda i: (me + i + 1) % size, lambda i: (me + size - i - 1) % size


def full_barrier():
    barrier = pltpu.get_barrier_semaphore()
    total = 0
    for axis in ("fsdp", "ctx"):
        count, ahead, _ = peers_of(axis)
        loop(
            count,
            lambda i, axis=axis, ahead=ahead: pl.semaphore_signal(
                barrier, inc=1, device_id={axis: ahead(i)}, device_id_type=MESH
            ),
        )
        total += count
    pl.semaphore_wait(barrier, total)


def gather_scratch(chips):
    return [pltpu.SemaphoreType.DMA((chips,)) for _ in range(6)]


class Gather:
    def __init__(self, land, sems, consume=None, part=None):
        self.part = part
        self.land = land
        self.sems = sems
        self.consume = consume
        self.me, self.chip, self.core, self.chips = line_position()

    def place(self, piece):
        return self.land.at[piece] if self.part is None else self.land.at[piece, self.part]

    def right(self, step, source):
        ref = self.place(2 * source + self.core)
        return send(ref, ref, self.sems[0].at[step], self.sems[1].at[step], "ctx", self.me + 2)

    def left(self, step, source):
        ref = self.place(2 * source + self.core)
        return send(ref, ref, self.sems[2].at[step], self.sems[3].at[step], "ctx", self.me - 2)

    def across(self, source, core):
        ref = self.place(2 * source + core)
        other = self.me + 1 - 2 * self.core
        return send(ref, ref, self.sems[4].at[source], self.sems[5].at[source], "ctx", other)

    def step(self, step):
        self.move(step)
        self.use(step)

    def move(self, step):
        chip, core, chips = self.chip, self.core, self.chips
        low, high = chip - step, chip + step
        has_low = low >= 0
        has_high = jnp.logical_and(high < chips, step > 0)

        @pl.when(jnp.logical_and(has_low, step > 0))
        def _():
            self.right(step - 1, low).wait_recv()

        @pl.when(jnp.logical_and(has_low, chip < chips - 1))
        def _():
            self.right(step, low).start()

        @pl.when(has_high)
        def _():
            self.left(step - 1, high).wait_recv()

        @pl.when(jnp.logical_and(high < chips, chip > 0))
        def _():
            self.left(step, high).start()

        @pl.when(has_low)
        def _():
            self.across(low, core).start()

        @pl.when(has_high)
        def _():
            self.across(high, core).start()

    def use(self, step):
        chip, core, chips = self.chip, self.core, self.chips
        low, high = chip - step, chip + step

        def one(kind):
            upward = kind % 2
            crossed = kind // 2
            source = jnp.where(upward == 1, high, low)
            valid = jnp.where(upward == 1, jnp.logical_and(high < chips, step > 0), low >= 0)
            parity = jnp.where(crossed == 1, 1 - core, core)

            @pl.when(valid)
            def _():
                @pl.when(crossed == 1)
                def _():
                    self.across(source, parity).wait_recv()

                if self.consume is not None:
                    self.consume(2 * source + parity)

        loop(4, one)

    def finish(self):
        chip, core, chips = self.chip, self.core, self.chips

        def one(step):
            @pl.when(jnp.logical_and(chip - step >= 0, chip < chips - 1))
            def _():
                self.right(step, chip - step).wait_send()

            @pl.when(jnp.logical_and(chip + step < chips, chip > 0))
            def _():
                self.left(step, chip + step).wait_send()

            self.across(step, core).wait_send()

        loop(chips, one)


def scatter_scratch(chips, rows):
    buffers = [VMEM((count, CHUNKS, rows, WIDE), BF16) for count in (chips + 1, 2, chips)]
    return buffers + [pltpu.SemaphoreType.DMA((chips, CHUNKS)) for _ in range(6)]


class Scatter:
    def __init__(self, scratch, produce, total, ready=None):
        self.ready = ready
        self.line, self.out, self.other = scratch[:3]
        self.sems = scratch[3:]
        self.produce = produce
        self.total = total
        self.me, self.chip, self.core, self.chips = line_position()


    def right(self, step, chunk):
        ref = self.line.at[step, chunk]
        sems = self.sems
        return send(ref, ref, sems[0].at[step, chunk], sems[1].at[step, chunk], "ctx", self.me + 2)

    def left(self, step, chunk):
        ref = self.line.at[self.chips - step, chunk]
        sems = self.sems
        return send(ref, ref, sems[2].at[step, chunk], sems[3].at[step, chunk], "ctx", self.me - 2)

    def across(self, target, chunk, slot=0):
        sems = self.sems
        return send(
            self.out.at[slot, chunk],
            self.other.at[target, chunk],
            sems[4].at[target, chunk],
            sems[5].at[target, chunk],
            "ctx",
            self.me + 1 - 2 * self.core,
        )

    def begin(self):
        def clear(index):
            slot, chunk = index // CHUNKS, index % CHUNKS
            at_left = jnp.logical_and(self.chip == 0, slot < self.chips)
            at_right = jnp.logical_and(self.chip == self.chips - 1, slot > 0)

            @pl.when(jnp.logical_or(at_left, at_right))
            def _():
                self.line[slot, chunk] = jnp.zeros(self.line.shape[2:], BF16)

        loop((self.chips + 1) * CHUNKS, clear)

    def when_right(self, time):
        return jnp.logical_and(time >= self.chip, time < self.chips - 1)

    def when_left(self, time):
        return jnp.logical_and(time >= self.chips - 1 - self.chip, time < self.chips - 1)

    def prepare(self, time):
        chip, chips = self.chip, self.chips

        def cross(target, slot, before, used):
            if self.ready is not None:
                self.ready(target)

            def one(chunk):
                @pl.when(used)
                def _():
                    self.across(before, chunk, slot).wait_send()

                piece = 2 * target + 1 - self.core
                self.out[slot, chunk] = self.produce(piece, chunk).astype(BF16)
                self.across(target, chunk, slot).start()

            loop(CHUNKS, one)

        @pl.when(self.when_right(time))
        def _():
            target = chips - 1 - time + chip
            cross(target, 0, target + 1, time > chip)

        @pl.when(self.when_left(time))
        def _():
            target = time - (chips - 1 - chip)
            cross(target, 1, target - 1, target > 0)

        @pl.when(time == chips - 1)
        def _():
            cross(chip, 0, chip + 1, chip < chips - 1)

    def step(self, time):
        chip, core, chips = self.chip, self.core, self.chips

        @pl.when(self.when_right(time))
        def _():
            step = time - chip
            target = chips - 1 - step

            def one(chunk):
                self.across(target, chunk).wait_recv()

                @pl.when(chip > 0)
                def _():
                    self.right(step, chunk).wait_recv()

                value = self.produce(2 * target + core, chunk) + self.other[target, chunk].astype(F32)
                value = value + self.line[step, chunk].astype(F32)
                self.line[step, chunk] = value.astype(BF16)
                self.right(step, chunk).start()

            loop(CHUNKS, one)

        @pl.when(self.when_left(time))
        def _():
            step = time - (chips - 1 - chip)

            def one(chunk):
                self.across(step, chunk).wait_recv()

                @pl.when(chip < chips - 1)
                def _():
                    self.left(step, chunk).wait_recv()

                value = self.produce(2 * step + core, chunk) + self.other[step, chunk].astype(F32)
                value = value + self.line[chips - step, chunk].astype(F32)
                self.line[chips - step, chunk] = value.astype(BF16)
                self.left(step, chunk).start()

            loop(CHUNKS, one)

    def finish(self):
        chip, core, chips = self.chip, self.core, self.chips
        last = chips - 1 - chip

        def one(chunk):
            self.across(chip, chunk).wait_recv()
            value = self.produce(2 * chip + core, chunk) + self.other[chip, chunk].astype(F32)

            @pl.when(chip > 0)
            def _():
                self.right(last, chunk).wait_recv()

            @pl.when(chip < chips - 1)
            def _():
                self.left(chip, chunk).wait_recv()

            value = value + self.line[last, chunk].astype(F32)
            value = value + self.line[chips - chip, chunk].astype(F32)
            self.total[:, pl.ds(pl.multiple_of(chunk * WIDE, WIDE), WIDE)] = value

        loop(CHUNKS, one)

        def drain(index):
            step, chunk = index // CHUNKS, index % CHUNKS

            @pl.when(step < last)
            def _():
                self.right(step, chunk).wait_send()

            @pl.when(step < chip)
            def _():
                self.left(step, chunk).wait_send()

            @pl.when(jnp.logical_or(step == chip, step == chip - 1))
            def _():
                self.across(step, chunk, jnp.where(step == chip, 0, 1)).wait_send()

        loop(chips * CHUNKS, drain)


def tile(index, size):
    return pl.ds(pl.multiple_of(index * size, size), size)


def row_blocks(rows, body, size=32):
    def one(index):
        body(pl.ds(pl.multiple_of(index * size, size), size))

    loop(rows // size, one)


def inverse_norm(value):
    return lax.rsqrt(jnp.mean(value * value, axis=-1, keepdims=True) + EPS)


def params(identity, megabytes):
    return pltpu.CompilerParams(
        collective_id=identity,
        has_side_effects=True,
        vmem_limit_bytes=megabytes * 1024 * 1024,
    )


def cost(microseconds):
    return pl.CostEstimate(
        flops=int(microseconds * 1.15e9), bytes_accessed=1024, transcendentals=0
    )


class FsdpSum:
    def __init__(self, grad, arrived, send_sems, recv_sems, own=None, part=slice(None)):
        self.grad, self.arrived, self.part = grad, arrived, part
        self.own = grad.at[lax.axis_index("fsdp")] if own is None else own
        self.sems = send_sems, recv_sems
        self.peers, self.ahead, _ = peers_of("fsdp")

    def copy(self, i):
        target = self.ahead(i)
        return send(
            self.grad.at[target, self.part], self.arrived.at[i], self.sems[0].at[i], self.sems[1].at[i], "fsdp", target
        )

    def start(self):
        loop(self.peers, lambda i: self.copy(i).start())

    def arrive(self):
        loop(self.peers, lambda i: self.copy(i).wait_recv())

    def collect(self, target):
        self.arrive()

        def add(block):
            value = self.own[block, :].astype(F32)
            for i in range(self.peers):
                value = value + self.arrived[i, block].astype(F32)
            target[block, :] = value.astype(BF16)

        row_blocks(self.own.shape[0], add)

    def finish(self):
        loop(self.peers, lambda i: self.copy(i).wait_send())


def fsdp_scratch(shards, rows, width):
    return [VMEM((shards - 1, rows, width), BF16)] + [pltpu.SemaphoreType.DMA((shards,))] * 2


def sine_cosine(angle):
    count = jnp.floor(angle * 0.6366197723675814 + 0.5)
    rest = angle - count * 1.5703125
    rest = rest - count * 4.837512969970703e-4
    rest = rest - count * 7.549789948768648e-8
    square = rest * rest
    sine = -1.9515295891e-4 * square + 8.3321608736e-3
    sine = rest + rest * square * (sine * square - 1.6666654611e-1)
    cosine = 2.443315711809948e-5 * square - 1.388731625493765e-3
    cosine = 1.0 - 0.5 * square + square * square * (cosine * square + 4.166664568298827e-2)
    quarter = jnp.bitwise_and(count.astype(jnp.int32), 3)
    odd = jnp.bitwise_and(quarter, 1) == 1
    sine, cosine = jnp.where(odd, cosine, sine), jnp.where(odd, sine, cosine)
    sine = jnp.where(quarter >= 2, -sine, sine)
    cosine = jnp.where(jnp.logical_or(quarter == 1, quarter == 2), -cosine, cosine)
    return sine, cosine


class Shares:
    def __init__(self, source, target_of, own_sem, sems):
        self.source, self.target_of = source, target_of
        self.own_sem, self.sems = own_sem, sems
        self.peers, self.ahead, self.behind = peers_of("fsdp")
        self.shard = lax.axis_index("fsdp")

    def copy(self, i, owner):
        sems = self.sems
        target = self.target_of(owner)
        return send(self.source, target, sems[0].at[i], sems[1].at[i], "fsdp", self.ahead(i))

    def own(self):
        return pltpu.make_async_copy(self.source, self.target_of(self.shard), self.own_sem)

    def start(self):
        loop(self.peers, lambda i: self.copy(i, self.shard).start())
        self.own().start()

    def arrive(self):
        self.own().wait()
        loop(self.peers, lambda i: self.copy(i, self.behind(i)).wait_recv())

    def finish(self):
        loop(self.peers, lambda i: self.copy(i, self.shard).wait_send())


def shares_scratch(count, shards):
    return [pltpu.SemaphoreType.DMA((count,))] + [pltpu.SemaphoreType.DMA((shards,))] * (2 * count)


def copy_in(source, target, sem):
    copy = pltpu.make_async_copy(source, target, sem)
    copy.start()
    return copy


QUERY_TILE = 256
KEY_TILE = 512


def reach(index, tokens):
    return jnp.minimum((index + 2) * QUERY_TILE + KEY_TILE - 1, tokens) // KEY_TILE


def head_norm(value, gain, cosine, sine):
    normed = value * inverse_norm(value) * gain
    return normed * cosine + pltpu.roll(normed, HEAD_SIZE // 2, 1) * sine


def forward_kernel(heads, *refs):
    x, grad, gains, token_info, freq = refs[:5]
    sources, refs = refs[5:12], refs[12:]
    normed_land, grad_land, two_land, activation, back = refs[:5]
    proj, cosine, sine, queries, keys, values, context, inverse = refs[5:13]
    middle, gain_rows, all_gains, all_tokens = refs[13:17]
    head_weight, out_weight, pair_weight, down_weight = refs[17:21]
    refs = refs[21:]
    pair, down, own, piece_in, grad_in, act_out, back_out, total, sems = refs[:9]
    small, refs = refs[9:13], refs[13:]
    share_own, share_sems, refs = refs[0], refs[1:15], refs[15:]
    first_sems, grad_sems, two_sems, scratch = refs[:6], refs[6:12], refs[12:18], refs[18:]
    me, _, _, chips = line_position()
    shard = lax.axis_index("fsdp")
    shards, ahead, behind = peers_of("fsdp")
    parts, next_part, past_part = peers_of("ctx")
    count = x.shape[0]
    tokens = 2 * chips * count
    width = heads * HEAD_SIZE
    feed_width = down.shape[0]
    rows = D // (shards + 1)
    lanes = rows // 128
    key_head = me // (2 * chips // KEY_VALUE_HEADS)

    def gain_copy(i, slot):
        return send(gains, all_gains.at[slot], small[0].at[i], small[1].at[i], "fsdp", ahead(i))

    def token_copy(i, slot):
        return send(token_info, all_tokens.at[slot], small[2].at[i], small[3].at[i], "ctx", next_part(i))

    def by_row(target, at, size):
        return lambda owner: target.at[tile(owner, rows), pl.ds(at, size)]

    def by_column(target):
        return lambda owner: target.at[:, tile(owner, rows)]

    places = (
        (sources[0].at[:, tile(me, width)], by_row(head_weight, 0, width)),
        (sources[1].at[:, tile(key_head, HEAD_SIZE)], by_row(head_weight, width, HEAD_SIZE)),
        (sources[2].at[:, tile(key_head, HEAD_SIZE)], by_row(head_weight, width + HEAD_SIZE, HEAD_SIZE)),
        (sources[3].at[tile(me, width), :], by_column(out_weight)),
        (sources[4].at[:, tile(me, feed_width)], by_row(pair, 0, feed_width)),
        (sources[5].at[:, tile(me, feed_width)], by_row(pair, feed_width, feed_width)),
        (sources[6].at[tile(me, feed_width), :], by_column(down)),
    )
    shares = [
        Shares(source, target_of, share_own.at[i], share_sems[2 * i : 2 * i + 2])
        for i, (source, target_of) in enumerate(places)
    ]

    full_barrier()
    loop(shards, lambda i: gain_copy(i, shard).start())
    loop(parts, lambda i: token_copy(i, me).start())
    for share in shares[:4]:
        share.start()
    grad_copy = copy_in(grad, grad_land.at[me], sems.at[0])
    all_gains[shard] = gains[...]
    all_tokens[me] = token_info[...]
    loop(shards, lambda i: gain_copy(i, behind(i)).wait_recv())
    for kind in range(2):
        for owner in range(shards + 1):
            for j in range(lanes):
                at = owner * rows + j * 128
                gain_rows[kind : kind + 1, at : at + 128] = all_gains[
                    owner, kind * lanes + j : kind * lanes + j + 1, :
                ]
    size = HEAD_SIZE // (shards + 1)
    for kind in range(2):
        gain_rows[2 + kind : 3 + kind, 0:HEAD_SIZE] = jnp.concatenate(
            [
                all_gains[
                    owner, 2 * lanes : 2 * lanes + 1, kind * size : (kind + 1) * size
                ]
                for owner in range(shards + 1)
            ],
            axis=1,
        )

    def norm(block):
        value = x[block, :].astype(F32)
        own[block, :] = (value * inverse_norm(value) * gain_rows[0:1, :]).astype(BF16)

    row_blocks(count, norm)
    own_copy = copy_in(own, normed_land.at[me], sems.at[1])
    own_copy.wait()

    def column(piece, row):
        values_in_lanes = all_tokens[piece, row : row + 1, :].astype(F32)
        return jnp.broadcast_to(values_in_lanes, (128, count)).T

    def project(piece):
        copy = copy_in(normed_land.at[piece], piece_in, sems.at[1])
        block = tile(piece, count)
        s, c = sine_cosine(column(piece, 0) * freq[0:1, :])
        lane = lax.broadcasted_iota(jnp.int32, s.shape, 1)
        s = jnp.where(lane < HEAD_SIZE // 2, -s, s)
        cosine[block, :] = c
        sine[block, :] = s
        copy.wait()
        proj[piece] = dot(piece_in[...], head_weight[...])

        def turned(at, row):
            return head_norm(proj[piece, :, at : at + HEAD_SIZE], gain_rows[row : row + 1, 0:HEAD_SIZE], c, s)

        for h in range(heads):
            at = h * HEAD_SIZE
            queries[block, at : at + HEAD_SIZE] = (turned(at, 2) * HEAD_SIZE ** (-0.5)).astype(BF16)
        keys[block, :] = turned(width, 3).astype(BF16)
        values[block, :] = proj[piece, :, width + HEAD_SIZE : width + 2 * HEAD_SIZE].astype(BF16)

    first_gather = Gather(normed_land, first_sems, project)
    grad_gather = Gather(grad_land, grad_sems)
    first_gather.move(0)
    loop(parts, lambda i: token_copy(i, past_part(i)).wait_recv())

    def first_step(step):
        first_gather.move(step + 1)

        @pl.when(step == 0)
        def _():
            for share in shares[:4]:
                share.arrive()
            for share in shares[4:]:
                share.start()

        first_gather.use(step)

    loop(chips - 1, first_step)
    grad_copy.wait()
    grad_gather.step(0)
    first_gather.use(chips - 1)

    def attend(index):
        block = tile(index, QUERY_TILE)
        query_ids = column(index, 1)[:, 0:1]
        for h in range(heads):
            head = slice(h * HEAD_SIZE, (h + 1) * HEAD_SIZE)
            query = queries[block, head]

            def one(key_tile, carry):
                sums, total = carry
                span = tile(key_tile, KEY_TILE)
                scores = rdot(query, keys[span, :])
                key_ids = jnp.concatenate(
                    [all_tokens[key_tile * each + j, 1:2, :] for j in range(each)], axis=1
                ).astype(F32)
                expon = jnp.where(key_ids <= query_ids, jnp.exp(scores), 0.0)
                sums = sums + dot(expon.astype(BF16), values[span, :])
                return sums, total + jnp.sum(expon, axis=1, keepdims=True)

            each = KEY_TILE // count
            start = (jnp.zeros((QUERY_TILE, HEAD_SIZE), F32), jnp.zeros((QUERY_TILE, 1), F32))
            sums, total = lax.fori_loop(0, reach(index, tokens), one, start)
            scale = 1.0 / total
            context[block, head] = (sums * scale).astype(BF16)
            inverse[h : h + 1, block] = jnp.broadcast_to(scale, (QUERY_TILE, HEAD_SIZE)).T[0:1, :]

    def ready(target):
        each = 2 * count // QUERY_TILE
        loop(each, lambda i: attend(target * each + i))

    def produce(piece, chunk):
        return dot(context[tile(piece, count), :], out_weight[:, tile(chunk, WIDE)])

    scatter = Scatter(scratch, produce, total, ready)
    scatter.begin()
    scatter.prepare(0)

    def scatter_step(time):
        scatter.step(time)
        scatter.prepare(time + 1)
        grad_gather.step(time + 1)

    loop(chips - 1, scatter_step)
    scatter.finish()

    def norm_two(block):
        value = x[block, :].astype(F32) + total[block, :]
        middle[block, :] = value
        own[block, :] = (value * inverse_norm(value) * gain_rows[1:2, :]).astype(BF16)

    row_blocks(count, norm_two)
    two_copy = copy_in(own, two_land.at[me], sems.at[1])
    two_copy.wait()
    for share in shares[4:]:
        share.arrive()
    outs = [
        copy_in(head_weight, refs_out, sems.at[2 + i])
        for i, (head_weight, refs_out) in enumerate(((pair, pair_weight), (down, down_weight)))
    ]
    feed_size = 256 if feed_width % 256 == 0 else 128

    def act_copy(piece):
        return pltpu.make_async_copy(act_out, activation.at[piece], sems.at[6])

    def back_copy(piece):
        return pltpu.make_async_copy(back_out, back.at[piece], sems.at[7])

    def feed(piece):
        copies = (
            copy_in(two_land.at[piece], piece_in, sems.at[4]),
            copy_in(grad_land.at[piece], grad_in, sems.at[5]),
        )
        for copy in copies:
            copy.wait()

        @pl.when(piece != me)
        def _():
            act_copy(piece).wait()
            back_copy(piece).wait()

        def one(index):
            def columns(kind):
                return pl.ds(pl.multiple_of(kind * feed_width + index * feed_size, 128), feed_size)

            gate = dot(piece_in[...], pair[:, columns(0)])
            up = dot(piece_in[...], pair[:, columns(1)])
            grad_act = rdot(grad_in[...], down[tile(index, feed_size), :])
            sigma = 1.0 / (1.0 + jnp.exp(-gate))
            act_out[:, columns(0)] = (gate * sigma * up).astype(BF16)
            back_out[:, columns(0)] = (
                grad_act * up * sigma * (1.0 + gate * (1.0 - sigma))
            ).astype(BF16)
            back_out[:, columns(1)] = (grad_act * gate * sigma).astype(BF16)

        loop(feed_width // feed_size, one)
        act_copy(piece).start()
        back_copy(piece).start()

    two_gather = Gather(two_land, two_sems, feed)
    loop(chips, two_gather.step)
    act_copy(0).wait()
    back_copy(0).wait()
    first_gather.finish()
    grad_gather.finish()
    two_gather.finish()
    for out in outs:
        out.wait()
    for share in shares:
        share.finish()
    loop(shards, lambda i: gain_copy(i, shard).wait_send())
    loop(parts, lambda i: token_copy(i, me).wait_send())


def forward(hidden, grad, gains, token_info, freq, weights, shards, parts, heads):
    count = hidden.shape[0]
    tokens = parts * count
    width = heads * HEAD_SIZE
    total_width = width + 2 * HEAD_SIZE
    feed_width = FF // parts
    chips = parts // 2
    shape = jax.ShapeDtypeStruct
    return pl.pallas_call(
        functools.partial(forward_kernel, heads),
        out_shape=(
            shape((parts, count, D), BF16),
            shape((parts, count, D), BF16),
            shape((parts, count, D), BF16),
            shape((parts, count, feed_width), BF16),
            shape((parts, count, 2 * feed_width), BF16),
            shape((parts, count, total_width), F32),
            shape((tokens, HEAD_SIZE), F32),
            shape((tokens, HEAD_SIZE), F32),
            shape((tokens, width), BF16),
            shape((tokens, HEAD_SIZE), BF16),
            shape((tokens, HEAD_SIZE), BF16),
            shape((tokens, width), BF16),
            shape((8, tokens), F32),
            shape((count, D), F32),
            shape((8, D), F32),
            shape((shards, *gains.shape), F32),
            shape((parts, *token_info.shape), jnp.int32),
            shape((D, total_width), BF16),
            shape((width, D), BF16),
            shape((D, 2 * feed_width), BF16),
            shape((feed_width, D), BF16),
        ),
        in_specs=[WHOLE] * 5 + [HBM] * 7,
        out_specs=(HBM,) * 5 + (WHOLE,) * 14 + (HBM,) * 2,
        scratch_shapes=[
            VMEM((D, 2 * feed_width), BF16),
            VMEM((feed_width, D), BF16),
            VMEM((count, D), BF16),
            VMEM((count, D), BF16),
            VMEM((count, D), BF16),
            VMEM((count, feed_width), BF16),
            VMEM((count, 2 * feed_width), BF16),
            VMEM((count, D), F32),
            pltpu.SemaphoreType.DMA((8,)),
        ]
        + [pltpu.SemaphoreType.DMA((shards,))] * 2
        + [pltpu.SemaphoreType.DMA((parts,))] * 2
        + shares_scratch(7, shards)
        + gather_scratch(chips)
        + gather_scratch(chips)
        + gather_scratch(chips)
        + scatter_scratch(chips, count),
        compiler_params=params(0, 63),
        cost_estimate=cost(280),
        name="forward",
    )(hidden, grad, gains, token_info, freq, *weights)


def slab_size(parts):
    return 256 if parts <= 8 else 128


class Slabs:
    def __init__(self, sources, buffers, out, target, sems, products):
        self.sources, self.buffers, self.out, self.target = sources, buffers, out, target
        self.sems, self.products = sems, products
        self.size = out.shape[0]
        self.count = D // self.size

    def copies(self, index):
        slot = index % 2
        return [
            pltpu.make_async_copy(
                source.at[:, :, tile(index, self.size)], buffer.at[slot], self.sems.at[2 * i + slot]
            )
            for i, (source, buffer) in enumerate(zip(self.sources, self.buffers))
        ]

    def fetch(self, index):
        for copy in self.copies(index):
            copy.start()

    def leave(self, index):
        each = self.target.shape[1] // self.size
        target = self.target.at[index // each, tile(index % each, self.size), :]
        return pltpu.make_async_copy(self.out, target, self.sems.at[2 * len(self.sources)])

    def run(self, begin, end):
        def one(index, carry):
            for copy in self.copies(index):
                copy.wait()

            @pl.when(index + 1 < self.count)
            def _():
                self.fetch(index + 1)

            @pl.when(index > 0)
            def _():
                self.leave(index - 1).wait()

            at = 0
            for left, right in self.products(index % 2):
                left = left.reshape(-1, self.size)
                right = right.reshape(left.shape[0], -1)
                width = right.shape[1]
                self.out[:, at : at + width] = tdot(left, right).astype(BF16)
                at += width
            self.leave(index).start()

            @pl.when(index == self.count - 1)
            def _():
                self.leave(index).wait()

            return carry

        lax.fori_loop(begin, end, one, 0)


def rms_back(value, gain, grad):
    inverse = inverse_norm(value)
    scaled = grad * gain
    inner = jnp.mean(scaled * value, axis=-1, keepdims=True)
    terms = grad * value * inverse
    return inverse * scaled - value * (inverse * inverse * inverse * inner), terms


def turn_kernel(*refs):
    back, pair_weight, down_weight, activation, out_weight = refs[:5]
    middle, grad, gain_rows, down_grad, normed = refs[5:10]
    grad_middle, land, gain_sum, down_land, context_grad, hidden, pair_in, pair_grad, pair_sum = refs[10:19]
    weight, data, total, low, own_down, sems = refs[19:25]
    slab, slab_out, slab_sems, sum_sems = refs[25:29]
    down_refs, down_sems = (refs[29:32], refs[32:35]), (refs[35:41], refs[41:47])
    gather_sems, pair_sems, first_scratch, second_scratch = refs[47:53], refs[53:55], refs[55:64], refs[64:]
    me, _, _, chips = line_position()
    width = back.shape[2] // 2
    weight_copy = copy_in(pair_weight, weight, sems.at[0])
    data_copy = copy_in(back, data, sems.at[1])
    own_copy = copy_in(down_grad.at[lax.axis_index("fsdp")], own_down, sems.at[3])

    def produce(piece, chunk):
        return rdot(data[piece], weight[pl.ds(pl.multiple_of(chunk * WIDE, WIDE), WIDE), :])

    each = 2 * width // WIDE

    def down_block(chunk):
        return tile(chunk // each, width), tile(chunk % each, WIDE)

    def down_copy(chunk):
        source = down_weight.at[:, tile(chunk, WIDE)]
        return pltpu.make_async_copy(source, weight.at[down_block(chunk)], sems.at[5 + chunk])

    def produce_hidden(piece, chunk):
        return dot(data[piece, :, :width], weight[down_block(chunk)])

    def consume(piece):
        copy = copy_in(land.at[piece], low, sems.at[4])
        copy.wait()
        context_grad[piece] = rdot(low[...], out_weight[...]).astype(BF16)

    def products(slot):
        return ((slab[slot], data[...]),)

    slabs = Slabs((normed,), (slab,), slab_out, pair_grad, slab_sems, products)
    half = own_down.shape[0] // 2
    halves = [pl.ds(h * half, half) for h in range(2)]
    downs = [
        FsdpSum(down_grad, *down_refs[h], own=own_down.at[halves[h]], part=halves[h]) for h in range(2)
    ]
    down_gathers = [Gather(down_land, down_sems[h], part=halves[h]) for h in range(2)]

    def down_ready(h):
        downs[h].collect(own_down.at[halves[h]])
        copy = copy_in(own_down.at[halves[h]], down_land.at[me, halves[h]], sems.at[3])
        copy.wait()
        down_gathers[h].step(0)

    pair = FsdpSum(pair_grad, pair_in, *pair_sems, own=own_down)
    gather = Gather(land, gather_sems, consume)
    scatter = Scatter(first_scratch, produce, total)
    hidden_scatter = Scatter(second_scratch, produce_hidden, total)
    scatter.begin()
    hidden_scatter.begin()
    full_barrier()
    for down in downs:
        down.start()
    slabs.fetch(0)
    weight_copy.wait()
    data_copy.wait()
    scatter.prepare(0)

    def step(time):
        scatter.step(time)
        scatter.prepare(time + 1)

        @pl.when(time == 0)
        def _():
            own_copy.wait()
            down_ready(0)

        @pl.when(time >= 1)
        def _():
            down_gathers[0].step(time)

        @pl.when(time == 1)
        def _():
            down_ready(1)

        @pl.when(time >= 2)
        def _():
            down_gathers[1].step(time - 1)

        @pl.when(time < 3)
        def _():
            slabs.run(time * slabs.count // 3, (time + 1) * slabs.count // 3)

        @pl.when(time == 2)
        def _():
            pair.start()

    loop(chips - 1, step)
    scatter.finish()
    down_gathers[0].step(chips - 1)
    down_gathers[1].step(chips - 2)
    for chunk in range(CHUNKS):
        down_copy(chunk).start()
    act_copy = copy_in(activation, data.at[:, :, pl.ds(0, width)], sems.at[1])
    gain_sum[...] = jnp.zeros_like(gain_sum)

    def norm(block):
        through, terms = rms_back(middle[block, :], gain_rows[1:2, :], total[block, :])
        value = grad[block, :].astype(F32) + through
        grad_middle[block, :] = value
        low[block, :] = value.astype(BF16)
        gain_sum[0:1, :] += jnp.sum(terms, axis=0, keepdims=True)

    row_blocks(middle.shape[0], norm)
    low_copy = copy_in(low, land.at[me], sems.at[3])
    low_copy.wait()
    gather.step(0)
    for chunk in range(CHUNKS):
        down_copy(chunk).wait()
    act_copy.wait()
    hidden_scatter.prepare(0)

    def add_pairs():
        pair.arrive()
        shard = lax.axis_index("fsdp")
        count, size = slab.shape[2], slab.shape[3]
        per = own_down.shape[0] // count
        tiles = 2 * width // size

        def arrivals(index):
            slot = index % 2
            copies = []
            for i in range(pair.peers + 1):
                source = pair_grad.at[shard] if i == 0 else pair_in.at[i - 1]
                for j in range(per):
                    at = i * per + j
                    block = source.at[pl.ds(j * count, count), tile(index, size)]
                    copies.append(
                        pltpu.make_async_copy(block, slab.at[slot, at], sum_sems.at[slot, at])
                    )
            return copies

        def leave(index):
            slot = index % 2
            return [
                pltpu.make_async_copy(
                    slab.at[slot, j],
                    pair_sum.at[pl.ds(j * count, count), tile(index, size)],
                    sum_sems.at[slot, j],
                )
                for j in range(per)
            ]

        for copy in arrivals(0):
            copy.start()

        def one(index):
            @pl.when(index > 0)
            def _():
                for copy in leave(index - 1):
                    copy.wait()

            @pl.when(index + 1 < tiles)
            def _():
                for copy in arrivals(index + 1):
                    copy.start()

            for copy in arrivals(index):
                copy.wait()
            slot = index % 2
            for j in range(per):
                value = slab[slot, j].astype(F32)
                for i in range(1, pair.peers + 1):
                    value = value + slab[slot, i * per + j].astype(F32)
                slab[slot, j] = value.astype(BF16)
            for copy in leave(index):
                copy.start()

        loop(tiles, one)
        for copy in leave(tiles - 1):
            copy.wait()

    def turn_step(time):
        hidden_scatter.step(time)
        hidden_scatter.prepare(time + 1)

        @pl.when(time == chips - 2)
        def _():
            add_pairs()

        gather.step(time + 1)

        @pl.when(time == 1)
        def _():
            down_gathers[1].step(chips - 1)

    loop(chips - 1, turn_step)
    hidden_scatter.finish()
    gather.finish()
    for h in range(2):
        down_gathers[h].finish()
        downs[h].finish()
    pair.finish()

    def add(block):
        hidden[block, :] = (middle[block, :] + total[block, :]).astype(BF16)

    row_blocks(middle.shape[0], add)


def turn(back, pair_weight, down_weight, activation, out_weight, middle, grad, gain_rows, down_grad, normed):
    parts, count, feed_width = activation.shape
    shards, rows, _ = down_grad.shape
    width = out_weight.shape[0]
    return pl.pallas_call(
        turn_kernel,
        out_shape=(
            jax.ShapeDtypeStruct((count, D), F32),
            jax.ShapeDtypeStruct((parts, count, D), BF16),
            jax.ShapeDtypeStruct((8, D), F32),
            jax.ShapeDtypeStruct((parts, rows, feed_width), BF16),
            jax.ShapeDtypeStruct((parts, count, width), BF16),
            jax.ShapeDtypeStruct((count, D), BF16),
            jax.ShapeDtypeStruct((shards - 1, rows, 2 * feed_width), BF16),
            jax.ShapeDtypeStruct((shards, rows, 2 * feed_width), BF16),
            jax.ShapeDtypeStruct((rows, 2 * feed_width), BF16),
        ),
        in_specs=[HBM] * 4 + [WHOLE] * 4 + [HBM] * 2,
        out_specs=(WHOLE, HBM, WHOLE, HBM, WHOLE, WHOLE, HBM, HBM, HBM),
        scratch_shapes=[
            VMEM((D, 2 * feed_width), BF16),
            VMEM((parts, count, 2 * feed_width), BF16),
            VMEM((count, D), F32),
            VMEM((count, D), BF16),
            VMEM((rows, feed_width), BF16),
            pltpu.SemaphoreType.DMA((5 + CHUNKS,)),
            VMEM((2, parts, count, slab_size(parts)), BF16),
            VMEM((slab_size(parts), 2 * feed_width), BF16),
            pltpu.SemaphoreType.DMA((3,)),
            pltpu.SemaphoreType.DMA((2, parts)),
        ]
        + fsdp_scratch(shards, rows // 2, feed_width)
        + fsdp_scratch(shards, rows // 2, feed_width)
        + gather_scratch(parts // 2)
        + gather_scratch(parts // 2)
        + gather_scratch(parts // 2)
        + [pltpu.SemaphoreType.DMA((shards,))] * 2
        + scatter_scratch(parts // 2, count)
        + scatter_scratch(parts // 2, count),
        compiler_params=params(3, 63),
        cost_estimate=cost(185),
        name="turn",
    )(
        back,
        pair_weight,
        down_weight,
        activation,
        out_weight,
        middle,
        grad,
        gain_rows,
        down_grad,
        normed,
    )


def last_kernel(*refs):
    back, weights, x, grad_middle, gain_rows, gain_two, gain_heads, context, normed, low = refs[:10]
    hidden, gain_out, head_grad, land = refs[10:14]
    weight, weight_sem, total, gain_one, pack, pack_in, shard_sum, shard_in = refs[14:22]
    slabs_in, slab_out, slab_sems, own_head, refs = refs[22:24], refs[24], refs[25], refs[26], refs[27:]
    small, head_refs, gather_sems, scratch = refs[:4], refs[4:7], refs[7:13], refs[13:]
    me, _, _, chips = line_position()
    shard = lax.axis_index("fsdp")
    shards, ahead, _ = peers_of("fsdp")
    parts, next_part, _ = peers_of("ctx")
    copy = copy_in(weights, weight, weight_sem)

    def produce(piece, chunk):
        return rdot(back[piece], weight[pl.ds(pl.multiple_of(chunk * WIDE, WIDE), WIDE), :])

    def products(slot):
        return (slabs_in[0][slot], back[...]), (slabs_in[1][slot], context[...])

    slabs = Slabs((normed, low), slabs_in, slab_out, head_grad, slab_sems, products)
    heads = FsdpSum(head_grad, *head_refs, own=own_head)
    scatter = Scatter(scratch, produce, total)
    gather = Gather(land, gather_sems)
    scatter.begin()
    slabs.fetch(0)
    full_barrier()
    copy.wait()
    slabs.run(0, slabs.count)
    heads.start()
    own = copy_in(head_grad.at[shard], own_head, weight_sem)
    own.wait()
    scatter.prepare(0)

    def step(time):
        scatter.step(time)
        scatter.prepare(time + 1)

        @pl.when(time == 1)
        def _():
            heads.collect(land.at[me])

        @pl.when(time >= 1)
        def _():
            gather.step(time - 1)

    loop(chips - 1, step)
    scatter.finish()
    gather.step(chips - 2)
    gain_one[...] = jnp.zeros_like(gain_one)

    def norm(block):
        through, terms = rms_back(x[block, :].astype(F32), gain_rows[0:1, :], total[block, :])
        hidden[block, :] = grad_middle[block, :] + through
        gain_one[0:1, :] += jnp.sum(terms, axis=0, keepdims=True)

    row_blocks(x.shape[0], norm)

    rows = D // (shards + 1)
    lanes = rows // 128
    pack[...] = jnp.zeros_like(pack)
    for owner in range(shards + 1):
        for j in range(lanes):
            at = owner * rows + j * 128
            pack[owner, j : j + 1, :] = gain_one[0:1, at : at + 128]
            pack[owner, lanes + j : lanes + j + 1, :] = gain_two[0:1, at : at + 128]
        pack[owner, 2 * lanes : 2 * lanes + 2, :] = gain_heads[0:2, :]

    def pack_copy(i):
        return send(pack.at[ahead(i)], pack_in.at[i], small[0].at[i], small[1].at[i], "fsdp", ahead(i))

    def sum_copy(i):
        return send(shard_sum, shard_in.at[i], small[2].at[i], small[3].at[i], "ctx", next_part(i))

    loop(shards, lambda i: pack_copy(i).start())
    shard_sum[...] = pack[shard]

    def add_pack(i):
        pack_copy(i).wait_recv()
        shard_sum[...] += pack_in[i]

    loop(shards, add_pack)
    loop(parts, lambda i: sum_copy(i).start())
    gain_out[...] = shard_sum[...]

    def add_sum(i):
        sum_copy(i).wait_recv()
        gain_out[...] += shard_in[i]

    loop(parts, add_sum)
    gather.step(chips - 1)
    gather.finish()
    heads.finish()
    loop(shards, lambda i: pack_copy(i).wait_send())
    loop(parts, lambda i: sum_copy(i).wait_send())


def last(back, weights, hidden, grad_middle, gain_rows, gain_two, gain_heads, context, normed, low, shards):
    parts, count, width = back.shape
    rows = D // shards
    query_width = context.shape[2]
    head_width = width + query_width
    return pl.pallas_call(
        last_kernel,
        out_shape=(
            jax.ShapeDtypeStruct((count, D), F32),
            jax.ShapeDtypeStruct((16, 128), F32),
            jax.ShapeDtypeStruct((shards, rows, head_width), BF16),
            jax.ShapeDtypeStruct((parts, rows, head_width), BF16),
        ),
        in_specs=[WHOLE, HBM] + [WHOLE] * 6 + [HBM] * 2,
        out_specs=(WHOLE, WHOLE, HBM, WHOLE),
        scratch_shapes=[
            VMEM((D, width), BF16),
            pltpu.SemaphoreType.DMA,
            VMEM((count, D), F32),
            VMEM((8, D), F32),
            VMEM((shards, 16, 128), F32),
            VMEM((shards, 16, 128), F32),
            VMEM((16, 128), F32),
            VMEM((parts, 16, 128), F32),
            VMEM((2, parts, count, slab_size(parts)), BF16),
            VMEM((2, parts, count, slab_size(parts)), BF16),
            VMEM((slab_size(parts), head_width), BF16),
            pltpu.SemaphoreType.DMA((5,)),
            VMEM((rows, head_width), BF16),
        ]
        + [pltpu.SemaphoreType.DMA((shards,))] * 2
        + [pltpu.SemaphoreType.DMA((parts,))] * 2
        + fsdp_scratch(shards, rows, head_width)
        + gather_scratch(parts // 2)
        + scatter_scratch(parts // 2, count),
        compiler_params=params(5, 60),
        cost_estimate=cost(90),
        name="last",
    )(back, weights, hidden, grad_middle, gain_rows, gain_two, gain_heads, context, normed, low)


def attention_back_kernel(heads, *refs):
    queries, keys, values, out_grad, inverse, context, proj, cosine, sine, gain = refs[:10]
    id_column, id_row, back, gain_sum, key_grad, value_grad, query_grad = refs[10:]
    tokens = proj.shape[0]
    key_at = heads * HEAD_SIZE
    key_grad[...] = jnp.zeros_like(key_grad)
    value_grad[...] = jnp.zeros_like(value_grad)
    gain_sum[...] = jnp.zeros_like(gain_sum)

    def through(block, lanes, grad, row):
        turned = pltpu.roll(grad, HEAD_SIZE // 2, 1)
        unrotated = grad * cosine[block, :] - turned * sine[block, :]
        result, terms = rms_back(proj[block, lanes], gain[row : row + 1, :], unrotated)
        back[block, lanes] = result.astype(BF16)
        gain_sum[row : row + 1, :] += jnp.sum(terms, axis=0, keepdims=True)

    def attend(index):
        block = pl.ds(pl.multiple_of(index * QUERY_TILE, QUERY_TILE), QUERY_TILE)
        query_ids = id_row[0:1, block]
        for h in range(heads):
            lanes = slice(h * HEAD_SIZE, (h + 1) * HEAD_SIZE)
            query = queries[block, lanes]
            grad = out_grad[block, lanes]
            scale = inverse[h : h + 1, block]
            products = grad.astype(F32) * context[block, lanes].astype(F32)
            shift = lax.dot_general(
                jnp.ones((8, HEAD_SIZE), F32),
                products,
                (((1,), (1,)), ((), ())),
                precision=lax.Precision.HIGHEST,
                preferred_element_type=F32,
            )[0:1, :]
            query_grad[...] = jnp.zeros_like(query_grad)

            def one(tile):
                span = pl.ds(pl.multiple_of(tile * KEY_TILE, KEY_TILE), KEY_TILE)
                key = keys[span, :]
                scores = rdot(key, query)
                probs = jnp.where(id_column[span, :] <= query_ids, jnp.exp(scores) * scale, 0.0)
                grad_scores = (probs * (rdot(values[span, :], grad) - shift)).astype(BF16)
                value_grad[span, :] += dot(probs.astype(BF16), grad)
                key_grad[span, :] += dot(grad_scores, query)
                query_grad[...] += tdot(grad_scores, key)

            loop(reach(index, tokens), one)
            through(block, lanes, query_grad[...] * HEAD_SIZE ** (-0.5), 0)

    loop(tokens // QUERY_TILE, attend)

    def finish(index):
        block = pl.ds(pl.multiple_of(index * QUERY_TILE, QUERY_TILE), QUERY_TILE)
        through(block, slice(key_at, key_at + HEAD_SIZE), key_grad[block, :], 1)
        back[block, key_at + HEAD_SIZE : key_at + 2 * HEAD_SIZE] = value_grad[block, :].astype(BF16)

    loop(tokens // QUERY_TILE, finish)


def attention_back(heads, *operands):
    tokens = operands[0].shape[0]
    width = heads * HEAD_SIZE
    return pl.pallas_call(
        functools.partial(attention_back_kernel, heads),
        out_shape=(
            jax.ShapeDtypeStruct((tokens, width + 2 * HEAD_SIZE), BF16),
            jax.ShapeDtypeStruct((8, HEAD_SIZE), F32),
        ),
        in_specs=[WHOLE] * len(operands),
        out_specs=(WHOLE,) * 2,
        scratch_shapes=[
            VMEM((tokens, HEAD_SIZE), F32),
            VMEM((tokens, HEAD_SIZE), F32),
            VMEM((QUERY_TILE, HEAD_SIZE), F32),
        ],
        compiler_params=pltpu.CompilerParams(vmem_limit_bytes=48 * 1024 * 1024),
        cost_estimate=cost(38),
        name="attention_back",
    )(*operands)


def spread_kernel(width, head_source, pair_source, down_source, *targets):
    query, key, value, out, gate, up, down = targets
    second = width + HEAD_SIZE
    third = second + HEAD_SIZE
    query[...] = head_source[0, :, :width].astype(F32)
    key[...] = head_source[0, :, width:second].astype(F32)
    value[...] = head_source[0, :, second:third].astype(F32)
    out[...] = head_source[0, :, third:].astype(F32).T
    feed_width = gate.shape[1]
    gate[...] = pair_source[0, :, :feed_width].astype(F32)
    up[...] = pair_source[0, :, feed_width:].astype(F32)
    down[...] = down_source[0].astype(F32).T


def spread(head_parts, pair_parts, down_parts, width):
    parts, rows, _ = head_parts.shape
    feed_width = down_parts.shape[2]
    sources = (head_parts, pair_parts, down_parts)

    def side_by_side(columns):
        shape = jax.ShapeDtypeStruct((rows, parts * columns), F32)
        return shape, pl.BlockSpec((rows, columns), lambda i: (0, i))

    def stacked(columns):
        shape = jax.ShapeDtypeStruct((parts * columns, rows), F32)
        return shape, pl.BlockSpec((columns, rows), lambda i: (i, 0))

    outs = (
        side_by_side(width),
        side_by_side(HEAD_SIZE),
        side_by_side(HEAD_SIZE),
        stacked(width),
        side_by_side(feed_width),
        side_by_side(feed_width),
        stacked(feed_width),
    )
    return pl.pallas_call(
        functools.partial(spread_kernel, width),
        out_shape=tuple(shape for shape, _ in outs),
        grid=(parts,),
        in_specs=[pl.BlockSpec((1, *source.shape[1:]), lambda i: (i, 0, 0)) for source in sources],
        out_specs=tuple(spec for _, spec in outs),
        compiler_params=pltpu.CompilerParams(vmem_limit_bytes=60 * 1024 * 1024),
        name="spread",
    )(*sources)


def by_row(array):
    return with_layout_constraint(array, Layout(major_to_minor=(0, 1)))


def local(
    hidden_in,
    weight_query,
    key_weight_matrix,
    weight_value,
    weight_out,
    weight_gate,
    weight_up,
    weight_down,
    gain_attention,
    gain_feed,
    gain_query,
    gain_key,
    positions,
    token_block_index,
    grad_out,
):
    parts = lax.axis_size("ctx")
    shards = lax.axis_size("fsdp")
    shard = lax.axis_index("fsdp")
    heads = QUERY_HEADS // parts
    sharers = parts // KEY_VALUE_HEADS
    width = heads * HEAD_SIZE
    feed_width = FF // parts
    rows = D // shards
    head_rows = HEAD_SIZE // shards
    count = hidden_in.shape[1]
    tokens = parts * count

    def gather_parts(piece):
        return lax.all_gather(piece, "ctx", axis=0)

    own_gains = jnp.concatenate([gain_attention, gain_feed, gain_query, gain_key]).astype(F32)
    own_gains = jnp.pad(own_gains, (0, 2048 - own_gains.shape[0])).reshape(16, 128)
    own_tokens = jnp.pad(jnp.stack([positions[0], token_block_index[0]]), ((0, 6), (0, 0)))
    half = HEAD_SIZE // 2
    freq = THETA ** (-(jnp.arange(half).astype(F32) * 2.0 / HEAD_SIZE))
    freq = jnp.broadcast_to(jnp.concatenate([freq, freq]), (8, HEAD_SIZE))
    hidden, grad = hidden_in[0], grad_out[0]
    weights = (
        weight_query,
        key_weight_matrix,
        weight_value,
        weight_out,
        weight_gate,
        weight_up,
        weight_down,
    )
    (
        normed_all,
        grad_all,
        normed_two_all,
        activation,
        back,
        proj,
        cosine,
        sine,
        queries,
        keys,
        values,
        context,
        inverse,
        middle,
        gain_rows,
        gains,
        whole,
        heads_weight,
        out_weight,
        pair_weight,
        down_weight,
    ) = forward(hidden, grad, own_gains, own_tokens, freq, weights, shards, parts, heads)
    head_gains = gain_rows[2:4, :HEAD_SIZE]
    ids = whole[:, 1].reshape(-1)
    id_row, id_column = ids[None, :], ids[:, None]
    proj = proj.reshape(tokens, width + 2 * HEAD_SIZE)

    flat_grad = grad_all.reshape(tokens, D)
    flat_activation = activation.reshape(tokens, feed_width)
    down_grad = by_row(tdot(flat_grad, flat_activation).astype(BF16))
    grad_middle, low_all, gain_two, down_parts, context_grad, hidden_out, _, _, feed_shard = turn(
        back,
        pair_weight,
        down_weight,
        activation,
        out_weight,
        middle,
        grad,
        gain_rows,
        down_grad.reshape(shards, rows, feed_width),
        normed_two_all,
    )
    feed_parts = gather_parts(feed_shard)
    context_grad = context_grad.reshape(tokens, width)
    grad_qkv, gain_heads = attention_back(
        heads,
        queries,
        keys,
        values,
        context_grad,
        inverse,
        context,
        proj,
        cosine,
        sine,
        head_gains,
        id_column,
        id_row,
    )
    grad_hidden, gain_sums, _, head_parts = last(
        grad_qkv.reshape(parts, count, -1),
        heads_weight,
        hidden,
        grad_middle,
        gain_rows,
        gain_two,
        gain_heads,
        context.reshape(parts, count, width),
        normed_all,
        low_all,
        shards,
    )

    gain_sums = gain_sums.reshape(-1)
    grad_query, grad_key, grad_value, grad_out_weight, grad_gate, grad_up, grad_down = spread(
        head_parts, feed_parts, down_parts, width
    )
    if sharers > 1:
        grad_key, grad_value = (
            part.reshape(rows, KEY_VALUE_HEADS, sharers, HEAD_SIZE).sum(axis=2).reshape(rows, -1)
            for part in (grad_key, grad_value)
        )
    return (
        hidden_out[None],
        grad_hidden[None],
        grad_query,
        grad_key,
        grad_value,
        grad_out_weight,
        grad_gate,
        grad_up,
        grad_down,
        gain_sums[:rows],
        gain_sums[rows : 2 * rows],
        lax.dynamic_slice_in_dim(gain_sums, 2 * rows + shard * head_rows, head_rows),
        lax.dynamic_slice_in_dim(gain_sums, 2 * rows + HEAD_SIZE + shard * head_rows, head_rows),
    )


def solution(mesh):
    tokens = P("fsdp", "ctx", None)
    by_rows = P("fsdp", None)
    by_columns = P(None, "fsdp")
    per_token = P("fsdp", "ctx")
    vector = P("fsdp")
    weights = (by_rows, by_rows, by_rows, by_columns, by_rows, by_rows, by_columns)
    return jax.shard_map(
        local,
        mesh=mesh,
        in_specs=(tokens, *weights, vector, vector, vector, vector, per_token, per_token, tokens),
        out_specs=(tokens, tokens, *weights, vector, vector, vector, vector),
        check_vma=False,
    )
```

```python
import functools

import jax
import jax.numpy as jnp
from jax import lax
from jax.experimental import pallas as pl
from jax.experimental.layout import Layout, with_layout_constraint
from jax.experimental.pallas import tpu as pltpu
from jax.sharding import PartitionSpec as P

D = 2048
QUERY_HEADS = 16
KEY_VALUE_HEADS = 8
HEAD_SIZE = 128
FF = 6144
EPS = 1e-06
THETA = 1000000.0
F32 = jnp.float32
BF16 = jnp.bfloat16
MESH = pl.DeviceIdType.MESH
VMEM = pltpu.VMEM
WHOLE = pl.BlockSpec(memory_space=pltpu.VMEM)
HBM = pl.BlockSpec(memory_space=pl.ANY)
CHUNKS = 4
WIDE = D // CHUNKS


def dot(left, right):
    return jnp.dot(left, right, preferred_element_type=F32)


def tdot(left, right):
    return lax.dot_general(left, right, (((0,), (0,)), ((), ())), preferred_element_type=F32)


def rdot(left, right):
    return lax.dot_general(left, right, (((1,), (1,)), ((), ())), preferred_element_type=F32)


def loop(count, body):
    def step(index, carry):
        body(index)
        return carry

    lax.fori_loop(0, count, step, 0)


def line_position():
    me = lax.axis_index("ctx")
    return me, me // 2, me % 2, lax.axis_size("ctx") // 2


def send(source, target, send_sem, recv_sem, axis, index):
    return pltpu.make_async_remote_copy(
        src_ref=source,
        dst_ref=target,
        send_sem=send_sem,
        recv_sem=recv_sem,
        device_id={axis: index},
        device_id_type=MESH,
    )


def line_barrier():
    me, chip, core, chips = line_position()
    barrier = pltpu.get_barrier_semaphore()

    def greet(index):
        pl.semaphore_signal(barrier, inc=1, device_id={"ctx": index}, device_id_type=MESH)

    greet(me + 1 - 2 * core)

    @pl.when(chip > 0)
    def _():
        greet(me - 2)

    @pl.when(chip < chips - 1)
    def _():
        greet(me + 2)

    peers = 1 + (chip > 0).astype(jnp.int32) + (chip < chips - 1).astype(jnp.int32)
    pl.semaphore_wait(barrier, peers)


def peers_of(axis):
    me, size = lax.axis_index(axis), lax.axis_size(axis)
    return size - 1, lambda i: (me + i + 1) % size, lambda i: (me + size - i - 1) % size


def full_barrier():
    barrier = pltpu.get_barrier_semaphore()
    total = 0
    for axis in ("fsdp", "ctx"):
        count, ahead, _ = peers_of(axis)
        loop(
            count,
            lambda i, axis=axis, ahead=ahead: pl.semaphore_signal(
                barrier, inc=1, device_id={axis: ahead(i)}, device_id_type=MESH
            ),
        )
        total += count
    pl.semaphore_wait(barrier, total)


def gather_scratch(chips):
    return [pltpu.SemaphoreType.DMA((chips,)) for _ in range(6)]


class Gather:
    def __init__(self, land, sems, consume=None, part=None):
        self.part = part
        self.land = land
        self.sems = sems
        self.consume = consume
        self.me, self.chip, self.core, self.chips = line_position()

    def place(self, piece):
        return self.land.at[piece] if self.part is None else self.land.at[piece, self.part]

    def right(self, step, source):
        ref = self.place(2 * source + self.core)
        return send(ref, ref, self.sems[0].at[step], self.sems[1].at[step], "ctx", self.me + 2)

    def left(self, step, source):
        ref = self.place(2 * source + self.core)
        return send(ref, ref, self.sems[2].at[step], self.sems[3].at[step], "ctx", self.me - 2)

    def across(self, source, core):
        ref = self.place(2 * source + core)
        other = self.me + 1 - 2 * self.core
        return send(ref, ref, self.sems[4].at[source], self.sems[5].at[source], "ctx", other)

    def step(self, step):
        self.move(step)
        self.use(step)

    def move(self, step):
        chip, core, chips = self.chip, self.core, self.chips
        low, high = chip - step, chip + step
        has_low = low >= 0
        has_high = jnp.logical_and(high < chips, step > 0)

        @pl.when(jnp.logical_and(has_low, step > 0))
        def _():
            self.right(step - 1, low).wait_recv()

        @pl.when(jnp.logical_and(has_low, chip < chips - 1))
        def _():
            self.right(step, low).start()

        @pl.when(has_high)
        def _():
            self.left(step - 1, high).wait_recv()

        @pl.when(jnp.logical_and(high < chips, chip > 0))
        def _():
            self.left(step, high).start()

        @pl.when(has_low)
        def _():
            self.across(low, core).start()

        @pl.when(has_high)
        def _():
            self.across(high, core).start()

    def use(self, step):
        chip, core, chips = self.chip, self.core, self.chips
        low, high = chip - step, chip + step

        def one(kind):
            upward = kind % 2
            crossed = kind // 2
            source = jnp.where(upward == 1, high, low)
            valid = jnp.where(upward == 1, jnp.logical_and(high < chips, step > 0), low >= 0)
            parity = jnp.where(crossed == 1, 1 - core, core)

            @pl.when(valid)
            def _():
                @pl.when(crossed == 1)
                def _():
                    self.across(source, parity).wait_recv()

                if self.consume is not None:
                    self.consume(2 * source + parity)

        loop(4, one)

    def finish(self):
        chip, core, chips = self.chip, self.core, self.chips

        def one(step):
            @pl.when(jnp.logical_and(chip - step >= 0, chip < chips - 1))
            def _():
                self.right(step, chip - step).wait_send()

            @pl.when(jnp.logical_and(chip + step < chips, chip > 0))
            def _():
                self.left(step, chip + step).wait_send()

            self.across(step, core).wait_send()

        loop(chips, one)


def scatter_scratch(chips, rows):
    buffers = [VMEM((count, CHUNKS, rows, WIDE), BF16) for count in (chips + 1, 2, chips)]
    return buffers + [pltpu.SemaphoreType.DMA((chips, CHUNKS)) for _ in range(6)]


class Scatter:
    def __init__(self, scratch, produce, total, ready=None):
        self.ready = ready
        self.line, self.out, self.other = scratch[:3]
        self.sems = scratch[3:]
        self.produce = produce
        self.total = total
        self.me, self.chip, self.core, self.chips = line_position()


    def right(self, step, chunk):
        ref = self.line.at[step, chunk]
        sems = self.sems
        return send(ref, ref, sems[0].at[step, chunk], sems[1].at[step, chunk], "ctx", self.me + 2)

    def left(self, step, chunk):
        ref = self.line.at[self.chips - step, chunk]
        sems = self.sems
        return send(ref, ref, sems[2].at[step, chunk], sems[3].at[step, chunk], "ctx", self.me - 2)

    def across(self, target, chunk, slot=0):
        sems = self.sems
        return send(
            self.out.at[slot, chunk],
            self.other.at[target, chunk],
            sems[4].at[target, chunk],
            sems[5].at[target, chunk],
            "ctx",
            self.me + 1 - 2 * self.core,
        )

    def begin(self):
        def clear(index):
            slot, chunk = index // CHUNKS, index % CHUNKS
            at_left = jnp.logical_and(self.chip == 0, slot < self.chips)
            at_right = jnp.logical_and(self.chip == self.chips - 1, slot > 0)

            @pl.when(jnp.logical_or(at_left, at_right))
            def _():
                self.line[slot, chunk] = jnp.zeros(self.line.shape[2:], BF16)

        loop((self.chips + 1) * CHUNKS, clear)

    def when_right(self, time):
        return jnp.logical_and(time >= self.chip, time < self.chips - 1)

    def when_left(self, time):
        return jnp.logical_and(time >= self.chips - 1 - self.chip, time < self.chips - 1)

    def prepare(self, time):
        chip, chips = self.chip, self.chips

        def cross(target, slot, before, used):
            if self.ready is not None:
                self.ready(target)

            def one(chunk):
                @pl.when(used)
                def _():
                    self.across(before, chunk, slot).wait_send()

                piece = 2 * target + 1 - self.core
                self.out[slot, chunk] = self.produce(piece, chunk).astype(BF16)
                self.across(target, chunk, slot).start()

            loop(CHUNKS, one)

        @pl.when(self.when_right(time))
        def _():
            target = chips - 1 - time + chip
            cross(target, 0, target + 1, time > chip)

        @pl.when(self.when_left(time))
        def _():
            target = time - (chips - 1 - chip)
            cross(target, 1, target - 1, target > 0)

        @pl.when(time == chips - 1)
        def _():
            cross(chip, 0, chip + 1, chip < chips - 1)

    def step(self, time):
        chip, core, chips = self.chip, self.core, self.chips

        @pl.when(self.when_right(time))
        def _():
            step = time - chip
            target = chips - 1 - step

            def one(chunk):
                self.across(target, chunk).wait_recv()

                @pl.when(chip > 0)
                def _():
                    self.right(step, chunk).wait_recv()

                value = self.produce(2 * target + core, chunk) + self.other[target, chunk].astype(F32)
                value = value + self.line[step, chunk].astype(F32)
                self.line[step, chunk] = value.astype(BF16)
                self.right(step, chunk).start()

            loop(CHUNKS, one)

        @pl.when(self.when_left(time))
        def _():
            step = time - (chips - 1 - chip)

            def one(chunk):
                self.across(step, chunk).wait_recv()

                @pl.when(chip < chips - 1)
                def _():
                    self.left(step, chunk).wait_recv()

                value = self.produce(2 * step + core, chunk) + self.other[step, chunk].astype(F32)
                value = value + self.line[chips - step, chunk].astype(F32)
                self.line[chips - step, chunk] = value.astype(BF16)
                self.left(step, chunk).start()

            loop(CHUNKS, one)

    def finish(self):
        chip, core, chips = self.chip, self.core, self.chips
        last = chips - 1 - chip

        def one(chunk):
            self.across(chip, chunk).wait_recv()
            value = self.produce(2 * chip + core, chunk) + self.other[chip, chunk].astype(F32)

            @pl.when(chip > 0)
            def _():
                self.right(last, chunk).wait_recv()

            @pl.when(chip < chips - 1)
            def _():
                self.left(chip, chunk).wait_recv()

            value = value + self.line[last, chunk].astype(F32)
            value = value + self.line[chips - chip, chunk].astype(F32)
            self.total[:, pl.ds(pl.multiple_of(chunk * WIDE, WIDE), WIDE)] = value

        loop(CHUNKS, one)

        def drain(index):
            step, chunk = index // CHUNKS, index % CHUNKS

            @pl.when(step < last)
            def _():
                self.right(step, chunk).wait_send()

            @pl.when(step < chip)
            def _():
                self.left(step, chunk).wait_send()

            @pl.when(jnp.logical_or(step == chip, step == chip - 1))
            def _():
                self.across(step, chunk, jnp.where(step == chip, 0, 1)).wait_send()

        loop(chips * CHUNKS, drain)


def tile(index, size):
    return pl.ds(pl.multiple_of(index * size, size), size)


def row_blocks(rows, body, size=32):
    def one(index):
        body(pl.ds(pl.multiple_of(index * size, size), size))

    loop(rows // size, one)


def inverse_norm(value):
    return lax.rsqrt(jnp.mean(value * value, axis=-1, keepdims=True) + EPS)


def params(identity, megabytes):
    return pltpu.CompilerParams(
        collective_id=identity,
        has_side_effects=True,
        vmem_limit_bytes=megabytes * 1024 * 1024,
    )


def cost(microseconds):
    return pl.CostEstimate(
        flops=int(microseconds * 1.15e9), bytes_accessed=1024, transcendentals=0
    )


class FsdpSum:
    def __init__(self, grad, arrived, send_sems, recv_sems, own=None, part=slice(None)):
        self.grad, self.arrived, self.part = grad, arrived, part
        self.own = grad.at[lax.axis_index("fsdp")] if own is None else own
        self.sems = send_sems, recv_sems
        self.peers, self.ahead, _ = peers_of("fsdp")

    def copy(self, i):
        target = self.ahead(i)
        return send(
            self.grad.at[target, self.part], self.arrived.at[i], self.sems[0].at[i], self.sems[1].at[i], "fsdp", target
        )

    def start(self):
        loop(self.peers, lambda i: self.copy(i).start())

    def arrive(self):
        loop(self.peers, lambda i: self.copy(i).wait_recv())

    def collect(self, target):
        self.arrive()
        self.add(target)

    def add(self, target):
        def one(block):
            value = self.own[block, :].astype(F32)
            for i in range(self.peers):
                value = value + self.arrived[i, block].astype(F32)
            target[block, :] = value.astype(BF16)

        row_blocks(self.own.shape[0], one)

    def finish(self):
        loop(self.peers, lambda i: self.copy(i).wait_send())


def fsdp_scratch(shards, rows, width):
    return [VMEM((shards - 1, rows, width), BF16)] + [pltpu.SemaphoreType.DMA((shards,))] * 2


def sine_cosine(angle):
    count = jnp.floor(angle * 0.6366197723675814 + 0.5)
    rest = angle - count * 1.5703125
    rest = rest - count * 4.837512969970703e-4
    rest = rest - count * 7.549789948768648e-8
    square = rest * rest
    sine = -1.9515295891e-4 * square + 8.3321608736e-3
    sine = rest + rest * square * (sine * square - 1.6666654611e-1)
    cosine = 2.443315711809948e-5 * square - 1.388731625493765e-3
    cosine = 1.0 - 0.5 * square + square * square * (cosine * square + 4.166664568298827e-2)
    quarter = jnp.bitwise_and(count.astype(jnp.int32), 3)
    odd = jnp.bitwise_and(quarter, 1) == 1
    sine, cosine = jnp.where(odd, cosine, sine), jnp.where(odd, sine, cosine)
    sine = jnp.where(quarter >= 2, -sine, sine)
    cosine = jnp.where(jnp.logical_or(quarter == 1, quarter == 2), -cosine, cosine)
    return sine, cosine


class Shares:
    def __init__(self, source, target_of, own_sem, sems):
        self.source, self.target_of = source, target_of
        self.own_sem, self.sems = own_sem, sems
        self.peers, self.ahead, self.behind = peers_of("fsdp")
        self.shard = lax.axis_index("fsdp")

    def copy(self, i, owner):
        sems = self.sems
        target = self.target_of(owner)
        return send(self.source, target, sems[0].at[i], sems[1].at[i], "fsdp", self.ahead(i))

    def own(self):
        return pltpu.make_async_copy(self.source, self.target_of(self.shard), self.own_sem)

    def start(self):
        loop(self.peers, lambda i: self.copy(i, self.shard).start())
        self.own().start()

    def arrive(self):
        self.own().wait()
        loop(self.peers, lambda i: self.copy(i, self.behind(i)).wait_recv())

    def finish(self):
        loop(self.peers, lambda i: self.copy(i, self.shard).wait_send())


def shares_scratch(count, shards):
    return [pltpu.SemaphoreType.DMA((count,))] + [pltpu.SemaphoreType.DMA((shards,))] * (2 * count)


def copy_in(source, target, sem):
    copy = pltpu.make_async_copy(source, target, sem)
    copy.start()
    return copy


QUERY_TILE = 256
KEY_TILE = 512


def reach(index, tokens):
    return jnp.minimum((index + 2) * QUERY_TILE + KEY_TILE - 1, tokens) // KEY_TILE


def head_norm(value, gain, cosine, sine):
    normed = value * inverse_norm(value) * gain
    return normed * cosine + pltpu.roll(normed, HEAD_SIZE // 2, 1) * sine


def forward_kernel(heads, *refs):
    x, grad, gains, token_info, freq = refs[:5]
    sources, refs = refs[5:12], refs[12:]
    normed_land, grad_land, two_land, activation, back = refs[:5]
    proj, cosine, sine, queries, keys, values, context, inverse = refs[5:13]
    middle, gain_rows, all_gains, all_tokens = refs[13:17]
    head_weight, out_weight, pair_weight, down_weight = refs[17:21]
    refs = refs[21:]
    pair, down, own, piece_in, grad_in, act_out, back_out, total, sems = refs[:9]
    small, refs = refs[9:13], refs[13:]
    share_own, share_sems, refs = refs[0], refs[1:15], refs[15:]
    first_sems, grad_sems, two_sems, scratch = refs[:6], refs[6:12], refs[12:18], refs[18:]
    me, _, _, chips = line_position()
    shard = lax.axis_index("fsdp")
    shards, ahead, behind = peers_of("fsdp")
    parts, next_part, past_part = peers_of("ctx")
    count = x.shape[0]
    tokens = 2 * chips * count
    width = heads * HEAD_SIZE
    feed_width = down.shape[0]
    rows = D // (shards + 1)
    lanes = rows // 128
    key_head = me // (2 * chips // KEY_VALUE_HEADS)

    def gain_copy(i, slot):
        return send(gains, all_gains.at[slot], small[0].at[i], small[1].at[i], "fsdp", ahead(i))

    def token_copy(i, slot):
        return send(token_info, all_tokens.at[slot], small[2].at[i], small[3].at[i], "ctx", next_part(i))

    def by_row(target, at, size):
        return lambda owner: target.at[tile(owner, rows), pl.ds(at, size)]

    def by_column(target):
        return lambda owner: target.at[:, tile(owner, rows)]

    places = (
        (sources[0].at[:, tile(me, width)], by_row(head_weight, 0, width)),
        (sources[1].at[:, tile(key_head, HEAD_SIZE)], by_row(head_weight, width, HEAD_SIZE)),
        (sources[2].at[:, tile(key_head, HEAD_SIZE)], by_row(head_weight, width + HEAD_SIZE, HEAD_SIZE)),
        (sources[3].at[tile(me, width), :], by_column(out_weight)),
        (sources[4].at[:, tile(me, feed_width)], by_row(pair, 0, feed_width)),
        (sources[5].at[:, tile(me, feed_width)], by_row(pair, feed_width, feed_width)),
        (sources[6].at[tile(me, feed_width), :], by_column(down)),
    )
    shares = [
        Shares(source, target_of, share_own.at[i], share_sems[2 * i : 2 * i + 2])
        for i, (source, target_of) in enumerate(places)
    ]

    full_barrier()
    loop(shards, lambda i: gain_copy(i, shard).start())
    loop(parts, lambda i: token_copy(i, me).start())
    for share in shares[:4]:
        share.start()
    grad_copy = copy_in(grad, grad_land.at[me], sems.at[0])
    all_gains[shard] = gains[...]
    all_tokens[me] = token_info[...]
    loop(shards, lambda i: gain_copy(i, behind(i)).wait_recv())
    for kind in range(2):
        for owner in range(shards + 1):
            for j in range(lanes):
                at = owner * rows + j * 128
                gain_rows[kind : kind + 1, at : at + 128] = all_gains[
                    owner, kind * lanes + j : kind * lanes + j + 1, :
                ]
    size = HEAD_SIZE // (shards + 1)
    for kind in range(2):
        gain_rows[2 + kind : 3 + kind, 0:HEAD_SIZE] = jnp.concatenate(
            [
                all_gains[
                    owner, 2 * lanes : 2 * lanes + 1, kind * size : (kind + 1) * size
                ]
                for owner in range(shards + 1)
            ],
            axis=1,
        )

    def norm(block):
        value = x[block, :].astype(F32)
        own[block, :] = (value * inverse_norm(value) * gain_rows[0:1, :]).astype(BF16)

    row_blocks(count, norm)
    own_copy = copy_in(own, normed_land.at[me], sems.at[1])
    own_copy.wait()

    def column(piece, row):
        values_in_lanes = all_tokens[piece, row : row + 1, :].astype(F32)
        return jnp.broadcast_to(values_in_lanes, (128, count)).T

    def project(piece):
        copy = copy_in(normed_land.at[piece], piece_in, sems.at[1])
        block = tile(piece, count)
        s, c = sine_cosine(column(piece, 0) * freq[0:1, :])
        lane = lax.broadcasted_iota(jnp.int32, s.shape, 1)
        s = jnp.where(lane < HEAD_SIZE // 2, -s, s)
        cosine[block, :] = c
        sine[block, :] = s
        copy.wait()
        proj[piece] = dot(piece_in[...], head_weight[...])

        def turned(at, row):
            return head_norm(proj[piece, :, at : at + HEAD_SIZE], gain_rows[row : row + 1, 0:HEAD_SIZE], c, s)

        for h in range(heads):
            at = h * HEAD_SIZE
            queries[block, at : at + HEAD_SIZE] = (turned(at, 2) * HEAD_SIZE ** (-0.5)).astype(BF16)
        keys[block, :] = turned(width, 3).astype(BF16)
        values[block, :] = proj[piece, :, width + HEAD_SIZE : width + 2 * HEAD_SIZE].astype(BF16)

    first_gather = Gather(normed_land, first_sems, project)
    grad_gather = Gather(grad_land, grad_sems)
    first_gather.move(0)
    loop(parts, lambda i: token_copy(i, past_part(i)).wait_recv())

    def first_step(step):
        first_gather.move(step + 1)

        @pl.when(step == 0)
        def _():
            for share in shares[:4]:
                share.arrive()
            for share in shares[4:]:
                share.start()

        first_gather.use(step)

    loop(chips - 1, first_step)
    grad_copy.wait()
    grad_gather.step(0)
    first_gather.use(chips - 1)

    def attend(index):
        block = tile(index, QUERY_TILE)
        query_ids = column(index, 1)[:, 0:1]
        each = KEY_TILE // count
        lanes_of = [slice(h * HEAD_SIZE, (h + 1) * HEAD_SIZE) for h in range(heads)]

        def one(key_tile, carry):
            span = tile(key_tile, KEY_TILE)
            key, value = keys[span, :], values[span, :]
            key_ids = jnp.concatenate(
                [all_tokens[key_tile * each + j, 1:2, :] for j in range(each)], axis=1
            ).astype(F32)
            allowed = key_ids <= query_ids
            result = []
            for head, (sums, total) in zip(lanes_of, carry):
                expon = jnp.where(allowed, jnp.exp(rdot(queries[block, head], key)), 0.0)
                sums = sums + dot(expon.astype(BF16), value)
                result.append((sums, total + jnp.sum(expon, axis=1, keepdims=True)))
            return tuple(result)

        start = (jnp.zeros((QUERY_TILE, HEAD_SIZE), F32), jnp.zeros((QUERY_TILE, 1), F32))
        results = lax.fori_loop(0, reach(index, tokens), one, (start,) * heads)
        for h, (head, (sums, total)) in enumerate(zip(lanes_of, results)):
            scale = 1.0 / total
            context[block, head] = (sums * scale).astype(BF16)
            inverse[h : h + 1, block] = jnp.broadcast_to(scale, (QUERY_TILE, HEAD_SIZE)).T[0:1, :]

    def ready(target):
        each = 2 * count // QUERY_TILE
        loop(each, lambda i: attend(target * each + i))

    def produce(piece, chunk):
        return dot(context[tile(piece, count), :], out_weight[:, tile(chunk, WIDE)])

    scatter = Scatter(scratch, produce, total, ready)
    scatter.begin()
    scatter.prepare(0)

    def scatter_step(time):
        scatter.step(time)
        scatter.prepare(time + 1)
        grad_gather.step(time + 1)

    loop(chips - 1, scatter_step)
    scatter.finish()

    def norm_two(block):
        value = x[block, :].astype(F32) + total[block, :]
        middle[block, :] = value
        own[block, :] = (value * inverse_norm(value) * gain_rows[1:2, :]).astype(BF16)

    row_blocks(count, norm_two)
    two_copy = copy_in(own, two_land.at[me], sems.at[1])
    two_copy.wait()
    for share in shares[4:]:
        share.arrive()
    outs = [
        copy_in(head_weight, refs_out, sems.at[2 + i])
        for i, (head_weight, refs_out) in enumerate(((pair, pair_weight), (down, down_weight)))
    ]
    feed_size = 256 if feed_width % 256 == 0 else 128

    def act_copy(piece):
        return pltpu.make_async_copy(act_out, activation.at[piece], sems.at[6])

    def back_copy(piece):
        return pltpu.make_async_copy(back_out, back.at[piece], sems.at[7])

    def feed(piece):
        copies = (
            copy_in(two_land.at[piece], piece_in, sems.at[4]),
            copy_in(grad_land.at[piece], grad_in, sems.at[5]),
        )
        for copy in copies:
            copy.wait()

        @pl.when(piece != me)
        def _():
            act_copy(piece).wait()
            back_copy(piece).wait()

        def one(index):
            def columns(kind):
                return pl.ds(pl.multiple_of(kind * feed_width + index * feed_size, 128), feed_size)

            gate = dot(piece_in[...], pair[:, columns(0)])
            up = dot(piece_in[...], pair[:, columns(1)])
            grad_act = rdot(grad_in[...], down[tile(index, feed_size), :])
            sigma = 1.0 / (1.0 + jnp.exp(-gate))
            act_out[:, columns(0)] = (gate * sigma * up).astype(BF16)
            back_out[:, columns(0)] = (
                grad_act * up * sigma * (1.0 + gate * (1.0 - sigma))
            ).astype(BF16)
            back_out[:, columns(1)] = (grad_act * gate * sigma).astype(BF16)

        loop(feed_width // feed_size, one)
        act_copy(piece).start()
        back_copy(piece).start()

    two_gather = Gather(two_land, two_sems, feed)
    loop(chips, two_gather.step)
    act_copy(0).wait()
    back_copy(0).wait()
    first_gather.finish()
    grad_gather.finish()
    two_gather.finish()
    for out in outs:
        out.wait()
    for share in shares:
        share.finish()
    loop(shards, lambda i: gain_copy(i, shard).wait_send())
    loop(parts, lambda i: token_copy(i, me).wait_send())


def forward(hidden, grad, gains, token_info, freq, weights, shards, parts, heads):
    count = hidden.shape[0]
    tokens = parts * count
    width = heads * HEAD_SIZE
    total_width = width + 2 * HEAD_SIZE
    feed_width = FF // parts
    chips = parts // 2
    shape = jax.ShapeDtypeStruct
    return pl.pallas_call(
        functools.partial(forward_kernel, heads),
        out_shape=(
            shape((parts, count, D), BF16),
            shape((parts, count, D), BF16),
            shape((parts, count, D), BF16),
            shape((parts, count, feed_width), BF16),
            shape((parts, count, 2 * feed_width), BF16),
            shape((parts, count, total_width), F32),
            shape((tokens, HEAD_SIZE), F32),
            shape((tokens, HEAD_SIZE), F32),
            shape((tokens, width), BF16),
            shape((tokens, HEAD_SIZE), BF16),
            shape((tokens, HEAD_SIZE), BF16),
            shape((tokens, width), BF16),
            shape((8, tokens), F32),
            shape((count, D), F32),
            shape((8, D), F32),
            shape((shards, *gains.shape), F32),
            shape((parts, *token_info.shape), jnp.int32),
            shape((D, total_width), BF16),
            shape((width, D), BF16),
            shape((D, 2 * feed_width), BF16),
            shape((feed_width, D), BF16),
        ),
        in_specs=[WHOLE] * 5 + [HBM] * 7,
        out_specs=(HBM,) * 5 + (WHOLE,) * 14 + (HBM,) * 2,
        scratch_shapes=[
            VMEM((D, 2 * feed_width), BF16),
            VMEM((feed_width, D), BF16),
            VMEM((count, D), BF16),
            VMEM((count, D), BF16),
            VMEM((count, D), BF16),
            VMEM((count, feed_width), BF16),
            VMEM((count, 2 * feed_width), BF16),
            VMEM((count, D), F32),
            pltpu.SemaphoreType.DMA((8,)),
        ]
        + [pltpu.SemaphoreType.DMA((shards,))] * 2
        + [pltpu.SemaphoreType.DMA((parts,))] * 2
        + shares_scratch(7, shards)
        + gather_scratch(chips)
        + gather_scratch(chips)
        + gather_scratch(chips)
        + scatter_scratch(chips, count),
        compiler_params=params(0, 63),
        cost_estimate=cost(280),
        name="forward",
    )(hidden, grad, gains, token_info, freq, *weights)


def slab_size(parts):
    return 256 if parts <= 8 else 128


class Slabs:
    def __init__(self, sources, buffers, out, target, sems, products, place=lambda index: index):
        self.place = place
        self.sources, self.buffers, self.out, self.target = sources, buffers, out, target
        self.sems, self.products = sems, products
        self.size = out.shape[0]
        self.count = D // self.size

    def copies(self, index):
        slot = index % 2
        return [
            pltpu.make_async_copy(
                source.at[:, :, tile(self.place(index), self.size)], buffer.at[slot], self.sems.at[2 * i + slot]
            )
            for i, (source, buffer) in enumerate(zip(self.sources, self.buffers))
        ]

    def fetch(self, index):
        for copy in self.copies(index):
            copy.start()

    def leave(self, index):
        each = self.target.shape[1] // self.size
        place = self.place(index)
        target = self.target.at[place // each, tile(place % each, self.size), :]
        return pltpu.make_async_copy(self.out, target, self.sems.at[2 * len(self.sources)])

    def run(self, begin, end):
        def one(index, carry):
            for copy in self.copies(index):
                copy.wait()

            @pl.when(index + 1 < self.count)
            def _():
                self.fetch(index + 1)

            @pl.when(index > begin)
            def _():
                self.leave(index - 1).wait()

            at = 0
            for left, right in self.products(index % 2):
                left = left.reshape(-1, self.size)
                right = right.reshape(left.shape[0], -1)
                width = right.shape[1]
                self.out[:, at : at + width] = tdot(left, right).astype(BF16)
                at += width
            self.leave(index).start()
            return carry

        lax.fori_loop(begin, end, one, 0)

    def settle(self, index):
        self.leave(index - 1).wait()


def rms_back(value, gain, grad):
    inverse = inverse_norm(value)
    scaled = grad * gain
    inner = jnp.mean(scaled * value, axis=-1, keepdims=True)
    terms = grad * value * inverse
    return inverse * scaled - value * (inverse * inverse * inverse * inner), terms


def turn_kernel(*refs):
    back, pair_weight, down_weight, activation, out_weight = refs[:5]
    middle, grad, gain_rows, down_grad, normed = refs[5:10]
    grad_middle, land, gain_sum, down_land, context_grad, hidden, pair_in, pair_grad, pair_sum = refs[10:19]
    weight, data, total, low, own_down, sems = refs[19:25]
    slab, slab_out, slab_sems, sum_sems = refs[25:29]
    down_refs, down_sems = (refs[29:32], refs[32:35]), (refs[35:41], refs[41:47])
    gather_sems, pair_sems, first_scratch, second_scratch = refs[47:53], refs[53:55], refs[55:64], refs[64:]
    me, _, _, chips = line_position()
    width = back.shape[2] // 2
    weight_copy = copy_in(pair_weight, weight, sems.at[0])
    data_copy = copy_in(back, data, sems.at[1])
    own_copy = copy_in(down_grad.at[lax.axis_index("fsdp")], own_down, sems.at[3])

    def produce(piece, chunk):
        return rdot(data[piece], weight[pl.ds(pl.multiple_of(chunk * WIDE, WIDE), WIDE), :])

    each = 2 * width // WIDE

    def down_block(chunk):
        return tile(chunk // each, width), tile(chunk % each, WIDE)

    def down_copy(chunk):
        source = down_weight.at[:, tile(chunk, WIDE)]
        return pltpu.make_async_copy(source, weight.at[down_block(chunk)], sems.at[5 + chunk])

    def produce_hidden(piece, chunk):
        return dot(data[piece, :, :width], weight[down_block(chunk)])

    def consume(piece):
        copy = copy_in(land.at[piece], low, sems.at[4])
        copy.wait()
        context_grad[piece] = rdot(low[...], out_weight[...]).astype(BF16)

    def products(slot):
        return ((slab[slot], data[...]),)

    slabs = Slabs((normed,), (slab,), slab_out, pair_grad, slab_sems, products)
    half = own_down.shape[0] // 2
    halves = [pl.ds(h * half, half) for h in range(2)]
    downs = [
        FsdpSum(down_grad, *down_refs[h], own=own_down.at[halves[h]], part=halves[h]) for h in range(2)
    ]
    down_gathers = [Gather(down_land, down_sems[h], part=halves[h]) for h in range(2)]

    def down_ready(h):
        downs[h].arrive()
        if h == 0:
            downs[1].start()
        downs[h].add(own_down.at[halves[h]])
        copy = copy_in(own_down.at[halves[h]], down_land.at[me, halves[h]], sems.at[3])
        copy.wait()
        down_gathers[h].step(0)

    pair = FsdpSum(pair_grad, pair_in, *pair_sems, own=own_down)
    gather = Gather(land, gather_sems, consume)
    scatter = Scatter(first_scratch, produce, total)
    hidden_scatter = Scatter(second_scratch, produce_hidden, total)
    scatter.begin()
    hidden_scatter.begin()
    full_barrier()
    downs[0].start()
    slabs.fetch(0)
    weight_copy.wait()
    data_copy.wait()
    scatter.prepare(0)

    def step(time):
        scatter.step(time)
        scatter.prepare(time + 1)

        @pl.when(time == 0)
        def _():
            own_copy.wait()
            down_ready(0)

        @pl.when(time >= 1)
        def _():
            down_gathers[0].step(time)

        @pl.when(time == 1)
        def _():
            down_ready(1)

        @pl.when(time >= 2)
        def _():
            down_gathers[1].step(time - 1)

        @pl.when(time < 3)
        def _():
            slabs.run(time * slabs.count // 3, (time + 1) * slabs.count // 3)
            slabs.settle((time + 1) * slabs.count // 3)

        @pl.when(time == 2)
        def _():
            pair.start()

    loop(chips - 1, step)
    scatter.finish()
    down_gathers[0].step(chips - 1)
    down_gathers[1].step(chips - 2)
    for chunk in range(CHUNKS):
        down_copy(chunk).start()
    act_copy = copy_in(activation, data.at[:, :, pl.ds(0, width)], sems.at[1])
    gain_sum[...] = jnp.zeros_like(gain_sum)

    def norm(block):
        through, terms = rms_back(middle[block, :], gain_rows[1:2, :], total[block, :])
        value = grad[block, :].astype(F32) + through
        grad_middle[block, :] = value
        low[block, :] = value.astype(BF16)
        gain_sum[0:1, :] += jnp.sum(terms, axis=0, keepdims=True)

    row_blocks(middle.shape[0], norm)
    low_copy = copy_in(low, land.at[me], sems.at[3])
    low_copy.wait()
    gather.step(0)
    for chunk in range(CHUNKS):
        down_copy(chunk).wait()
    act_copy.wait()
    hidden_scatter.prepare(0)

    def add_pairs():
        pair.arrive()
        shard = lax.axis_index("fsdp")
        count, size = slab.shape[2], slab.shape[3]
        per = own_down.shape[0] // count
        tiles = 2 * width // size

        def arrivals(index):
            slot = index % 2
            copies = []
            for i in range(pair.peers + 1):
                source = pair_grad.at[shard] if i == 0 else pair_in.at[i - 1]
                for j in range(per):
                    at = i * per + j
                    block = source.at[pl.ds(j * count, count), tile(index, size)]
                    copies.append(
                        pltpu.make_async_copy(block, slab.at[slot, at], sum_sems.at[slot, at])
                    )
            return copies

        def leave(index):
            slot = index % 2
            return [
                pltpu.make_async_copy(
                    slab.at[slot, j],
                    pair_sum.at[pl.ds(j * count, count), tile(index, size)],
                    sum_sems.at[slot, j],
                )
                for j in range(per)
            ]

        for copy in arrivals(0):
            copy.start()

        def one(index):
            @pl.when(index > 0)
            def _():
                for copy in leave(index - 1):
                    copy.wait()

            @pl.when(index + 1 < tiles)
            def _():
                for copy in arrivals(index + 1):
                    copy.start()

            for copy in arrivals(index):
                copy.wait()
            slot = index % 2
            for j in range(per):
                value = slab[slot, j].astype(F32)
                for i in range(1, pair.peers + 1):
                    value = value + slab[slot, i * per + j].astype(F32)
                slab[slot, j] = value.astype(BF16)
            for copy in leave(index):
                copy.start()

        loop(tiles, one)
        for copy in leave(tiles - 1):
            copy.wait()

    def turn_step(time):
        hidden_scatter.step(time)
        hidden_scatter.prepare(time + 1)

        @pl.when(time == chips - 2)
        def _():
            add_pairs()

        gather.step(time + 1)

        @pl.when(time == 1)
        def _():
            down_gathers[1].step(chips - 1)

    loop(chips - 1, turn_step)
    hidden_scatter.finish()
    gather.finish()
    for h in range(2):
        down_gathers[h].finish()
        downs[h].finish()
    pair.finish()

    def add(block):
        hidden[block, :] = (middle[block, :] + total[block, :]).astype(BF16)

    row_blocks(middle.shape[0], add)


def turn(back, pair_weight, down_weight, activation, out_weight, middle, grad, gain_rows, down_grad, normed):
    parts, count, feed_width = activation.shape
    shards, rows, _ = down_grad.shape
    width = out_weight.shape[0]
    return pl.pallas_call(
        turn_kernel,
        out_shape=(
            jax.ShapeDtypeStruct((count, D), F32),
            jax.ShapeDtypeStruct((parts, count, D), BF16),
            jax.ShapeDtypeStruct((8, D), F32),
            jax.ShapeDtypeStruct((parts, rows, feed_width), BF16),
            jax.ShapeDtypeStruct((parts, count, width), BF16),
            jax.ShapeDtypeStruct((count, D), BF16),
            jax.ShapeDtypeStruct((shards - 1, rows, 2 * feed_width), BF16),
            jax.ShapeDtypeStruct((shards, rows, 2 * feed_width), BF16),
            jax.ShapeDtypeStruct((rows, 2 * feed_width), BF16),
        ),
        in_specs=[HBM] * 4 + [WHOLE] * 4 + [HBM] * 2,
        out_specs=(WHOLE, HBM, WHOLE, HBM, WHOLE, WHOLE, HBM, HBM, HBM),
        scratch_shapes=[
            VMEM((D, 2 * feed_width), BF16),
            VMEM((parts, count, 2 * feed_width), BF16),
            VMEM((count, D), F32),
            VMEM((count, D), BF16),
            VMEM((rows, feed_width), BF16),
            pltpu.SemaphoreType.DMA((5 + CHUNKS,)),
            VMEM((2, parts, count, slab_size(parts)), BF16),
            VMEM((slab_size(parts), 2 * feed_width), BF16),
            pltpu.SemaphoreType.DMA((3,)),
            pltpu.SemaphoreType.DMA((2, parts)),
        ]
        + fsdp_scratch(shards, rows // 2, feed_width)
        + fsdp_scratch(shards, rows // 2, feed_width)
        + gather_scratch(parts // 2)
        + gather_scratch(parts // 2)
        + gather_scratch(parts // 2)
        + [pltpu.SemaphoreType.DMA((shards,))] * 2
        + scatter_scratch(parts // 2, count)
        + scatter_scratch(parts // 2, count),
        compiler_params=params(3, 63),
        cost_estimate=cost(185),
        name="turn",
    )(
        back,
        pair_weight,
        down_weight,
        activation,
        out_weight,
        middle,
        grad,
        gain_rows,
        down_grad,
        normed,
    )


def last_kernel(*refs):
    back, weights, x, grad_middle, gain_rows, gain_two, gain_heads, context, normed, low = refs[:10]
    hidden, gain_out, head_grad, land = refs[10:14]
    weight, weight_sem, total, gain_one, pack, pack_in, shard_sum, shard_in = refs[14:22]
    slabs_in, slab_out, slab_sems, own_head, refs = refs[22:24], refs[24], refs[25], refs[26], refs[27:]
    small, head_refs, refs = refs[:4], (refs[4:7], refs[7:10]), refs[10:]
    gather_sems, scratch = (refs[:6], refs[6:12]), refs[12:]
    me, _, _, chips = line_position()
    shard = lax.axis_index("fsdp")
    shards, ahead, _ = peers_of("fsdp")
    parts, next_part, _ = peers_of("ctx")
    copy = copy_in(weights, weight, weight_sem)

    def produce(piece, chunk):
        return rdot(back[piece], weight[pl.ds(pl.multiple_of(chunk * WIDE, WIDE), WIDE), :])

    def products(slot):
        return (slabs_in[0][slot], back[...]), (slabs_in[1][slot], context[...])

    half = own_head.shape[0] // 2
    halves = [pl.ds(h * half, half) for h in range(2)]
    per_half = (D // half) // 2 * half // slab_out.shape[0]
    inner = half // slab_out.shape[0]

    def place(index):
        side, rest = index // per_half, index % per_half
        return (rest // inner) * 2 * inner + side * inner + rest % inner

    slabs = Slabs((normed, low), slabs_in, slab_out, head_grad, slab_sems, products, place)
    heads = [
        FsdpSum(head_grad, *head_refs[h], own=own_head.at[halves[h]], part=halves[h]) for h in range(2)
    ]
    gathers = [Gather(land, gather_sems[h], part=halves[h]) for h in range(2)]

    def head_ready(h):
        heads[h].collect(land.at[me, halves[h]])
        gathers[h].step(0)
    scatter = Scatter(scratch, produce, total)
    scatter.begin()
    slabs.fetch(0)
    full_barrier()
    copy.wait()
    for h in range(2):
        slabs.run(h * per_half, (h + 1) * per_half)
        slabs.settle((h + 1) * per_half)
        heads[h].start()
    own = copy_in(head_grad.at[shard], own_head, weight_sem)
    own.wait()
    scatter.prepare(0)

    def step(time):
        scatter.step(time)
        scatter.prepare(time + 1)

        @pl.when(time == 0)
        def _():
            head_ready(0)

        @pl.when(time >= 1)
        def _():
            gathers[0].step(time)

        @pl.when(time == 1)
        def _():
            head_ready(1)

        @pl.when(time >= 2)
        def _():
            gathers[1].step(time - 1)

    loop(chips - 1, step)
    scatter.finish()
    gathers[0].step(chips - 1)
    gathers[1].step(chips - 2)
    gain_one[...] = jnp.zeros_like(gain_one)

    def norm(block):
        through, terms = rms_back(x[block, :].astype(F32), gain_rows[0:1, :], total[block, :])
        hidden[block, :] = grad_middle[block, :] + through
        gain_one[0:1, :] += jnp.sum(terms, axis=0, keepdims=True)

    row_blocks(x.shape[0], norm)

    rows = D // (shards + 1)
    lanes = rows // 128
    pack[...] = jnp.zeros_like(pack)
    for owner in range(shards + 1):
        for j in range(lanes):
            at = owner * rows + j * 128
            pack[owner, j : j + 1, :] = gain_one[0:1, at : at + 128]
            pack[owner, lanes + j : lanes + j + 1, :] = gain_two[0:1, at : at + 128]
        pack[owner, 2 * lanes : 2 * lanes + 2, :] = gain_heads[0:2, :]

    def pack_copy(i):
        return send(pack.at[ahead(i)], pack_in.at[i], small[0].at[i], small[1].at[i], "fsdp", ahead(i))

    def sum_copy(i):
        return send(shard_sum, shard_in.at[i], small[2].at[i], small[3].at[i], "ctx", next_part(i))

    loop(shards, lambda i: pack_copy(i).start())
    shard_sum[...] = pack[shard]

    def add_pack(i):
        pack_copy(i).wait_recv()
        shard_sum[...] += pack_in[i]

    loop(shards, add_pack)
    loop(parts, lambda i: sum_copy(i).start())
    gain_out[...] = shard_sum[...]

    def add_sum(i):
        sum_copy(i).wait_recv()
        gain_out[...] += shard_in[i]

    loop(parts, add_sum)
    gathers[1].step(chips - 1)
    for h in range(2):
        gathers[h].finish()
        heads[h].finish()
    loop(shards, lambda i: pack_copy(i).wait_send())
    loop(parts, lambda i: sum_copy(i).wait_send())


def last(back, weights, hidden, grad_middle, gain_rows, gain_two, gain_heads, context, normed, low, shards):
    parts, count, width = back.shape
    rows = D // shards
    query_width = context.shape[2]
    head_width = width + query_width
    return pl.pallas_call(
        last_kernel,
        out_shape=(
            jax.ShapeDtypeStruct((count, D), F32),
            jax.ShapeDtypeStruct((16, 128), F32),
            jax.ShapeDtypeStruct((shards, rows, head_width), BF16),
            jax.ShapeDtypeStruct((parts, rows, head_width), BF16),
        ),
        in_specs=[WHOLE, HBM] + [WHOLE] * 6 + [HBM] * 2,
        out_specs=(WHOLE, WHOLE, HBM, WHOLE),
        scratch_shapes=[
            VMEM((D, width), BF16),
            pltpu.SemaphoreType.DMA,
            VMEM((count, D), F32),
            VMEM((8, D), F32),
            VMEM((shards, 16, 128), F32),
            VMEM((shards, 16, 128), F32),
            VMEM((16, 128), F32),
            VMEM((parts, 16, 128), F32),
            VMEM((2, parts, count, slab_size(parts)), BF16),
            VMEM((2, parts, count, slab_size(parts)), BF16),
            VMEM((slab_size(parts), head_width), BF16),
            pltpu.SemaphoreType.DMA((5,)),
            VMEM((rows, head_width), BF16),
        ]
        + [pltpu.SemaphoreType.DMA((shards,))] * 2
        + [pltpu.SemaphoreType.DMA((parts,))] * 2
        + fsdp_scratch(shards, rows // 2, head_width)
        + fsdp_scratch(shards, rows // 2, head_width)
        + gather_scratch(parts // 2)
        + gather_scratch(parts // 2)
        + scatter_scratch(parts // 2, count),
        compiler_params=params(5, 60),
        cost_estimate=cost(90),
        name="last",
    )(back, weights, hidden, grad_middle, gain_rows, gain_two, gain_heads, context, normed, low)


def attention_back_kernel(heads, *refs):
    queries, keys, values, out_grad, inverse, context, proj, cosine, sine, gain_rows = refs[:10]
    token_info, back, gain_sum, key_grad, value_grad, query_grad = refs[10:]
    tokens = proj.shape[0]
    key_at = heads * HEAD_SIZE
    key_grad[...] = jnp.zeros_like(key_grad)
    value_grad[...] = jnp.zeros_like(value_grad)
    gain_sum[...] = jnp.zeros_like(gain_sum)

    def through(block, lanes, grad, row):
        turned = pltpu.roll(grad, HEAD_SIZE // 2, 1)
        unrotated = grad * cosine[block, :] - turned * sine[block, :]
        result, terms = rms_back(proj[block, lanes], gain_rows[row + 2 : row + 3, :HEAD_SIZE], unrotated)
        back[block, lanes] = result.astype(BF16)
        gain_sum[row : row + 1, :] += jnp.sum(terms, axis=0, keepdims=True)

    count = token_info.shape[2]
    each = KEY_TILE // count

    def attend(index):
        block = tile(index, QUERY_TILE)
        query_ids = token_info[index, 1:2, :].astype(F32)
        shifts = []
        for h in range(heads):
            lanes = slice(h * HEAD_SIZE, (h + 1) * HEAD_SIZE)
            products = out_grad[block, lanes].astype(F32) * context[block, lanes].astype(F32)
            shift = lax.dot_general(
                jnp.ones((8, HEAD_SIZE), F32),
                products,
                (((1,), (1,)), ((), ())),
                precision=lax.Precision.HIGHEST,
                preferred_element_type=F32,
            )[0:1, :]
            shifts.append(shift)
        query_grad[...] = jnp.zeros_like(query_grad)

        def one(key_tile):
            span = tile(key_tile, KEY_TILE)
            key, value = keys[span, :], values[span, :]
            key_ids = jnp.concatenate(
                [
                    jnp.broadcast_to(
                        token_info[key_tile * each + j, 1:2, :].astype(F32), (128, count)
                    ).T[:, 0:1]
                    for j in range(each)
                ],
                axis=0,
            )
            allowed = key_ids <= query_ids
            for h in range(heads):
                lanes = slice(h * HEAD_SIZE, (h + 1) * HEAD_SIZE)
                query, grad = queries[block, lanes], out_grad[block, lanes]
                expon = jnp.exp(rdot(key, query)) * inverse[h : h + 1, block]
                probs = jnp.where(allowed, expon, 0.0)
                grad_scores = (probs * (rdot(value, grad) - shifts[h])).astype(BF16)
                value_grad[span, :] += dot(probs.astype(BF16), grad)
                key_grad[span, :] += dot(grad_scores, query)
                query_grad[:, lanes] += tdot(grad_scores, key)

        loop(reach(index, tokens), one)
        for h in range(heads):
            lanes = slice(h * HEAD_SIZE, (h + 1) * HEAD_SIZE)
            through(block, lanes, query_grad[:, lanes] * HEAD_SIZE ** (-0.5), 0)

    loop(tokens // QUERY_TILE, attend)

    def finish(index):
        block = pl.ds(pl.multiple_of(index * QUERY_TILE, QUERY_TILE), QUERY_TILE)
        through(block, slice(key_at, key_at + HEAD_SIZE), key_grad[block, :], 1)
        back[block, key_at + HEAD_SIZE : key_at + 2 * HEAD_SIZE] = value_grad[block, :].astype(BF16)

    loop(tokens // QUERY_TILE, finish)


def attention_back(heads, *operands):
    tokens = operands[0].shape[0]
    width = heads * HEAD_SIZE
    return pl.pallas_call(
        functools.partial(attention_back_kernel, heads),
        out_shape=(
            jax.ShapeDtypeStruct((tokens, width + 2 * HEAD_SIZE), BF16),
            jax.ShapeDtypeStruct((8, HEAD_SIZE), F32),
        ),
        in_specs=[WHOLE] * len(operands),
        out_specs=(WHOLE,) * 2,
        scratch_shapes=[
            VMEM((tokens, HEAD_SIZE), F32),
            VMEM((tokens, HEAD_SIZE), F32),
            VMEM((QUERY_TILE, width), F32),
        ],
        compiler_params=pltpu.CompilerParams(vmem_limit_bytes=62 * 1024 * 1024),
        cost_estimate=cost(38),
        name="attention_back",
    )(*operands)


def spread_kernel(width, head_source, pair_source, down_source, *targets):
    query, key, value, out, gate, up, down = targets
    second = width + HEAD_SIZE
    third = second + HEAD_SIZE
    query[...] = head_source[0, :, :width].astype(F32)
    key[...] = head_source[0, :, width:second].astype(F32)
    value[...] = head_source[0, :, second:third].astype(F32)
    out[...] = head_source[0, :, third:].astype(F32).T
    feed_width = gate.shape[1]
    gate[...] = pair_source[0, :, :feed_width].astype(F32)
    up[...] = pair_source[0, :, feed_width:].astype(F32)
    down[...] = down_source[0].astype(F32).T


def spread(head_parts, pair_parts, down_parts, width):
    parts, rows, _ = head_parts.shape
    feed_width = down_parts.shape[2]
    sources = (head_parts, pair_parts, down_parts)

    def side_by_side(columns):
        shape = jax.ShapeDtypeStruct((rows, parts * columns), F32)
        return shape, pl.BlockSpec((rows, columns), lambda i: (0, i))

    def stacked(columns):
        shape = jax.ShapeDtypeStruct((parts * columns, rows), F32)
        return shape, pl.BlockSpec((columns, rows), lambda i: (i, 0))

    outs = (
        side_by_side(width),
        side_by_side(HEAD_SIZE),
        side_by_side(HEAD_SIZE),
        stacked(width),
        side_by_side(feed_width),
        side_by_side(feed_width),
        stacked(feed_width),
    )
    return pl.pallas_call(
        functools.partial(spread_kernel, width),
        out_shape=tuple(shape for shape, _ in outs),
        grid=(parts,),
        in_specs=[pl.BlockSpec((1, *source.shape[1:]), lambda i: (i, 0, 0)) for source in sources],
        out_specs=tuple(spec for _, spec in outs),
        compiler_params=pltpu.CompilerParams(vmem_limit_bytes=60 * 1024 * 1024),
        name="spread",
    )(*sources)


def by_row(array):
    return with_layout_constraint(array, Layout(major_to_minor=(0, 1)))


def local(
    hidden_in,
    weight_query,
    key_weight_matrix,
    weight_value,
    weight_out,
    weight_gate,
    weight_up,
    weight_down,
    gain_attention,
    gain_feed,
    gain_query,
    gain_key,
    positions,
    token_block_index,
    grad_out,
):
    parts = lax.axis_size("ctx")
    shards = lax.axis_size("fsdp")
    shard = lax.axis_index("fsdp")
    heads = QUERY_HEADS // parts
    sharers = parts // KEY_VALUE_HEADS
    width = heads * HEAD_SIZE
    feed_width = FF // parts
    rows = D // shards
    head_rows = HEAD_SIZE // shards
    count = hidden_in.shape[1]
    tokens = parts * count

    def gather_parts(piece):
        return lax.all_gather(piece, "ctx", axis=0)

    own_gains = jnp.concatenate([gain_attention, gain_feed, gain_query, gain_key]).astype(F32)
    own_gains = jnp.pad(own_gains, (0, 2048 - own_gains.shape[0])).reshape(16, 128)
    own_tokens = jnp.pad(jnp.stack([positions[0], token_block_index[0]]), ((0, 6), (0, 0)))
    half = HEAD_SIZE // 2
    freq = THETA ** (-(jnp.arange(half).astype(F32) * 2.0 / HEAD_SIZE))
    freq = jnp.broadcast_to(jnp.concatenate([freq, freq]), (8, HEAD_SIZE))
    hidden, grad = hidden_in[0], grad_out[0]
    weights = (
        weight_query,
        key_weight_matrix,
        weight_value,
        weight_out,
        weight_gate,
        weight_up,
        weight_down,
    )
    (
        normed_all,
        grad_all,
        normed_two_all,
        activation,
        back,
        proj,
        cosine,
        sine,
        queries,
        keys,
        values,
        context,
        inverse,
        middle,
        gain_rows,
        gains,
        whole,
        heads_weight,
        out_weight,
        pair_weight,
        down_weight,
    ) = forward(hidden, grad, own_gains, own_tokens, freq, weights, shards, parts, heads)
    proj = proj.reshape(tokens, width + 2 * HEAD_SIZE)

    flat_grad = grad_all.reshape(tokens, D)
    flat_activation = activation.reshape(tokens, feed_width)
    down_grad = by_row(tdot(flat_grad, flat_activation).astype(BF16))
    grad_middle, low_all, gain_two, down_parts, context_grad, hidden_out, _, _, feed_shard = turn(
        back,
        pair_weight,
        down_weight,
        activation,
        out_weight,
        middle,
        grad,
        gain_rows,
        down_grad.reshape(shards, rows, feed_width),
        normed_two_all,
    )
    feed_parts = gather_parts(feed_shard)
    context_grad = context_grad.reshape(tokens, width)
    grad_qkv, gain_heads = attention_back(
        heads,
        queries,
        keys,
        values,
        context_grad,
        inverse,
        context,
        proj,
        cosine,
        sine,
        gain_rows,
        whole,
    )
    grad_hidden, gain_sums, _, head_parts = last(
        grad_qkv.reshape(parts, count, -1),
        heads_weight,
        hidden,
        grad_middle,
        gain_rows,
        gain_two,
        gain_heads,
        context.reshape(parts, count, width),
        normed_all,
        low_all,
        shards,
    )

    gain_sums = gain_sums.reshape(-1)
    grad_query, grad_key, grad_value, grad_out_weight, grad_gate, grad_up, grad_down = spread(
        head_parts, feed_parts, down_parts, width
    )
    if sharers > 1:
        grad_key, grad_value = (
            part.reshape(rows, KEY_VALUE_HEADS, sharers, HEAD_SIZE).sum(axis=2).reshape(rows, -1)
            for part in (grad_key, grad_value)
        )
    return (
        hidden_out[None],
        grad_hidden[None],
        grad_query,
        grad_key,
        grad_value,
        grad_out_weight,
        grad_gate,
        grad_up,
        grad_down,
        gain_sums[:rows],
        gain_sums[rows : 2 * rows],
        lax.dynamic_slice_in_dim(gain_sums, 2 * rows + shard * head_rows, head_rows),
        lax.dynamic_slice_in_dim(gain_sums, 2 * rows + HEAD_SIZE + shard * head_rows, head_rows),
    )


def solution(mesh):
    tokens = P("fsdp", "ctx", None)
    by_rows = P("fsdp", None)
    by_columns = P(None, "fsdp")
    per_token = P("fsdp", "ctx")
    vector = P("fsdp")
    weights = (by_rows, by_rows, by_rows, by_columns, by_rows, by_rows, by_columns)
    return jax.shard_map(
        local,
        mesh=mesh,
        in_specs=(tokens, *weights, vector, vector, vector, vector, per_token, per_token, tokens),
        out_specs=(tokens, tokens, *weights, vector, vector, vector, vector),
        check_vma=False,
    )
```

```python
import functools

import jax
import jax.numpy as jnp
from jax import lax
from jax.experimental import pallas as pl
from jax.experimental.layout import Layout, with_layout_constraint
from jax.experimental.pallas import tpu as pltpu
from jax.sharding import PartitionSpec as P

D = 2048
QUERY_HEADS = 16
KEY_VALUE_HEADS = 8
HEAD_SIZE = 128
FF = 6144
EPS = 1e-06
THETA = 1000000.0
F32 = jnp.float32
BF16 = jnp.bfloat16
MESH = pl.DeviceIdType.MESH
VMEM = pltpu.VMEM
WHOLE = pl.BlockSpec(memory_space=pltpu.VMEM)
HBM = pl.BlockSpec(memory_space=pl.ANY)
CHUNKS = 4
WIDE = D // CHUNKS


def dot(left, right):
    return jnp.dot(left, right, preferred_element_type=F32)


def tdot(left, right):
    return lax.dot_general(left, right, (((0,), (0,)), ((), ())), preferred_element_type=F32)


def rdot(left, right):
    return lax.dot_general(left, right, (((1,), (1,)), ((), ())), preferred_element_type=F32)


def loop(count, body):
    def step(index, carry):
        body(index)
        return carry

    lax.fori_loop(0, count, step, 0)


def line_position():
    me = lax.axis_index("ctx")
    return me, me // 2, me % 2, lax.axis_size("ctx") // 2


def send(source, target, send_sem, recv_sem, axis, index):
    return pltpu.make_async_remote_copy(
        src_ref=source,
        dst_ref=target,
        send_sem=send_sem,
        recv_sem=recv_sem,
        device_id={axis: index},
        device_id_type=MESH,
    )


def line_barrier():
    me, chip, core, chips = line_position()
    barrier = pltpu.get_barrier_semaphore()

    def greet(index):
        pl.semaphore_signal(barrier, inc=1, device_id={"ctx": index}, device_id_type=MESH)

    greet(me + 1 - 2 * core)

    @pl.when(chip > 0)
    def _():
        greet(me - 2)

    @pl.when(chip < chips - 1)
    def _():
        greet(me + 2)

    peers = 1 + (chip > 0).astype(jnp.int32) + (chip < chips - 1).astype(jnp.int32)
    pl.semaphore_wait(barrier, peers)


def peers_of(axis):
    me, size = lax.axis_index(axis), lax.axis_size(axis)
    return size - 1, lambda i: (me + i + 1) % size, lambda i: (me + size - i - 1) % size


def full_barrier():
    barrier = pltpu.get_barrier_semaphore()
    total = 0
    for axis in ("fsdp", "ctx"):
        count, ahead, _ = peers_of(axis)
        loop(
            count,
            lambda i, axis=axis, ahead=ahead: pl.semaphore_signal(
                barrier, inc=1, device_id={axis: ahead(i)}, device_id_type=MESH
            ),
        )
        total += count
    pl.semaphore_wait(barrier, total)


def gather_scratch(chips):
    return [pltpu.SemaphoreType.DMA((chips,)) for _ in range(6)]


class Gather:
    def __init__(self, land, sems, consume=None, part=None):
        self.part = part
        self.land = land
        self.sems = sems
        self.consume = consume
        self.me, self.chip, self.core, self.chips = line_position()

    def place(self, piece):
        return self.land.at[piece] if self.part is None else self.land.at[piece, self.part]

    def right(self, step, source):
        ref = self.place(2 * source + self.core)
        return send(ref, ref, self.sems[0].at[step], self.sems[1].at[step], "ctx", self.me + 2)

    def left(self, step, source):
        ref = self.place(2 * source + self.core)
        return send(ref, ref, self.sems[2].at[step], self.sems[3].at[step], "ctx", self.me - 2)

    def across(self, source, core):
        ref = self.place(2 * source + core)
        other = self.me + 1 - 2 * self.core
        return send(ref, ref, self.sems[4].at[source], self.sems[5].at[source], "ctx", other)

    def step(self, step):
        self.move(step)
        self.use(step)

    def move(self, step):
        chip, core, chips = self.chip, self.core, self.chips
        low, high = chip - step, chip + step
        has_low = low >= 0
        has_high = jnp.logical_and(high < chips, step > 0)

        @pl.when(jnp.logical_and(has_low, step > 0))
        def _():
            self.right(step - 1, low).wait_recv()

        @pl.when(jnp.logical_and(has_low, chip < chips - 1))
        def _():
            self.right(step, low).start()

        @pl.when(has_high)
        def _():
            self.left(step - 1, high).wait_recv()

        @pl.when(jnp.logical_and(high < chips, chip > 0))
        def _():
            self.left(step, high).start()

        @pl.when(has_low)
        def _():
            self.across(low, core).start()

        @pl.when(has_high)
        def _():
            self.across(high, core).start()

    def use(self, step):
        chip, core, chips = self.chip, self.core, self.chips
        low, high = chip - step, chip + step

        def one(kind):
            upward = kind % 2
            crossed = kind // 2
            source = jnp.where(upward == 1, high, low)
            valid = jnp.where(upward == 1, jnp.logical_and(high < chips, step > 0), low >= 0)
            parity = jnp.where(crossed == 1, 1 - core, core)

            @pl.when(valid)
            def _():
                @pl.when(crossed == 1)
                def _():
                    self.across(source, parity).wait_recv()

                if self.consume is not None:
                    self.consume(2 * source + parity)

        loop(4, one)

    def finish(self):
        chip, core, chips = self.chip, self.core, self.chips

        def one(step):
            @pl.when(jnp.logical_and(chip - step >= 0, chip < chips - 1))
            def _():
                self.right(step, chip - step).wait_send()

            @pl.when(jnp.logical_and(chip + step < chips, chip > 0))
            def _():
                self.left(step, chip + step).wait_send()

            self.across(step, core).wait_send()

        loop(chips, one)


def scatter_scratch(chips, rows):
    buffers = [VMEM((count, CHUNKS, rows, WIDE), BF16) for count in (chips + 1, 2, chips)]
    return buffers + [pltpu.SemaphoreType.DMA((chips, CHUNKS)) for _ in range(6)]


class Scatter:
    def __init__(self, scratch, produce, total, ready=None):
        self.ready = ready
        self.line, self.out, self.other = scratch[:3]
        self.sems = scratch[3:]
        self.produce = produce
        self.total = total
        self.me, self.chip, self.core, self.chips = line_position()


    def right(self, step, chunk):
        ref = self.line.at[step, chunk]
        sems = self.sems
        return send(ref, ref, sems[0].at[step, chunk], sems[1].at[step, chunk], "ctx", self.me + 2)

    def left(self, step, chunk):
        ref = self.line.at[self.chips - step, chunk]
        sems = self.sems
        return send(ref, ref, sems[2].at[step, chunk], sems[3].at[step, chunk], "ctx", self.me - 2)

    def across(self, target, chunk, slot=0):
        sems = self.sems
        return send(
            self.out.at[slot, chunk],
            self.other.at[target, chunk],
            sems[4].at[target, chunk],
            sems[5].at[target, chunk],
            "ctx",
            self.me + 1 - 2 * self.core,
        )

    def begin(self):
        def clear(index):
            slot, chunk = index // CHUNKS, index % CHUNKS
            at_left = jnp.logical_and(self.chip == 0, slot < self.chips)
            at_right = jnp.logical_and(self.chip == self.chips - 1, slot > 0)

            @pl.when(jnp.logical_or(at_left, at_right))
            def _():
                self.line[slot, chunk] = jnp.zeros(self.line.shape[2:], BF16)

        loop((self.chips + 1) * CHUNKS, clear)

    def when_right(self, time):
        return jnp.logical_and(time >= self.chip, time < self.chips - 1)

    def when_left(self, time):
        return jnp.logical_and(time >= self.chips - 1 - self.chip, time < self.chips - 1)

    def prepare(self, time):
        chip, chips = self.chip, self.chips

        def cross(target, slot, before, used):
            if self.ready is not None:
                self.ready(target)

            def one(chunk):
                @pl.when(used)
                def _():
                    self.across(before, chunk, slot).wait_send()

                piece = 2 * target + 1 - self.core
                self.out[slot, chunk] = self.produce(piece, chunk).astype(BF16)
                self.across(target, chunk, slot).start()

            loop(CHUNKS, one)

        @pl.when(self.when_right(time))
        def _():
            target = chips - 1 - time + chip
            cross(target, 0, target + 1, time > chip)

        @pl.when(self.when_left(time))
        def _():
            target = time - (chips - 1 - chip)
            cross(target, 1, target - 1, target > 0)

        @pl.when(time == chips - 1)
        def _():
            cross(chip, 0, chip + 1, chip < chips - 1)

    def step(self, time):
        chip, core, chips = self.chip, self.core, self.chips

        @pl.when(self.when_right(time))
        def _():
            step = time - chip
            target = chips - 1 - step

            def one(chunk):
                self.across(target, chunk).wait_recv()

                @pl.when(chip > 0)
                def _():
                    self.right(step, chunk).wait_recv()

                value = self.produce(2 * target + core, chunk) + self.other[target, chunk].astype(F32)
                value = value + self.line[step, chunk].astype(F32)
                self.line[step, chunk] = value.astype(BF16)
                self.right(step, chunk).start()

            loop(CHUNKS, one)

        @pl.when(self.when_left(time))
        def _():
            step = time - (chips - 1 - chip)

            def one(chunk):
                self.across(step, chunk).wait_recv()

                @pl.when(chip < chips - 1)
                def _():
                    self.left(step, chunk).wait_recv()

                value = self.produce(2 * step + core, chunk) + self.other[step, chunk].astype(F32)
                value = value + self.line[chips - step, chunk].astype(F32)
                self.line[chips - step, chunk] = value.astype(BF16)
                self.left(step, chunk).start()

            loop(CHUNKS, one)

    def finish(self):
        chip, core, chips = self.chip, self.core, self.chips
        last = chips - 1 - chip

        def one(chunk):
            self.across(chip, chunk).wait_recv()
            value = self.produce(2 * chip + core, chunk) + self.other[chip, chunk].astype(F32)

            @pl.when(chip > 0)
            def _():
                self.right(last, chunk).wait_recv()

            @pl.when(chip < chips - 1)
            def _():
                self.left(chip, chunk).wait_recv()

            value = value + self.line[last, chunk].astype(F32)
            value = value + self.line[chips - chip, chunk].astype(F32)
            self.total[:, pl.ds(pl.multiple_of(chunk * WIDE, WIDE), WIDE)] = value

        loop(CHUNKS, one)

        def drain(index):
            step, chunk = index // CHUNKS, index % CHUNKS

            @pl.when(step < last)
            def _():
                self.right(step, chunk).wait_send()

            @pl.when(step < chip)
            def _():
                self.left(step, chunk).wait_send()

            @pl.when(jnp.logical_or(step == chip, step == chip - 1))
            def _():
                self.across(step, chunk, jnp.where(step == chip, 0, 1)).wait_send()

        loop(chips * CHUNKS, drain)


def tile(index, size):
    return pl.ds(pl.multiple_of(index * size, size), size)


def row_blocks(rows, body, size=32):
    def one(index):
        body(pl.ds(pl.multiple_of(index * size, size), size))

    loop(rows // size, one)


def inverse_norm(value):
    return lax.rsqrt(jnp.mean(value * value, axis=-1, keepdims=True) + EPS)


def params(identity, megabytes):
    return pltpu.CompilerParams(
        collective_id=identity,
        has_side_effects=True,
        vmem_limit_bytes=megabytes * 1024 * 1024,
    )


def cost(microseconds):
    return pl.CostEstimate(
        flops=int(microseconds * 1.15e9), bytes_accessed=1024, transcendentals=0
    )


class FsdpSum:
    def __init__(self, grad, arrived, send_sems, recv_sems, own=None, part=slice(None)):
        self.grad, self.arrived, self.part = grad, arrived, part
        self.own = grad.at[lax.axis_index("fsdp")] if own is None else own
        self.sems = send_sems, recv_sems
        self.peers, self.ahead, _ = peers_of("fsdp")

    def copy(self, i):
        target = self.ahead(i)
        return send(
            self.grad.at[target, self.part], self.arrived.at[i], self.sems[0].at[i], self.sems[1].at[i], "fsdp", target
        )

    def start(self):
        loop(self.peers, lambda i: self.copy(i).start())

    def arrive(self):
        loop(self.peers, lambda i: self.copy(i).wait_recv())

    def collect(self, target):
        self.arrive()
        self.add(target)

    def add(self, target):
        def one(block):
            value = self.own[block, :].astype(F32)
            for i in range(self.peers):
                value = value + self.arrived[i, block].astype(F32)
            target[block, :] = value.astype(BF16)

        row_blocks(self.own.shape[0], one)

    def finish(self):
        loop(self.peers, lambda i: self.copy(i).wait_send())


def fsdp_scratch(shards, rows, width):
    return [VMEM((shards - 1, rows, width), BF16)] + [pltpu.SemaphoreType.DMA((shards,))] * 2


def sine_cosine(angle):
    count = jnp.floor(angle * 0.6366197723675814 + 0.5)
    rest = angle - count * 1.5703125
    rest = rest - count * 4.837512969970703e-4
    rest = rest - count * 7.549789948768648e-8
    square = rest * rest
    sine = -1.9515295891e-4 * square + 8.3321608736e-3
    sine = rest + rest * square * (sine * square - 1.6666654611e-1)
    cosine = 2.443315711809948e-5 * square - 1.388731625493765e-3
    cosine = 1.0 - 0.5 * square + square * square * (cosine * square + 4.166664568298827e-2)
    quarter = jnp.bitwise_and(count.astype(jnp.int32), 3)
    odd = jnp.bitwise_and(quarter, 1) == 1
    sine, cosine = jnp.where(odd, cosine, sine), jnp.where(odd, sine, cosine)
    sine = jnp.where(quarter >= 2, -sine, sine)
    cosine = jnp.where(jnp.logical_or(quarter == 1, quarter == 2), -cosine, cosine)
    return sine, cosine


class Shares:
    def __init__(self, source, target_of, own_sem, sems):
        self.source, self.target_of = source, target_of
        self.own_sem, self.sems = own_sem, sems
        self.peers, self.ahead, self.behind = peers_of("fsdp")
        self.shard = lax.axis_index("fsdp")

    def copy(self, i, owner):
        sems = self.sems
        target = self.target_of(owner)
        return send(self.source, target, sems[0].at[i], sems[1].at[i], "fsdp", self.ahead(i))

    def own(self):
        return pltpu.make_async_copy(self.source, self.target_of(self.shard), self.own_sem)

    def start(self):
        loop(self.peers, lambda i: self.copy(i, self.shard).start())
        self.own().start()

    def arrive(self):
        self.own().wait()
        loop(self.peers, lambda i: self.copy(i, self.behind(i)).wait_recv())

    def finish(self):
        loop(self.peers, lambda i: self.copy(i, self.shard).wait_send())


def shares_scratch(count, shards):
    return [pltpu.SemaphoreType.DMA((count,))] + [pltpu.SemaphoreType.DMA((shards,))] * (2 * count)


def copy_in(source, target, sem):
    copy = pltpu.make_async_copy(source, target, sem)
    copy.start()
    return copy


QUERY_TILE = 256
KEY_TILE = 512


def reach(index, tokens):
    return jnp.minimum((index + 2) * QUERY_TILE + KEY_TILE - 1, tokens) // KEY_TILE


def head_norm(value, gain, cosine, sine):
    normed = value * inverse_norm(value) * gain
    return normed * cosine + pltpu.roll(normed, HEAD_SIZE // 2, 1) * sine


def forward_kernel(heads, *refs):
    x, grad, gains, token_info, freq = refs[:5]
    sources, refs = refs[5:12], refs[12:]
    normed_land, grad_land, two_land, activation, back = refs[:5]
    proj, cosine, sine, queries, keys, values, context, inverse = refs[5:13]
    middle, gain_rows, all_gains, all_tokens = refs[13:17]
    head_weight, out_weight, pair_weight, down_weight = refs[17:21]
    refs = refs[21:]
    pair, down, own, piece_in, grad_in, act_out, back_out, total, sems = refs[:9]
    small, refs = refs[9:13], refs[13:]
    share_own, share_sems, refs = refs[0], refs[1:15], refs[15:]
    first_sems, grad_sems, two_sems, scratch = refs[:6], refs[6:12], refs[12:18], refs[18:]
    me, _, _, chips = line_position()
    shard = lax.axis_index("fsdp")
    shards, ahead, behind = peers_of("fsdp")
    parts, next_part, past_part = peers_of("ctx")
    count = x.shape[0]
    tokens = 2 * chips * count
    width = heads * HEAD_SIZE
    feed_width = down.shape[0]
    rows = D // (shards + 1)
    lanes = rows // 128
    key_head = me // (2 * chips // KEY_VALUE_HEADS)

    def gain_copy(i, slot):
        return send(gains, all_gains.at[slot], small[0].at[i], small[1].at[i], "fsdp", ahead(i))

    def token_copy(i, slot):
        return send(token_info, all_tokens.at[slot], small[2].at[i], small[3].at[i], "ctx", next_part(i))

    def by_row(target, at, size):
        return lambda owner: target.at[tile(owner, rows), pl.ds(at, size)]

    def by_column(target):
        return lambda owner: target.at[:, tile(owner, rows)]

    places = (
        (sources[0].at[:, tile(me, width)], by_row(head_weight, 0, width)),
        (sources[1].at[:, tile(key_head, HEAD_SIZE)], by_row(head_weight, width, HEAD_SIZE)),
        (sources[2].at[:, tile(key_head, HEAD_SIZE)], by_row(head_weight, width + HEAD_SIZE, HEAD_SIZE)),
        (sources[3].at[tile(me, width), :], by_column(out_weight)),
        (sources[4].at[:, tile(me, feed_width)], by_row(pair, 0, feed_width)),
        (sources[5].at[:, tile(me, feed_width)], by_row(pair, feed_width, feed_width)),
        (sources[6].at[tile(me, feed_width), :], by_column(down)),
    )
    shares = [
        Shares(source, target_of, share_own.at[i], share_sems[2 * i : 2 * i + 2])
        for i, (source, target_of) in enumerate(places)
    ]

    full_barrier()
    loop(shards, lambda i: gain_copy(i, shard).start())
    loop(parts, lambda i: token_copy(i, me).start())
    for share in shares[:4]:
        share.start()
    grad_copy = copy_in(grad, grad_land.at[me], sems.at[0])
    all_gains[shard] = gains[...]
    all_tokens[me] = token_info[...]
    loop(shards, lambda i: gain_copy(i, behind(i)).wait_recv())
    for kind in range(2):
        for owner in range(shards + 1):
            for j in range(lanes):
                at = owner * rows + j * 128
                gain_rows[kind : kind + 1, at : at + 128] = all_gains[
                    owner, kind * lanes + j : kind * lanes + j + 1, :
                ]
    size = HEAD_SIZE // (shards + 1)
    for kind in range(2):
        gain_rows[2 + kind : 3 + kind, 0:HEAD_SIZE] = jnp.concatenate(
            [
                all_gains[
                    owner, 2 * lanes : 2 * lanes + 1, kind * size : (kind + 1) * size
                ]
                for owner in range(shards + 1)
            ],
            axis=1,
        )

    def norm(block):
        value = x[block, :].astype(F32)
        own[block, :] = (value * inverse_norm(value) * gain_rows[0:1, :]).astype(BF16)

    row_blocks(count, norm)
    own_copy = copy_in(own, normed_land.at[me], sems.at[1])
    own_copy.wait()

    def column(piece, row):
        values_in_lanes = all_tokens[piece, row : row + 1, :].astype(F32)
        return jnp.broadcast_to(values_in_lanes, (128, count)).T

    def project(piece):
        copy = copy_in(normed_land.at[piece], piece_in, sems.at[1])
        block = tile(piece, count)
        s, c = sine_cosine(column(piece, 0) * freq[0:1, :])
        lane = lax.broadcasted_iota(jnp.int32, s.shape, 1)
        s = jnp.where(lane < HEAD_SIZE // 2, -s, s)
        cosine[block, :] = c
        sine[block, :] = s
        copy.wait()
        proj[piece] = dot(piece_in[...], head_weight[...])

        def turned(at, row):
            return head_norm(proj[piece, :, at : at + HEAD_SIZE], gain_rows[row : row + 1, 0:HEAD_SIZE], c, s)

        for h in range(heads):
            at = h * HEAD_SIZE
            queries[block, at : at + HEAD_SIZE] = (turned(at, 2) * HEAD_SIZE ** (-0.5)).astype(BF16)
        keys[block, :] = turned(width, 3).astype(BF16)
        values[block, :] = proj[piece, :, width + HEAD_SIZE : width + 2 * HEAD_SIZE].astype(BF16)

    first_gather = Gather(normed_land, first_sems, project)
    grad_gather = Gather(grad_land, grad_sems)
    first_gather.move(0)
    loop(parts, lambda i: token_copy(i, past_part(i)).wait_recv())

    def first_step(step):
        first_gather.move(step + 1)

        @pl.when(step == 0)
        def _():
            for share in shares[:4]:
                share.arrive()
            for share in shares[4:]:
                share.start()

        first_gather.use(step)

    loop(chips - 1, first_step)
    grad_copy.wait()
    grad_gather.step(0)
    first_gather.use(chips - 1)

    def attend(index):
        block = tile(index, QUERY_TILE)
        query_ids = column(index, 1)[:, 0:1]
        each = KEY_TILE // count
        lanes_of = [slice(h * HEAD_SIZE, (h + 1) * HEAD_SIZE) for h in range(heads)]

        def one(key_tile, carry):
            span = tile(key_tile, KEY_TILE)
            key, value = keys[span, :], values[span, :]
            key_ids = jnp.concatenate(
                [all_tokens[key_tile * each + j, 1:2, :] for j in range(each)], axis=1
            ).astype(F32)
            allowed = key_ids <= query_ids
            result = []
            for head, (sums, total) in zip(lanes_of, carry):
                expon = jnp.where(allowed, jnp.exp(rdot(queries[block, head], key)), 0.0)
                sums = sums + dot(expon.astype(BF16), value)
                result.append((sums, total + jnp.sum(expon, axis=1, keepdims=True)))
            return tuple(result)

        start = (jnp.zeros((QUERY_TILE, HEAD_SIZE), F32), jnp.zeros((QUERY_TILE, 1), F32))
        results = lax.fori_loop(0, reach(index, tokens), one, (start,) * heads)
        for h, (head, (sums, total)) in enumerate(zip(lanes_of, results)):
            scale = 1.0 / total
            context[block, head] = (sums * scale).astype(BF16)
            inverse[h : h + 1, block] = jnp.broadcast_to(scale, (QUERY_TILE, HEAD_SIZE)).T[0:1, :]

    def ready(target):
        each = 2 * count // QUERY_TILE
        loop(each, lambda i: attend(target * each + i))

    def produce(piece, chunk):
        return dot(context[tile(piece, count), :], out_weight[:, tile(chunk, WIDE)])

    scatter = Scatter(scratch, produce, total, ready)
    scatter.begin()
    scatter.prepare(0)

    def scatter_step(time):
        scatter.step(time)
        scatter.prepare(time + 1)
        grad_gather.step(time + 1)

    loop(chips - 1, scatter_step)
    scatter.finish()

    def norm_two(block):
        value = x[block, :].astype(F32) + total[block, :]
        middle[block, :] = value
        own[block, :] = (value * inverse_norm(value) * gain_rows[1:2, :]).astype(BF16)

    row_blocks(count, norm_two)
    two_copy = copy_in(own, two_land.at[me], sems.at[1])
    two_copy.wait()
    for share in shares[4:]:
        share.arrive()
    outs = [
        copy_in(head_weight, refs_out, sems.at[2 + i])
        for i, (head_weight, refs_out) in enumerate(((pair, pair_weight), (down, down_weight)))
    ]
    feed_size = 256 if feed_width % 256 == 0 else 128

    def act_copy(piece):
        return pltpu.make_async_copy(act_out, activation.at[piece], sems.at[6])

    def back_copy(piece):
        return pltpu.make_async_copy(back_out, back.at[piece], sems.at[7])

    def feed(piece):
        copies = (
            copy_in(two_land.at[piece], piece_in, sems.at[4]),
            copy_in(grad_land.at[piece], grad_in, sems.at[5]),
        )
        for copy in copies:
            copy.wait()

        @pl.when(piece != me)
        def _():
            act_copy(piece).wait()
            back_copy(piece).wait()

        def one(index):
            def columns(kind):
                return pl.ds(pl.multiple_of(kind * feed_width + index * feed_size, 128), feed_size)

            gate = dot(piece_in[...], pair[:, columns(0)])
            up = dot(piece_in[...], pair[:, columns(1)])
            grad_act = rdot(grad_in[...], down[tile(index, feed_size), :])
            sigma = 1.0 / (1.0 + jnp.exp(-gate))
            act_out[:, columns(0)] = (gate * sigma * up).astype(BF16)
            back_out[:, columns(0)] = (
                grad_act * up * sigma * (1.0 + gate * (1.0 - sigma))
            ).astype(BF16)
            back_out[:, columns(1)] = (grad_act * gate * sigma).astype(BF16)

        loop(feed_width // feed_size, one)
        act_copy(piece).start()
        back_copy(piece).start()

    two_gather = Gather(two_land, two_sems, feed)
    loop(chips, two_gather.step)
    act_copy(0).wait()
    back_copy(0).wait()
    first_gather.finish()
    grad_gather.finish()
    two_gather.finish()
    for out in outs:
        out.wait()
    for share in shares:
        share.finish()
    loop(shards, lambda i: gain_copy(i, shard).wait_send())
    loop(parts, lambda i: token_copy(i, me).wait_send())


def forward(hidden, grad, gains, token_info, freq, weights, shards, parts, heads):
    count = hidden.shape[0]
    tokens = parts * count
    width = heads * HEAD_SIZE
    total_width = width + 2 * HEAD_SIZE
    feed_width = FF // parts
    chips = parts // 2
    shape = jax.ShapeDtypeStruct
    return pl.pallas_call(
        functools.partial(forward_kernel, heads),
        out_shape=(
            shape((parts, count, D), BF16),
            shape((parts, count, D), BF16),
            shape((parts, count, D), BF16),
            shape((parts, count, feed_width), BF16),
            shape((parts, count, 2 * feed_width), BF16),
            shape((parts, count, total_width), F32),
            shape((tokens, HEAD_SIZE), F32),
            shape((tokens, HEAD_SIZE), F32),
            shape((tokens, width), BF16),
            shape((tokens, HEAD_SIZE), BF16),
            shape((tokens, HEAD_SIZE), BF16),
            shape((tokens, width), BF16),
            shape((8, tokens), F32),
            shape((count, D), F32),
            shape((8, D), F32),
            shape((shards, *gains.shape), F32),
            shape((parts, *token_info.shape), jnp.int32),
            shape((D, total_width), BF16),
            shape((width, D), BF16),
            shape((D, 2 * feed_width), BF16),
            shape((feed_width, D), BF16),
        ),
        in_specs=[WHOLE] * 5 + [HBM] * 7,
        out_specs=(HBM,) * 5 + (WHOLE,) * 14 + (HBM,) * 2,
        scratch_shapes=[
            VMEM((D, 2 * feed_width), BF16),
            VMEM((feed_width, D), BF16),
            VMEM((count, D), BF16),
            VMEM((count, D), BF16),
            VMEM((count, D), BF16),
            VMEM((count, feed_width), BF16),
            VMEM((count, 2 * feed_width), BF16),
            VMEM((count, D), F32),
            pltpu.SemaphoreType.DMA((8,)),
        ]
        + [pltpu.SemaphoreType.DMA((shards,))] * 2
        + [pltpu.SemaphoreType.DMA((parts,))] * 2
        + shares_scratch(7, shards)
        + gather_scratch(chips)
        + gather_scratch(chips)
        + gather_scratch(chips)
        + scatter_scratch(chips, count),
        compiler_params=params(0, 63),
        cost_estimate=cost(280),
        name="forward",
    )(hidden, grad, gains, token_info, freq, *weights)


def slab_size(parts):
    return 256 if parts <= 8 else 128


class Slabs:
    def __init__(self, sources, buffers, out, target, sems, products, place=lambda index: index):
        self.place = place
        self.sources, self.buffers, self.out, self.target = sources, buffers, out, target
        self.sems, self.products = sems, products
        self.size = out.shape[0]
        self.count = D // self.size

    def copies(self, index):
        slot = index % 2
        return [
            pltpu.make_async_copy(
                source.at[:, :, tile(self.place(index), self.size)], buffer.at[slot], self.sems.at[2 * i + slot]
            )
            for i, (source, buffer) in enumerate(zip(self.sources, self.buffers))
        ]

    def fetch(self, index):
        for copy in self.copies(index):
            copy.start()

    def leave(self, index):
        each = self.target.shape[1] // self.size
        place = self.place(index)
        target = self.target.at[place // each, tile(place % each, self.size), :]
        return pltpu.make_async_copy(self.out, target, self.sems.at[2 * len(self.sources)])

    def run(self, begin, end):
        def one(index, carry):
            for copy in self.copies(index):
                copy.wait()

            @pl.when(index + 1 < self.count)
            def _():
                self.fetch(index + 1)

            @pl.when(index > begin)
            def _():
                self.leave(index - 1).wait()

            at = 0
            for left, right in self.products(index % 2):
                left = left.reshape(-1, self.size)
                right = right.reshape(left.shape[0], -1)
                width = right.shape[1]
                self.out[:, at : at + width] = tdot(left, right).astype(BF16)
                at += width
            self.leave(index).start()
            return carry

        lax.fori_loop(begin, end, one, 0)

    def settle(self, index):
        self.leave(index - 1).wait()


def rms_back(value, gain, grad):
    inverse = inverse_norm(value)
    scaled = grad * gain
    inner = jnp.mean(scaled * value, axis=-1, keepdims=True)
    terms = grad * value * inverse
    return inverse * scaled - value * (inverse * inverse * inverse * inner), terms


def turn_kernel(*refs):
    back, pair_weight, down_weight, activation, out_weight = refs[:5]
    middle, grad, gain_rows, down_grad, normed = refs[5:10]
    grad_middle, land, gain_sum, down_land, context_grad, hidden, pair_in, pair_grad, pair_sum = refs[10:19]
    weight, data, total, low, own_down, sems = refs[19:25]
    slab, slab_out, slab_sems, sum_sems = refs[25:29]
    down_refs, down_sems = (refs[29:32], refs[32:35]), (refs[35:41], refs[41:47])
    gather_sems, pair_sems, first_scratch, second_scratch = refs[47:53], refs[53:55], refs[55:64], refs[64:]
    me, _, _, chips = line_position()
    width = back.shape[2] // 2
    weight_copy = copy_in(pair_weight, weight, sems.at[0])
    data_copy = copy_in(back, data, sems.at[1])
    own_copy = copy_in(down_grad.at[lax.axis_index("fsdp")], own_down, sems.at[3])

    def produce(piece, chunk):
        return rdot(data[piece], weight[pl.ds(pl.multiple_of(chunk * WIDE, WIDE), WIDE), :])

    each = 2 * width // WIDE

    def down_block(chunk):
        return tile(chunk // each, width), tile(chunk % each, WIDE)

    def down_copy(chunk):
        source = down_weight.at[:, tile(chunk, WIDE)]
        return pltpu.make_async_copy(source, weight.at[down_block(chunk)], sems.at[5 + chunk])

    def produce_hidden(piece, chunk):
        return dot(data[piece, :, :width], weight[down_block(chunk)])

    def consume(piece):
        copy = copy_in(land.at[piece], low, sems.at[4])
        copy.wait()
        context_grad[piece] = rdot(low[...], out_weight[...]).astype(BF16)

    def products(slot):
        return ((slab[slot], data[...]),)

    slabs = Slabs((normed,), (slab,), slab_out, pair_grad, slab_sems, products)
    half = own_down.shape[0] // 2
    halves = [pl.ds(h * half, half) for h in range(2)]
    downs = [
        FsdpSum(down_grad, *down_refs[h], own=own_down.at[halves[h]], part=halves[h]) for h in range(2)
    ]
    down_gathers = [Gather(down_land, down_sems[h], part=halves[h]) for h in range(2)]

    def down_ready(h):
        downs[h].arrive()
        if h == 0:
            downs[1].start()
        downs[h].add(own_down.at[halves[h]])
        copy = copy_in(own_down.at[halves[h]], down_land.at[me, halves[h]], sems.at[3])
        copy.wait()
        down_gathers[h].step(0)

    pair = FsdpSum(pair_grad, pair_in, *pair_sems, own=own_down)
    gather = Gather(land, gather_sems, consume)
    scatter = Scatter(first_scratch, produce, total)
    hidden_scatter = Scatter(second_scratch, produce_hidden, total)
    scatter.begin()
    hidden_scatter.begin()
    full_barrier()
    downs[0].start()
    slabs.fetch(0)
    weight_copy.wait()
    data_copy.wait()
    scatter.prepare(0)

    def step(time):
        scatter.step(time)
        scatter.prepare(time + 1)

        @pl.when(time == 0)
        def _():
            own_copy.wait()
            down_ready(0)

        @pl.when(time >= 1)
        def _():
            down_gathers[0].step(time)

        @pl.when(time == 1)
        def _():
            down_ready(1)

        @pl.when(time >= 2)
        def _():
            down_gathers[1].step(time - 1)

        @pl.when(time < 3)
        def _():
            slabs.run(time * slabs.count // 3, (time + 1) * slabs.count // 3)
            slabs.settle((time + 1) * slabs.count // 3)

        @pl.when(time == 2)
        def _():
            pair.start()

    loop(chips - 1, step)
    scatter.finish()
    down_gathers[0].step(chips - 1)
    down_gathers[1].step(chips - 2)
    for chunk in range(CHUNKS):
        down_copy(chunk).start()
    act_copy = copy_in(activation, data.at[:, :, pl.ds(0, width)], sems.at[1])
    gain_sum[...] = jnp.zeros_like(gain_sum)

    def norm(block):
        through, terms = rms_back(middle[block, :], gain_rows[1:2, :], total[block, :])
        value = grad[block, :].astype(F32) + through
        grad_middle[block, :] = value
        low[block, :] = value.astype(BF16)
        gain_sum[0:1, :] += jnp.sum(terms, axis=0, keepdims=True)

    row_blocks(middle.shape[0], norm)
    low_copy = copy_in(low, land.at[me], sems.at[3])
    low_copy.wait()
    gather.step(0)
    for chunk in range(CHUNKS):
        down_copy(chunk).wait()
    act_copy.wait()
    hidden_scatter.prepare(0)

    def add_pairs():
        pair.arrive()
        shard = lax.axis_index("fsdp")
        count, size = slab.shape[2], slab.shape[3]
        per = own_down.shape[0] // count
        tiles = 2 * width // size

        def arrivals(index):
            slot = index % 2
            copies = []
            for i in range(pair.peers + 1):
                source = pair_grad.at[shard] if i == 0 else pair_in.at[i - 1]
                for j in range(per):
                    at = i * per + j
                    block = source.at[pl.ds(j * count, count), tile(index, size)]
                    copies.append(
                        pltpu.make_async_copy(block, slab.at[slot, at], sum_sems.at[slot, at])
                    )
            return copies

        def leave(index):
            slot = index % 2
            return [
                pltpu.make_async_copy(
                    slab.at[slot, j],
                    pair_sum.at[pl.ds(j * count, count), tile(index, size)],
                    sum_sems.at[slot, j],
                )
                for j in range(per)
            ]

        for copy in arrivals(0):
            copy.start()

        def one(index):
            @pl.when(index > 0)
            def _():
                for copy in leave(index - 1):
                    copy.wait()

            @pl.when(index + 1 < tiles)
            def _():
                for copy in arrivals(index + 1):
                    copy.start()

            for copy in arrivals(index):
                copy.wait()
            slot = index % 2
            for j in range(per):
                value = slab[slot, j].astype(F32)
                for i in range(1, pair.peers + 1):
                    value = value + slab[slot, i * per + j].astype(F32)
                slab[slot, j] = value.astype(BF16)
            for copy in leave(index):
                copy.start()

        loop(tiles, one)
        for copy in leave(tiles - 1):
            copy.wait()

    def turn_step(time):
        hidden_scatter.step(time)
        hidden_scatter.prepare(time + 1)

        @pl.when(time == chips - 2)
        def _():
            add_pairs()

        gather.step(time + 1)

        @pl.when(time == 1)
        def _():
            down_gathers[1].step(chips - 1)

    loop(chips - 1, turn_step)
    hidden_scatter.finish()
    gather.finish()
    for h in range(2):
        down_gathers[h].finish()
        downs[h].finish()
    pair.finish()

    def add(block):
        hidden[block, :] = (middle[block, :] + total[block, :]).astype(BF16)

    row_blocks(middle.shape[0], add)


def turn(back, pair_weight, down_weight, activation, out_weight, middle, grad, gain_rows, down_grad, normed):
    parts, count, feed_width = activation.shape
    shards, rows, _ = down_grad.shape
    width = out_weight.shape[0]
    return pl.pallas_call(
        turn_kernel,
        out_shape=(
            jax.ShapeDtypeStruct((count, D), F32),
            jax.ShapeDtypeStruct((parts, count, D), BF16),
            jax.ShapeDtypeStruct((8, D), F32),
            jax.ShapeDtypeStruct((parts, rows, feed_width), BF16),
            jax.ShapeDtypeStruct((parts, count, width), BF16),
            jax.ShapeDtypeStruct((count, D), BF16),
            jax.ShapeDtypeStruct((shards - 1, rows, 2 * feed_width), BF16),
            jax.ShapeDtypeStruct((shards, rows, 2 * feed_width), BF16),
            jax.ShapeDtypeStruct((rows, 2 * feed_width), BF16),
        ),
        in_specs=[HBM] * 4 + [WHOLE] * 4 + [HBM] * 2,
        out_specs=(WHOLE, HBM, WHOLE, HBM, WHOLE, WHOLE, HBM, HBM, HBM),
        scratch_shapes=[
            VMEM((D, 2 * feed_width), BF16),
            VMEM((parts, count, 2 * feed_width), BF16),
            VMEM((count, D), F32),
            VMEM((count, D), BF16),
            VMEM((rows, feed_width), BF16),
            pltpu.SemaphoreType.DMA((5 + CHUNKS,)),
            VMEM((2, parts, count, slab_size(parts)), BF16),
            VMEM((slab_size(parts), 2 * feed_width), BF16),
            pltpu.SemaphoreType.DMA((3,)),
            pltpu.SemaphoreType.DMA((2, parts)),
        ]
        + fsdp_scratch(shards, rows // 2, feed_width)
        + fsdp_scratch(shards, rows // 2, feed_width)
        + gather_scratch(parts // 2)
        + gather_scratch(parts // 2)
        + gather_scratch(parts // 2)
        + [pltpu.SemaphoreType.DMA((shards,))] * 2
        + scatter_scratch(parts // 2, count)
        + scatter_scratch(parts // 2, count),
        compiler_params=params(3, 63),
        cost_estimate=cost(185),
        name="turn",
    )(
        back,
        pair_weight,
        down_weight,
        activation,
        out_weight,
        middle,
        grad,
        gain_rows,
        down_grad,
        normed,
    )


PAIR_PARTS = 4


def last_kernel(heads, *refs):
    queries, keys, values, out_grad, inverse, context, proj, cosine, sine, token_info = refs[:10]
    weights, x, grad_middle, gain_rows, gain_two, normed, low, pair_sum = refs[10:18]
    hidden, gain_out, head_grad, land, pair_land = refs[18:23]
    back, gain_heads, key_grad, value_grad, query_grad, pair_own, pair_sem = refs[23:30]
    pair_sems, refs = refs[30:36], refs[36:]
    weight, weight_sem, total, gain_one, pack, pack_in, shard_sum, shard_in = refs[:8]
    slabs_in, slab_out, slab_sems, own_head, refs = refs[8:10], refs[10], refs[11], refs[12], refs[13:]
    small, head_refs, refs = refs[:4], (refs[4:7], refs[7:10]), refs[10:]
    gather_sems, scratch = (refs[:6], refs[6:12]), refs[12:]
    me, _, _, chips = line_position()
    shard = lax.axis_index("fsdp")
    shards, ahead, _ = peers_of("fsdp")
    parts, next_part, _ = peers_of("ctx")
    tokens = queries.shape[0]
    key_at = heads * HEAD_SIZE
    copy = copy_in(weights, weight, weight_sem)
    pair_copy = copy_in(pair_sum, pair_own, pair_sem)
    pair_size = pair_own.shape[0] // PAIR_PARTS

    def pump(begin, end):
        def one(index, carry):
            part = index % PAIR_PARTS
            sems = [ref.at[part] for ref in pair_sems]
            Gather(pair_land, sems, part=tile(part, pair_size)).step(index // PAIR_PARTS)
            return carry

        lax.fori_loop(begin, end, one, 0)

    def produce(piece, chunk):
        return rdot(back[piece], weight[pl.ds(pl.multiple_of(chunk * WIDE, WIDE), WIDE), :])

    def products(slot):
        return (slabs_in[0][slot], back[...]), (slabs_in[1][slot], context[...])

    half = own_head.shape[0] // 2
    halves = [pl.ds(h * half, half) for h in range(2)]
    per_half = (D // half) // 2 * half // slab_out.shape[0]
    inner = half // slab_out.shape[0]

    def place(index):
        side, rest = index // per_half, index % per_half
        return (rest // inner) * 2 * inner + side * inner + rest % inner

    slabs = Slabs((normed, low), slabs_in, slab_out, head_grad, slab_sems, products, place)
    head_sums = [
        FsdpSum(head_grad, *head_refs[h], own=own_head.at[halves[h]], part=halves[h]) for h in range(2)
    ]
    gathers = [Gather(land, gather_sems[h], part=halves[h]) for h in range(2)]

    def head_ready(h):
        head_sums[h].collect(land.at[me, halves[h]])
        gathers[h].step(0)
    scatter = Scatter(scratch, produce, total)
    scatter.begin()
    slabs.fetch(0)
    full_barrier()
    pair_copy.wait()
    pair_copy = copy_in(pair_own, pair_land.at[me], pair_sem)
    pair_copy.wait()
    pump(0, PAIR_PARTS)
    key_grad[...] = jnp.zeros_like(key_grad)
    value_grad[...] = jnp.zeros_like(value_grad)
    gain_heads[...] = jnp.zeros_like(gain_heads)

    def through(index, lanes, grad, row):
        block = tile(index, QUERY_TILE)
        turned = pltpu.roll(grad, HEAD_SIZE // 2, 1)
        unrotated = grad * cosine[block, :] - turned * sine[block, :]
        result, terms = rms_back(proj[index, :, lanes], gain_rows[row + 2 : row + 3, :HEAD_SIZE], unrotated)
        back[index, :, lanes] = result.astype(BF16)
        gain_heads[row : row + 1, :] += jnp.sum(terms, axis=0, keepdims=True)

    count = token_info.shape[2]
    each = KEY_TILE // count

    def attend(index):
        block = tile(index, QUERY_TILE)
        query_ids = token_info[index, 1:2, :].astype(F32)
        shifts = []
        for h in range(heads):
            lanes = slice(h * HEAD_SIZE, (h + 1) * HEAD_SIZE)
            products = out_grad[index, :, lanes].astype(F32) * context[index, :, lanes].astype(F32)
            shift = lax.dot_general(
                jnp.ones((8, HEAD_SIZE), F32),
                products,
                (((1,), (1,)), ((), ())),
                precision=lax.Precision.HIGHEST,
                preferred_element_type=F32,
            )[0:1, :]
            shifts.append(shift)
        query_grad[...] = jnp.zeros_like(query_grad)

        def one(key_tile):
            span = tile(key_tile, KEY_TILE)
            key, value = keys[span, :], values[span, :]
            key_ids = jnp.concatenate(
                [
                    jnp.broadcast_to(
                        token_info[key_tile * each + j, 1:2, :].astype(F32), (128, count)
                    ).T[:, 0:1]
                    for j in range(each)
                ],
                axis=0,
            )
            allowed = key_ids <= query_ids
            for h in range(heads):
                lanes = slice(h * HEAD_SIZE, (h + 1) * HEAD_SIZE)
                query, grad = queries[block, lanes], out_grad[index, :, lanes]
                expon = jnp.exp(rdot(key, query)) * inverse[h : h + 1, block]
                probs = jnp.where(allowed, expon, 0.0)
                grad_scores = (probs * (rdot(value, grad) - shifts[h])).astype(BF16)
                value_grad[span, :] += dot(probs.astype(BF16), grad)
                key_grad[span, :] += dot(grad_scores, query)
                query_grad[:, lanes] += tdot(grad_scores, key)

        loop(reach(index, tokens), one)
        for h in range(heads):
            lanes = slice(h * HEAD_SIZE, (h + 1) * HEAD_SIZE)
            through(index, lanes, query_grad[:, lanes] * HEAD_SIZE ** (-0.5), 0)

    def finish_keys(index):
        block = tile(index, QUERY_TILE)
        through(index, slice(key_at, key_at + HEAD_SIZE), key_grad[block, :], 1)
        back[index, :, key_at + HEAD_SIZE :] = value_grad[block, :].astype(BF16)

    tiles = tokens // QUERY_TILE
    marks = (0, 3 * tiles // 8, 5 * tiles // 8, 6 * tiles // 8, tiles)
    for i in range(4):
        loop(marks[i + 1] - marks[i], lambda index, i=i: attend(marks[i] + index))
        pump(PAIR_PARTS + i, PAIR_PARTS + i + 1)
    loop(tiles, finish_keys)
    copy.wait()
    for h in range(2):
        slabs.run(h * per_half, (h + 1) * per_half)
        slabs.settle((h + 1) * per_half)
        head_sums[h].start()
        pump(2 * PAIR_PARTS + h, 2 * PAIR_PARTS + h + 1)
    own = copy_in(head_grad.at[shard], own_head, weight_sem)
    own.wait()
    scatter.prepare(0)

    def step(time):
        scatter.step(time)
        scatter.prepare(time + 1)
        begin = 2 * PAIR_PARTS + 2
        span = PAIR_PARTS * (chips - 3)
        pump(begin + time * span // (chips - 1), begin + (time + 1) * span // (chips - 1))

        @pl.when(time == 0)
        def _():
            head_ready(0)

        @pl.when(time >= 1)
        def _():
            gathers[0].step(time)

        @pl.when(time == 1)
        def _():
            head_ready(1)

        @pl.when(time >= 2)
        def _():
            gathers[1].step(time - 1)

    loop(chips - 1, step)
    scatter.finish()
    gathers[0].step(chips - 1)
    gathers[1].step(chips - 2)
    gain_one[...] = jnp.zeros_like(gain_one)

    def norm(block):
        through, terms = rms_back(x[block, :].astype(F32), gain_rows[0:1, :], total[block, :])
        hidden[block, :] = grad_middle[block, :] + through
        gain_one[0:1, :] += jnp.sum(terms, axis=0, keepdims=True)

    row_blocks(x.shape[0], norm)

    rows = D // (shards + 1)
    lanes = rows // 128
    pack[...] = jnp.zeros_like(pack)
    for owner in range(shards + 1):
        for j in range(lanes):
            at = owner * rows + j * 128
            pack[owner, j : j + 1, :] = gain_one[0:1, at : at + 128]
            pack[owner, lanes + j : lanes + j + 1, :] = gain_two[0:1, at : at + 128]
        pack[owner, 2 * lanes : 2 * lanes + 2, :] = gain_heads[0:2, :]

    def pack_copy(i):
        return send(pack.at[ahead(i)], pack_in.at[i], small[0].at[i], small[1].at[i], "fsdp", ahead(i))

    def sum_copy(i):
        return send(shard_sum, shard_in.at[i], small[2].at[i], small[3].at[i], "ctx", next_part(i))

    loop(shards, lambda i: pack_copy(i).start())
    shard_sum[...] = pack[shard]

    def add_pack(i):
        pack_copy(i).wait_recv()
        shard_sum[...] += pack_in[i]

    loop(shards, add_pack)
    loop(parts, lambda i: sum_copy(i).start())
    gain_out[...] = shard_sum[...]

    def add_sum(i):
        sum_copy(i).wait_recv()
        gain_out[...] += shard_in[i]

    loop(parts, add_sum)
    gathers[1].step(chips - 1)
    pump(PAIR_PARTS * (chips - 1) + 2, PAIR_PARTS * chips)

    def settle_pair(part):
        sems = [ref.at[part] for ref in pair_sems]
        Gather(pair_land, sems, part=tile(part, pair_size)).finish()

    loop(PAIR_PARTS, settle_pair)
    for h in range(2):
        gathers[h].finish()
        head_sums[h].finish()
    loop(shards, lambda i: pack_copy(i).wait_send())
    loop(parts, lambda i: sum_copy(i).wait_send())


def last(*operands):
    tokens, query_width = operands[0].shape
    heads = query_width // HEAD_SIZE
    parts = operands[5].shape[0]
    count = tokens // parts
    width = query_width + 2 * HEAD_SIZE
    head_width = width + query_width
    rows, pair_width = operands[-1].shape
    shards = D // rows
    chips = parts // 2
    return pl.pallas_call(
        functools.partial(last_kernel, heads),
        out_shape=(
            jax.ShapeDtypeStruct((count, D), F32),
            jax.ShapeDtypeStruct((16, 128), F32),
            jax.ShapeDtypeStruct((shards, rows, head_width), BF16),
            jax.ShapeDtypeStruct((parts, rows, head_width), BF16),
            jax.ShapeDtypeStruct((parts, rows, pair_width), BF16),
        ),
        in_specs=[WHOLE] * 10 + [HBM] + [WHOLE] * 4 + [HBM] * 3,
        out_specs=(WHOLE, WHOLE, HBM, WHOLE, HBM),
        scratch_shapes=[
            VMEM((parts, count, width), BF16),
            VMEM((8, HEAD_SIZE), F32),
            VMEM((tokens, HEAD_SIZE), F32),
            VMEM((tokens, HEAD_SIZE), F32),
            VMEM((QUERY_TILE, query_width), F32),
            VMEM((rows, pair_width), BF16),
            pltpu.SemaphoreType.DMA,
        ]
        + [pltpu.SemaphoreType.DMA((PAIR_PARTS, chips)) for _ in range(6)]
        + [
            VMEM((D, width), BF16),
            pltpu.SemaphoreType.DMA,
            VMEM((count, D), F32),
            VMEM((8, D), F32),
            VMEM((shards, 16, 128), F32),
            VMEM((shards, 16, 128), F32),
            VMEM((16, 128), F32),
            VMEM((parts, 16, 128), F32),
            VMEM((2, parts, count, slab_size(parts)), BF16),
            VMEM((2, parts, count, slab_size(parts)), BF16),
            VMEM((slab_size(parts), head_width), BF16),
            pltpu.SemaphoreType.DMA((5,)),
            VMEM((rows, head_width), BF16),
        ]
        + [pltpu.SemaphoreType.DMA((shards,))] * 2
        + [pltpu.SemaphoreType.DMA((parts,))] * 2
        + fsdp_scratch(shards, rows // 2, head_width)
        + fsdp_scratch(shards, rows // 2, head_width)
        + gather_scratch(chips)
        + gather_scratch(chips)
        + scatter_scratch(chips, count),
        compiler_params=params(5, 63),
        cost_estimate=cost(190),
        name="last",
    )(*operands)


def spread_kernel(width, head_source, pair_source, down_source, *targets):
    query, key, value, out, gate, up, down = targets
    second = width + HEAD_SIZE
    third = second + HEAD_SIZE
    query[...] = head_source[0, :, :width].astype(F32)
    key[...] = head_source[0, :, width:second].astype(F32)
    value[...] = head_source[0, :, second:third].astype(F32)
    out[...] = head_source[0, :, third:].astype(F32).T
    feed_width = gate.shape[1]
    gate[...] = pair_source[0, :, :feed_width].astype(F32)
    up[...] = pair_source[0, :, feed_width:].astype(F32)
    down[...] = down_source[0].astype(F32).T


def spread(head_parts, pair_parts, down_parts, width):
    parts, rows, _ = head_parts.shape
    feed_width = down_parts.shape[2]
    sources = (head_parts, pair_parts, down_parts)

    def side_by_side(columns):
        shape = jax.ShapeDtypeStruct((rows, parts * columns), F32)
        return shape, pl.BlockSpec((rows, columns), lambda i: (0, i))

    def stacked(columns):
        shape = jax.ShapeDtypeStruct((parts * columns, rows), F32)
        return shape, pl.BlockSpec((columns, rows), lambda i: (i, 0))

    outs = (
        side_by_side(width),
        side_by_side(HEAD_SIZE),
        side_by_side(HEAD_SIZE),
        stacked(width),
        side_by_side(feed_width),
        side_by_side(feed_width),
        stacked(feed_width),
    )
    return pl.pallas_call(
        functools.partial(spread_kernel, width),
        out_shape=tuple(shape for shape, _ in outs),
        grid=(parts,),
        in_specs=[pl.BlockSpec((1, *source.shape[1:]), lambda i: (i, 0, 0)) for source in sources],
        out_specs=tuple(spec for _, spec in outs),
        compiler_params=pltpu.CompilerParams(vmem_limit_bytes=60 * 1024 * 1024),
        name="spread",
    )(*sources)


def by_row(array):
    return with_layout_constraint(array, Layout(major_to_minor=(0, 1)))


def local(
    hidden_in,
    weight_query,
    key_weight_matrix,
    weight_value,
    weight_out,
    weight_gate,
    weight_up,
    weight_down,
    gain_attention,
    gain_feed,
    gain_query,
    gain_key,
    positions,
    token_block_index,
    grad_out,
):
    parts = lax.axis_size("ctx")
    shards = lax.axis_size("fsdp")
    shard = lax.axis_index("fsdp")
    heads = QUERY_HEADS // parts
    sharers = parts // KEY_VALUE_HEADS
    width = heads * HEAD_SIZE
    feed_width = FF // parts
    rows = D // shards
    head_rows = HEAD_SIZE // shards
    count = hidden_in.shape[1]
    tokens = parts * count

    own_gains = jnp.concatenate([gain_attention, gain_feed, gain_query, gain_key]).astype(F32)
    own_gains = jnp.pad(own_gains, (0, 2048 - own_gains.shape[0])).reshape(16, 128)
    own_tokens = jnp.pad(jnp.stack([positions[0], token_block_index[0]]), ((0, 6), (0, 0)))
    half = HEAD_SIZE // 2
    freq = THETA ** (-(jnp.arange(half).astype(F32) * 2.0 / HEAD_SIZE))
    freq = jnp.broadcast_to(jnp.concatenate([freq, freq]), (8, HEAD_SIZE))
    hidden, grad = hidden_in[0], grad_out[0]
    weights = (
        weight_query,
        key_weight_matrix,
        weight_value,
        weight_out,
        weight_gate,
        weight_up,
        weight_down,
    )
    (
        normed_all,
        grad_all,
        normed_two_all,
        activation,
        back,
        proj,
        cosine,
        sine,
        queries,
        keys,
        values,
        context,
        inverse,
        middle,
        gain_rows,
        gains,
        whole,
        heads_weight,
        out_weight,
        pair_weight,
        down_weight,
    ) = forward(hidden, grad, own_gains, own_tokens, freq, weights, shards, parts, heads)

    flat_grad = grad_all.reshape(tokens, D)
    flat_activation = activation.reshape(tokens, feed_width)
    down_grad = by_row(tdot(flat_grad, flat_activation).astype(BF16))
    grad_middle, low_all, gain_two, down_parts, context_grad, hidden_out, _, _, feed_shard = turn(
        back,
        pair_weight,
        down_weight,
        activation,
        out_weight,
        middle,
        grad,
        gain_rows,
        down_grad.reshape(shards, rows, feed_width),
        normed_two_all,
    )
    grad_hidden, gain_sums, _, head_parts, feed_parts = last(
        queries,
        keys,
        values,
        context_grad,
        inverse,
        context.reshape(parts, count, width),
        proj,
        cosine,
        sine,
        whole,
        heads_weight,
        hidden,
        grad_middle,
        gain_rows,
        gain_two,
        normed_all,
        low_all,
        feed_shard,
    )

    gain_sums = gain_sums.reshape(-1)
    grad_query, grad_key, grad_value, grad_out_weight, grad_gate, grad_up, grad_down = spread(
        head_parts, feed_parts, down_parts, width
    )
    if sharers > 1:
        grad_key, grad_value = (
            part.reshape(rows, KEY_VALUE_HEADS, sharers, HEAD_SIZE).sum(axis=2).reshape(rows, -1)
            for part in (grad_key, grad_value)
        )
    return (
        hidden_out[None],
        grad_hidden[None],
        grad_query,
        grad_key,
        grad_value,
        grad_out_weight,
        grad_gate,
        grad_up,
        grad_down,
        gain_sums[:rows],
        gain_sums[rows : 2 * rows],
        lax.dynamic_slice_in_dim(gain_sums, 2 * rows + shard * head_rows, head_rows),
        lax.dynamic_slice_in_dim(gain_sums, 2 * rows + HEAD_SIZE + shard * head_rows, head_rows),
    )


def solution(mesh):
    tokens = P("fsdp", "ctx", None)
    by_rows = P("fsdp", None)
    by_columns = P(None, "fsdp")
    per_token = P("fsdp", "ctx")
    vector = P("fsdp")
    weights = (by_rows, by_rows, by_rows, by_columns, by_rows, by_rows, by_columns)
    return jax.shard_map(
        local,
        mesh=mesh,
        in_specs=(tokens, *weights, vector, vector, vector, vector, per_token, per_token, tokens),
        out_specs=(tokens, tokens, *weights, vector, vector, vector, vector),
        check_vma=False,
    )
```

```python
import functools

import jax
import jax.numpy as jnp
from jax import lax
from jax.experimental import pallas as pl
from jax.experimental.pallas import tpu as pltpu
from jax.sharding import PartitionSpec as P

D = 2048
QUERY_HEADS = 16
KEY_VALUE_HEADS = 8
HEAD_SIZE = 128
FF = 6144
EPS = 1e-06
THETA = 1000000.0
F32 = jnp.float32
BF16 = jnp.bfloat16
MESH = pl.DeviceIdType.MESH
VMEM = pltpu.VMEM
WHOLE = pl.BlockSpec(memory_space=pltpu.VMEM)
HBM = pl.BlockSpec(memory_space=pl.ANY)
CHUNKS = 4
WIDE = D // CHUNKS


def dot(left, right):
    return jnp.dot(left, right, preferred_element_type=F32)


def tdot(left, right):
    return lax.dot_general(left, right, (((0,), (0,)), ((), ())), preferred_element_type=F32)


def rdot(left, right):
    return lax.dot_general(left, right, (((1,), (1,)), ((), ())), preferred_element_type=F32)


def loop(count, body):
    def step(index, carry):
        body(index)
        return carry

    lax.fori_loop(0, count, step, 0)


def line_position():
    me = lax.axis_index("ctx")
    return me, me // 2, me % 2, lax.axis_size("ctx") // 2


def send(source, target, send_sem, recv_sem, axis, index):
    return pltpu.make_async_remote_copy(
        src_ref=source,
        dst_ref=target,
        send_sem=send_sem,
        recv_sem=recv_sem,
        device_id={axis: index},
        device_id_type=MESH,
    )


def line_barrier():
    me, chip, core, chips = line_position()
    barrier = pltpu.get_barrier_semaphore()

    def greet(index):
        pl.semaphore_signal(barrier, inc=1, device_id={"ctx": index}, device_id_type=MESH)

    greet(me + 1 - 2 * core)

    @pl.when(chip > 0)
    def _():
        greet(me - 2)

    @pl.when(chip < chips - 1)
    def _():
        greet(me + 2)

    peers = 1 + (chip > 0).astype(jnp.int32) + (chip < chips - 1).astype(jnp.int32)
    pl.semaphore_wait(barrier, peers)


def peers_of(axis):
    me, size = lax.axis_index(axis), lax.axis_size(axis)
    return size - 1, lambda i: (me + i + 1) % size, lambda i: (me + size - i - 1) % size


def full_barrier():
    barrier = pltpu.get_barrier_semaphore()
    total = 0
    for axis in ("fsdp", "ctx"):
        count, ahead, _ = peers_of(axis)
        loop(
            count,
            lambda i, axis=axis, ahead=ahead: pl.semaphore_signal(
                barrier, inc=1, device_id={axis: ahead(i)}, device_id_type=MESH
            ),
        )
        total += count
    pl.semaphore_wait(barrier, total)


def gather_scratch(chips):
    return [pltpu.SemaphoreType.DMA((chips,)) for _ in range(6)]


class Gather:
    def __init__(self, land, sems, consume=None, part=None):
        self.part = part
        self.land = land
        self.sems = sems
        self.consume = consume
        self.me, self.chip, self.core, self.chips = line_position()

    def place(self, piece):
        return self.land.at[piece] if self.part is None else self.land.at[piece, self.part]

    def right(self, step, source):
        ref = self.place(2 * source + self.core)
        return send(ref, ref, self.sems[0].at[step], self.sems[1].at[step], "ctx", self.me + 2)

    def left(self, step, source):
        ref = self.place(2 * source + self.core)
        return send(ref, ref, self.sems[2].at[step], self.sems[3].at[step], "ctx", self.me - 2)

    def across(self, source, core):
        ref = self.place(2 * source + core)
        other = self.me + 1 - 2 * self.core
        return send(ref, ref, self.sems[4].at[source], self.sems[5].at[source], "ctx", other)

    def step(self, step):
        self.move(step)
        self.use(step)

    def move(self, step):
        chip, core, chips = self.chip, self.core, self.chips
        low, high = chip - step, chip + step
        has_low = low >= 0
        has_high = jnp.logical_and(high < chips, step > 0)

        @pl.when(jnp.logical_and(has_low, step > 0))
        def _():
            self.right(step - 1, low).wait_recv()

        @pl.when(jnp.logical_and(has_low, chip < chips - 1))
        def _():
            self.right(step, low).start()

        @pl.when(has_high)
        def _():
            self.left(step - 1, high).wait_recv()

        @pl.when(jnp.logical_and(high < chips, chip > 0))
        def _():
            self.left(step, high).start()

        @pl.when(has_low)
        def _():
            self.across(low, core).start()

        @pl.when(has_high)
        def _():
            self.across(high, core).start()

    def use(self, step):
        chip, core, chips = self.chip, self.core, self.chips
        low, high = chip - step, chip + step

        def one(kind):
            upward = kind % 2
            crossed = kind // 2
            source = jnp.where(upward == 1, high, low)
            valid = jnp.where(upward == 1, jnp.logical_and(high < chips, step > 0), low >= 0)
            parity = jnp.where(crossed == 1, 1 - core, core)

            @pl.when(valid)
            def _():
                @pl.when(crossed == 1)
                def _():
                    self.across(source, parity).wait_recv()

                if self.consume is not None:
                    self.consume(2 * source + parity)

        loop(4, one)

    def finish(self):
        chip, core, chips = self.chip, self.core, self.chips

        def one(step):
            @pl.when(jnp.logical_and(chip - step >= 0, chip < chips - 1))
            def _():
                self.right(step, chip - step).wait_send()

            @pl.when(jnp.logical_and(chip + step < chips, chip > 0))
            def _():
                self.left(step, chip + step).wait_send()

            self.across(step, core).wait_send()

        loop(chips, one)


def scatter_scratch(chips, rows):
    buffers = [VMEM((count, CHUNKS, rows, WIDE), BF16) for count in (chips + 1, 2, chips)]
    return buffers + [pltpu.SemaphoreType.DMA((chips, CHUNKS)) for _ in range(6)]


class Scatter:
    def __init__(self, scratch, produce, total, ready=None):
        self.ready = ready
        self.line, self.out, self.other = scratch[:3]
        self.sems = scratch[3:]
        self.produce = produce
        self.total = total
        self.me, self.chip, self.core, self.chips = line_position()


    def right(self, step, chunk):
        ref = self.line.at[step, chunk]
        sems = self.sems
        return send(ref, ref, sems[0].at[step, chunk], sems[1].at[step, chunk], "ctx", self.me + 2)

    def left(self, step, chunk):
        ref = self.line.at[self.chips - step, chunk]
        sems = self.sems
        return send(ref, ref, sems[2].at[step, chunk], sems[3].at[step, chunk], "ctx", self.me - 2)

    def across(self, target, chunk, slot=0):
        sems = self.sems
        return send(
            self.out.at[slot, chunk],
            self.other.at[target, chunk],
            sems[4].at[target, chunk],
            sems[5].at[target, chunk],
            "ctx",
            self.me + 1 - 2 * self.core,
        )

    def begin(self):
        def clear(index):
            slot, chunk = index // CHUNKS, index % CHUNKS
            at_left = jnp.logical_and(self.chip == 0, slot < self.chips)
            at_right = jnp.logical_and(self.chip == self.chips - 1, slot > 0)

            @pl.when(jnp.logical_or(at_left, at_right))
            def _():
                self.line[slot, chunk] = jnp.zeros(self.line.shape[2:], BF16)

        loop((self.chips + 1) * CHUNKS, clear)

    def when_right(self, time):
        return jnp.logical_and(time >= self.chip, time < self.chips - 1)

    def when_left(self, time):
        return jnp.logical_and(time >= self.chips - 1 - self.chip, time < self.chips - 1)

    def prepare(self, time):
        chip, chips = self.chip, self.chips

        def cross(target, slot, before, used):
            if self.ready is not None:
                self.ready(target)

            def one(chunk):
                @pl.when(used)
                def _():
                    self.across(before, chunk, slot).wait_send()

                piece = 2 * target + 1 - self.core
                self.out[slot, chunk] = self.produce(piece, chunk).astype(BF16)
                self.across(target, chunk, slot).start()

            loop(CHUNKS, one)

        @pl.when(self.when_right(time))
        def _():
            target = chips - 1 - time + chip
            cross(target, 0, target + 1, time > chip)

        @pl.when(self.when_left(time))
        def _():
            target = time - (chips - 1 - chip)
            cross(target, 1, target - 1, target > 0)

        @pl.when(time == chips - 1)
        def _():
            cross(chip, 0, chip + 1, chip < chips - 1)

    def step(self, time):
        chip, core, chips = self.chip, self.core, self.chips

        @pl.when(self.when_right(time))
        def _():
            step = time - chip
            target = chips - 1 - step

            def one(chunk):
                self.across(target, chunk).wait_recv()

                @pl.when(chip > 0)
                def _():
                    self.right(step, chunk).wait_recv()

                value = self.produce(2 * target + core, chunk) + self.other[target, chunk].astype(F32)
                value = value + self.line[step, chunk].astype(F32)
                self.line[step, chunk] = value.astype(BF16)
                self.right(step, chunk).start()

            loop(CHUNKS, one)

        @pl.when(self.when_left(time))
        def _():
            step = time - (chips - 1 - chip)

            def one(chunk):
                self.across(step, chunk).wait_recv()

                @pl.when(chip < chips - 1)
                def _():
                    self.left(step, chunk).wait_recv()

                value = self.produce(2 * step + core, chunk) + self.other[step, chunk].astype(F32)
                value = value + self.line[chips - step, chunk].astype(F32)
                self.line[chips - step, chunk] = value.astype(BF16)
                self.left(step, chunk).start()

            loop(CHUNKS, one)

    def finish(self):
        chip, core, chips = self.chip, self.core, self.chips
        last = chips - 1 - chip

        def one(chunk):
            self.across(chip, chunk).wait_recv()
            value = self.produce(2 * chip + core, chunk) + self.other[chip, chunk].astype(F32)

            @pl.when(chip > 0)
            def _():
                self.right(last, chunk).wait_recv()

            @pl.when(chip < chips - 1)
            def _():
                self.left(chip, chunk).wait_recv()

            value = value + self.line[last, chunk].astype(F32)
            value = value + self.line[chips - chip, chunk].astype(F32)
            self.total[:, pl.ds(pl.multiple_of(chunk * WIDE, WIDE), WIDE)] = value

        loop(CHUNKS, one)

        def drain(index):
            step, chunk = index // CHUNKS, index % CHUNKS

            @pl.when(step < last)
            def _():
                self.right(step, chunk).wait_send()

            @pl.when(step < chip)
            def _():
                self.left(step, chunk).wait_send()

            @pl.when(jnp.logical_or(step == chip, step == chip - 1))
            def _():
                self.across(step, chunk, jnp.where(step == chip, 0, 1)).wait_send()

        loop(chips * CHUNKS, drain)


def tile(index, size):
    return pl.ds(pl.multiple_of(index * size, size), size)


def row_blocks(rows, body, size=32):
    def one(index):
        body(pl.ds(pl.multiple_of(index * size, size), size))

    loop(rows // size, one)


def inverse_norm(value):
    return lax.rsqrt(jnp.mean(value * value, axis=-1, keepdims=True) + EPS)


def params(identity, megabytes):
    return pltpu.CompilerParams(
        collective_id=identity,
        has_side_effects=True,
        vmem_limit_bytes=megabytes * 1024 * 1024,
    )


def cost(microseconds):
    return pl.CostEstimate(
        flops=int(microseconds * 1.15e9), bytes_accessed=1024, transcendentals=0
    )


class FsdpSum:
    def __init__(self, grad, arrived, send_sems, recv_sems, own=None, part=slice(None)):
        self.grad, self.arrived, self.part = grad, arrived, part
        self.own = grad.at[lax.axis_index("fsdp")] if own is None else own
        self.sems = send_sems, recv_sems
        self.peers, self.ahead, _ = peers_of("fsdp")

    def copy(self, i):
        target = self.ahead(i)
        return send(
            self.grad.at[target, self.part], self.arrived.at[i], self.sems[0].at[i], self.sems[1].at[i], "fsdp", target
        )

    def start(self):
        loop(self.peers, lambda i: self.copy(i).start())

    def arrive(self):
        loop(self.peers, lambda i: self.copy(i).wait_recv())

    def collect(self, target):
        self.arrive()
        self.add(target)

    def add(self, target):
        def one(block):
            value = self.own[block, :].astype(F32)
            for i in range(self.peers):
                value = value + self.arrived[i, block].astype(F32)
            target[block, :] = value.astype(BF16)

        row_blocks(self.own.shape[0], one)

    def finish(self):
        loop(self.peers, lambda i: self.copy(i).wait_send())


def fsdp_scratch(shards, rows, width):
    return [VMEM((shards - 1, rows, width), BF16)] + [pltpu.SemaphoreType.DMA((shards,))] * 2


def sine_cosine(angle):
    count = jnp.floor(angle * 0.6366197723675814 + 0.5)
    rest = angle - count * 1.5703125
    rest = rest - count * 4.837512969970703e-4
    rest = rest - count * 7.549789948768648e-8
    square = rest * rest
    sine = -1.9515295891e-4 * square + 8.3321608736e-3
    sine = rest + rest * square * (sine * square - 1.6666654611e-1)
    cosine = 2.443315711809948e-5 * square - 1.388731625493765e-3
    cosine = 1.0 - 0.5 * square + square * square * (cosine * square + 4.166664568298827e-2)
    quarter = jnp.bitwise_and(count.astype(jnp.int32), 3)
    odd = jnp.bitwise_and(quarter, 1) == 1
    sine, cosine = jnp.where(odd, cosine, sine), jnp.where(odd, sine, cosine)
    sine = jnp.where(quarter >= 2, -sine, sine)
    cosine = jnp.where(jnp.logical_or(quarter == 1, quarter == 2), -cosine, cosine)
    return sine, cosine


class Shares:
    def __init__(self, source, target_of, own_sem, sems):
        self.source, self.target_of = source, target_of
        self.own_sem, self.sems = own_sem, sems
        self.peers, self.ahead, self.behind = peers_of("fsdp")
        self.shard = lax.axis_index("fsdp")

    def copy(self, i, owner):
        sems = self.sems
        target = self.target_of(owner)
        return send(self.source, target, sems[0].at[i], sems[1].at[i], "fsdp", self.ahead(i))

    def own(self):
        return pltpu.make_async_copy(self.source, self.target_of(self.shard), self.own_sem)

    def start(self):
        loop(self.peers, lambda i: self.copy(i, self.shard).start())
        self.own().start()

    def arrive(self):
        self.own().wait()
        loop(self.peers, lambda i: self.copy(i, self.behind(i)).wait_recv())

    def finish(self):
        loop(self.peers, lambda i: self.copy(i, self.shard).wait_send())


def shares_scratch(count, shards):
    return [pltpu.SemaphoreType.DMA((count,))] + [pltpu.SemaphoreType.DMA((shards,))] * (2 * count)


def copy_in(source, target, sem):
    copy = pltpu.make_async_copy(source, target, sem)
    copy.start()
    return copy


QUERY_TILE = 256
KEY_TILE = 512


def reach(index, tokens):
    return jnp.minimum((index + 2) * QUERY_TILE + KEY_TILE - 1, tokens) // KEY_TILE


def head_norm(value, gain, cosine, sine):
    normed = value * inverse_norm(value) * gain
    return normed * cosine + pltpu.roll(normed, HEAD_SIZE // 2, 1) * sine


def forward_kernel(heads, *refs):
    x, grad, gains, token_info, freq = refs[:5]
    sources, refs = refs[5:12], refs[12:]
    normed_land, grad_land, two_land, activation, back = refs[:5]
    proj, cosine, sine, queries, keys, values, context, inverse = refs[5:13]
    middle, gain_rows, all_gains, all_tokens = refs[13:17]
    head_weight, out_weight, pair_weight, down_weight = refs[17:21]
    refs = refs[21:]
    pair, down, own, piece_in, grad_in, act_out, back_out, total, sems = refs[:9]
    small, refs = refs[9:13], refs[13:]
    share_own, share_sems, refs = refs[0], refs[1:15], refs[15:]
    first_sems, grad_sems, refs = refs[:6], (refs[6:12], refs[12:18]), refs[18:]
    two_sems, scratch = refs[:6], refs[6:]
    me, _, _, chips = line_position()
    shard = lax.axis_index("fsdp")
    shards, ahead, behind = peers_of("fsdp")
    parts, next_part, past_part = peers_of("ctx")
    count = x.shape[0]
    tokens = 2 * chips * count
    width = heads * HEAD_SIZE
    feed_width = down.shape[0]
    rows = D // (shards + 1)
    lanes = rows // 128
    key_head = me // (2 * chips // KEY_VALUE_HEADS)

    def gain_copy(i, slot):
        return send(gains, all_gains.at[slot], small[0].at[i], small[1].at[i], "fsdp", ahead(i))

    def token_copy(i, slot):
        return send(token_info, all_tokens.at[slot], small[2].at[i], small[3].at[i], "ctx", next_part(i))

    def by_row(target, at, size):
        return lambda owner: target.at[tile(owner, rows), pl.ds(at, size)]

    def by_column(target):
        return lambda owner: target.at[:, tile(owner, rows)]

    places = (
        (sources[0].at[:, tile(me, width)], by_row(head_weight, 0, width)),
        (sources[1].at[:, tile(key_head, HEAD_SIZE)], by_row(head_weight, width, HEAD_SIZE)),
        (sources[2].at[:, tile(key_head, HEAD_SIZE)], by_row(head_weight, width + HEAD_SIZE, HEAD_SIZE)),
        (sources[3].at[tile(me, width), :], by_column(out_weight)),
        (sources[4].at[:, tile(me, feed_width)], by_row(pair, 0, feed_width)),
        (sources[5].at[:, tile(me, feed_width)], by_row(pair, feed_width, feed_width)),
        (sources[6].at[tile(me, feed_width), :], by_column(down)),
    )
    shares = [
        Shares(source, target_of, share_own.at[i], share_sems[2 * i : 2 * i + 2])
        for i, (source, target_of) in enumerate(places)
    ]

    full_barrier()
    loop(shards, lambda i: gain_copy(i, shard).start())
    loop(parts, lambda i: token_copy(i, me).start())
    for share in shares[:4]:
        share.start()
    grad_copy = copy_in(grad, grad_land.at[me], sems.at[0])
    all_gains[shard] = gains[...]
    all_tokens[me] = token_info[...]
    loop(shards, lambda i: gain_copy(i, behind(i)).wait_recv())
    for kind in range(2):
        for owner in range(shards + 1):
            for j in range(lanes):
                at = owner * rows + j * 128
                gain_rows[kind : kind + 1, at : at + 128] = all_gains[
                    owner, kind * lanes + j : kind * lanes + j + 1, :
                ]
    size = HEAD_SIZE // (shards + 1)
    for kind in range(2):
        gain_rows[2 + kind : 3 + kind, 0:HEAD_SIZE] = jnp.concatenate(
            [
                all_gains[
                    owner, 2 * lanes : 2 * lanes + 1, kind * size : (kind + 1) * size
                ]
                for owner in range(shards + 1)
            ],
            axis=1,
        )

    def norm(block):
        value = x[block, :].astype(F32)
        own[block, :] = (value * inverse_norm(value) * gain_rows[0:1, :]).astype(BF16)

    row_blocks(count, norm)
    own_copy = copy_in(own, normed_land.at[me], sems.at[1])
    own_copy.wait()

    def column(piece, row):
        values_in_lanes = all_tokens[piece, row : row + 1, :].astype(F32)
        return jnp.broadcast_to(values_in_lanes, (128, count)).T

    def project(piece):
        copy = copy_in(normed_land.at[piece], piece_in, sems.at[1])
        block = tile(piece, count)
        s, c = sine_cosine(column(piece, 0) * freq[0:1, :])
        lane = lax.broadcasted_iota(jnp.int32, s.shape, 1)
        s = jnp.where(lane < HEAD_SIZE // 2, -s, s)
        cosine[block, :] = c
        sine[block, :] = s
        copy.wait()
        proj[piece] = dot(piece_in[...], head_weight[...])

        def turned(at, row):
            return head_norm(proj[piece, :, at : at + HEAD_SIZE], gain_rows[row : row + 1, 0:HEAD_SIZE], c, s)

        for h in range(heads):
            at = h * HEAD_SIZE
            queries[block, at : at + HEAD_SIZE] = (turned(at, 2) * HEAD_SIZE ** (-0.5)).astype(BF16)
        keys[block, :] = turned(width, 3).astype(BF16)
        values[block, :] = proj[piece, :, width + HEAD_SIZE : width + 2 * HEAD_SIZE].astype(BF16)

    first_gather = Gather(normed_land, first_sems, project)
    grad_gathers = [
        Gather(grad_land, grad_sems[h], part=pl.ds(h * (count // 2), count // 2)) for h in range(2)
    ]
    first_gather.move(0)
    loop(parts, lambda i: token_copy(i, past_part(i)).wait_recv())

    def first_step(step):
        first_gather.move(step + 1)

        @pl.when(step == 0)
        def _():
            for share in shares[:4]:
                share.arrive()
            for share in shares[4:]:
                share.start()

        first_gather.use(step)

    loop(chips - 1, first_step)
    grad_copy.wait()
    for gather in grad_gathers:
        gather.step(0)
    first_gather.use(chips - 1)

    def attend(index):
        block = tile(index, QUERY_TILE)
        query_ids = column(index, 1)[:, 0:1]
        each = KEY_TILE // count
        lanes_of = [slice(h * HEAD_SIZE, (h + 1) * HEAD_SIZE) for h in range(heads)]

        def one(key_tile, carry):
            span = tile(key_tile, KEY_TILE)
            key, value = keys[span, :], values[span, :]
            key_ids = jnp.concatenate(
                [all_tokens[key_tile * each + j, 1:2, :] for j in range(each)], axis=1
            ).astype(F32)
            allowed = key_ids <= query_ids
            result = []
            for head, (sums, total) in zip(lanes_of, carry):
                expon = jnp.where(allowed, jnp.exp(rdot(queries[block, head], key)), 0.0)
                sums = sums + dot(expon.astype(BF16), value)
                result.append((sums, total + jnp.sum(expon, axis=1, keepdims=True)))
            return tuple(result)

        start = (jnp.zeros((QUERY_TILE, HEAD_SIZE), F32), jnp.zeros((QUERY_TILE, 1), F32))
        results = lax.fori_loop(0, reach(index, tokens), one, (start,) * heads)
        for h, (head, (sums, total)) in enumerate(zip(lanes_of, results)):
            scale = 1.0 / total
            context[block, head] = (sums * scale).astype(BF16)
            inverse[h : h + 1, block] = jnp.broadcast_to(scale, (QUERY_TILE, HEAD_SIZE)).T[0:1, :]

    def ready(target):
        each = 2 * count // QUERY_TILE
        loop(each, lambda i: attend(target * each + i))

    def produce(piece, chunk):
        return dot(context[tile(piece, count), :], out_weight[:, tile(chunk, WIDE)])

    scatter = Scatter(scratch, produce, total, ready)
    scatter.begin()
    scatter.prepare(0)

    def scatter_step(time):
        scatter.step(time)
        grad_gathers[0].step(time + 1)
        scatter.prepare(time + 1)
        grad_gathers[1].step(time + 1)

    loop(chips - 1, scatter_step)
    scatter.finish()

    def norm_two(block):
        value = x[block, :].astype(F32) + total[block, :]
        middle[block, :] = value
        own[block, :] = (value * inverse_norm(value) * gain_rows[1:2, :]).astype(BF16)

    row_blocks(count, norm_two)
    two_copy = copy_in(own, two_land.at[me], sems.at[1])
    two_copy.wait()
    for share in shares[4:]:
        share.arrive()
    outs = [
        copy_in(head_weight, refs_out, sems.at[2 + i])
        for i, (head_weight, refs_out) in enumerate(((pair, pair_weight), (down, down_weight)))
    ]
    feed_size = 256 if feed_width % 256 == 0 else 128

    def act_copy(piece):
        return pltpu.make_async_copy(act_out, activation.at[piece], sems.at[6])

    def back_copy(piece):
        return pltpu.make_async_copy(back_out, back.at[piece], sems.at[7])

    def feed(piece):
        copies = (
            copy_in(two_land.at[piece], piece_in, sems.at[4]),
            copy_in(grad_land.at[piece], grad_in, sems.at[5]),
        )
        for copy in copies:
            copy.wait()

        @pl.when(piece != me)
        def _():
            act_copy(piece).wait()
            back_copy(piece).wait()

        def one(index):
            def columns(kind):
                return pl.ds(pl.multiple_of(kind * feed_width + index * feed_size, 128), feed_size)

            gate = dot(piece_in[...], pair[:, columns(0)])
            up = dot(piece_in[...], pair[:, columns(1)])
            grad_act = rdot(grad_in[...], down[tile(index, feed_size), :])
            sigma = 1.0 / (1.0 + jnp.exp(-gate))
            act_out[:, columns(0)] = (gate * sigma * up).astype(BF16)
            back_out[:, columns(0)] = (
                grad_act * up * sigma * (1.0 + gate * (1.0 - sigma))
            ).astype(BF16)
            back_out[:, columns(1)] = (grad_act * gate * sigma).astype(BF16)

        loop(feed_width // feed_size, one)
        act_copy(piece).start()
        back_copy(piece).start()

    two_gather = Gather(two_land, two_sems, feed)
    loop(chips, two_gather.step)
    act_copy(0).wait()
    back_copy(0).wait()
    first_gather.finish()
    for gather in grad_gathers:
        gather.finish()
    two_gather.finish()
    for out in outs:
        out.wait()
    for share in shares:
        share.finish()
    loop(shards, lambda i: gain_copy(i, shard).wait_send())
    loop(parts, lambda i: token_copy(i, me).wait_send())


def forward(hidden, grad, gains, token_info, freq, weights, shards, parts, heads):
    count = hidden.shape[0]
    tokens = parts * count
    width = heads * HEAD_SIZE
    total_width = width + 2 * HEAD_SIZE
    feed_width = FF // parts
    chips = parts // 2
    shape = jax.ShapeDtypeStruct
    return pl.pallas_call(
        functools.partial(forward_kernel, heads),
        out_shape=(
            shape((parts, count, D), BF16),
            shape((parts, count, D), BF16),
            shape((parts, count, D), BF16),
            shape((parts, count, feed_width), BF16),
            shape((parts, count, 2 * feed_width), BF16),
            shape((parts, count, total_width), F32),
            shape((tokens, HEAD_SIZE), F32),
            shape((tokens, HEAD_SIZE), F32),
            shape((tokens, width), BF16),
            shape((tokens, HEAD_SIZE), BF16),
            shape((tokens, HEAD_SIZE), BF16),
            shape((tokens, width), BF16),
            shape((8, tokens), F32),
            shape((count, D), F32),
            shape((8, D), F32),
            shape((shards, *gains.shape), F32),
            shape((parts, *token_info.shape), jnp.int32),
            shape((D, total_width), BF16),
            shape((width, D), BF16),
            shape((D, 2 * feed_width), BF16),
            shape((feed_width, D), BF16),
        ),
        in_specs=[WHOLE] * 5 + [HBM] * 7,
        out_specs=(HBM,) * 5 + (WHOLE,) * 14 + (HBM,) * 2,
        scratch_shapes=[
            VMEM((D, 2 * feed_width), BF16),
            VMEM((feed_width, D), BF16),
            VMEM((count, D), BF16),
            VMEM((count, D), BF16),
            VMEM((count, D), BF16),
            VMEM((count, feed_width), BF16),
            VMEM((count, 2 * feed_width), BF16),
            VMEM((count, D), F32),
            pltpu.SemaphoreType.DMA((8,)),
        ]
        + [pltpu.SemaphoreType.DMA((shards,))] * 2
        + [pltpu.SemaphoreType.DMA((parts,))] * 2
        + shares_scratch(7, shards)
        + gather_scratch(chips)
        + gather_scratch(chips)
        + gather_scratch(chips)
        + gather_scratch(chips)
        + scatter_scratch(chips, count),
        compiler_params=params(0, 63),
        cost_estimate=cost(280),
        name="forward",
    )(hidden, grad, gains, token_info, freq, *weights)


def slab_size(parts):
    return 256 if parts <= 8 else 128


class Slabs:
    def __init__(self, sources, buffers, out, target, sems, products, place=lambda index: index):
        self.place = place
        self.sources, self.buffers, self.out, self.target = sources, buffers, out, target
        self.sems, self.products = sems, products
        self.size = out.shape[0]
        self.count = D // self.size

    def copies(self, index):
        slot = index % 2
        return [
            pltpu.make_async_copy(
                source.at[:, :, tile(self.place(index), self.size)], buffer.at[slot], self.sems.at[2 * i + slot]
            )
            for i, (source, buffer) in enumerate(zip(self.sources, self.buffers))
        ]

    def fetch(self, index):
        for copy in self.copies(index):
            copy.start()

    def leave(self, index):
        each = self.target.shape[1] // self.size
        place = self.place(index)
        target = self.target.at[place // each, tile(place % each, self.size), :]
        return pltpu.make_async_copy(self.out, target, self.sems.at[2 * len(self.sources)])

    def run(self, begin, end):
        def one(index, carry):
            for copy in self.copies(index):
                copy.wait()

            @pl.when(index + 1 < self.count)
            def _():
                self.fetch(index + 1)

            @pl.when(index > begin)
            def _():
                self.leave(index - 1).wait()

            at = 0
            for left, right in self.products(index % 2):
                left = left.reshape(-1, self.size)
                right = right.reshape(left.shape[0], -1)
                width = right.shape[1]
                self.out[:, at : at + width] = tdot(left, right).astype(BF16)
                at += width
            self.leave(index).start()
            return carry

        lax.fori_loop(begin, end, one, 0)

    def settle(self, index):
        self.leave(index - 1).wait()


def halves_first(half, size):
    inner = half // size
    per_half = D // size // 2

    def place(index):
        side, rest = index // per_half, index % per_half
        return (rest // inner) * 2 * inner + side * inner + rest % inner

    return place


def rms_back(value, gain, grad):
    inverse = inverse_norm(value)
    scaled = grad * gain
    inner = jnp.mean(scaled * value, axis=-1, keepdims=True)
    terms = grad * value * inverse
    return inverse * scaled - value * (inverse * inverse * inverse * inner), terms


def turn_kernel(*refs):
    back, pair_weight, down_weight, activation, out_weight = refs[:5]
    middle, gain_rows, grads, normed = refs[5:9]
    grad_middle, land, gain_sum, down_land, context_grad, hidden = refs[9:15]
    pair_in, pair_grad, pair_sum, down_grad, refs = *refs[15:19], refs[19:]
    weight, data, act, mid, total, low, own_down, sems = refs[:8]
    slab, slab_out, down_out, slab_sems, sum_sems, refs = *refs[8:13], refs[13:]
    down_refs, down_sems, refs = (refs[:3], refs[3:6]), (refs[6:12], refs[12:18]), refs[18:]
    gather_sems, pair_sems, refs = (refs[:6], refs[6:12]), refs[12:14], refs[14:]
    first_scratch, second_scratch = refs[:9], refs[9:]
    me, _, _, chips = line_position()
    width = back.shape[2] // 2
    weight_copy = copy_in(pair_weight, weight, sems.at[0])
    data_copy = copy_in(back, data, sems.at[1])
    act_copy = copy_in(activation, act, sems.at[3])
    mid_copy = copy_in(middle, mid, sems.at[2])
    low_copy = copy_in(grads.at[me], low, sems.at[4])

    def produce(piece, chunk):
        return rdot(data[piece], weight[pl.ds(pl.multiple_of(chunk * WIDE, WIDE), WIDE), :])

    each = 2 * width // WIDE

    def down_block(chunk):
        return tile(chunk // each, width), tile(chunk % each, WIDE)

    def down_copy(chunk):
        source = down_weight.at[:, tile(chunk, WIDE)]
        return pltpu.make_async_copy(source, weight.at[down_block(chunk)], sems.at[5 + chunk])

    def produce_hidden(piece, chunk):
        return dot(act[piece], weight[down_block(chunk)])

    side = low.shape[0] // 2

    def consume_of(part):
        def consume(piece):
            copy = copy_in(land.at[piece, part], low.at[part], sems.at[4])
            copy.wait()
            context_grad[piece, part] = rdot(low[part, :], out_weight[...]).astype(BF16)

        return consume

    sides = [pl.ds(h * side, side) for h in range(2)]
    gathers = [
        Gather(land, gather_sems[h], consume_of(sides[h]), part=sides[h]) for h in range(2)
    ]

    def products(slot):
        return ((slab[slot], data[...]),)

    def down_products(slot):
        return ((slab[slot], act[...]),)

    slabs = Slabs((normed,), (slab,), slab_out, pair_grad, slab_sems, products)
    half = own_down.shape[0] // 2
    halves = [pl.ds(h * half, half) for h in range(2)]
    order = halves_first(half, down_out.shape[0])
    down_slabs = Slabs((grads,), (slab,), down_out, down_grad, slab_sems, down_products, order)
    downs = [
        FsdpSum(down_grad, *down_refs[h], own=own_down.at[halves[h]], part=halves[h]) for h in range(2)
    ]
    down_gathers = [Gather(down_land, down_sems[h], part=halves[h]) for h in range(2)]

    def down_ready(h):
        downs[h].collect(own_down.at[halves[h]])
        copy = copy_in(own_down.at[halves[h]], down_land.at[me, halves[h]], sems.at[3])
        copy.wait()
        down_gathers[h].step(0)

    pair = FsdpSum(pair_grad, pair_in, *pair_sems, own=own_down)
    scatter = Scatter(first_scratch, produce, total)
    hidden_scatter = Scatter(second_scratch, produce_hidden, total)
    scatter.begin()
    hidden_scatter.begin()
    full_barrier()
    down_slabs.fetch(0)
    weight_copy.wait()
    data_copy.wait()
    scatter.prepare(0)

    def step(time):
        scatter.step(time)
        scatter.prepare(time + 1)

        @pl.when(time == 0)
        def _():
            act_copy.wait()
            for h in range(2):
                begin, end = h * down_slabs.count // 2, (h + 1) * down_slabs.count // 2
                down_slabs.run(begin, end)
                down_slabs.settle(end)
                downs[h].start()
            slabs.fetch(0)
            own_copy = copy_in(down_grad.at[lax.axis_index("fsdp")], own_down, sems.at[3])
            own_copy.wait()

        @pl.when(time == 1)
        def _():
            down_ready(0)

        @pl.when(time >= 2)
        def _():
            down_gathers[0].step(time - 1)

        @pl.when(time == 2)
        def _():
            down_ready(1)

        @pl.when(time >= 3)
        def _():
            down_gathers[1].step(time - 2)

        @pl.when(jnp.logical_or(time == 1, time == 2))
        def _():
            slabs.run((time - 1) * slabs.count // 2, time * slabs.count // 2)
            slabs.settle(time * slabs.count // 2)

        @pl.when(time == 2)
        def _():
            pair.start()

    loop(chips - 1, step)
    scatter.finish()
    down_gathers[0].step(chips - 2)
    down_gathers[1].step(chips - 3)
    for chunk in range(CHUNKS):
        down_copy(chunk).start()
    mid_copy.wait()
    low_copy.wait()
    gain_sum[...] = jnp.zeros_like(gain_sum)

    def norm(block):
        through, terms = rms_back(mid[block, :], gain_rows[1:2, :], total[block, :])
        value = low[block, :].astype(F32) + through
        mid[block, :] = value
        low[block, :] = value.astype(BF16)
        gain_sum[0:1, :] += jnp.sum(terms, axis=0, keepdims=True)

    row_blocks(mid.shape[0], norm)
    mid_out = copy_in(mid, grad_middle, sems.at[2])
    low_copy = copy_in(low, land.at[me], sems.at[3])
    low_copy.wait()
    for gather in gathers:
        gather.step(0)
    for chunk in range(CHUNKS):
        down_copy(chunk).wait()
    hidden_scatter.prepare(0)
    mid_out.wait()
    mid_copy = copy_in(middle, mid, sems.at[2])

    def add_pairs():
        pair.arrive()
        shard = lax.axis_index("fsdp")
        count, size = slab.shape[2], slab.shape[3]
        per = own_down.shape[0] // count
        tiles = 2 * width // size

        def arrivals(index):
            slot = index % 2
            copies = []
            for i in range(pair.peers + 1):
                source = pair_grad.at[shard] if i == 0 else pair_in.at[i - 1]
                for j in range(per):
                    at = i * per + j
                    block = source.at[pl.ds(j * count, count), tile(index, size)]
                    copies.append(
                        pltpu.make_async_copy(block, slab.at[slot, at], sum_sems.at[slot, at])
                    )
            return copies

        def leave(index):
            slot = index % 2
            return [
                pltpu.make_async_copy(
                    slab.at[slot, j],
                    pair_sum.at[pl.ds(j * count, count), tile(index, size)],
                    sum_sems.at[slot, j],
                )
                for j in range(per)
            ]

        for copy in arrivals(0):
            copy.start()

        def one(index):
            @pl.when(index > 0)
            def _():
                for copy in leave(index - 1):
                    copy.wait()

            @pl.when(index + 1 < tiles)
            def _():
                for copy in arrivals(index + 1):
                    copy.start()

            for copy in arrivals(index):
                copy.wait()
            slot = index % 2
            for j in range(per):
                value = slab[slot, j].astype(F32)
                for i in range(1, pair.peers + 1):
                    value = value + slab[slot, i * per + j].astype(F32)
                slab[slot, j] = value.astype(BF16)
            for copy in leave(index):
                copy.start()

        loop(tiles, one)
        for copy in leave(tiles - 1):
            copy.wait()

    def turn_step(time):
        hidden_scatter.step(time)
        gathers[0].step(time + 1)
        hidden_scatter.prepare(time + 1)

        @pl.when(time == chips - 2)
        def _():
            add_pairs()

        gathers[1].step(time + 1)

        @pl.when(time == 0)
        def _():
            down_gathers[0].step(chips - 1)
            down_gathers[1].step(chips - 2)

        @pl.when(time == 1)
        def _():
            down_gathers[1].step(chips - 1)

    loop(chips - 1, turn_step)
    hidden_scatter.finish()
    for h in range(2):
        gathers[h].finish()
        down_gathers[h].finish()
        downs[h].finish()
    pair.finish()
    mid_copy.wait()

    def add(block):
        hidden[block, :] = (mid[block, :] + total[block, :]).astype(BF16)

    row_blocks(mid.shape[0], add)


def turn(back, pair_weight, down_weight, activation, out_weight, middle, gain_rows, grads, normed, shards):
    parts, count, feed_width = activation.shape
    rows = D // shards
    width = out_weight.shape[0]
    return pl.pallas_call(
        turn_kernel,
        out_shape=(
            jax.ShapeDtypeStruct((count, D), F32),
            jax.ShapeDtypeStruct((parts, count, D), BF16),
            jax.ShapeDtypeStruct((8, D), F32),
            jax.ShapeDtypeStruct((parts, rows, feed_width), BF16),
            jax.ShapeDtypeStruct((parts, count, width), BF16),
            jax.ShapeDtypeStruct((count, D), BF16),
            jax.ShapeDtypeStruct((shards - 1, rows, 2 * feed_width), BF16),
            jax.ShapeDtypeStruct((shards, rows, 2 * feed_width), BF16),
            jax.ShapeDtypeStruct((rows, 2 * feed_width), BF16),
            jax.ShapeDtypeStruct((shards, rows, feed_width), BF16),
        ),
        in_specs=[HBM] * 4 + [WHOLE, HBM, WHOLE] + [HBM] * 2,
        out_specs=(HBM, HBM, WHOLE, HBM, WHOLE, WHOLE) + (HBM,) * 4,
        scratch_shapes=[
            VMEM((D, 2 * feed_width), BF16),
            VMEM((parts, count, 2 * feed_width), BF16),
            VMEM((parts, count, feed_width), BF16),
            VMEM((count, D), F32),
            VMEM((count, D), F32),
            VMEM((count, D), BF16),
            VMEM((rows, feed_width), BF16),
            pltpu.SemaphoreType.DMA((5 + CHUNKS,)),
            VMEM((2, parts, count, slab_size(parts)), BF16),
            VMEM((slab_size(parts), 2 * feed_width), BF16),
            VMEM((slab_size(parts), feed_width), BF16),
            pltpu.SemaphoreType.DMA((3,)),
            pltpu.SemaphoreType.DMA((2, parts)),
        ]
        + fsdp_scratch(shards, rows // 2, feed_width)
        + fsdp_scratch(shards, rows // 2, feed_width)
        + gather_scratch(parts // 2)
        + gather_scratch(parts // 2)
        + gather_scratch(parts // 2)
        + gather_scratch(parts // 2)
        + [pltpu.SemaphoreType.DMA((shards,))] * 2
        + scatter_scratch(parts // 2, count)
        + scatter_scratch(parts // 2, count),
        compiler_params=params(3, 63),
        cost_estimate=cost(185),
        name="turn",
    )(
        back,
        pair_weight,
        down_weight,
        activation,
        out_weight,
        middle,
        gain_rows,
        grads,
        normed,
    )


PAIR_PARTS = 4


def last_kernel(heads, *refs):
    queries, keys, values, out_grad, inverse, context, proj, cosine, sine, token_info = refs[:10]
    weights, x, grad_middle, gain_rows, gain_two, normed, low, pair_sum = refs[10:18]
    hidden, gain_out, head_grad, land, pair_land = refs[18:23]
    back, gain_heads, key_grad, value_grad, query_grad, pair_own, pair_sem = refs[23:30]
    pair_sems, refs = refs[30:36], refs[36:]
    weight, weight_sem, total, gain_one, pack, pack_in, shard_sum, shard_in = refs[:8]
    slabs_in, slab_out, slab_sems, own_head, refs = refs[8:10], refs[10], refs[11], refs[12], refs[13:]
    small, head_refs, refs = refs[:4], (refs[4:7], refs[7:10]), refs[10:]
    gather_sems, scratch = (refs[:6], refs[6:12]), refs[12:]
    me, _, _, chips = line_position()
    shard = lax.axis_index("fsdp")
    shards, ahead, _ = peers_of("fsdp")
    parts, next_part, _ = peers_of("ctx")
    tokens = queries.shape[0]
    key_at = heads * HEAD_SIZE
    copy = copy_in(weights, weight, weight_sem)
    pair_copy = copy_in(pair_sum, pair_own, pair_sem)
    pair_size = pair_own.shape[0] // PAIR_PARTS

    def pump(begin, end):
        def one(index, carry):
            part = index % PAIR_PARTS
            sems = [ref.at[part] for ref in pair_sems]
            Gather(pair_land, sems, part=tile(part, pair_size)).step(index // PAIR_PARTS)
            return carry

        lax.fori_loop(begin, end, one, 0)

    def produce(piece, chunk):
        return rdot(back[piece], weight[pl.ds(pl.multiple_of(chunk * WIDE, WIDE), WIDE), :])

    def products(slot):
        return (slabs_in[0][slot], back[...]), (slabs_in[1][slot], context[...])

    half = own_head.shape[0] // 2
    halves = [pl.ds(h * half, half) for h in range(2)]
    per_half = D // slab_out.shape[0] // 2
    place = halves_first(half, slab_out.shape[0])
    slabs = Slabs((normed, low), slabs_in, slab_out, head_grad, slab_sems, products, place)
    head_sums = [
        FsdpSum(head_grad, *head_refs[h], own=own_head.at[halves[h]], part=halves[h]) for h in range(2)
    ]
    gathers = [Gather(land, gather_sems[h], part=halves[h]) for h in range(2)]

    def head_ready(h):
        head_sums[h].collect(land.at[me, halves[h]])
        gathers[h].step(0)
    scatter = Scatter(scratch, produce, total)
    scatter.begin()
    slabs.fetch(0)
    full_barrier()
    pair_copy.wait()
    pair_copy = copy_in(pair_own, pair_land.at[me], pair_sem)
    pair_copy.wait()
    pump(0, PAIR_PARTS)
    key_grad[...] = jnp.zeros_like(key_grad)
    value_grad[...] = jnp.zeros_like(value_grad)
    gain_heads[...] = jnp.zeros_like(gain_heads)

    def through(index, lanes, grad, row):
        block = tile(index, QUERY_TILE)
        turned = pltpu.roll(grad, HEAD_SIZE // 2, 1)
        unrotated = grad * cosine[block, :] - turned * sine[block, :]
        result, terms = rms_back(proj[index, :, lanes], gain_rows[row + 2 : row + 3, :HEAD_SIZE], unrotated)
        back[index, :, lanes] = result.astype(BF16)
        gain_heads[row : row + 1, :] += jnp.sum(terms, axis=0, keepdims=True)

    count = token_info.shape[2]
    each = KEY_TILE // count

    def attend(index):
        block = tile(index, QUERY_TILE)
        query_ids = token_info[index, 1:2, :].astype(F32)
        shifts = []
        for h in range(heads):
            lanes = slice(h * HEAD_SIZE, (h + 1) * HEAD_SIZE)
            products = out_grad[index, :, lanes].astype(F32) * context[index, :, lanes].astype(F32)
            shift = lax.dot_general(
                jnp.ones((8, HEAD_SIZE), F32),
                products,
                (((1,), (1,)), ((), ())),
                precision=lax.Precision.HIGHEST,
                preferred_element_type=F32,
            )[0:1, :]
            shifts.append(shift)
        query_grad[...] = jnp.zeros_like(query_grad)

        def one(key_tile):
            span = tile(key_tile, KEY_TILE)
            key, value = keys[span, :], values[span, :]
            key_ids = jnp.concatenate(
                [
                    jnp.broadcast_to(
                        token_info[key_tile * each + j, 1:2, :].astype(F32), (128, count)
                    ).T[:, 0:1]
                    for j in range(each)
                ],
                axis=0,
            )
            allowed = key_ids <= query_ids
            for h in range(heads):
                lanes = slice(h * HEAD_SIZE, (h + 1) * HEAD_SIZE)
                query, grad = queries[block, lanes], out_grad[index, :, lanes]
                expon = jnp.exp(rdot(key, query)) * inverse[h : h + 1, block]
                probs = jnp.where(allowed, expon, 0.0)
                grad_scores = (probs * (rdot(value, grad) - shifts[h])).astype(BF16)
                value_grad[span, :] += dot(probs.astype(BF16), grad)
                key_grad[span, :] += dot(grad_scores, query)
                query_grad[:, lanes] += tdot(grad_scores, key)

        loop(reach(index, tokens), one)
        for h in range(heads):
            lanes = slice(h * HEAD_SIZE, (h + 1) * HEAD_SIZE)
            through(index, lanes, query_grad[:, lanes] * HEAD_SIZE ** (-0.5), 0)

    def finish_keys(index):
        block = tile(index, QUERY_TILE)
        through(index, slice(key_at, key_at + HEAD_SIZE), key_grad[block, :], 1)
        back[index, :, key_at + HEAD_SIZE :] = value_grad[block, :].astype(BF16)

    tiles = tokens // QUERY_TILE
    marks = (0, 3 * tiles // 8, 5 * tiles // 8, 6 * tiles // 8, tiles)
    for i in range(4):
        loop(marks[i + 1] - marks[i], lambda index, i=i: attend(marks[i] + index))
        pump(PAIR_PARTS + i, PAIR_PARTS + i + 1)
    loop(tiles, finish_keys)
    copy.wait()
    for h in range(2):
        slabs.run(h * per_half, (h + 1) * per_half)
        slabs.settle((h + 1) * per_half)
        head_sums[h].start()
        pump(2 * PAIR_PARTS + h, 2 * PAIR_PARTS + h + 1)
    own = copy_in(head_grad.at[shard], own_head, weight_sem)
    own.wait()
    scatter.prepare(0)

    def step(time):
        scatter.step(time)
        scatter.prepare(time + 1)
        begin = 2 * PAIR_PARTS + 2
        span = PAIR_PARTS * (chips - 3)
        pump(begin + time * span // (chips - 1), begin + (time + 1) * span // (chips - 1))

        @pl.when(time == 0)
        def _():
            head_ready(0)

        @pl.when(time >= 1)
        def _():
            gathers[0].step(time)

        @pl.when(time == 1)
        def _():
            head_ready(1)

        @pl.when(time >= 2)
        def _():
            gathers[1].step(time - 1)

    loop(chips - 1, step)
    scatter.finish()
    gathers[0].step(chips - 1)
    gathers[1].step(chips - 2)
    gain_one[...] = jnp.zeros_like(gain_one)

    def norm(block):
        through, terms = rms_back(x[block, :].astype(F32), gain_rows[0:1, :], total[block, :])
        hidden[block, :] = grad_middle[block, :] + through
        gain_one[0:1, :] += jnp.sum(terms, axis=0, keepdims=True)

    row_blocks(x.shape[0], norm)

    rows = D // (shards + 1)
    lanes = rows // 128
    pack[...] = jnp.zeros_like(pack)
    for owner in range(shards + 1):
        for j in range(lanes):
            at = owner * rows + j * 128
            pack[owner, j : j + 1, :] = gain_one[0:1, at : at + 128]
            pack[owner, lanes + j : lanes + j + 1, :] = gain_two[0:1, at : at + 128]
        pack[owner, 2 * lanes : 2 * lanes + 2, :] = gain_heads[0:2, :]

    def pack_copy(i):
        return send(pack.at[ahead(i)], pack_in.at[i], small[0].at[i], small[1].at[i], "fsdp", ahead(i))

    def sum_copy(i):
        return send(shard_sum, shard_in.at[i], small[2].at[i], small[3].at[i], "ctx", next_part(i))

    loop(shards, lambda i: pack_copy(i).start())
    shard_sum[...] = pack[shard]

    def add_pack(i):
        pack_copy(i).wait_recv()
        shard_sum[...] += pack_in[i]

    loop(shards, add_pack)
    loop(parts, lambda i: sum_copy(i).start())
    gain_out[...] = shard_sum[...]

    def add_sum(i):
        sum_copy(i).wait_recv()
        gain_out[...] += shard_in[i]

    loop(parts, add_sum)
    gathers[1].step(chips - 1)
    pump(PAIR_PARTS * (chips - 1) + 2, PAIR_PARTS * chips)

    def settle_pair(part):
        sems = [ref.at[part] for ref in pair_sems]
        Gather(pair_land, sems, part=tile(part, pair_size)).finish()

    loop(PAIR_PARTS, settle_pair)
    for h in range(2):
        gathers[h].finish()
        head_sums[h].finish()
    loop(shards, lambda i: pack_copy(i).wait_send())
    loop(parts, lambda i: sum_copy(i).wait_send())


def last(*operands):
    tokens, query_width = operands[0].shape
    heads = query_width // HEAD_SIZE
    parts = operands[5].shape[0]
    count = tokens // parts
    width = query_width + 2 * HEAD_SIZE
    head_width = width + query_width
    rows, pair_width = operands[-1].shape
    shards = D // rows
    chips = parts // 2
    return pl.pallas_call(
        functools.partial(last_kernel, heads),
        out_shape=(
            jax.ShapeDtypeStruct((count, D), F32),
            jax.ShapeDtypeStruct((16, 128), F32),
            jax.ShapeDtypeStruct((shards, rows, head_width), BF16),
            jax.ShapeDtypeStruct((parts, rows, head_width), BF16),
            jax.ShapeDtypeStruct((parts, rows, pair_width), BF16),
        ),
        in_specs=[WHOLE] * 10 + [HBM] + [WHOLE] * 4 + [HBM] * 3,
        out_specs=(WHOLE, WHOLE, HBM, WHOLE, HBM),
        scratch_shapes=[
            VMEM((parts, count, width), BF16),
            VMEM((8, HEAD_SIZE), F32),
            VMEM((tokens, HEAD_SIZE), F32),
            VMEM((tokens, HEAD_SIZE), F32),
            VMEM((QUERY_TILE, query_width), F32),
            VMEM((rows, pair_width), BF16),
            pltpu.SemaphoreType.DMA,
        ]
        + [pltpu.SemaphoreType.DMA((PAIR_PARTS, chips)) for _ in range(6)]
        + [
            VMEM((D, width), BF16),
            pltpu.SemaphoreType.DMA,
            VMEM((count, D), F32),
            VMEM((8, D), F32),
            VMEM((shards, 16, 128), F32),
            VMEM((shards, 16, 128), F32),
            VMEM((16, 128), F32),
            VMEM((parts, 16, 128), F32),
            VMEM((2, parts, count, slab_size(parts)), BF16),
            VMEM((2, parts, count, slab_size(parts)), BF16),
            VMEM((slab_size(parts), head_width), BF16),
            pltpu.SemaphoreType.DMA((5,)),
            VMEM((rows, head_width), BF16),
        ]
        + [pltpu.SemaphoreType.DMA((shards,))] * 2
        + [pltpu.SemaphoreType.DMA((parts,))] * 2
        + fsdp_scratch(shards, rows // 2, head_width)
        + fsdp_scratch(shards, rows // 2, head_width)
        + gather_scratch(chips)
        + gather_scratch(chips)
        + scatter_scratch(chips, count),
        compiler_params=params(5, 63),
        cost_estimate=cost(190),
        name="last",
    )(*operands)


def spread_kernel(width, head_source, pair_source, down_source, *targets):
    query, key, value, out, gate, up, down = targets
    second = width + HEAD_SIZE
    third = second + HEAD_SIZE
    query[...] = head_source[0, :, :width].astype(F32)
    key[...] = head_source[0, :, width:second].astype(F32)
    value[...] = head_source[0, :, second:third].astype(F32)
    out[...] = head_source[0, :, third:].astype(F32).T
    feed_width = gate.shape[1]
    gate[...] = pair_source[0, :, :feed_width].astype(F32)
    up[...] = pair_source[0, :, feed_width:].astype(F32)
    down[...] = down_source[0].astype(F32).T


def spread(head_parts, pair_parts, down_parts, width):
    parts, rows, _ = head_parts.shape
    feed_width = down_parts.shape[2]
    sources = (head_parts, pair_parts, down_parts)

    def side_by_side(columns):
        shape = jax.ShapeDtypeStruct((rows, parts * columns), F32)
        return shape, pl.BlockSpec((rows, columns), lambda i: (0, i))

    def stacked(columns):
        shape = jax.ShapeDtypeStruct((parts * columns, rows), F32)
        return shape, pl.BlockSpec((columns, rows), lambda i: (i, 0))

    outs = (
        side_by_side(width),
        side_by_side(HEAD_SIZE),
        side_by_side(HEAD_SIZE),
        stacked(width),
        side_by_side(feed_width),
        side_by_side(feed_width),
        stacked(feed_width),
    )
    return pl.pallas_call(
        functools.partial(spread_kernel, width),
        out_shape=tuple(shape for shape, _ in outs),
        grid=(parts,),
        in_specs=[pl.BlockSpec((1, *source.shape[1:]), lambda i: (i, 0, 0)) for source in sources],
        out_specs=tuple(spec for _, spec in outs),
        compiler_params=pltpu.CompilerParams(vmem_limit_bytes=60 * 1024 * 1024),
        name="spread",
    )(*sources)


def local(
    hidden_in,
    weight_query,
    key_weight_matrix,
    weight_value,
    weight_out,
    weight_gate,
    weight_up,
    weight_down,
    gain_attention,
    gain_feed,
    gain_query,
    gain_key,
    positions,
    token_block_index,
    grad_out,
):
    parts = lax.axis_size("ctx")
    shards = lax.axis_size("fsdp")
    shard = lax.axis_index("fsdp")
    heads = QUERY_HEADS // parts
    sharers = parts // KEY_VALUE_HEADS
    width = heads * HEAD_SIZE
    feed_width = FF // parts
    rows = D // shards
    head_rows = HEAD_SIZE // shards
    count = hidden_in.shape[1]
    tokens = parts * count

    own_gains = jnp.concatenate([gain_attention, gain_feed, gain_query, gain_key]).astype(F32)
    own_gains = jnp.pad(own_gains, (0, 2048 - own_gains.shape[0])).reshape(16, 128)
    own_tokens = jnp.pad(jnp.stack([positions[0], token_block_index[0]]), ((0, 6), (0, 0)))
    half = HEAD_SIZE // 2
    freq = THETA ** (-(jnp.arange(half).astype(F32) * 2.0 / HEAD_SIZE))
    freq = jnp.broadcast_to(jnp.concatenate([freq, freq]), (8, HEAD_SIZE))
    hidden, grad = hidden_in[0], grad_out[0]
    weights = (
        weight_query,
        key_weight_matrix,
        weight_value,
        weight_out,
        weight_gate,
        weight_up,
        weight_down,
    )
    (
        normed_all,
        grad_all,
        normed_two_all,
        activation,
        back,
        proj,
        cosine,
        sine,
        queries,
        keys,
        values,
        context,
        inverse,
        middle,
        gain_rows,
        gains,
        whole,
        heads_weight,
        out_weight,
        pair_weight,
        down_weight,
    ) = forward(hidden, grad, own_gains, own_tokens, freq, weights, shards, parts, heads)

    grad_middle, low_all, gain_two, down_parts, context_grad, hidden_out, _, _, feed_shard, _ = turn(
        back,
        pair_weight,
        down_weight,
        activation,
        out_weight,
        middle,
        gain_rows,
        grad_all,
        normed_two_all,
        shards,
    )
    grad_hidden, gain_sums, _, head_parts, feed_parts = last(
        queries,
        keys,
        values,
        context_grad,
        inverse,
        context.reshape(parts, count, width),
        proj,
        cosine,
        sine,
        whole,
        heads_weight,
        hidden,
        grad_middle,
        gain_rows,
        gain_two,
        normed_all,
        low_all,
        feed_shard,
    )

    gain_sums = gain_sums.reshape(-1)
    grad_query, grad_key, grad_value, grad_out_weight, grad_gate, grad_up, grad_down = spread(
        head_parts, feed_parts, down_parts, width
    )
    if sharers > 1:
        grad_key, grad_value = (
            part.reshape(rows, KEY_VALUE_HEADS, sharers, HEAD_SIZE).sum(axis=2).reshape(rows, -1)
            for part in (grad_key, grad_value)
        )
    return (
        hidden_out[None],
        grad_hidden[None],
        grad_query,
        grad_key,
        grad_value,
        grad_out_weight,
        grad_gate,
        grad_up,
        grad_down,
        gain_sums[:rows],
        gain_sums[rows : 2 * rows],
        lax.dynamic_slice_in_dim(gain_sums, 2 * rows + shard * head_rows, head_rows),
        lax.dynamic_slice_in_dim(gain_sums, 2 * rows + HEAD_SIZE + shard * head_rows, head_rows),
    )


def solution(mesh):
    tokens = P("fsdp", "ctx", None)
    by_rows = P("fsdp", None)
    by_columns = P(None, "fsdp")
    per_token = P("fsdp", "ctx")
    vector = P("fsdp")
    weights = (by_rows, by_rows, by_rows, by_columns, by_rows, by_rows, by_columns)
    return jax.shard_map(
        local,
        mesh=mesh,
        in_specs=(tokens, *weights, vector, vector, vector, vector, per_token, per_token, tokens),
        out_specs=(tokens, tokens, *weights, vector, vector, vector, vector),
        check_vma=False,
    )
```

```python
import functools

import jax
import jax.numpy as jnp
from jax import lax
from jax.experimental import pallas as pl
from jax.experimental.pallas import tpu as pltpu
from jax.sharding import PartitionSpec as P

D = 2048
QUERY_HEADS = 16
KEY_VALUE_HEADS = 8
HEAD_SIZE = 128
FF = 6144
EPS = 1e-06
THETA = 1000000.0
F32 = jnp.float32
BF16 = jnp.bfloat16
MESH = pl.DeviceIdType.MESH
VMEM = pltpu.VMEM
WHOLE = pl.BlockSpec(memory_space=pltpu.VMEM)
HBM = pl.BlockSpec(memory_space=pl.ANY)
CHUNKS = 4
WIDE = D // CHUNKS


def dot(left, right):
    return jnp.dot(left, right, preferred_element_type=F32)


def tdot(left, right):
    return lax.dot_general(left, right, (((0,), (0,)), ((), ())), preferred_element_type=F32)


def rdot(left, right):
    return lax.dot_general(left, right, (((1,), (1,)), ((), ())), preferred_element_type=F32)


def loop(count, body):
    def step(index, carry):
        body(index)
        return carry

    lax.fori_loop(0, count, step, 0)


def line_position():
    me = lax.axis_index("ctx")
    return me, me // 2, me % 2, lax.axis_size("ctx") // 2


def send(source, target, send_sem, recv_sem, axis, index):
    return pltpu.make_async_remote_copy(
        src_ref=source,
        dst_ref=target,
        send_sem=send_sem,
        recv_sem=recv_sem,
        device_id={axis: index},
        device_id_type=MESH,
    )


def line_barrier():
    me, chip, core, chips = line_position()
    barrier = pltpu.get_barrier_semaphore()

    def greet(index):
        pl.semaphore_signal(barrier, inc=1, device_id={"ctx": index}, device_id_type=MESH)

    greet(me + 1 - 2 * core)

    @pl.when(chip > 0)
    def _():
        greet(me - 2)

    @pl.when(chip < chips - 1)
    def _():
        greet(me + 2)

    peers = 1 + (chip > 0).astype(jnp.int32) + (chip < chips - 1).astype(jnp.int32)
    pl.semaphore_wait(barrier, peers)


def peers_of(axis):
    me, size = lax.axis_index(axis), lax.axis_size(axis)
    return size - 1, lambda i: (me + i + 1) % size, lambda i: (me + size - i - 1) % size


def full_barrier():
    barrier = pltpu.get_barrier_semaphore()
    total = 0
    for axis in ("fsdp", "ctx"):
        count, ahead, _ = peers_of(axis)
        loop(
            count,
            lambda i, axis=axis, ahead=ahead: pl.semaphore_signal(
                barrier, inc=1, device_id={axis: ahead(i)}, device_id_type=MESH
            ),
        )
        total += count
    pl.semaphore_wait(barrier, total)


def gather_scratch(chips):
    return [pltpu.SemaphoreType.DMA((chips,)) for _ in range(6)]


class Gather:
    def __init__(self, land, sems, consume=None, part=None):
        self.part = part
        self.land = land
        self.sems = sems
        self.consume = consume
        self.me, self.chip, self.core, self.chips = line_position()

    def place(self, piece):
        return self.land.at[piece] if self.part is None else self.land.at[piece, self.part]

    def right(self, step, source):
        ref = self.place(2 * source + self.core)
        return send(ref, ref, self.sems[0].at[step], self.sems[1].at[step], "ctx", self.me + 2)

    def left(self, step, source):
        ref = self.place(2 * source + self.core)
        return send(ref, ref, self.sems[2].at[step], self.sems[3].at[step], "ctx", self.me - 2)

    def across(self, source, core):
        ref = self.place(2 * source + core)
        other = self.me + 1 - 2 * self.core
        return send(ref, ref, self.sems[4].at[source], self.sems[5].at[source], "ctx", other)

    def step(self, step):
        self.move(step)
        self.use(step)

    def move(self, step):
        chip, core, chips = self.chip, self.core, self.chips
        low, high = chip - step, chip + step
        has_low = low >= 0
        has_high = jnp.logical_and(high < chips, step > 0)

        @pl.when(jnp.logical_and(has_low, step > 0))
        def _():
            self.right(step - 1, low).wait_recv()

        @pl.when(jnp.logical_and(has_low, chip < chips - 1))
        def _():
            self.right(step, low).start()

        @pl.when(has_high)
        def _():
            self.left(step - 1, high).wait_recv()

        @pl.when(jnp.logical_and(high < chips, chip > 0))
        def _():
            self.left(step, high).start()

        @pl.when(has_low)
        def _():
            self.across(low, core).start()

        @pl.when(has_high)
        def _():
            self.across(high, core).start()

    def use(self, step):
        chip, core, chips = self.chip, self.core, self.chips
        low, high = chip - step, chip + step

        def one(kind):
            upward = kind % 2
            crossed = kind // 2
            source = jnp.where(upward == 1, high, low)
            valid = jnp.where(upward == 1, jnp.logical_and(high < chips, step > 0), low >= 0)
            parity = jnp.where(crossed == 1, 1 - core, core)

            @pl.when(valid)
            def _():
                @pl.when(crossed == 1)
                def _():
                    self.across(source, parity).wait_recv()

                if self.consume is not None:
                    self.consume(2 * source + parity)

        loop(4, one)

    def finish(self):
        chip, core, chips = self.chip, self.core, self.chips

        def one(step):
            @pl.when(jnp.logical_and(chip - step >= 0, chip < chips - 1))
            def _():
                self.right(step, chip - step).wait_send()

            @pl.when(jnp.logical_and(chip + step < chips, chip > 0))
            def _():
                self.left(step, chip + step).wait_send()

            self.across(step, core).wait_send()

        loop(chips, one)


def scatter_scratch(chips, rows):
    buffers = [VMEM((count, CHUNKS, rows, WIDE), BF16) for count in (chips + 1, 2, chips)]
    return buffers + [pltpu.SemaphoreType.DMA((chips, CHUNKS)) for _ in range(6)]


class Scatter:
    def __init__(self, scratch, produce, total, ready=None):
        self.ready = ready
        self.line, self.out, self.other = scratch[:3]
        self.sems = scratch[3:]
        self.produce = produce
        self.total = total
        self.me, self.chip, self.core, self.chips = line_position()


    def right(self, step, chunk):
        ref = self.line.at[step, chunk]
        sems = self.sems
        return send(ref, ref, sems[0].at[step, chunk], sems[1].at[step, chunk], "ctx", self.me + 2)

    def left(self, step, chunk):
        ref = self.line.at[self.chips - step, chunk]
        sems = self.sems
        return send(ref, ref, sems[2].at[step, chunk], sems[3].at[step, chunk], "ctx", self.me - 2)

    def across(self, target, chunk, slot=0):
        sems = self.sems
        return send(
            self.out.at[slot, chunk],
            self.other.at[target, chunk],
            sems[4].at[target, chunk],
            sems[5].at[target, chunk],
            "ctx",
            self.me + 1 - 2 * self.core,
        )

    def begin(self):
        def clear(index):
            slot, chunk = index // CHUNKS, index % CHUNKS
            at_left = jnp.logical_and(self.chip == 0, slot < self.chips)
            at_right = jnp.logical_and(self.chip == self.chips - 1, slot > 0)

            @pl.when(jnp.logical_or(at_left, at_right))
            def _():
                self.line[slot, chunk] = jnp.zeros(self.line.shape[2:], BF16)

        loop((self.chips + 1) * CHUNKS, clear)

    def when_right(self, time):
        return jnp.logical_and(time >= self.chip, time < self.chips - 1)

    def when_left(self, time):
        return jnp.logical_and(time >= self.chips - 1 - self.chip, time < self.chips - 1)

    def prepare(self, time):
        chip, chips = self.chip, self.chips

        def cross(target, slot, before, used):
            if self.ready is not None:
                self.ready(target)

            def one(chunk):
                @pl.when(used)
                def _():
                    self.across(before, chunk, slot).wait_send()

                piece = 2 * target + 1 - self.core
                self.out[slot, chunk] = self.produce(piece, chunk).astype(BF16)
                self.across(target, chunk, slot).start()

            loop(CHUNKS, one)

        @pl.when(self.when_right(time))
        def _():
            target = chips - 1 - time + chip
            cross(target, 0, target + 1, time > chip)

        @pl.when(self.when_left(time))
        def _():
            target = time - (chips - 1 - chip)
            cross(target, 1, target - 1, target > 0)

        @pl.when(time == chips - 1)
        def _():
            cross(chip, 0, chip + 1, chip < chips - 1)

    def step(self, time):
        chip, core, chips = self.chip, self.core, self.chips

        @pl.when(self.when_right(time))
        def _():
            step = time - chip
            target = chips - 1 - step

            def one(chunk):
                self.across(target, chunk).wait_recv()

                @pl.when(chip > 0)
                def _():
                    self.right(step, chunk).wait_recv()

                value = self.produce(2 * target + core, chunk) + self.other[target, chunk].astype(F32)
                value = value + self.line[step, chunk].astype(F32)
                self.line[step, chunk] = value.astype(BF16)
                self.right(step, chunk).start()

            loop(CHUNKS, one)

        @pl.when(self.when_left(time))
        def _():
            step = time - (chips - 1 - chip)

            def one(chunk):
                self.across(step, chunk).wait_recv()

                @pl.when(chip < chips - 1)
                def _():
                    self.left(step, chunk).wait_recv()

                value = self.produce(2 * step + core, chunk) + self.other[step, chunk].astype(F32)
                value = value + self.line[chips - step, chunk].astype(F32)
                self.line[chips - step, chunk] = value.astype(BF16)
                self.left(step, chunk).start()

            loop(CHUNKS, one)

    def finish(self):
        chip, core, chips = self.chip, self.core, self.chips
        last = chips - 1 - chip

        def one(chunk):
            self.across(chip, chunk).wait_recv()
            value = self.produce(2 * chip + core, chunk) + self.other[chip, chunk].astype(F32)

            @pl.when(chip > 0)
            def _():
                self.right(last, chunk).wait_recv()

            @pl.when(chip < chips - 1)
            def _():
                self.left(chip, chunk).wait_recv()

            value = value + self.line[last, chunk].astype(F32)
            value = value + self.line[chips - chip, chunk].astype(F32)
            self.total[:, pl.ds(pl.multiple_of(chunk * WIDE, WIDE), WIDE)] = value

        loop(CHUNKS, one)

        def drain(index):
            step, chunk = index // CHUNKS, index % CHUNKS

            @pl.when(step < last)
            def _():
                self.right(step, chunk).wait_send()

            @pl.when(step < chip)
            def _():
                self.left(step, chunk).wait_send()

            @pl.when(jnp.logical_or(step == chip, step == chip - 1))
            def _():
                self.across(step, chunk, jnp.where(step == chip, 0, 1)).wait_send()

        loop(chips * CHUNKS, drain)


def tile(index, size):
    return pl.ds(pl.multiple_of(index * size, size), size)


def row_blocks(rows, body, size=32):
    def one(index):
        body(pl.ds(pl.multiple_of(index * size, size), size))

    loop(rows // size, one)


def inverse_norm(value):
    return lax.rsqrt(jnp.mean(value * value, axis=-1, keepdims=True) + EPS)


def params(identity, megabytes):
    return pltpu.CompilerParams(
        collective_id=identity,
        has_side_effects=True,
        vmem_limit_bytes=megabytes * 1024 * 1024,
    )


def cost(microseconds):
    return pl.CostEstimate(
        flops=int(microseconds * 1.15e9), bytes_accessed=1024, transcendentals=0
    )


class FsdpSum:
    def __init__(self, grad, arrived, send_sems, recv_sems, own=None, part=slice(None)):
        self.grad, self.arrived, self.part = grad, arrived, part
        self.own = grad.at[lax.axis_index("fsdp")] if own is None else own
        self.sems = send_sems, recv_sems
        self.peers, self.ahead, _ = peers_of("fsdp")

    def copy(self, i):
        target = self.ahead(i)
        return send(
            self.grad.at[target, self.part], self.arrived.at[i], self.sems[0].at[i], self.sems[1].at[i], "fsdp", target
        )

    def start(self):
        loop(self.peers, lambda i: self.copy(i).start())

    def arrive(self):
        loop(self.peers, lambda i: self.copy(i).wait_recv())

    def collect(self, target):
        self.arrive()
        self.add(target)

    def add(self, target):
        def one(block):
            value = self.own[block, :].astype(F32)
            for i in range(self.peers):
                value = value + self.arrived[i, block].astype(F32)
            target[block, :] = value.astype(BF16)

        row_blocks(self.own.shape[0], one)

    def finish(self):
        loop(self.peers, lambda i: self.copy(i).wait_send())


def fsdp_scratch(shards, rows, width):
    return [VMEM((shards - 1, rows, width), BF16)] + [pltpu.SemaphoreType.DMA((shards,))] * 2


def sine_cosine(angle):
    count = jnp.floor(angle * 0.6366197723675814 + 0.5)
    rest = angle - count * 1.5703125
    rest = rest - count * 4.837512969970703e-4
    rest = rest - count * 7.549789948768648e-8
    square = rest * rest
    sine = -1.9515295891e-4 * square + 8.3321608736e-3
    sine = rest + rest * square * (sine * square - 1.6666654611e-1)
    cosine = 2.443315711809948e-5 * square - 1.388731625493765e-3
    cosine = 1.0 - 0.5 * square + square * square * (cosine * square + 4.166664568298827e-2)
    quarter = jnp.bitwise_and(count.astype(jnp.int32), 3)
    odd = jnp.bitwise_and(quarter, 1) == 1
    sine, cosine = jnp.where(odd, cosine, sine), jnp.where(odd, sine, cosine)
    sine = jnp.where(quarter >= 2, -sine, sine)
    cosine = jnp.where(jnp.logical_or(quarter == 1, quarter == 2), -cosine, cosine)
    return sine, cosine


class Shares:
    def __init__(self, source, target_of, own_sem, sems):
        self.source, self.target_of = source, target_of
        self.own_sem, self.sems = own_sem, sems
        self.peers, self.ahead, self.behind = peers_of("fsdp")
        self.shard = lax.axis_index("fsdp")

    def copy(self, i, owner):
        sems = self.sems
        target = self.target_of(owner)
        return send(self.source, target, sems[0].at[i], sems[1].at[i], "fsdp", self.ahead(i))

    def own(self):
        return pltpu.make_async_copy(self.source, self.target_of(self.shard), self.own_sem)

    def start(self):
        loop(self.peers, lambda i: self.copy(i, self.shard).start())
        self.own().start()

    def arrive(self):
        self.own().wait()
        loop(self.peers, lambda i: self.copy(i, self.behind(i)).wait_recv())

    def finish(self):
        loop(self.peers, lambda i: self.copy(i, self.shard).wait_send())


def shares_scratch(count, shards):
    return [pltpu.SemaphoreType.DMA((count,))] + [pltpu.SemaphoreType.DMA((shards,))] * (2 * count)


def copy_in(source, target, sem):
    copy = pltpu.make_async_copy(source, target, sem)
    copy.start()
    return copy


QUERY_TILE = 256
KEY_TILE = 512


def reach(index, tokens):
    return jnp.minimum((index + 2) * QUERY_TILE + KEY_TILE - 1, tokens) // KEY_TILE


def head_norm(value, gain, cosine, sine):
    normed = value * inverse_norm(value) * gain
    return normed * cosine + pltpu.roll(normed, HEAD_SIZE // 2, 1) * sine


def forward_kernel(heads, *refs):
    x, grad, gains, token_info, freq = refs[:5]
    sources, refs = refs[5:12], refs[12:]
    normed_land, grad_land, two_land, activation, back = refs[:5]
    proj, cosine, sine, queries, keys, values, context, inverse = refs[5:13]
    middle, gain_rows, all_gains, all_tokens = refs[13:17]
    head_weight, out_weight, pair_weight, down_weight = refs[17:21]
    refs = refs[21:]
    pair, down, own, piece_in, grad_in, act_out, back_out, total, sems = refs[:9]
    small, refs = refs[9:13], refs[13:]
    share_own, share_sems, refs = refs[0], refs[1:15], refs[15:]
    first_sems, grad_sems, two_sems, scratch = refs[:6], refs[6:12], refs[12:18], refs[18:]
    me, _, _, chips = line_position()
    shard = lax.axis_index("fsdp")
    shards, ahead, behind = peers_of("fsdp")
    parts, next_part, past_part = peers_of("ctx")
    count = x.shape[0]
    tokens = 2 * chips * count
    width = heads * HEAD_SIZE
    feed_width = down.shape[0]
    rows = D // (shards + 1)
    lanes = rows // 128
    key_head = me // (2 * chips // KEY_VALUE_HEADS)

    def gain_copy(i, slot):
        return send(gains, all_gains.at[slot], small[0].at[i], small[1].at[i], "fsdp", ahead(i))

    def token_copy(i, slot):
        return send(token_info, all_tokens.at[slot], small[2].at[i], small[3].at[i], "ctx", next_part(i))

    def by_row(target, at, size):
        return lambda owner: target.at[tile(owner, rows), pl.ds(at, size)]

    def by_column(target):
        return lambda owner: target.at[:, tile(owner, rows)]

    places = (
        (sources[0].at[:, tile(me, width)], by_row(head_weight, 0, width)),
        (sources[1].at[:, tile(key_head, HEAD_SIZE)], by_row(head_weight, width, HEAD_SIZE)),
        (sources[2].at[:, tile(key_head, HEAD_SIZE)], by_row(head_weight, width + HEAD_SIZE, HEAD_SIZE)),
        (sources[3].at[tile(me, width), :], by_column(out_weight)),
        (sources[4].at[:, tile(me, feed_width)], by_row(pair, 0, feed_width)),
        (sources[5].at[:, tile(me, feed_width)], by_row(pair, feed_width, feed_width)),
        (sources[6].at[tile(me, feed_width), :], by_column(down)),
    )
    shares = [
        Shares(source, target_of, share_own.at[i], share_sems[2 * i : 2 * i + 2])
        for i, (source, target_of) in enumerate(places)
    ]

    full_barrier()
    loop(shards, lambda i: gain_copy(i, shard).start())
    loop(parts, lambda i: token_copy(i, me).start())
    for share in shares[:4]:
        share.start()
    grad_copy = copy_in(grad, grad_land.at[me], sems.at[0])
    all_gains[shard] = gains[...]
    all_tokens[me] = token_info[...]
    loop(shards, lambda i: gain_copy(i, behind(i)).wait_recv())
    for kind in range(2):
        for owner in range(shards + 1):
            for j in range(lanes):
                at = owner * rows + j * 128
                gain_rows[kind : kind + 1, at : at + 128] = all_gains[
                    owner, kind * lanes + j : kind * lanes + j + 1, :
                ]
    size = HEAD_SIZE // (shards + 1)
    for kind in range(2):
        gain_rows[2 + kind : 3 + kind, 0:HEAD_SIZE] = jnp.concatenate(
            [
                all_gains[
                    owner, 2 * lanes : 2 * lanes + 1, kind * size : (kind + 1) * size
                ]
                for owner in range(shards + 1)
            ],
            axis=1,
        )

    def norm(block):
        value = x[block, :].astype(F32)
        own[block, :] = (value * inverse_norm(value) * gain_rows[0:1, :]).astype(BF16)

    row_blocks(count, norm)
    own_copy = copy_in(own, normed_land.at[me], sems.at[1])
    own_copy.wait()

    def column(piece, row):
        values_in_lanes = all_tokens[piece, row : row + 1, :].astype(F32)
        return jnp.broadcast_to(values_in_lanes, (128, count)).T

    def project(piece):
        copy = copy_in(normed_land.at[piece], piece_in, sems.at[1])
        block = tile(piece, count)
        s, c = sine_cosine(column(piece, 0) * freq[0:1, :])
        lane = lax.broadcasted_iota(jnp.int32, s.shape, 1)
        s = jnp.where(lane < HEAD_SIZE // 2, -s, s)
        cosine[block, :] = c
        sine[block, :] = s
        copy.wait()
        proj[piece] = dot(piece_in[...], head_weight[...])

        def turned(at, row):
            return head_norm(proj[piece, :, at : at + HEAD_SIZE], gain_rows[row : row + 1, 0:HEAD_SIZE], c, s)

        for h in range(heads):
            at = h * HEAD_SIZE
            queries[block, at : at + HEAD_SIZE] = (turned(at, 2) * HEAD_SIZE ** (-0.5)).astype(BF16)
        keys[block, :] = turned(width, 3).astype(BF16)
        values[block, :] = proj[piece, :, width + HEAD_SIZE : width + 2 * HEAD_SIZE].astype(BF16)

    first_gather = Gather(normed_land, first_sems, project)
    grad_gather = Gather(grad_land, grad_sems)
    first_gather.move(0)
    loop(parts, lambda i: token_copy(i, past_part(i)).wait_recv())

    def first_step(step):
        first_gather.move(step + 1)

        @pl.when(step == 0)
        def _():
            for share in shares[:4]:
                share.arrive()
            for share in shares[4:]:
                share.start()

        first_gather.use(step)

    loop(chips - 1, first_step)
    grad_copy.wait()
    grad_gather.step(0)
    first_gather.use(chips - 1)

    def attend(index):
        block = tile(index, QUERY_TILE)
        query_ids = column(index, 1)[:, 0:1]
        each = KEY_TILE // count
        lanes_of = [slice(h * HEAD_SIZE, (h + 1) * HEAD_SIZE) for h in range(heads)]

        def one(key_tile, carry):
            span = tile(key_tile, KEY_TILE)
            key, value = keys[span, :], values[span, :]
            key_ids = jnp.concatenate(
                [all_tokens[key_tile * each + j, 1:2, :] for j in range(each)], axis=1
            ).astype(F32)
            allowed = key_ids <= query_ids
            result = []
            for head, (sums, total) in zip(lanes_of, carry):
                expon = jnp.where(allowed, jnp.exp(rdot(queries[block, head], key)), 0.0)
                sums = sums + dot(expon.astype(BF16), value)
                result.append((sums, total + jnp.sum(expon, axis=1, keepdims=True)))
            return tuple(result)

        start = (jnp.zeros((QUERY_TILE, HEAD_SIZE), F32), jnp.zeros((QUERY_TILE, 1), F32))
        results = lax.fori_loop(0, reach(index, tokens), one, (start,) * heads)
        for h, (head, (sums, total)) in enumerate(zip(lanes_of, results)):
            scale = 1.0 / total
            context[block, head] = (sums * scale).astype(BF16)
            inverse[h : h + 1, block] = jnp.broadcast_to(scale, (QUERY_TILE, HEAD_SIZE)).T[0:1, :]

    def ready(target):
        each = 2 * count // QUERY_TILE
        loop(each, lambda i: attend(target * each + i))

    def produce(piece, chunk):
        return dot(context[tile(piece, count), :], out_weight[:, tile(chunk, WIDE)])

    scatter = Scatter(scratch, produce, total, ready)
    scatter.begin()
    scatter.prepare(0)

    def scatter_step(time):
        scatter.step(time)
        scatter.prepare(time + 1)
        grad_gather.step(time + 1)

    loop(chips - 1, scatter_step)
    scatter.finish()

    def norm_two(block):
        value = x[block, :].astype(F32) + total[block, :]
        middle[block, :] = value
        own[block, :] = (value * inverse_norm(value) * gain_rows[1:2, :]).astype(BF16)

    row_blocks(count, norm_two)
    two_copy = copy_in(own, two_land.at[me], sems.at[1])
    two_copy.wait()
    for share in shares[4:]:
        share.arrive()
    outs = [
        copy_in(head_weight, refs_out, sems.at[2 + i])
        for i, (head_weight, refs_out) in enumerate(((pair, pair_weight), (down, down_weight)))
    ]
    feed_size = 256 if feed_width % 256 == 0 else 128

    def act_copy(piece):
        return pltpu.make_async_copy(act_out, activation.at[piece], sems.at[6])

    def back_copy(piece):
        return pltpu.make_async_copy(back_out, back.at[piece], sems.at[7])

    def feed(piece):
        copies = (
            copy_in(two_land.at[piece], piece_in, sems.at[4]),
            copy_in(grad_land.at[piece], grad_in, sems.at[5]),
        )
        for copy in copies:
            copy.wait()

        @pl.when(piece != me)
        def _():
            act_copy(piece).wait()
            back_copy(piece).wait()

        def one(index):
            def columns(kind):
                return pl.ds(pl.multiple_of(kind * feed_width + index * feed_size, 128), feed_size)

            gate = dot(piece_in[...], pair[:, columns(0)])
            up = dot(piece_in[...], pair[:, columns(1)])
            grad_act = rdot(grad_in[...], down[tile(index, feed_size), :])
            sigma = 1.0 / (1.0 + jnp.exp(-gate))
            act_out[:, columns(0)] = (gate * sigma * up).astype(BF16)
            back_out[:, columns(0)] = (
                grad_act * up * sigma * (1.0 + gate * (1.0 - sigma))
            ).astype(BF16)
            back_out[:, columns(1)] = (grad_act * gate * sigma).astype(BF16)

        loop(feed_width // feed_size, one)
        act_copy(piece).start()
        back_copy(piece).start()

    two_gather = Gather(two_land, two_sems, feed)
    loop(chips, two_gather.step)
    act_copy(0).wait()
    back_copy(0).wait()
    first_gather.finish()
    grad_gather.finish()
    two_gather.finish()
    for out in outs:
        out.wait()
    for share in shares:
        share.finish()
    loop(shards, lambda i: gain_copy(i, shard).wait_send())
    loop(parts, lambda i: token_copy(i, me).wait_send())


def forward(hidden, grad, gains, token_info, freq, weights, shards, parts, heads):
    count = hidden.shape[0]
    tokens = parts * count
    width = heads * HEAD_SIZE
    total_width = width + 2 * HEAD_SIZE
    feed_width = FF // parts
    chips = parts // 2
    shape = jax.ShapeDtypeStruct
    return pl.pallas_call(
        functools.partial(forward_kernel, heads),
        out_shape=(
            shape((parts, count, D), BF16),
            shape((parts, count, D), BF16),
            shape((parts, count, D), BF16),
            shape((parts, count, feed_width), BF16),
            shape((parts, count, 2 * feed_width), BF16),
            shape((parts, count, total_width), F32),
            shape((tokens, HEAD_SIZE), F32),
            shape((tokens, HEAD_SIZE), F32),
            shape((tokens, width), BF16),
            shape((tokens, HEAD_SIZE), BF16),
            shape((tokens, HEAD_SIZE), BF16),
            shape((tokens, width), BF16),
            shape((8, tokens), F32),
            shape((count, D), F32),
            shape((8, D), F32),
            shape((shards, *gains.shape), F32),
            shape((parts, *token_info.shape), jnp.int32),
            shape((D, total_width), BF16),
            shape((width, D), BF16),
            shape((D, 2 * feed_width), BF16),
            shape((feed_width, D), BF16),
        ),
        in_specs=[WHOLE] * 5 + [HBM] * 7,
        out_specs=(HBM,) * 5 + (WHOLE,) * 14 + (HBM,) * 2,
        scratch_shapes=[
            VMEM((D, 2 * feed_width), BF16),
            VMEM((feed_width, D), BF16),
            VMEM((count, D), BF16),
            VMEM((count, D), BF16),
            VMEM((count, D), BF16),
            VMEM((count, feed_width), BF16),
            VMEM((count, 2 * feed_width), BF16),
            VMEM((count, D), F32),
            pltpu.SemaphoreType.DMA((8,)),
        ]
        + [pltpu.SemaphoreType.DMA((shards,))] * 2
        + [pltpu.SemaphoreType.DMA((parts,))] * 2
        + shares_scratch(7, shards)
        + gather_scratch(chips)
        + gather_scratch(chips)
        + gather_scratch(chips)
        + scatter_scratch(chips, count),
        compiler_params=params(0, 63),
        cost_estimate=cost(280),
        name="forward",
    )(hidden, grad, gains, token_info, freq, *weights)


def slab_size(parts):
    return 256 if parts <= 8 else 128


class Slabs:
    def __init__(self, sources, buffers, out, target, sems, products, place=lambda index: index):
        self.place = place
        self.sources, self.buffers, self.out, self.target = sources, buffers, out, target
        self.sems, self.products = sems, products
        self.size = out.shape[0]
        self.count = D // self.size

    def copies(self, index):
        slot = index % 2
        return [
            pltpu.make_async_copy(
                source.at[:, :, tile(self.place(index), self.size)], buffer.at[slot], self.sems.at[2 * i + slot]
            )
            for i, (source, buffer) in enumerate(zip(self.sources, self.buffers))
        ]

    def fetch(self, index):
        for copy in self.copies(index):
            copy.start()

    def leave(self, index):
        each = self.target.shape[1] // self.size
        place = self.place(index)
        target = self.target.at[place // each, tile(place % each, self.size), :]
        return pltpu.make_async_copy(self.out, target, self.sems.at[2 * len(self.sources)])

    def run(self, begin, end):
        def one(index, carry):
            for copy in self.copies(index):
                copy.wait()

            @pl.when(index + 1 < self.count)
            def _():
                self.fetch(index + 1)

            @pl.when(index > begin)
            def _():
                self.leave(index - 1).wait()

            at = 0
            for left, right in self.products(index % 2):
                left = left.reshape(-1, self.size)
                right = right.reshape(left.shape[0], -1)
                width = right.shape[1]
                self.out[:, at : at + width] = tdot(left, right).astype(BF16)
                at += width
            self.leave(index).start()
            return carry

        lax.fori_loop(begin, end, one, 0)

    def settle(self, index):
        self.leave(index - 1).wait()


def halves_first(half, size):
    inner = half // size
    per_half = D // size // 2

    def place(index):
        side, rest = index // per_half, index % per_half
        return (rest // inner) * 2 * inner + side * inner + rest % inner

    return place


def rms_back(value, gain, grad):
    inverse = inverse_norm(value)
    scaled = grad * gain
    inner = jnp.mean(scaled * value, axis=-1, keepdims=True)
    terms = grad * value * inverse
    return inverse * scaled - value * (inverse * inverse * inverse * inner), terms


def turn_kernel(*refs):
    back, pair_weight, down_weight, activation, out_weight = refs[:5]
    middle, gain_rows, grads, normed = refs[5:9]
    grad_middle, land, gain_sum, down_land, context_grad, hidden = refs[9:15]
    pair_in, pair_grad, pair_sum, down_grad, refs = *refs[15:19], refs[19:]
    weight, data, act, mid, total, low, own_down, sems = refs[:8]
    slab, slab_out, down_out, slab_sems, sum_sems, refs = *refs[8:13], refs[13:]
    down_refs, down_sems, refs = (refs[:3], refs[3:6]), (refs[6:12], refs[12:18]), refs[18:]
    gather_sems, pair_sems, refs = (refs[:6], refs[6:12]), refs[12:14], refs[14:]
    first_scratch, second_scratch = refs[:9], refs[9:]
    me, _, _, chips = line_position()
    width = back.shape[2] // 2
    weight_copy = copy_in(pair_weight, weight, sems.at[0])
    data_copy = copy_in(back, data, sems.at[1])
    act_copy = copy_in(activation, act, sems.at[3])
    mid_copy = copy_in(middle, mid, sems.at[2])
    low_copy = copy_in(grads.at[me], low, sems.at[4])

    def produce(piece, chunk):
        return rdot(data[piece], weight[pl.ds(pl.multiple_of(chunk * WIDE, WIDE), WIDE), :])

    each = 2 * width // WIDE

    def down_block(chunk):
        return tile(chunk // each, width), tile(chunk % each, WIDE)

    def down_copy(chunk):
        source = down_weight.at[:, tile(chunk, WIDE)]
        return pltpu.make_async_copy(source, weight.at[down_block(chunk)], sems.at[5 + chunk])

    def produce_hidden(piece, chunk):
        return dot(act[piece], weight[down_block(chunk)])

    side = low.shape[0] // 2

    def consume_of(part):
        def consume(piece):
            copy = copy_in(land.at[piece, part], low.at[part], sems.at[4])
            copy.wait()
            context_grad[piece, part] = rdot(low[part, :], out_weight[...]).astype(BF16)

        return consume

    sides = [pl.ds(h * side, side) for h in range(2)]
    gathers = [
        Gather(land, gather_sems[h], consume_of(sides[h]), part=sides[h]) for h in range(2)
    ]

    def products(slot):
        return ((slab[slot], data[...]),)

    def down_products(slot):
        return ((slab[slot], act[...]),)

    slabs = Slabs((normed,), (slab,), slab_out, pair_grad, slab_sems, products)
    half = own_down.shape[0] // 2
    halves = [pl.ds(h * half, half) for h in range(2)]
    order = halves_first(half, down_out.shape[0])
    down_slabs = Slabs((grads,), (slab,), down_out, down_grad, slab_sems, down_products, order)
    downs = [
        FsdpSum(down_grad, *down_refs[h], own=own_down.at[halves[h]], part=halves[h]) for h in range(2)
    ]
    down_gathers = [Gather(down_land, down_sems[h], part=halves[h]) for h in range(2)]

    def down_ready(h):
        downs[h].collect(own_down.at[halves[h]])
        copy = copy_in(own_down.at[halves[h]], down_land.at[me, halves[h]], sems.at[3])
        copy.wait()
        down_gathers[h].step(0)

    pair = FsdpSum(pair_grad, pair_in, *pair_sems, own=own_down)
    scatter = Scatter(first_scratch, produce, total)
    hidden_scatter = Scatter(second_scratch, produce_hidden, total)
    scatter.begin()
    hidden_scatter.begin()
    full_barrier()
    down_slabs.fetch(0)
    weight_copy.wait()
    data_copy.wait()
    scatter.prepare(0)

    def step(time):
        scatter.step(time)
        scatter.prepare(time + 1)

        @pl.when(time == 0)
        def _():
            act_copy.wait()
            for h in range(2):
                begin, end = h * down_slabs.count // 2, (h + 1) * down_slabs.count // 2
                down_slabs.run(begin, end)
                down_slabs.settle(end)
                downs[h].start()
            slabs.fetch(0)
            own_copy = copy_in(down_grad.at[lax.axis_index("fsdp")], own_down, sems.at[3])
            own_copy.wait()

        @pl.when(time == 1)
        def _():
            down_ready(0)

        @pl.when(time >= 2)
        def _():
            down_gathers[0].step(time - 1)

        @pl.when(time == 2)
        def _():
            down_ready(1)

        @pl.when(time >= 3)
        def _():
            down_gathers[1].step(time - 2)

        @pl.when(jnp.logical_or(time == 1, time == 2))
        def _():
            slabs.run((time - 1) * slabs.count // 2, time * slabs.count // 2)
            slabs.settle(time * slabs.count // 2)

        @pl.when(time == 2)
        def _():
            pair.start()

    loop(chips - 1, step)
    scatter.finish()
    down_gathers[0].step(chips - 2)
    down_gathers[1].step(chips - 3)
    for chunk in range(CHUNKS):
        down_copy(chunk).start()
    mid_copy.wait()
    low_copy.wait()
    gain_sum[...] = jnp.zeros_like(gain_sum)

    def norm(block):
        through, terms = rms_back(mid[block, :], gain_rows[1:2, :], total[block, :])
        value = low[block, :].astype(F32) + through
        mid[block, :] = value
        low[block, :] = value.astype(BF16)
        gain_sum[0:1, :] += jnp.sum(terms, axis=0, keepdims=True)

    row_blocks(mid.shape[0], norm)
    mid_out = copy_in(mid, grad_middle, sems.at[2])
    low_copy = copy_in(low, land.at[me], sems.at[3])
    low_copy.wait()
    for gather in gathers:
        gather.step(0)
    for chunk in range(CHUNKS):
        down_copy(chunk).wait()
    hidden_scatter.prepare(0)
    mid_out.wait()
    mid_copy = copy_in(middle, mid, sems.at[2])

    def add_pairs():
        pair.arrive()
        shard = lax.axis_index("fsdp")
        count, size = slab.shape[2], slab.shape[3]
        per = own_down.shape[0] // count
        tiles = 2 * width // size

        def arrivals(index):
            slot = index % 2
            copies = []
            for i in range(pair.peers + 1):
                source = pair_grad.at[shard] if i == 0 else pair_in.at[i - 1]
                for j in range(per):
                    at = i * per + j
                    block = source.at[pl.ds(j * count, count), tile(index, size)]
                    copies.append(
                        pltpu.make_async_copy(block, slab.at[slot, at], sum_sems.at[slot, at])
                    )
            return copies

        def leave(index):
            slot = index % 2
            return [
                pltpu.make_async_copy(
                    slab.at[slot, j],
                    pair_sum.at[pl.ds(j * count, count), tile(index, size)],
                    sum_sems.at[slot, j],
                )
                for j in range(per)
            ]

        for copy in arrivals(0):
            copy.start()

        def one(index):
            @pl.when(index > 0)
            def _():
                for copy in leave(index - 1):
                    copy.wait()

            @pl.when(index + 1 < tiles)
            def _():
                for copy in arrivals(index + 1):
                    copy.start()

            for copy in arrivals(index):
                copy.wait()
            slot = index % 2
            for j in range(per):
                value = slab[slot, j].astype(F32)
                for i in range(1, pair.peers + 1):
                    value = value + slab[slot, i * per + j].astype(F32)
                slab[slot, j] = value.astype(BF16)
            for copy in leave(index):
                copy.start()

        loop(tiles, one)
        for copy in leave(tiles - 1):
            copy.wait()

    def turn_step(time):
        gathers[0].step(time + 1)
        hidden_scatter.step(time)
        hidden_scatter.prepare(time + 1)

        @pl.when(time == chips - 2)
        def _():
            add_pairs()

        gathers[1].step(time + 1)

        @pl.when(time == 0)
        def _():
            down_gathers[0].step(chips - 1)
            down_gathers[1].step(chips - 2)

        @pl.when(time == 1)
        def _():
            down_gathers[1].step(chips - 1)

    loop(chips - 1, turn_step)
    hidden_scatter.finish()
    for h in range(2):
        gathers[h].finish()
        down_gathers[h].finish()
        downs[h].finish()
    pair.finish()
    mid_copy.wait()

    def add(block):
        hidden[block, :] = (mid[block, :] + total[block, :]).astype(BF16)

    row_blocks(mid.shape[0], add)


def turn(back, pair_weight, down_weight, activation, out_weight, middle, gain_rows, grads, normed, shards):
    parts, count, feed_width = activation.shape
    rows = D // shards
    width = out_weight.shape[0]
    return pl.pallas_call(
        turn_kernel,
        out_shape=(
            jax.ShapeDtypeStruct((count, D), F32),
            jax.ShapeDtypeStruct((parts, count, D), BF16),
            jax.ShapeDtypeStruct((8, D), F32),
            jax.ShapeDtypeStruct((parts, rows, feed_width), BF16),
            jax.ShapeDtypeStruct((parts, count, width), BF16),
            jax.ShapeDtypeStruct((count, D), BF16),
            jax.ShapeDtypeStruct((shards - 1, rows, 2 * feed_width), BF16),
            jax.ShapeDtypeStruct((shards, rows, 2 * feed_width), BF16),
            jax.ShapeDtypeStruct((rows, 2 * feed_width), BF16),
            jax.ShapeDtypeStruct((shards, rows, feed_width), BF16),
        ),
        in_specs=[HBM] * 4 + [WHOLE, HBM, WHOLE] + [HBM] * 2,
        out_specs=(HBM, HBM, WHOLE, HBM, WHOLE, WHOLE) + (HBM,) * 4,
        scratch_shapes=[
            VMEM((D, 2 * feed_width), BF16),
            VMEM((parts, count, 2 * feed_width), BF16),
            VMEM((parts, count, feed_width), BF16),
            VMEM((count, D), F32),
            VMEM((count, D), F32),
            VMEM((count, D), BF16),
            VMEM((rows, feed_width), BF16),
            pltpu.SemaphoreType.DMA((5 + CHUNKS,)),
            VMEM((2, parts, count, slab_size(parts)), BF16),
            VMEM((slab_size(parts), 2 * feed_width), BF16),
            VMEM((slab_size(parts), feed_width), BF16),
            pltpu.SemaphoreType.DMA((3,)),
            pltpu.SemaphoreType.DMA((2, parts)),
        ]
        + fsdp_scratch(shards, rows // 2, feed_width)
        + fsdp_scratch(shards, rows // 2, feed_width)
        + gather_scratch(parts // 2)
        + gather_scratch(parts // 2)
        + gather_scratch(parts // 2)
        + gather_scratch(parts // 2)
        + [pltpu.SemaphoreType.DMA((shards,))] * 2
        + scatter_scratch(parts // 2, count)
        + scatter_scratch(parts // 2, count),
        compiler_params=params(3, 63),
        cost_estimate=cost(185),
        name="turn",
    )(
        back,
        pair_weight,
        down_weight,
        activation,
        out_weight,
        middle,
        gain_rows,
        grads,
        normed,
    )


PAIR_PARTS = 4


def last_kernel(heads, *refs):
    queries, keys, values, out_grad, inverse, context, proj, cosine, sine, token_info = refs[:10]
    weights, x, grad_middle, gain_rows, gain_two, normed, low, pair_sum = refs[10:18]
    hidden, gain_out, head_grad, land, pair_land = refs[18:23]
    back, gain_heads, key_grad, value_grad, query_grad, pair_own, pair_sem = refs[23:30]
    pair_sems, refs = refs[30:36], refs[36:]
    weight, weight_sem, total, gain_one, pack, pack_in, shard_sum, shard_in = refs[:8]
    slabs_in, slab_out, slab_sems, own_head, refs = refs[8:10], refs[10], refs[11], refs[12], refs[13:]
    small, head_refs, refs = refs[:4], (refs[4:7], refs[7:10]), refs[10:]
    gather_sems, scratch = (refs[:6], refs[6:12]), refs[12:]
    me, _, _, chips = line_position()
    shard = lax.axis_index("fsdp")
    shards, ahead, _ = peers_of("fsdp")
    parts, next_part, _ = peers_of("ctx")
    tokens = queries.shape[0]
    key_at = heads * HEAD_SIZE
    copy = copy_in(weights, weight, weight_sem)
    pair_copy = copy_in(pair_sum, pair_own, pair_sem)
    pair_size = pair_own.shape[0] // PAIR_PARTS

    def pump(begin, end):
        def one(index, carry):
            part = index % PAIR_PARTS
            sems = [ref.at[part] for ref in pair_sems]
            Gather(pair_land, sems, part=tile(part, pair_size)).step(index // PAIR_PARTS)
            return carry

        lax.fori_loop(begin, end, one, 0)

    def produce(piece, chunk):
        return rdot(back[piece], weight[pl.ds(pl.multiple_of(chunk * WIDE, WIDE), WIDE), :])

    def products(slot):
        return (slabs_in[0][slot], back[...]), (slabs_in[1][slot], context[...])

    half = own_head.shape[0] // 2
    halves = [pl.ds(h * half, half) for h in range(2)]
    per_half = D // slab_out.shape[0] // 2
    place = halves_first(half, slab_out.shape[0])
    slabs = Slabs((normed, low), slabs_in, slab_out, head_grad, slab_sems, products, place)
    head_sums = [
        FsdpSum(head_grad, *head_refs[h], own=own_head.at[halves[h]], part=halves[h]) for h in range(2)
    ]
    gathers = [Gather(land, gather_sems[h], part=halves[h]) for h in range(2)]

    def head_ready(h):
        head_sums[h].collect(land.at[me, halves[h]])
        gathers[h].step(0)
    scatter = Scatter(scratch, produce, total)
    scatter.begin()
    slabs.fetch(0)
    full_barrier()
    pair_copy.wait()
    pair_copy = copy_in(pair_own, pair_land.at[me], pair_sem)
    pair_copy.wait()
    pump(0, PAIR_PARTS)
    key_grad[...] = jnp.zeros_like(key_grad)
    value_grad[...] = jnp.zeros_like(value_grad)
    gain_heads[...] = jnp.zeros_like(gain_heads)

    def through(index, lanes, grad, row):
        block = tile(index, QUERY_TILE)
        turned = pltpu.roll(grad, HEAD_SIZE // 2, 1)
        unrotated = grad * cosine[block, :] - turned * sine[block, :]
        result, terms = rms_back(proj[index, :, lanes], gain_rows[row + 2 : row + 3, :HEAD_SIZE], unrotated)
        back[index, :, lanes] = result.astype(BF16)
        gain_heads[row : row + 1, :] += jnp.sum(terms, axis=0, keepdims=True)

    count = token_info.shape[2]
    each = KEY_TILE // count

    def attend(index):
        block = tile(index, QUERY_TILE)
        query_ids = token_info[index, 1:2, :].astype(F32)
        shifts = []
        for h in range(heads):
            lanes = slice(h * HEAD_SIZE, (h + 1) * HEAD_SIZE)
            products = out_grad[index, :, lanes].astype(F32) * context[index, :, lanes].astype(F32)
            shift = lax.dot_general(
                jnp.ones((8, HEAD_SIZE), F32),
                products,
                (((1,), (1,)), ((), ())),
                precision=lax.Precision.HIGHEST,
                preferred_element_type=F32,
            )[0:1, :]
            shifts.append(shift)
        query_grad[...] = jnp.zeros_like(query_grad)

        def one(key_tile):
            span = tile(key_tile, KEY_TILE)
            key, value = keys[span, :], values[span, :]
            key_ids = jnp.concatenate(
                [
                    jnp.broadcast_to(
                        token_info[key_tile * each + j, 1:2, :].astype(F32), (128, count)
                    ).T[:, 0:1]
                    for j in range(each)
                ],
                axis=0,
            )
            allowed = key_ids <= query_ids
            for h in range(heads):
                lanes = slice(h * HEAD_SIZE, (h + 1) * HEAD_SIZE)
                query, grad = queries[block, lanes], out_grad[index, :, lanes]
                expon = jnp.exp(rdot(key, query)) * inverse[h : h + 1, block]
                probs = jnp.where(allowed, expon, 0.0)
                grad_scores = (probs * (rdot(value, grad) - shifts[h])).astype(BF16)
                value_grad[span, :] += dot(probs.astype(BF16), grad)
                key_grad[span, :] += dot(grad_scores, query)
                query_grad[:, lanes] += tdot(grad_scores, key)

        loop(reach(index, tokens), one)
        for h in range(heads):
            lanes = slice(h * HEAD_SIZE, (h + 1) * HEAD_SIZE)
            through(index, lanes, query_grad[:, lanes] * HEAD_SIZE ** (-0.5), 0)

    def finish_keys(index):
        block = tile(index, QUERY_TILE)
        through(index, slice(key_at, key_at + HEAD_SIZE), key_grad[block, :], 1)
        back[index, :, key_at + HEAD_SIZE :] = value_grad[block, :].astype(BF16)

    tiles = tokens // QUERY_TILE
    marks = (0, 3 * tiles // 8, 5 * tiles // 8, 6 * tiles // 8, tiles)
    for i in range(4):
        loop(marks[i + 1] - marks[i], lambda index, i=i: attend(marks[i] + index))
        pump(PAIR_PARTS + i, PAIR_PARTS + i + 1)
    loop(tiles, finish_keys)
    copy.wait()
    for h in range(2):
        slabs.run(h * per_half, (h + 1) * per_half)
        slabs.settle((h + 1) * per_half)
        head_sums[h].start()
        pump(2 * PAIR_PARTS + h, 2 * PAIR_PARTS + h + 1)
    own = copy_in(head_grad.at[shard], own_head, weight_sem)
    own.wait()
    scatter.prepare(0)

    def step(time):
        scatter.step(time)
        scatter.prepare(time + 1)
        begin = 2 * PAIR_PARTS + 2
        span = PAIR_PARTS * (chips - 3)
        pump(begin + time * span // (chips - 1), begin + (time + 1) * span // (chips - 1))

        @pl.when(time == 0)
        def _():
            head_ready(0)

        @pl.when(time >= 1)
        def _():
            gathers[0].step(time)

        @pl.when(time == 1)
        def _():
            head_ready(1)

        @pl.when(time >= 2)
        def _():
            gathers[1].step(time - 1)

    loop(chips - 1, step)
    scatter.finish()
    gathers[0].step(chips - 1)
    gathers[1].step(chips - 2)
    gain_one[...] = jnp.zeros_like(gain_one)

    def norm(block):
        through, terms = rms_back(x[block, :].astype(F32), gain_rows[0:1, :], total[block, :])
        hidden[block, :] = grad_middle[block, :] + through
        gain_one[0:1, :] += jnp.sum(terms, axis=0, keepdims=True)

    row_blocks(x.shape[0], norm)

    rows = D // (shards + 1)
    lanes = rows // 128
    pack[...] = jnp.zeros_like(pack)
    for owner in range(shards + 1):
        for j in range(lanes):
            at = owner * rows + j * 128
            pack[owner, j : j + 1, :] = gain_one[0:1, at : at + 128]
            pack[owner, lanes + j : lanes + j + 1, :] = gain_two[0:1, at : at + 128]
        pack[owner, 2 * lanes : 2 * lanes + 2, :] = gain_heads[0:2, :]

    def pack_copy(i):
        return send(pack.at[ahead(i)], pack_in.at[i], small[0].at[i], small[1].at[i], "fsdp", ahead(i))

    def sum_copy(i):
        return send(shard_sum, shard_in.at[i], small[2].at[i], small[3].at[i], "ctx", next_part(i))

    loop(shards, lambda i: pack_copy(i).start())
    shard_sum[...] = pack[shard]

    def add_pack(i):
        pack_copy(i).wait_recv()
        shard_sum[...] += pack_in[i]

    loop(shards, add_pack)
    loop(parts, lambda i: sum_copy(i).start())
    gain_out[...] = shard_sum[...]

    def add_sum(i):
        sum_copy(i).wait_recv()
        gain_out[...] += shard_in[i]

    loop(parts, add_sum)
    gathers[1].step(chips - 1)
    pump(PAIR_PARTS * (chips - 1) + 2, PAIR_PARTS * chips)

    def settle_pair(part):
        sems = [ref.at[part] for ref in pair_sems]
        Gather(pair_land, sems, part=tile(part, pair_size)).finish()

    loop(PAIR_PARTS, settle_pair)
    for h in range(2):
        gathers[h].finish()
        head_sums[h].finish()
    loop(shards, lambda i: pack_copy(i).wait_send())
    loop(parts, lambda i: sum_copy(i).wait_send())


def last(*operands):
    tokens, query_width = operands[0].shape
    heads = query_width // HEAD_SIZE
    parts = operands[5].shape[0]
    count = tokens // parts
    width = query_width + 2 * HEAD_SIZE
    head_width = width + query_width
    rows, pair_width = operands[-1].shape
    shards = D // rows
    chips = parts // 2
    return pl.pallas_call(
        functools.partial(last_kernel, heads),
        out_shape=(
            jax.ShapeDtypeStruct((count, D), F32),
            jax.ShapeDtypeStruct((16, 128), F32),
            jax.ShapeDtypeStruct((shards, rows, head_width), BF16),
            jax.ShapeDtypeStruct((parts, rows, head_width), BF16),
            jax.ShapeDtypeStruct((parts, rows, pair_width), BF16),
        ),
        in_specs=[WHOLE] * 10 + [HBM] + [WHOLE] * 4 + [HBM] * 3,
        out_specs=(WHOLE, WHOLE, HBM, WHOLE, HBM),
        scratch_shapes=[
            VMEM((parts, count, width), BF16),
            VMEM((8, HEAD_SIZE), F32),
            VMEM((tokens, HEAD_SIZE), F32),
            VMEM((tokens, HEAD_SIZE), F32),
            VMEM((QUERY_TILE, query_width), F32),
            VMEM((rows, pair_width), BF16),
            pltpu.SemaphoreType.DMA,
        ]
        + [pltpu.SemaphoreType.DMA((PAIR_PARTS, chips)) for _ in range(6)]
        + [
            VMEM((D, width), BF16),
            pltpu.SemaphoreType.DMA,
            VMEM((count, D), F32),
            VMEM((8, D), F32),
            VMEM((shards, 16, 128), F32),
            VMEM((shards, 16, 128), F32),
            VMEM((16, 128), F32),
            VMEM((parts, 16, 128), F32),
            VMEM((2, parts, count, slab_size(parts)), BF16),
            VMEM((2, parts, count, slab_size(parts)), BF16),
            VMEM((slab_size(parts), head_width), BF16),
            pltpu.SemaphoreType.DMA((5,)),
            VMEM((rows, head_width), BF16),
        ]
        + [pltpu.SemaphoreType.DMA((shards,))] * 2
        + [pltpu.SemaphoreType.DMA((parts,))] * 2
        + fsdp_scratch(shards, rows // 2, head_width)
        + fsdp_scratch(shards, rows // 2, head_width)
        + gather_scratch(chips)
        + gather_scratch(chips)
        + scatter_scratch(chips, count),
        compiler_params=params(5, 63),
        cost_estimate=cost(190),
        name="last",
    )(*operands)


def spread_kernel(width, head_source, pair_source, down_source, *targets):
    query, key, value, out, gate, up, down = targets
    second = width + HEAD_SIZE
    third = second + HEAD_SIZE
    query[...] = head_source[0, :, :width].astype(F32)
    key[...] = head_source[0, :, width:second].astype(F32)
    value[...] = head_source[0, :, second:third].astype(F32)
    out[...] = head_source[0, :, third:].astype(F32).T
    feed_width = gate.shape[1]
    gate[...] = pair_source[0, :, :feed_width].astype(F32)
    up[...] = pair_source[0, :, feed_width:].astype(F32)
    down[...] = down_source[0].astype(F32).T


def spread(head_parts, pair_parts, down_parts, width):
    parts, rows, _ = head_parts.shape
    feed_width = down_parts.shape[2]
    sources = (head_parts, pair_parts, down_parts)

    def side_by_side(columns):
        shape = jax.ShapeDtypeStruct((rows, parts * columns), F32)
        return shape, pl.BlockSpec((rows, columns), lambda i: (0, i))

    def stacked(columns):
        shape = jax.ShapeDtypeStruct((parts * columns, rows), F32)
        return shape, pl.BlockSpec((columns, rows), lambda i: (i, 0))

    outs = (
        side_by_side(width),
        side_by_side(HEAD_SIZE),
        side_by_side(HEAD_SIZE),
        stacked(width),
        side_by_side(feed_width),
        side_by_side(feed_width),
        stacked(feed_width),
    )
    return pl.pallas_call(
        functools.partial(spread_kernel, width),
        out_shape=tuple(shape for shape, _ in outs),
        grid=(parts,),
        in_specs=[pl.BlockSpec((1, *source.shape[1:]), lambda i: (i, 0, 0)) for source in sources],
        out_specs=tuple(spec for _, spec in outs),
        compiler_params=pltpu.CompilerParams(vmem_limit_bytes=60 * 1024 * 1024),
        name="spread",
    )(*sources)


def local(
    hidden_in,
    weight_query,
    key_weight_matrix,
    weight_value,
    weight_out,
    weight_gate,
    weight_up,
    weight_down,
    gain_attention,
    gain_feed,
    gain_query,
    gain_key,
    positions,
    token_block_index,
    grad_out,
):
    parts = lax.axis_size("ctx")
    shards = lax.axis_size("fsdp")
    shard = lax.axis_index("fsdp")
    heads = QUERY_HEADS // parts
    sharers = parts // KEY_VALUE_HEADS
    width = heads * HEAD_SIZE
    feed_width = FF // parts
    rows = D // shards
    head_rows = HEAD_SIZE // shards
    count = hidden_in.shape[1]
    tokens = parts * count

    own_gains = jnp.concatenate([gain_attention, gain_feed, gain_query, gain_key]).astype(F32)
    own_gains = jnp.pad(own_gains, (0, 2048 - own_gains.shape[0])).reshape(16, 128)
    own_tokens = jnp.pad(jnp.stack([positions[0], token_block_index[0]]), ((0, 6), (0, 0)))
    half = HEAD_SIZE // 2
    freq = THETA ** (-(jnp.arange(half).astype(F32) * 2.0 / HEAD_SIZE))
    freq = jnp.broadcast_to(jnp.concatenate([freq, freq]), (8, HEAD_SIZE))
    hidden, grad = hidden_in[0], grad_out[0]
    weights = (
        weight_query,
        key_weight_matrix,
        weight_value,
        weight_out,
        weight_gate,
        weight_up,
        weight_down,
    )
    (
        normed_all,
        grad_all,
        normed_two_all,
        activation,
        back,
        proj,
        cosine,
        sine,
        queries,
        keys,
        values,
        context,
        inverse,
        middle,
        gain_rows,
        gains,
        whole,
        heads_weight,
        out_weight,
        pair_weight,
        down_weight,
    ) = forward(hidden, grad, own_gains, own_tokens, freq, weights, shards, parts, heads)

    grad_middle, low_all, gain_two, down_parts, context_grad, hidden_out, _, _, feed_shard, _ = turn(
        back,
        pair_weight,
        down_weight,
        activation,
        out_weight,
        middle,
        gain_rows,
        grad_all,
        normed_two_all,
        shards,
    )
    grad_hidden, gain_sums, _, head_parts, feed_parts = last(
        queries,
        keys,
        values,
        context_grad,
        inverse,
        context.reshape(parts, count, width),
        proj,
        cosine,
        sine,
        whole,
        heads_weight,
        hidden,
        grad_middle,
        gain_rows,
        gain_two,
        normed_all,
        low_all,
        feed_shard,
    )

    gain_sums = gain_sums.reshape(-1)
    grad_query, grad_key, grad_value, grad_out_weight, grad_gate, grad_up, grad_down = spread(
        head_parts, feed_parts, down_parts, width
    )
    if sharers > 1:
        grad_key, grad_value = (
            part.reshape(rows, KEY_VALUE_HEADS, sharers, HEAD_SIZE).sum(axis=2).reshape(rows, -1)
            for part in (grad_key, grad_value)
        )
    return (
        hidden_out[None],
        grad_hidden[None],
        grad_query,
        grad_key,
        grad_value,
        grad_out_weight,
        grad_gate,
        grad_up,
        grad_down,
        gain_sums[:rows],
        gain_sums[rows : 2 * rows],
        lax.dynamic_slice_in_dim(gain_sums, 2 * rows + shard * head_rows, head_rows),
        lax.dynamic_slice_in_dim(gain_sums, 2 * rows + HEAD_SIZE + shard * head_rows, head_rows),
    )


def solution(mesh):
    tokens = P("fsdp", "ctx", None)
    by_rows = P("fsdp", None)
    by_columns = P(None, "fsdp")
    per_token = P("fsdp", "ctx")
    vector = P("fsdp")
    weights = (by_rows, by_rows, by_rows, by_columns, by_rows, by_rows, by_columns)
    return jax.shard_map(
        local,
        mesh=mesh,
        in_specs=(tokens, *weights, vector, vector, vector, vector, per_token, per_token, tokens),
        out_specs=(tokens, tokens, *weights, vector, vector, vector, vector),
        check_vma=False,
    )
```

```python
import functools

import jax
import jax.numpy as jnp
from jax import lax
from jax.experimental import pallas as pl
from jax.experimental.pallas import tpu as pltpu
from jax.sharding import PartitionSpec as P

D = 2048
QUERY_HEADS = 16
KEY_VALUE_HEADS = 8
HEAD_SIZE = 128
FF = 6144
EPS = 1e-06
THETA = 1000000.0
F32 = jnp.float32
BF16 = jnp.bfloat16
MESH = pl.DeviceIdType.MESH
VMEM = pltpu.VMEM
WHOLE = pl.BlockSpec(memory_space=pltpu.VMEM)
HBM = pl.BlockSpec(memory_space=pl.ANY)
CHUNKS = 4
WIDE = D // CHUNKS


def dot(left, right):
    return jnp.dot(left, right, preferred_element_type=F32)


def tdot(left, right):
    return lax.dot_general(left, right, (((0,), (0,)), ((), ())), preferred_element_type=F32)


def rdot(left, right):
    return lax.dot_general(left, right, (((1,), (1,)), ((), ())), preferred_element_type=F32)


def loop(count, body):
    def step(index, carry):
        body(index)
        return carry

    lax.fori_loop(0, count, step, 0)


def line_position():
    me = lax.axis_index("ctx")
    return me, me // 2, me % 2, lax.axis_size("ctx") // 2


def send(source, target, send_sem, recv_sem, axis, index):
    return pltpu.make_async_remote_copy(
        src_ref=source,
        dst_ref=target,
        send_sem=send_sem,
        recv_sem=recv_sem,
        device_id={axis: index},
        device_id_type=MESH,
    )


def line_barrier():
    me, chip, core, chips = line_position()
    barrier = pltpu.get_barrier_semaphore()

    def greet(index):
        pl.semaphore_signal(barrier, inc=1, device_id={"ctx": index}, device_id_type=MESH)

    greet(me + 1 - 2 * core)

    @pl.when(chip > 0)
    def _():
        greet(me - 2)

    @pl.when(chip < chips - 1)
    def _():
        greet(me + 2)

    peers = 1 + (chip > 0).astype(jnp.int32) + (chip < chips - 1).astype(jnp.int32)
    pl.semaphore_wait(barrier, peers)


def peers_of(axis):
    me, size = lax.axis_index(axis), lax.axis_size(axis)
    return size - 1, lambda i: (me + i + 1) % size, lambda i: (me + size - i - 1) % size


def full_barrier():
    barrier = pltpu.get_barrier_semaphore()
    total = 0
    for axis in ("fsdp", "ctx"):
        count, ahead, _ = peers_of(axis)
        loop(
            count,
            lambda i, axis=axis, ahead=ahead: pl.semaphore_signal(
                barrier, inc=1, device_id={axis: ahead(i)}, device_id_type=MESH
            ),
        )
        total += count
    pl.semaphore_wait(barrier, total)


def gather_scratch(chips):
    return [pltpu.SemaphoreType.DMA((chips,)) for _ in range(6)]


class Gather:
    def __init__(self, land, sems, consume=None, part=None):
        self.part = part
        self.land = land
        self.sems = sems
        self.consume = consume
        self.me, self.chip, self.core, self.chips = line_position()

    def place(self, piece):
        return self.land.at[piece] if self.part is None else self.land.at[piece, self.part]

    def right(self, step, source):
        ref = self.place(2 * source + self.core)
        return send(ref, ref, self.sems[0].at[step], self.sems[1].at[step], "ctx", self.me + 2)

    def left(self, step, source):
        ref = self.place(2 * source + self.core)
        return send(ref, ref, self.sems[2].at[step], self.sems[3].at[step], "ctx", self.me - 2)

    def across(self, source, core):
        ref = self.place(2 * source + core)
        other = self.me + 1 - 2 * self.core
        return send(ref, ref, self.sems[4].at[source], self.sems[5].at[source], "ctx", other)

    def step(self, step):
        self.move(step)
        self.use(step)

    def move(self, step):
        chip, core, chips = self.chip, self.core, self.chips
        low, high = chip - step, chip + step
        has_low = low >= 0
        has_high = jnp.logical_and(high < chips, step > 0)

        @pl.when(jnp.logical_and(has_low, step > 0))
        def _():
            self.right(step - 1, low).wait_recv()

        @pl.when(jnp.logical_and(has_low, chip < chips - 1))
        def _():
            self.right(step, low).start()

        @pl.when(has_high)
        def _():
            self.left(step - 1, high).wait_recv()

        @pl.when(jnp.logical_and(high < chips, chip > 0))
        def _():
            self.left(step, high).start()

        @pl.when(has_low)
        def _():
            self.across(low, core).start()

        @pl.when(has_high)
        def _():
            self.across(high, core).start()

    def use(self, step):
        chip, core, chips = self.chip, self.core, self.chips
        low, high = chip - step, chip + step

        def one(kind):
            upward = kind % 2
            crossed = kind // 2
            source = jnp.where(upward == 1, high, low)
            valid = jnp.where(upward == 1, jnp.logical_and(high < chips, step > 0), low >= 0)
            parity = jnp.where(crossed == 1, 1 - core, core)

            @pl.when(valid)
            def _():
                @pl.when(crossed == 1)
                def _():
                    self.across(source, parity).wait_recv()

                if self.consume is not None:
                    self.consume(2 * source + parity)

        loop(4, one)

    def finish(self):
        chip, core, chips = self.chip, self.core, self.chips

        def one(step):
            @pl.when(jnp.logical_and(chip - step >= 0, chip < chips - 1))
            def _():
                self.right(step, chip - step).wait_send()

            @pl.when(jnp.logical_and(chip + step < chips, chip > 0))
            def _():
                self.left(step, chip + step).wait_send()

            self.across(step, core).wait_send()

        loop(chips, one)


def scatter_scratch(chips, rows):
    buffers = [VMEM((count, CHUNKS, rows, WIDE), BF16) for count in (chips + 1, 2, chips)]
    return buffers + [pltpu.SemaphoreType.DMA((chips, CHUNKS)) for _ in range(6)]


class Scatter:
    def __init__(self, scratch, produce, total, ready=None):
        self.ready = ready
        self.line, self.out, self.other = scratch[:3]
        self.sems = scratch[3:]
        self.produce = produce
        self.total = total
        self.me, self.chip, self.core, self.chips = line_position()


    def right(self, step, chunk):
        ref = self.line.at[step, chunk]
        sems = self.sems
        return send(ref, ref, sems[0].at[step, chunk], sems[1].at[step, chunk], "ctx", self.me + 2)

    def left(self, step, chunk):
        ref = self.line.at[self.chips - step, chunk]
        sems = self.sems
        return send(ref, ref, sems[2].at[step, chunk], sems[3].at[step, chunk], "ctx", self.me - 2)

    def across(self, target, chunk, slot=0):
        sems = self.sems
        return send(
            self.out.at[slot, chunk],
            self.other.at[target, chunk],
            sems[4].at[target, chunk],
            sems[5].at[target, chunk],
            "ctx",
            self.me + 1 - 2 * self.core,
        )

    def begin(self):
        def clear(index):
            slot, chunk = index // CHUNKS, index % CHUNKS
            at_left = jnp.logical_and(self.chip == 0, slot < self.chips)
            at_right = jnp.logical_and(self.chip == self.chips - 1, slot > 0)

            @pl.when(jnp.logical_or(at_left, at_right))
            def _():
                self.line[slot, chunk] = jnp.zeros(self.line.shape[2:], BF16)

        loop((self.chips + 1) * CHUNKS, clear)

    def when_right(self, time):
        return jnp.logical_and(time >= self.chip, time < self.chips - 1)

    def when_left(self, time):
        return jnp.logical_and(time >= self.chips - 1 - self.chip, time < self.chips - 1)

    def prepare(self, time):
        chip, chips = self.chip, self.chips

        def cross(target, slot, before, used):
            if self.ready is not None:
                self.ready(target)

            def one(chunk):
                @pl.when(used)
                def _():
                    self.across(before, chunk, slot).wait_send()

                piece = 2 * target + 1 - self.core
                self.out[slot, chunk] = self.produce(piece, chunk).astype(BF16)
                self.across(target, chunk, slot).start()

            loop(CHUNKS, one)

        @pl.when(self.when_right(time))
        def _():
            target = chips - 1 - time + chip
            cross(target, 0, target + 1, time > chip)

        @pl.when(self.when_left(time))
        def _():
            target = time - (chips - 1 - chip)
            cross(target, 1, target - 1, target > 0)

        @pl.when(time == chips - 1)
        def _():
            cross(chip, 0, chip + 1, chip < chips - 1)

    def step(self, time):
        chip, core, chips = self.chip, self.core, self.chips

        @pl.when(self.when_right(time))
        def _():
            step = time - chip
            target = chips - 1 - step

            def one(chunk):
                self.across(target, chunk).wait_recv()

                @pl.when(chip > 0)
                def _():
                    self.right(step, chunk).wait_recv()

                value = self.produce(2 * target + core, chunk) + self.other[target, chunk].astype(F32)
                value = value + self.line[step, chunk].astype(F32)
                self.line[step, chunk] = value.astype(BF16)
                self.right(step, chunk).start()

            loop(CHUNKS, one)

        @pl.when(self.when_left(time))
        def _():
            step = time - (chips - 1 - chip)

            def one(chunk):
                self.across(step, chunk).wait_recv()

                @pl.when(chip < chips - 1)
                def _():
                    self.left(step, chunk).wait_recv()

                value = self.produce(2 * step + core, chunk) + self.other[step, chunk].astype(F32)
                value = value + self.line[chips - step, chunk].astype(F32)
                self.line[chips - step, chunk] = value.astype(BF16)
                self.left(step, chunk).start()

            loop(CHUNKS, one)

    def finish(self):
        chip, core, chips = self.chip, self.core, self.chips
        last = chips - 1 - chip

        def one(chunk):
            self.across(chip, chunk).wait_recv()
            value = self.produce(2 * chip + core, chunk) + self.other[chip, chunk].astype(F32)

            @pl.when(chip > 0)
            def _():
                self.right(last, chunk).wait_recv()

            @pl.when(chip < chips - 1)
            def _():
                self.left(chip, chunk).wait_recv()

            value = value + self.line[last, chunk].astype(F32)
            value = value + self.line[chips - chip, chunk].astype(F32)
            self.total[:, pl.ds(pl.multiple_of(chunk * WIDE, WIDE), WIDE)] = value

        loop(CHUNKS, one)

        def drain(index):
            step, chunk = index // CHUNKS, index % CHUNKS

            @pl.when(step < last)
            def _():
                self.right(step, chunk).wait_send()

            @pl.when(step < chip)
            def _():
                self.left(step, chunk).wait_send()

            @pl.when(jnp.logical_or(step == chip, step == chip - 1))
            def _():
                self.across(step, chunk, jnp.where(step == chip, 0, 1)).wait_send()

        loop(chips * CHUNKS, drain)


def tile(index, size):
    return pl.ds(pl.multiple_of(index * size, size), size)


def row_blocks(rows, body, size=32):
    def one(index):
        body(pl.ds(pl.multiple_of(index * size, size), size))

    loop(rows // size, one)


def inverse_norm(value):
    return lax.rsqrt(jnp.mean(value * value, axis=-1, keepdims=True) + EPS)


def params(identity, megabytes):
    return pltpu.CompilerParams(
        collective_id=identity,
        has_side_effects=True,
        vmem_limit_bytes=megabytes * 1024 * 1024,
    )


def cost(microseconds):
    return pl.CostEstimate(
        flops=int(microseconds * 1.15e9), bytes_accessed=1024, transcendentals=0
    )


class FsdpSum:
    def __init__(self, grad, arrived, send_sems, recv_sems, own=None, part=slice(None)):
        self.grad, self.arrived, self.part = grad, arrived, part
        self.own = grad.at[lax.axis_index("fsdp")] if own is None else own
        self.sems = send_sems, recv_sems
        self.peers, self.ahead, _ = peers_of("fsdp")

    def copy(self, i):
        target = self.ahead(i)
        return send(
            self.grad.at[target, self.part], self.arrived.at[i], self.sems[0].at[i], self.sems[1].at[i], "fsdp", target
        )

    def start(self):
        loop(self.peers, lambda i: self.copy(i).start())

    def arrive(self):
        loop(self.peers, lambda i: self.copy(i).wait_recv())

    def collect(self, target):
        self.arrive()
        self.add(target)

    def add(self, target):
        def one(block):
            value = self.own[block, :].astype(F32)
            for i in range(self.peers):
                value = value + self.arrived[i, block].astype(F32)
            target[block, :] = value.astype(BF16)

        row_blocks(self.own.shape[0], one)

    def finish(self):
        loop(self.peers, lambda i: self.copy(i).wait_send())


def fsdp_scratch(shards, rows, width):
    return [VMEM((shards - 1, rows, width), BF16)] + [pltpu.SemaphoreType.DMA((shards,))] * 2


def sine_cosine(angle):
    count = jnp.floor(angle * 0.6366197723675814 + 0.5)
    rest = angle - count * 1.5703125
    rest = rest - count * 4.837512969970703e-4
    rest = rest - count * 7.549789948768648e-8
    square = rest * rest
    sine = -1.9515295891e-4 * square + 8.3321608736e-3
    sine = rest + rest * square * (sine * square - 1.6666654611e-1)
    cosine = 2.443315711809948e-5 * square - 1.388731625493765e-3
    cosine = 1.0 - 0.5 * square + square * square * (cosine * square + 4.166664568298827e-2)
    quarter = jnp.bitwise_and(count.astype(jnp.int32), 3)
    odd = jnp.bitwise_and(quarter, 1) == 1
    sine, cosine = jnp.where(odd, cosine, sine), jnp.where(odd, sine, cosine)
    sine = jnp.where(quarter >= 2, -sine, sine)
    cosine = jnp.where(jnp.logical_or(quarter == 1, quarter == 2), -cosine, cosine)
    return sine, cosine


class Shares:
    def __init__(self, source, target_of, own_sem, sems):
        self.source, self.target_of = source, target_of
        self.own_sem, self.sems = own_sem, sems
        self.peers, self.ahead, self.behind = peers_of("fsdp")
        self.shard = lax.axis_index("fsdp")

    def copy(self, i, owner):
        sems = self.sems
        target = self.target_of(owner)
        return send(self.source, target, sems[0].at[i], sems[1].at[i], "fsdp", self.ahead(i))

    def own(self):
        return pltpu.make_async_copy(self.source, self.target_of(self.shard), self.own_sem)

    def start(self):
        loop(self.peers, lambda i: self.copy(i, self.shard).start())
        self.own().start()

    def arrive(self):
        self.own().wait()
        loop(self.peers, lambda i: self.copy(i, self.behind(i)).wait_recv())

    def finish(self):
        loop(self.peers, lambda i: self.copy(i, self.shard).wait_send())


def shares_scratch(count, shards):
    return [pltpu.SemaphoreType.DMA((count,))] + [pltpu.SemaphoreType.DMA((shards,))] * (2 * count)


def copy_in(source, target, sem):
    copy = pltpu.make_async_copy(source, target, sem)
    copy.start()
    return copy


QUERY_TILE = 256
KEY_TILE = 512


def reach(index, tokens):
    return jnp.minimum((index + 2) * QUERY_TILE + KEY_TILE - 1, tokens) // KEY_TILE


def head_norm(value, gain, cosine, sine):
    normed = value * inverse_norm(value) * gain
    return normed * cosine + pltpu.roll(normed, HEAD_SIZE // 2, 1) * sine


def forward_kernel(heads, *refs):
    x, grad, gains, token_info, freq = refs[:5]
    sources, refs = refs[5:12], refs[12:]
    normed_land, grad_land, two_land, activation, back = refs[:5]
    proj, cosine, sine, queries, keys, values, context, inverse = refs[5:13]
    middle, gain_rows, all_gains, all_tokens = refs[13:17]
    head_weight, out_weight, pair_weight, down_weight = refs[17:21]
    refs = refs[21:]
    pair, down, own, piece_in, grad_in, act_out, back_out, total, sems = refs[:9]
    small, refs = refs[9:13], refs[13:]
    share_own, share_sems, refs = refs[0], refs[1:15], refs[15:]
    first_sems, grad_sems, two_sems, scratch = refs[:6], refs[6:12], refs[12:18], refs[18:]
    me, _, _, chips = line_position()
    shard = lax.axis_index("fsdp")
    shards, ahead, behind = peers_of("fsdp")
    parts, next_part, past_part = peers_of("ctx")
    count = x.shape[0]
    tokens = 2 * chips * count
    width = heads * HEAD_SIZE
    feed_width = down.shape[0]
    rows = D // (shards + 1)
    lanes = rows // 128
    key_head = me // (2 * chips // KEY_VALUE_HEADS)

    def gain_copy(i, slot):
        return send(gains, all_gains.at[slot], small[0].at[i], small[1].at[i], "fsdp", ahead(i))

    def token_copy(i, slot):
        return send(token_info, all_tokens.at[slot], small[2].at[i], small[3].at[i], "ctx", next_part(i))

    def by_row(target, at, size):
        return lambda owner: target.at[tile(owner, rows), pl.ds(at, size)]

    def by_column(target):
        return lambda owner: target.at[:, tile(owner, rows)]

    places = (
        (sources[0].at[:, tile(me, width)], by_row(head_weight, 0, width)),
        (sources[1].at[:, tile(key_head, HEAD_SIZE)], by_row(head_weight, width, HEAD_SIZE)),
        (sources[2].at[:, tile(key_head, HEAD_SIZE)], by_row(head_weight, width + HEAD_SIZE, HEAD_SIZE)),
        (sources[3].at[tile(me, width), :], by_column(out_weight)),
        (sources[4].at[:, tile(me, feed_width)], by_row(pair, 0, feed_width)),
        (sources[5].at[:, tile(me, feed_width)], by_row(pair, feed_width, feed_width)),
        (sources[6].at[tile(me, feed_width), :], by_column(down)),
    )
    shares = [
        Shares(source, target_of, share_own.at[i], share_sems[2 * i : 2 * i + 2])
        for i, (source, target_of) in enumerate(places)
    ]

    full_barrier()
    loop(shards, lambda i: gain_copy(i, shard).start())
    loop(parts, lambda i: token_copy(i, me).start())
    for share in shares[:4]:
        share.start()
    grad_copy = copy_in(grad, grad_land.at[me], sems.at[0])
    all_gains[shard] = gains[...]
    all_tokens[me] = token_info[...]
    loop(shards, lambda i: gain_copy(i, behind(i)).wait_recv())
    for kind in range(2):
        for owner in range(shards + 1):
            for j in range(lanes):
                at = owner * rows + j * 128
                gain_rows[kind : kind + 1, at : at + 128] = all_gains[
                    owner, kind * lanes + j : kind * lanes + j + 1, :
                ]
    size = HEAD_SIZE // (shards + 1)
    for kind in range(2):
        gain_rows[2 + kind : 3 + kind, 0:HEAD_SIZE] = jnp.concatenate(
            [
                all_gains[
                    owner, 2 * lanes : 2 * lanes + 1, kind * size : (kind + 1) * size
                ]
                for owner in range(shards + 1)
            ],
            axis=1,
        )

    def norm(block):
        value = x[block, :].astype(F32)
        own[block, :] = (value * inverse_norm(value) * gain_rows[0:1, :]).astype(BF16)

    row_blocks(count, norm)
    own_copy = copy_in(own, normed_land.at[me], sems.at[1])
    own_copy.wait()

    def column(piece, row):
        values_in_lanes = all_tokens[piece, row : row + 1, :].astype(F32)
        return jnp.broadcast_to(values_in_lanes, (128, count)).T

    def project(piece):
        copy = copy_in(normed_land.at[piece], piece_in, sems.at[1])
        block = tile(piece, count)
        s, c = sine_cosine(column(piece, 0) * freq[0:1, :])
        lane = lax.broadcasted_iota(jnp.int32, s.shape, 1)
        s = jnp.where(lane < HEAD_SIZE // 2, -s, s)
        cosine[block, :] = c
        sine[block, :] = s
        copy.wait()
        proj[piece] = dot(piece_in[...], head_weight[...])

        def turned(at, row):
            return head_norm(proj[piece, :, at : at + HEAD_SIZE], gain_rows[row : row + 1, 0:HEAD_SIZE], c, s)

        for h in range(heads):
            at = h * HEAD_SIZE
            queries[block, at : at + HEAD_SIZE] = (turned(at, 2) * HEAD_SIZE ** (-0.5)).astype(BF16)
        keys[block, :] = turned(width, 3).astype(BF16)
        values[block, :] = proj[piece, :, width + HEAD_SIZE : width + 2 * HEAD_SIZE].astype(BF16)

    first_gather = Gather(normed_land, first_sems, project)
    grad_gather = Gather(grad_land, grad_sems)
    first_gather.move(0)
    loop(parts, lambda i: token_copy(i, past_part(i)).wait_recv())

    def first_step(step):
        first_gather.move(step + 1)

        @pl.when(step == 0)
        def _():
            for share in shares[:4]:
                share.arrive()
            for share in shares[4:]:
                share.start()

        first_gather.use(step)

    loop(chips - 1, first_step)
    grad_copy.wait()
    grad_gather.step(0)
    first_gather.use(chips - 1)

    def attend(index):
        block = tile(index, QUERY_TILE)
        query_ids = column(index, 1)[:, 0:1]
        each = KEY_TILE // count
        lanes_of = [slice(h * HEAD_SIZE, (h + 1) * HEAD_SIZE) for h in range(heads)]

        def one(key_tile, carry):
            span = tile(key_tile, KEY_TILE)
            key, value = keys[span, :], values[span, :]
            key_ids = jnp.concatenate(
                [all_tokens[key_tile * each + j, 1:2, :] for j in range(each)], axis=1
            ).astype(F32)
            allowed = key_ids <= query_ids
            result = []
            for head, (sums, total) in zip(lanes_of, carry):
                expon = jnp.where(allowed, jnp.exp(rdot(queries[block, head], key)), 0.0)
                sums = sums + dot(expon.astype(BF16), value)
                result.append((sums, total + jnp.sum(expon, axis=1, keepdims=True)))
            return tuple(result)

        start = (jnp.zeros((QUERY_TILE, HEAD_SIZE), F32), jnp.zeros((QUERY_TILE, 1), F32))
        results = lax.fori_loop(0, reach(index, tokens), one, (start,) * heads)
        for h, (head, (sums, total)) in enumerate(zip(lanes_of, results)):
            scale = 1.0 / total
            context[block, head] = (sums * scale).astype(BF16)
            inverse[h : h + 1, block] = jnp.broadcast_to(scale, (QUERY_TILE, HEAD_SIZE)).T[0:1, :]

    def ready(target):
        each = 2 * count // QUERY_TILE
        loop(each, lambda i: attend(target * each + i))

    def produce(piece, chunk):
        return dot(context[tile(piece, count), :], out_weight[:, tile(chunk, WIDE)])

    scatter = Scatter(scratch, produce, total, ready)
    scatter.begin()
    scatter.prepare(0)

    def scatter_step(time):
        scatter.step(time)
        scatter.prepare(time + 1)
        grad_gather.step(time + 1)

    loop(chips - 1, scatter_step)
    scatter.finish()

    def norm_two(block):
        value = x[block, :].astype(F32) + total[block, :]
        middle[block, :] = value
        own[block, :] = (value * inverse_norm(value) * gain_rows[1:2, :]).astype(BF16)

    row_blocks(count, norm_two)
    two_copy = copy_in(own, two_land.at[me], sems.at[1])
    two_copy.wait()
    for share in shares[4:]:
        share.arrive()
    outs = [
        copy_in(head_weight, refs_out, sems.at[2 + i])
        for i, (head_weight, refs_out) in enumerate(((pair, pair_weight), (down, down_weight)))
    ]
    feed_size = 256 if feed_width % 256 == 0 else 128

    def act_copy(piece):
        return pltpu.make_async_copy(act_out, activation.at[piece], sems.at[6])

    def back_copy(piece):
        return pltpu.make_async_copy(back_out, back.at[piece], sems.at[7])

    def feed(piece):
        copies = (
            copy_in(two_land.at[piece], piece_in, sems.at[4]),
            copy_in(grad_land.at[piece], grad_in, sems.at[5]),
        )
        for copy in copies:
            copy.wait()

        @pl.when(piece != me)
        def _():
            act_copy(piece).wait()
            back_copy(piece).wait()

        def one(index):
            def columns(kind):
                return pl.ds(pl.multiple_of(kind * feed_width + index * feed_size, 128), feed_size)

            gate = dot(piece_in[...], pair[:, columns(0)])
            up = dot(piece_in[...], pair[:, columns(1)])
            grad_act = rdot(grad_in[...], down[tile(index, feed_size), :])
            sigma = 1.0 / (1.0 + jnp.exp(-gate))
            act_out[:, columns(0)] = (gate * sigma * up).astype(BF16)
            back_out[:, columns(0)] = (
                grad_act * up * sigma * (1.0 + gate * (1.0 - sigma))
            ).astype(BF16)
            back_out[:, columns(1)] = (grad_act * gate * sigma).astype(BF16)

        loop(feed_width // feed_size, one)
        act_copy(piece).start()
        back_copy(piece).start()

    two_gather = Gather(two_land, two_sems, feed)
    loop(chips, two_gather.step)
    act_copy(0).wait()
    back_copy(0).wait()
    first_gather.finish()
    grad_gather.finish()
    two_gather.finish()
    for out in outs:
        out.wait()
    for share in shares:
        share.finish()
    loop(shards, lambda i: gain_copy(i, shard).wait_send())
    loop(parts, lambda i: token_copy(i, me).wait_send())


def forward(hidden, grad, gains, token_info, freq, weights, shards, parts, heads):
    count = hidden.shape[0]
    tokens = parts * count
    width = heads * HEAD_SIZE
    total_width = width + 2 * HEAD_SIZE
    feed_width = FF // parts
    chips = parts // 2
    shape = jax.ShapeDtypeStruct
    return pl.pallas_call(
        functools.partial(forward_kernel, heads),
        out_shape=(
            shape((parts, count, D), BF16),
            shape((parts, count, D), BF16),
            shape((parts, count, D), BF16),
            shape((parts, count, feed_width), BF16),
            shape((parts, count, 2 * feed_width), BF16),
            shape((parts, count, total_width), F32),
            shape((tokens, HEAD_SIZE), F32),
            shape((tokens, HEAD_SIZE), F32),
            shape((tokens, width), BF16),
            shape((tokens, HEAD_SIZE), BF16),
            shape((tokens, HEAD_SIZE), BF16),
            shape((tokens, width), BF16),
            shape((8, tokens), F32),
            shape((count, D), F32),
            shape((8, D), F32),
            shape((shards, *gains.shape), F32),
            shape((parts, *token_info.shape), jnp.int32),
            shape((D, total_width), BF16),
            shape((width, D), BF16),
            shape((D, 2 * feed_width), BF16),
            shape((feed_width, D), BF16),
        ),
        in_specs=[WHOLE] * 5 + [HBM] * 7,
        out_specs=(HBM,) * 5 + (WHOLE,) * 14 + (HBM,) * 2,
        scratch_shapes=[
            VMEM((D, 2 * feed_width), BF16),
            VMEM((feed_width, D), BF16),
            VMEM((count, D), BF16),
            VMEM((count, D), BF16),
            VMEM((count, D), BF16),
            VMEM((count, feed_width), BF16),
            VMEM((count, 2 * feed_width), BF16),
            VMEM((count, D), F32),
            pltpu.SemaphoreType.DMA((8,)),
        ]
        + [pltpu.SemaphoreType.DMA((shards,))] * 2
        + [pltpu.SemaphoreType.DMA((parts,))] * 2
        + shares_scratch(7, shards)
        + gather_scratch(chips)
        + gather_scratch(chips)
        + gather_scratch(chips)
        + scatter_scratch(chips, count),
        compiler_params=params(0, 63),
        cost_estimate=cost(280),
        name="forward",
    )(hidden, grad, gains, token_info, freq, *weights)


def slab_size(parts):
    return 256 if parts <= 8 else 128


class Slabs:
    def __init__(self, sources, buffers, out, target, sems, products, place=lambda index: index):
        self.place = place
        self.sources, self.buffers, self.out, self.target = sources, buffers, out, target
        self.sems, self.products = sems, products
        self.size = out.shape[0]
        self.count = D // self.size

    def copies(self, index):
        slot = index % 2
        return [
            pltpu.make_async_copy(
                source.at[:, :, tile(self.place(index), self.size)], buffer.at[slot], self.sems.at[2 * i + slot]
            )
            for i, (source, buffer) in enumerate(zip(self.sources, self.buffers))
        ]

    def fetch(self, index):
        for copy in self.copies(index):
            copy.start()

    def leave(self, index):
        each = self.target.shape[1] // self.size
        place = self.place(index)
        target = self.target.at[place // each, tile(place % each, self.size), :]
        return pltpu.make_async_copy(self.out, target, self.sems.at[2 * len(self.sources)])

    def run(self, begin, end):
        def one(index, carry):
            for copy in self.copies(index):
                copy.wait()

            @pl.when(index + 1 < self.count)
            def _():
                self.fetch(index + 1)

            @pl.when(index > begin)
            def _():
                self.leave(index - 1).wait()

            at = 0
            for left, right in self.products(index % 2):
                left = left.reshape(-1, self.size)
                right = right.reshape(left.shape[0], -1)
                width = right.shape[1]
                self.out[:, at : at + width] = tdot(left, right).astype(BF16)
                at += width
            self.leave(index).start()
            return carry

        lax.fori_loop(begin, end, one, 0)

    def settle(self, index):
        self.leave(index - 1).wait()


def halves_first(half, size):
    inner = half // size
    per_half = D // size // 2

    def place(index):
        side, rest = index // per_half, index % per_half
        return (rest // inner) * 2 * inner + side * inner + rest % inner

    return place


def rms_back(value, gain, grad):
    inverse = inverse_norm(value)
    scaled = grad * gain
    inner = jnp.mean(scaled * value, axis=-1, keepdims=True)
    terms = grad * value * inverse
    return inverse * scaled - value * (inverse * inverse * inverse * inner), terms


def turn_kernel(*refs):
    back, pair_weight, down_weight, activation, out_weight = refs[:5]
    middle, gain_rows, grads, normed = refs[5:9]
    grad_middle, land, gain_sum, down_land, context_grad, hidden = refs[9:15]
    pair_in, pair_grad, pair_sum, down_grad, refs = *refs[15:19], refs[19:]
    weight, data, act, mid, total, low, own_down, sems = refs[:8]
    slab, slab_out, down_out, slab_sems, sum_sems, refs = *refs[8:13], refs[13:]
    down_refs, down_sems, refs = (refs[:3], refs[3:6]), (refs[6:12], refs[12:18]), refs[18:]
    gather_sems, pair_sems, refs = (refs[:6], refs[6:12]), refs[12:14], refs[14:]
    first_scratch, second_scratch = refs[:9], refs[9:]
    me, _, _, chips = line_position()
    width = back.shape[2] // 2
    weight_copy = copy_in(pair_weight, weight, sems.at[0])
    data_copy = copy_in(back, data, sems.at[1])
    act_copy = copy_in(activation, act, sems.at[3])
    mid_copy = copy_in(middle, mid, sems.at[2])
    low_copy = copy_in(grads.at[me], low, sems.at[4])

    def produce(piece, chunk):
        return rdot(data[piece], weight[pl.ds(pl.multiple_of(chunk * WIDE, WIDE), WIDE), :])

    each = 2 * width // WIDE

    def down_block(chunk):
        return tile(chunk // each, width), tile(chunk % each, WIDE)

    def down_copy(chunk):
        source = down_weight.at[:, tile(chunk, WIDE)]
        return pltpu.make_async_copy(source, weight.at[down_block(chunk)], sems.at[5 + chunk])

    def produce_hidden(piece, chunk):
        return dot(act[piece], weight[down_block(chunk)])

    side = low.shape[0] // 2

    def consume_of(part):
        def consume(piece):
            copy = copy_in(land.at[piece, part], low.at[part], sems.at[4])
            copy.wait()
            context_grad[piece, part] = rdot(low[part, :], out_weight[...]).astype(BF16)

        return consume

    sides = [pl.ds(h * side, side) for h in range(2)]
    gathers = [
        Gather(land, gather_sems[h], consume_of(sides[h]), part=sides[h]) for h in range(2)
    ]

    def products(slot):
        return ((slab[slot], data[...]),)

    def down_products(slot):
        return ((slab[slot], act[...]),)

    slabs = Slabs((normed,), (slab,), slab_out, pair_grad, slab_sems, products)
    half = own_down.shape[0] // 2
    halves = [pl.ds(h * half, half) for h in range(2)]
    order = halves_first(half, down_out.shape[0])
    down_slabs = Slabs((grads,), (slab,), down_out, down_grad, slab_sems, down_products, order)
    downs = [
        FsdpSum(down_grad, *down_refs[h], own=own_down.at[halves[h]], part=halves[h]) for h in range(2)
    ]
    down_gathers = [Gather(down_land, down_sems[h], part=halves[h]) for h in range(2)]

    def down_ready(h):
        downs[h].collect(own_down.at[halves[h]])
        copy = copy_in(own_down.at[halves[h]], down_land.at[me, halves[h]], sems.at[3])
        copy.wait()
        down_gathers[h].step(0)

    pair = FsdpSum(pair_grad, pair_in, *pair_sems, own=own_down)
    scatter = Scatter(first_scratch, produce, total)
    hidden_scatter = Scatter(second_scratch, produce_hidden, total)
    scatter.begin()
    hidden_scatter.begin()
    full_barrier()
    down_slabs.fetch(0)
    weight_copy.wait()
    data_copy.wait()
    scatter.prepare(0)

    def step(time):
        scatter.step(time)
        scatter.prepare(time + 1)

        @pl.when(time == 0)
        def _():
            act_copy.wait()
            for h in range(2):
                begin, end = h * down_slabs.count // 2, (h + 1) * down_slabs.count // 2
                down_slabs.run(begin, end)
                down_slabs.settle(end)
                downs[h].start()
            slabs.fetch(0)
            own_copy = copy_in(down_grad.at[lax.axis_index("fsdp")], own_down, sems.at[3])
            own_copy.wait()

        @pl.when(time == 1)
        def _():
            down_ready(0)

        @pl.when(time >= 2)
        def _():
            down_gathers[0].step(time - 1)

        @pl.when(time == 2)
        def _():
            down_ready(1)

        @pl.when(time >= 3)
        def _():
            down_gathers[1].step(time - 2)

        @pl.when(jnp.logical_or(time == 1, time == 2))
        def _():
            slabs.run((time - 1) * slabs.count // 2, time * slabs.count // 2)
            slabs.settle(time * slabs.count // 2)

        @pl.when(time == 2)
        def _():
            pair.start()

    loop(chips - 1, step)
    scatter.finish()
    down_gathers[0].step(chips - 2)
    down_gathers[1].step(chips - 3)
    for chunk in range(CHUNKS):
        down_copy(chunk).start()
    mid_copy.wait()
    low_copy.wait()
    gain_sum[...] = jnp.zeros_like(gain_sum)

    def norm(block):
        through, terms = rms_back(mid[block, :], gain_rows[1:2, :], total[block, :])
        value = low[block, :].astype(F32) + through
        mid[block, :] = value
        low[block, :] = value.astype(BF16)
        gain_sum[0:1, :] += jnp.sum(terms, axis=0, keepdims=True)

    row_blocks(mid.shape[0], norm)
    mid_out = copy_in(mid, grad_middle, sems.at[2])
    low_copy = copy_in(low, land.at[me], sems.at[3])
    low_copy.wait()
    for gather in gathers:
        gather.step(0)
    for chunk in range(CHUNKS):
        down_copy(chunk).wait()
    hidden_scatter.prepare(0)
    mid_out.wait()
    mid_copy = copy_in(middle, mid, sems.at[2])

    def add_pairs():
        pair.arrive()
        shard = lax.axis_index("fsdp")
        count, size = slab.shape[2], slab.shape[3]
        per = own_down.shape[0] // count
        tiles = 2 * width // size

        def arrivals(index):
            slot = index % 2
            copies = []
            for i in range(pair.peers + 1):
                source = pair_grad.at[shard] if i == 0 else pair_in.at[i - 1]
                for j in range(per):
                    at = i * per + j
                    block = source.at[pl.ds(j * count, count), tile(index, size)]
                    copies.append(
                        pltpu.make_async_copy(block, slab.at[slot, at], sum_sems.at[slot, at])
                    )
            return copies

        def leave(index):
            slot = index % 2
            return [
                pltpu.make_async_copy(
                    slab.at[slot, j],
                    pair_sum.at[pl.ds(j * count, count), tile(index, size)],
                    sum_sems.at[slot, j],
                )
                for j in range(per)
            ]

        for copy in arrivals(0):
            copy.start()

        def one(index):
            @pl.when(index > 0)
            def _():
                for copy in leave(index - 1):
                    copy.wait()

            @pl.when(index + 1 < tiles)
            def _():
                for copy in arrivals(index + 1):
                    copy.start()

            for copy in arrivals(index):
                copy.wait()
            slot = index % 2
            for j in range(per):
                value = slab[slot, j].astype(F32)
                for i in range(1, pair.peers + 1):
                    value = value + slab[slot, i * per + j].astype(F32)
                slab[slot, j] = value.astype(BF16)
            for copy in leave(index):
                copy.start()

        loop(tiles, one)
        for copy in leave(tiles - 1):
            copy.wait()

    def turn_step(time):
        gathers[0].step(time + 1)
        hidden_scatter.step(time)
        hidden_scatter.prepare(time + 1)

        @pl.when(time == chips - 2)
        def _():
            add_pairs()

        gathers[1].step(time + 1)

        @pl.when(time == 0)
        def _():
            down_gathers[0].step(chips - 1)
            down_gathers[1].step(chips - 2)

        @pl.when(time == 1)
        def _():
            down_gathers[1].step(chips - 1)

    loop(chips - 1, turn_step)
    hidden_scatter.finish()
    for h in range(2):
        gathers[h].finish()
        down_gathers[h].finish()
        downs[h].finish()
    pair.finish()
    mid_copy.wait()

    def add(block):
        hidden[block, :] = (mid[block, :] + total[block, :]).astype(BF16)

    row_blocks(mid.shape[0], add)


def turn(back, pair_weight, down_weight, activation, out_weight, middle, gain_rows, grads, normed, shards):
    parts, count, feed_width = activation.shape
    rows = D // shards
    width = out_weight.shape[0]
    return pl.pallas_call(
        turn_kernel,
        out_shape=(
            jax.ShapeDtypeStruct((count, D), F32),
            jax.ShapeDtypeStruct((parts, count, D), BF16),
            jax.ShapeDtypeStruct((8, D), F32),
            jax.ShapeDtypeStruct((parts, rows, feed_width), BF16),
            jax.ShapeDtypeStruct((parts, count, width), BF16),
            jax.ShapeDtypeStruct((count, D), BF16),
            jax.ShapeDtypeStruct((shards - 1, rows, 2 * feed_width), BF16),
            jax.ShapeDtypeStruct((shards, rows, 2 * feed_width), BF16),
            jax.ShapeDtypeStruct((rows, 2 * feed_width), BF16),
            jax.ShapeDtypeStruct((shards, rows, feed_width), BF16),
        ),
        in_specs=[HBM] * 4 + [WHOLE, HBM, WHOLE] + [HBM] * 2,
        out_specs=(HBM, HBM, WHOLE, HBM, WHOLE, WHOLE) + (HBM,) * 4,
        scratch_shapes=[
            VMEM((D, 2 * feed_width), BF16),
            VMEM((parts, count, 2 * feed_width), BF16),
            VMEM((parts, count, feed_width), BF16),
            VMEM((count, D), F32),
            VMEM((count, D), F32),
            VMEM((count, D), BF16),
            VMEM((rows, feed_width), BF16),
            pltpu.SemaphoreType.DMA((5 + CHUNKS,)),
            VMEM((2, parts, count, slab_size(parts)), BF16),
            VMEM((slab_size(parts), 2 * feed_width), BF16),
            VMEM((slab_size(parts), feed_width), BF16),
            pltpu.SemaphoreType.DMA((3,)),
            pltpu.SemaphoreType.DMA((2, parts)),
        ]
        + fsdp_scratch(shards, rows // 2, feed_width)
        + fsdp_scratch(shards, rows // 2, feed_width)
        + gather_scratch(parts // 2)
        + gather_scratch(parts // 2)
        + gather_scratch(parts // 2)
        + gather_scratch(parts // 2)
        + [pltpu.SemaphoreType.DMA((shards,))] * 2
        + scatter_scratch(parts // 2, count)
        + scatter_scratch(parts // 2, count),
        compiler_params=params(3, 63),
        cost_estimate=cost(185),
        name="turn",
    )(
        back,
        pair_weight,
        down_weight,
        activation,
        out_weight,
        middle,
        gain_rows,
        grads,
        normed,
    )


PAIR_PARTS = 4


def last_kernel(heads, *refs):
    queries, keys, values, out_grad, inverse, context, proj, cosine, sine, token_info = refs[:10]
    weights, x, grad_middle, gain_rows, gain_two, normed, low, pair_sum = refs[10:18]
    hidden, gain_out, head_grad, land, pair_land = refs[18:23]
    back, gain_heads, key_grad, value_grad, query_grad, pair_own, pair_sem = refs[23:30]
    pair_sems, refs = refs[30:36], refs[36:]
    weight, weight_sem, total, gain_one, pack, pack_in, shard_sum, shard_in = refs[:8]
    slabs_in, slab_out, slab_sems, own_head, refs = refs[8:10], refs[10], refs[11], refs[12], refs[13:]
    small, head_refs, refs = refs[:4], (refs[4:7], refs[7:10]), refs[10:]
    gather_sems, scratch = (refs[:6], refs[6:12]), refs[12:]
    me, _, _, chips = line_position()
    shard = lax.axis_index("fsdp")
    shards, ahead, _ = peers_of("fsdp")
    parts, next_part, _ = peers_of("ctx")
    tokens = queries.shape[0]
    key_at = heads * HEAD_SIZE
    copy = copy_in(weights, weight, weight_sem)
    pair_copy = copy_in(pair_sum, pair_own, pair_sem)
    pair_size = pair_own.shape[0] // PAIR_PARTS

    def pump(begin, end):
        def one(index, carry):
            part = index % PAIR_PARTS
            sems = [ref.at[part] for ref in pair_sems]
            Gather(pair_land, sems, part=tile(part, pair_size)).step(index // PAIR_PARTS)
            return carry

        lax.fori_loop(begin, end, one, 0)

    def produce(piece, chunk):
        return rdot(back[piece], weight[pl.ds(pl.multiple_of(chunk * WIDE, WIDE), WIDE), :])

    def products(slot):
        return (slabs_in[0][slot], back[...]), (slabs_in[1][slot], context[...])

    half = own_head.shape[0] // 2
    halves = [pl.ds(h * half, half) for h in range(2)]
    per_half = D // slab_out.shape[0] // 2
    place = halves_first(half, slab_out.shape[0])
    slabs = Slabs((normed, low), slabs_in, slab_out, head_grad, slab_sems, products, place)
    head_sums = [
        FsdpSum(head_grad, *head_refs[h], own=own_head.at[halves[h]], part=halves[h]) for h in range(2)
    ]
    gathers = [Gather(land, gather_sems[h], part=halves[h]) for h in range(2)]

    def head_ready(h):
        head_sums[h].collect(land.at[me, halves[h]])
        gathers[h].step(0)
    scatter = Scatter(scratch, produce, total)
    scatter.begin()
    slabs.fetch(0)
    full_barrier()
    pair_copy.wait()
    pair_copy = copy_in(pair_own, pair_land.at[me], pair_sem)
    pair_copy.wait()
    pump(0, PAIR_PARTS)
    key_grad[...] = jnp.zeros_like(key_grad)
    value_grad[...] = jnp.zeros_like(value_grad)
    gain_heads[...] = jnp.zeros_like(gain_heads)

    def through(index, lanes, grad, row):
        block = tile(index, QUERY_TILE)
        turned = pltpu.roll(grad, HEAD_SIZE // 2, 1)
        unrotated = grad * cosine[block, :] - turned * sine[block, :]
        result, terms = rms_back(proj[index, :, lanes], gain_rows[row + 2 : row + 3, :HEAD_SIZE], unrotated)
        back[index, :, lanes] = result.astype(BF16)
        gain_heads[row : row + 1, :] += jnp.sum(terms, axis=0, keepdims=True)

    count = token_info.shape[2]
    each = KEY_TILE // count

    def attend(index):
        block = tile(index, QUERY_TILE)
        query_ids = token_info[index, 1:2, :].astype(F32)
        shifts = []
        for h in range(heads):
            lanes = slice(h * HEAD_SIZE, (h + 1) * HEAD_SIZE)
            products = out_grad[index, :, lanes].astype(F32) * context[index, :, lanes].astype(F32)
            shift = lax.dot_general(
                jnp.ones((8, HEAD_SIZE), F32),
                products,
                (((1,), (1,)), ((), ())),
                precision=lax.Precision.HIGHEST,
                preferred_element_type=F32,
            )[0:1, :]
            shifts.append(shift)
        query_grad[...] = jnp.zeros_like(query_grad)

        def one(key_tile):
            span = tile(key_tile, KEY_TILE)
            key, value = keys[span, :], values[span, :]
            key_ids = jnp.concatenate(
                [
                    jnp.broadcast_to(
                        token_info[key_tile * each + j, 1:2, :].astype(F32), (128, count)
                    ).T[:, 0:1]
                    for j in range(each)
                ],
                axis=0,
            )
            allowed = key_ids <= query_ids
            for h in range(heads):
                lanes = slice(h * HEAD_SIZE, (h + 1) * HEAD_SIZE)
                query, grad = queries[block, lanes], out_grad[index, :, lanes]
                expon = jnp.exp(rdot(key, query)) * inverse[h : h + 1, block]
                probs = jnp.where(allowed, expon, 0.0)
                grad_scores = (probs * (rdot(value, grad) - shifts[h])).astype(BF16)
                value_grad[span, :] += dot(probs.astype(BF16), grad)
                key_grad[span, :] += dot(grad_scores, query)
                query_grad[:, lanes] += tdot(grad_scores, key)

        loop(reach(index, tokens), one)
        for h in range(heads):
            lanes = slice(h * HEAD_SIZE, (h + 1) * HEAD_SIZE)
            through(index, lanes, query_grad[:, lanes] * HEAD_SIZE ** (-0.5), 0)

    def finish_keys(index):
        block = tile(index, QUERY_TILE)
        through(index, slice(key_at, key_at + HEAD_SIZE), key_grad[block, :], 1)
        back[index, :, key_at + HEAD_SIZE :] = value_grad[block, :].astype(BF16)

    tiles = tokens // QUERY_TILE
    marks = (0, 3 * tiles // 8, 5 * tiles // 8, 6 * tiles // 8, tiles)
    for i in range(4):
        loop(marks[i + 1] - marks[i], lambda index, i=i: attend(marks[i] + index))
        pump(PAIR_PARTS + i, PAIR_PARTS + i + 1)
    loop(tiles, finish_keys)
    copy.wait()
    scatter.prepare(0)
    for h in range(2):
        slabs.run(h * per_half, (h + 1) * per_half)
        slabs.settle((h + 1) * per_half)
        head_sums[h].start()
        pump(2 * PAIR_PARTS + h, 2 * PAIR_PARTS + h + 1)
    own = copy_in(head_grad.at[shard], own_head, weight_sem)
    own.wait()

    def step(time):
        scatter.step(time)
        scatter.prepare(time + 1)
        begin = 2 * PAIR_PARTS + 2
        span = PAIR_PARTS * (chips - 3)
        pump(begin + time * span // (chips - 1), begin + (time + 1) * span // (chips - 1))

        @pl.when(time == 0)
        def _():
            head_ready(0)

        @pl.when(time >= 1)
        def _():
            gathers[0].step(time)

        @pl.when(time == 1)
        def _():
            head_ready(1)

        @pl.when(time >= 2)
        def _():
            gathers[1].step(time - 1)

    loop(chips - 1, step)
    scatter.finish()
    gathers[0].step(chips - 1)
    gathers[1].step(chips - 2)
    gain_one[...] = jnp.zeros_like(gain_one)

    def norm(block):
        through, terms = rms_back(x[block, :].astype(F32), gain_rows[0:1, :], total[block, :])
        hidden[block, :] = grad_middle[block, :] + through
        gain_one[0:1, :] += jnp.sum(terms, axis=0, keepdims=True)

    row_blocks(x.shape[0], norm)

    rows = D // (shards + 1)
    lanes = rows // 128
    pack[...] = jnp.zeros_like(pack)
    for owner in range(shards + 1):
        for j in range(lanes):
            at = owner * rows + j * 128
            pack[owner, j : j + 1, :] = gain_one[0:1, at : at + 128]
            pack[owner, lanes + j : lanes + j + 1, :] = gain_two[0:1, at : at + 128]
        pack[owner, 2 * lanes : 2 * lanes + 2, :] = gain_heads[0:2, :]

    def pack_copy(i):
        return send(pack.at[ahead(i)], pack_in.at[i], small[0].at[i], small[1].at[i], "fsdp", ahead(i))

    def sum_copy(i):
        return send(shard_sum, shard_in.at[i], small[2].at[i], small[3].at[i], "ctx", next_part(i))

    loop(shards, lambda i: pack_copy(i).start())
    shard_sum[...] = pack[shard]

    def add_pack(i):
        pack_copy(i).wait_recv()
        shard_sum[...] += pack_in[i]

    loop(shards, add_pack)
    loop(parts, lambda i: sum_copy(i).start())
    gain_out[...] = shard_sum[...]

    def add_sum(i):
        sum_copy(i).wait_recv()
        gain_out[...] += shard_in[i]

    loop(parts, add_sum)
    gathers[1].step(chips - 1)
    pump(PAIR_PARTS * (chips - 1) + 2, PAIR_PARTS * chips)

    def settle_pair(part):
        sems = [ref.at[part] for ref in pair_sems]
        Gather(pair_land, sems, part=tile(part, pair_size)).finish()

    loop(PAIR_PARTS, settle_pair)
    for h in range(2):
        gathers[h].finish()
        head_sums[h].finish()
    loop(shards, lambda i: pack_copy(i).wait_send())
    loop(parts, lambda i: sum_copy(i).wait_send())


def last(*operands):
    tokens, query_width = operands[0].shape
    heads = query_width // HEAD_SIZE
    parts = operands[5].shape[0]
    count = tokens // parts
    width = query_width + 2 * HEAD_SIZE
    head_width = width + query_width
    rows, pair_width = operands[-1].shape
    shards = D // rows
    chips = parts // 2
    return pl.pallas_call(
        functools.partial(last_kernel, heads),
        out_shape=(
            jax.ShapeDtypeStruct((count, D), F32),
            jax.ShapeDtypeStruct((16, 128), F32),
            jax.ShapeDtypeStruct((shards, rows, head_width), BF16),
            jax.ShapeDtypeStruct((parts, rows, head_width), BF16),
            jax.ShapeDtypeStruct((parts, rows, pair_width), BF16),
        ),
        in_specs=[WHOLE] * 10 + [HBM] + [WHOLE] * 4 + [HBM] * 3,
        out_specs=(WHOLE, WHOLE, HBM, WHOLE, HBM),
        scratch_shapes=[
            VMEM((parts, count, width), BF16),
            VMEM((8, HEAD_SIZE), F32),
            VMEM((tokens, HEAD_SIZE), F32),
            VMEM((tokens, HEAD_SIZE), F32),
            VMEM((QUERY_TILE, query_width), F32),
            VMEM((rows, pair_width), BF16),
            pltpu.SemaphoreType.DMA,
        ]
        + [pltpu.SemaphoreType.DMA((PAIR_PARTS, chips)) for _ in range(6)]
        + [
            VMEM((D, width), BF16),
            pltpu.SemaphoreType.DMA,
            VMEM((count, D), F32),
            VMEM((8, D), F32),
            VMEM((shards, 16, 128), F32),
            VMEM((shards, 16, 128), F32),
            VMEM((16, 128), F32),
            VMEM((parts, 16, 128), F32),
            VMEM((2, parts, count, slab_size(parts)), BF16),
            VMEM((2, parts, count, slab_size(parts)), BF16),
            VMEM((slab_size(parts), head_width), BF16),
            pltpu.SemaphoreType.DMA((5,)),
            VMEM((rows, head_width), BF16),
        ]
        + [pltpu.SemaphoreType.DMA((shards,))] * 2
        + [pltpu.SemaphoreType.DMA((parts,))] * 2
        + fsdp_scratch(shards, rows // 2, head_width)
        + fsdp_scratch(shards, rows // 2, head_width)
        + gather_scratch(chips)
        + gather_scratch(chips)
        + scatter_scratch(chips, count),
        compiler_params=params(5, 63),
        cost_estimate=cost(190),
        name="last",
    )(*operands)


def spread_kernel(width, head_source, pair_source, down_source, *targets):
    query, key, value, out, gate, up, down = targets
    second = width + HEAD_SIZE
    third = second + HEAD_SIZE
    query[...] = head_source[0, :, :width].astype(F32)
    key[...] = head_source[0, :, width:second].astype(F32)
    value[...] = head_source[0, :, second:third].astype(F32)
    out[...] = head_source[0, :, third:].astype(F32).T
    feed_width = gate.shape[1]
    gate[...] = pair_source[0, :, :feed_width].astype(F32)
    up[...] = pair_source[0, :, feed_width:].astype(F32)
    down[...] = down_source[0].astype(F32).T


def spread(head_parts, pair_parts, down_parts, width):
    parts, rows, _ = head_parts.shape
    feed_width = down_parts.shape[2]
    sources = (head_parts, pair_parts, down_parts)

    def side_by_side(columns):
        shape = jax.ShapeDtypeStruct((rows, parts * columns), F32)
        return shape, pl.BlockSpec((rows, columns), lambda i: (0, i))

    def stacked(columns):
        shape = jax.ShapeDtypeStruct((parts * columns, rows), F32)
        return shape, pl.BlockSpec((columns, rows), lambda i: (i, 0))

    outs = (
        side_by_side(width),
        side_by_side(HEAD_SIZE),
        side_by_side(HEAD_SIZE),
        stacked(width),
        side_by_side(feed_width),
        side_by_side(feed_width),
        stacked(feed_width),
    )
    return pl.pallas_call(
        functools.partial(spread_kernel, width),
        out_shape=tuple(shape for shape, _ in outs),
        grid=(parts,),
        in_specs=[pl.BlockSpec((1, *source.shape[1:]), lambda i: (i, 0, 0)) for source in sources],
        out_specs=tuple(spec for _, spec in outs),
        compiler_params=pltpu.CompilerParams(vmem_limit_bytes=60 * 1024 * 1024),
        name="spread",
    )(*sources)


def local(
    hidden_in,
    weight_query,
    key_weight_matrix,
    weight_value,
    weight_out,
    weight_gate,
    weight_up,
    weight_down,
    gain_attention,
    gain_feed,
    gain_query,
    gain_key,
    positions,
    token_block_index,
    grad_out,
):
    parts = lax.axis_size("ctx")
    shards = lax.axis_size("fsdp")
    shard = lax.axis_index("fsdp")
    heads = QUERY_HEADS // parts
    sharers = parts // KEY_VALUE_HEADS
    width = heads * HEAD_SIZE
    feed_width = FF // parts
    rows = D // shards
    head_rows = HEAD_SIZE // shards
    count = hidden_in.shape[1]
    tokens = parts * count

    own_gains = jnp.concatenate([gain_attention, gain_feed, gain_query, gain_key]).astype(F32)
    own_gains = jnp.pad(own_gains, (0, 2048 - own_gains.shape[0])).reshape(16, 128)
    own_tokens = jnp.pad(jnp.stack([positions[0], token_block_index[0]]), ((0, 6), (0, 0)))
    half = HEAD_SIZE // 2
    freq = THETA ** (-(jnp.arange(half).astype(F32) * 2.0 / HEAD_SIZE))
    freq = jnp.broadcast_to(jnp.concatenate([freq, freq]), (8, HEAD_SIZE))
    hidden, grad = hidden_in[0], grad_out[0]
    weights = (
        weight_query,
        key_weight_matrix,
        weight_value,
        weight_out,
        weight_gate,
        weight_up,
        weight_down,
    )
    (
        normed_all,
        grad_all,
        normed_two_all,
        activation,
        back,
        proj,
        cosine,
        sine,
        queries,
        keys,
        values,
        context,
        inverse,
        middle,
        gain_rows,
        gains,
        whole,
        heads_weight,
        out_weight,
        pair_weight,
        down_weight,
    ) = forward(hidden, grad, own_gains, own_tokens, freq, weights, shards, parts, heads)

    grad_middle, low_all, gain_two, down_parts, context_grad, hidden_out, _, _, feed_shard, _ = turn(
        back,
        pair_weight,
        down_weight,
        activation,
        out_weight,
        middle,
        gain_rows,
        grad_all,
        normed_two_all,
        shards,
    )
    grad_hidden, gain_sums, _, head_parts, feed_parts = last(
        queries,
        keys,
        values,
        context_grad,
        inverse,
        context.reshape(parts, count, width),
        proj,
        cosine,
        sine,
        whole,
        heads_weight,
        hidden,
        grad_middle,
        gain_rows,
        gain_two,
        normed_all,
        low_all,
        feed_shard,
    )

    gain_sums = gain_sums.reshape(-1)
    grad_query, grad_key, grad_value, grad_out_weight, grad_gate, grad_up, grad_down = spread(
        head_parts, feed_parts, down_parts, width
    )
    if sharers > 1:
        grad_key, grad_value = (
            part.reshape(rows, KEY_VALUE_HEADS, sharers, HEAD_SIZE).sum(axis=2).reshape(rows, -1)
            for part in (grad_key, grad_value)
        )
    return (
        hidden_out[None],
        grad_hidden[None],
        grad_query,
        grad_key,
        grad_value,
        grad_out_weight,
        grad_gate,
        grad_up,
        grad_down,
        gain_sums[:rows],
        gain_sums[rows : 2 * rows],
        lax.dynamic_slice_in_dim(gain_sums, 2 * rows + shard * head_rows, head_rows),
        lax.dynamic_slice_in_dim(gain_sums, 2 * rows + HEAD_SIZE + shard * head_rows, head_rows),
    )


def solution(mesh):
    tokens = P("fsdp", "ctx", None)
    by_rows = P("fsdp", None)
    by_columns = P(None, "fsdp")
    per_token = P("fsdp", "ctx")
    vector = P("fsdp")
    weights = (by_rows, by_rows, by_rows, by_columns, by_rows, by_rows, by_columns)
    return jax.shard_map(
        local,
        mesh=mesh,
        in_specs=(tokens, *weights, vector, vector, vector, vector, per_token, per_token, tokens),
        out_specs=(tokens, tokens, *weights, vector, vector, vector, vector),
        check_vma=False,
    )
```
